32 devices in a mesh: seq: 2 (over core), narrow: 4 (over y, x), wide: 4 (over z).
Axes of the slice: x: 2, y: 2, z: 4, core: 2. Of those that a mesh axis runs over, the one named last changes fastest.
Arguments:
- tokens: bfloat16 [8192, 2048], P('seq', 'narrow'), may hold values from -6 to 6
- attn_gain: float32 [2048], P('narrow'), may hold values from 0.5 to 1.5
- w_query: bfloat16 [2048, 2048], P('narrow', 'wide'), may hold values from -0.125 to 0.125
- w_key: bfloat16 [2048, 512], P('narrow', 'wide'), may hold values from -0.125 to 0.125
- w_value: bfloat16 [2048, 512], P('narrow', 'wide'), may hold values from -0.125 to 0.125
- w_out: bfloat16 [2048, 2048], P('wide', 'narrow'), may hold values from -2 to 2
- ffn_gain: float32 [2048], P('narrow'), may hold values from 0.5 to 1.5
- w_gate: bfloat16 [2048, 8192], P('narrow', 'wide'), may hold values from -0.125 to 0.125
- w_up: bfloat16 [2048, 8192], P('narrow', 'wide'), may hold values from -0.125 to 0.125
- w_down: bfloat16 [8192, 2048], P('wide', 'narrow'), may hold values from -0.0625 to 0.0625
- segment_ids: int32 [8192], replicated, may hold values from 0 to 2, as said below
- token_mask: int32 [8192], replicated, may hold values from 0 to 1, as said below
- out_grad: bfloat16 [8192, 2048], P('seq', 'narrow'), may hold values from -6 to 6
Outputs:
- result: bfloat16 [8192, 2048], P('seq', 'narrow')
- input_grad: float32 [8192, 2048], P('seq', 'narrow')
- grad_attn_gain: float32 [2048], P('narrow')
- grad_w_query: float32 [2048, 2048], P('narrow', 'wide')
- grad_w_key: float32 [2048, 512], P('narrow', 'wide')
- grad_w_value: float32 [2048, 512], P('narrow', 'wide')
- grad_w_out: float32 [2048, 2048], P('wide', 'narrow')
- grad_ffn_gain: float32 [2048], P('narrow')
- grad_w_gate: float32 [2048, 8192], P('narrow', 'wide')
- grad_w_up: float32 [2048, 8192], P('narrow', 'wide')
- grad_w_down: float32 [8192, 2048], P('wide', 'narrow')
The draws below stay inside these ranges and needn't reach their ends.
Inputs may be any that keep to these rules, and one draw needn't show every extreme that they name: `segment_ids`: the pack holds three sequences in order, ids 0, 1, 2, never falling: the first and the last hold 2 to 256 positions each, the middle one all the rest. `token_mask`: padding is the last positions of each sequence: 1 to 255 of the middle one; of the first and the last, one or more and fewer than the sequence's length; the first position of each sequence is a real token.
All inputs are finite; a program needn't handle non-finite values.
Results may differ from the reference program's by a relative error of at most 0.018.
Values may be sent and summed in bfloat16 or wider, within the bound.
A program may use at most 384 MiB of HBM per device.

```python
import jax
import jax.numpy as jnp
from jax import lax

D = 2048
HEADS = 32
KV_HEADS = 8
HD = 64
FF = 8192
TOKENS = 8192
QDIM = 2048
KVDIM = 512
PAD = 256


def pack_layout(key):
    layout_key = jax.random.fold_in(key, 4242)
    first_key, last_key, pad_first_key, pad_middle_key, pad_last_key = jax.random.split(layout_key, 5)
    first_len = jax.random.randint(first_key, (), 2, PAD + 1, dtype=jnp.int32)
    last_len = jax.random.randint(last_key, (), 2, PAD + 1, dtype=jnp.int32)
    first_cut = first_len
    second_cut = jnp.int32(TOKENS) - last_len
    token_index = jnp.arange(TOKENS, dtype=jnp.int32)
    segment = (token_index >= first_cut).astype(jnp.int32) + (token_index >= second_cut).astype(jnp.int32)
    pad_first = jax.random.randint(pad_first_key, (), 1, first_len, dtype=jnp.int32)
    pad_middle = jax.random.randint(pad_middle_key, (), 1, PAD, dtype=jnp.int32)
    pad_last = jax.random.randint(pad_last_key, (), 1, last_len, dtype=jnp.int32)
    seg_ends = jnp.stack([first_cut - pad_first, second_cut - pad_middle, jnp.int32(TOKENS) - pad_last])
    valid_end = jnp.where(segment == 0, seg_ends[0], jnp.where(segment == 1, seg_ends[1], seg_ends[2]))
    valid_flags = (token_index < valid_end).astype(jnp.int32)
    return (segment, valid_flags)


def draw_segment_ids(key, part):
    return pack_layout(key)[0]


def draw_token_mask(key, part):
    return pack_layout(key)[1]


def block_scale(rng, extent, cuts, smallest, largest):
    def one(dim, blocks):
        draws = jax.random.uniform(jax.random.fold_in(jax.random.fold_in(rng, 6), dim), (blocks,), jnp.float32, smallest / len(cuts), largest / len(cuts))
        return jnp.repeat(jnp.exp(draws), extent[dim] // blocks).reshape((-1,) + (1,) * (len(extent) - dim - 1))

    level = one(*cuts[0])
    for cut in cuts[1:]:
        level = level * one(*cut)
    return level


def scatter_about(key, extent, scale, limit, cuts=(), kind=jnp.bfloat16):
    level = block_scale(key, extent, cuts, -0.22, 0.18) if cuts else 1.0
    array = jax.random.normal(key, extent, jnp.float32) * scale * level
    return jnp.minimum(jnp.maximum(array, -limit), limit).astype(kind)


def setup_inputs(seed: int = 0) -> dict:
    streams_of = jax.random.split(jax.random.key(seed), 14)
    tokens = scatter_about(streams_of[0], (TOKENS, D), 1.0, 6.0, ((0, 2), (1, 4)))
    attn_gain = jnp.clip(1.0 + 0.1 * jax.random.normal(streams_of[1], (D,), jnp.float32), 0.5, 1.5)
    w_query = scatter_about(streams_of[2], (D, QDIM), D ** -0.5, 0.125, ((0, 4), (1, 4)))
    w_key = scatter_about(streams_of[3], (D, KVDIM), D ** -0.5, 0.125, ((0, 4), (1, 4)))
    w_value = scatter_about(streams_of[4], (D, KVDIM), D ** -0.5, 0.125, ((0, 4), (1, 4)))
    w_out = scatter_about(streams_of[5], (QDIM, D), (max(QDIM // 256, 1)) ** -0.5, 2.0, ((0, 4), (1, 4)))
    ffn_gain = jnp.clip(1.0 + 0.1 * jax.random.normal(streams_of[6], (D,), jnp.float32), 0.5, 1.5)
    w_gate = scatter_about(streams_of[7], (D, FF), D ** -0.5, 0.125, ((0, 4), (1, 4)))
    w_up = scatter_about(streams_of[8], (D, FF), D ** -0.5, 0.125, ((0, 4), (1, 4)))
    w_down = scatter_about(streams_of[9], (FF, D), FF ** -0.5, 0.0625, ((0, 4), (1, 4)))
    segment_ids = draw_segment_ids(jax.random.fold_in(streams_of[13], 71), 0)
    token_mask = draw_token_mask(jax.random.fold_in(streams_of[13], 71), 0)
    out_grad = scatter_about(streams_of[12], (TOKENS, D), 1.0, 6.0, ((0, 2), (1, 4)))
    return dict(tokens=tokens, attn_gain=attn_gain, w_query=w_query, w_key=w_key, w_value=w_value, w_out=w_out, ffn_gain=ffn_gain, w_gate=w_gate, w_up=w_up, w_down=w_down, segment_ids=segment_ids, token_mask=token_mask, out_grad=out_grad)


EPS = 1e-05
THETA = 500000.0
NEG = -1e+30

@jax.custom_vjp
def low(v):
    return lax.optimization_barrier(v.astype(jnp.bfloat16)).astype(jnp.float32)

@jax.custom_vjp
def low_back(v):
    return v

def low_keep(v):
    return (low(v), None)

def low_pass(kept, grad):
    return (grad,)

def back_keep(v):
    return (v, None)

def back_low(kept, grad):
    return (low(grad),)
low.defvjp(low_keep, low_pass)
low_back.defvjp(back_keep, back_low)

def positions(segment_ids):
    token_index = jnp.arange(segment_ids.shape[0], dtype=jnp.int32)
    seg_first = jnp.concatenate([jnp.ones((1,), dtype=bool), segment_ids[1:] != segment_ids[:-1]])
    seg_start = lax.cummax(jnp.where(seg_first, token_index, jnp.zeros_like(token_index)), axis=0)
    return token_index - seg_start

def rotation(token_pos):
    half_dim = HD // 2
    frequency = THETA ** (-2.0 * jnp.arange(half_dim, dtype=jnp.float32) / HD)
    angles = token_pos.astype(jnp.float32)[:, None] * frequency[None, :]
    cosine_table = jnp.concatenate([jnp.cos(angles), jnp.cos(angles)], axis=1)
    sine_table = jnp.concatenate([jnp.sin(angles), jnp.sin(angles)], axis=1)
    return (cosine_table, sine_table)

def rotate(vectors, cosine_table, sine_table, turn_sign):
    half_dim = HD // 2
    turned = jnp.concatenate([-vectors[..., half_dim:], vectors[..., :half_dim]], axis=-1)
    return vectors * cosine_table[:, None, :] + turn_sign * turned * sine_table[:, None, :]

def reference(tokens, attn_gain, w_query, w_key, w_value, w_out, ffn_gain, w_gate, w_up, w_down, segment_ids, token_mask, out_grad):
    total_tokens = segment_ids.shape[0]
    token_index = jnp.arange(total_tokens, dtype=jnp.int32)
    cosine_table, sine_table = rotation(positions(segment_ids))
    allowed = (segment_ids[:, None] == segment_ids[None, :]) & (token_index[None, :] <= token_index[:, None]) & (token_mask[None, :] == 1)
    group_size = HEADS // KV_HEADS
    score_scale = HD ** (-0.5)
    highest = lax.Precision.HIGHEST

    def matmul(left_side, right_side):
        return jnp.dot(left_side, right_side, precision=highest, preferred_element_type=jnp.float32)

    def head_attend(packed):
        query_one, key_one, value_one = packed
        scores = low_back(jnp.dot(query_one, key_one.T, precision=highest) * score_scale)
        scores = jnp.where(allowed, scores, NEG)
        row_top = lax.optimization_barrier(jnp.max(scores, axis=1, keepdims=True))
        exp_scores = jnp.exp(scores - row_top)
        attn_prob = low(exp_scores / lax.optimization_barrier(jnp.sum(exp_scores, axis=1, keepdims=True)))
        return jnp.dot(attn_prob, value_one, precision=highest)
    attend = jax.checkpoint(head_attend)

    def forward(layer_in, gain_first, query_w, key_w, value_w, out_w, gain_second, gate_w, up_w, down_w):
        scale_one = lax.rsqrt(lax.optimization_barrier(jnp.mean(layer_in * layer_in, axis=1, keepdims=True)) + EPS)
        h_one = low(layer_in * scale_one * gain_first)
        query_lin = low_back(matmul(h_one, query_w))
        key_lin = low_back(matmul(h_one, key_w))
        value_lin = low_back(matmul(h_one, value_w))
        query_rot = low(rotate(query_lin.reshape(total_tokens, HEADS, HD), cosine_table, sine_table, 1.0))
        key_rot = low(rotate(key_lin.reshape(total_tokens, KV_HEADS, HD), cosine_table, sine_table, 1.0))
        value_low = low(value_lin).reshape(total_tokens, KV_HEADS, HD)
        query_heads = jnp.transpose(query_rot, (1, 0, 2))
        key_heads = jnp.repeat(jnp.transpose(key_rot, (1, 0, 2)), group_size, axis=0)
        value_heads = jnp.repeat(jnp.transpose(value_low, (1, 0, 2)), group_size, axis=0)
        head_out = lax.map(attend, (query_heads, key_heads, value_heads))
        attn_heads = low(low_back(jnp.transpose(head_out, (1, 0, 2)).reshape(total_tokens, HEADS * HD)))
        middle = layer_in + low_back(matmul(attn_heads, out_w))
        scale_two = lax.rsqrt(lax.optimization_barrier(jnp.mean(middle * middle, axis=1, keepdims=True)) + EPS)
        h_two = low(middle * scale_two * gain_second)
        gate_lin = low_back(matmul(h_two, gate_w))
        up_lin = low_back(matmul(h_two, up_w))
        act_low = low(jax.nn.silu(gate_lin) * up_lin)
        return middle + matmul(act_low, down_w)
    result, pullback = jax.vjp(forward, tokens.astype(jnp.float32), attn_gain.astype(jnp.float32), w_query.astype(jnp.float32), w_key.astype(jnp.float32), w_value.astype(jnp.float32), w_out.astype(jnp.float32), ffn_gain.astype(jnp.float32), w_gate.astype(jnp.float32), w_up.astype(jnp.float32), w_down.astype(jnp.float32))
    cotangent = out_grad.astype(jnp.float32) * token_mask[:, None].astype(jnp.float32)
    gradients = pullback(cotangent)
    return (result.astype(jnp.bfloat16), gradients[0], gradients[1], gradients[2], gradients[3], gradients[4], gradients[5], gradients[6], gradients[7], gradients[8], gradients[9])
```

```python
import functools

import jax
import jax.numpy as jnp
from jax import lax
from jax.experimental import pallas as pl
from jax.experimental.pallas import tpu as pltpu
from jax.sharding import PartitionSpec as P

HD = 64
EPS = 1e-05
THETA = 500000.0
NEG = -1e30
SN = ("seq", "narrow")
NS = ("narrow", "seq")
BF = jnp.bfloat16
F32 = jnp.float32
NT = (((1,), (1,)), ((), ()))
TN = (((0,), (0,)), ((), ()))


def pieces_of(value):
    first = value.astype(BF).astype(F32)
    second = (value - first).astype(BF).astype(F32)
    third = (value - first - second).astype(BF).astype(F32)
    return first, second, third


def qkv_kernel(qw, x_ref, gain_ref, w_ref, cos_ref, sin_ref, h_ref, q_ref, kv_ref):
    x = x_ref[...].astype(F32)
    mean = jnp.mean(x * x, axis=1, keepdims=True)
    h = (x * lax.rsqrt(mean + EPS) * gain_ref[...]).astype(BF)
    h_ref[...] = h
    t = jnp.dot(h, w_ref[...], preferred_element_type=F32)
    width = t.shape[1]
    lane = lax.broadcasted_iota(jnp.int32, t.shape, 1)
    turned = jnp.where(
        lane % HD < HD // 2, -pltpu.roll(t, width - HD // 2, 1), pltpu.roll(t, HD // 2, 1)
    )
    copies = width // 128
    cos = jnp.concatenate([cos_ref[...]] * copies, axis=1)
    sin = jnp.concatenate([sin_ref[...]] * copies, axis=1)
    plain = (lane >= qw) & (lane % 128 >= HD)
    out = jnp.where(plain, t, t * cos + turned * sin)
    q_ref[...] = (out[:, :qw] * (HD ** -0.5)).astype(BF)
    kv_ref[...] = out[:, qw:].astype(BF)


def qkv_call(x, gain, w, cos, sin, qw):
    rows, d = x.shape
    width = w.shape[1]
    bm = min(256, rows)
    return pl.pallas_call(
        functools.partial(qkv_kernel, qw),
        grid=(rows // bm,),
        in_specs=[
            pl.BlockSpec((bm, d), lambda r: (r, 0)),
            pl.BlockSpec((1, d), lambda r: (0, 0)),
            pl.BlockSpec((d, width), lambda r: (0, 0)),
            pl.BlockSpec((bm, 128), lambda r: (r, 0)),
            pl.BlockSpec((bm, 128), lambda r: (r, 0)),
        ],
        out_specs=[
            pl.BlockSpec((bm, d), lambda r: (r, 0)),
            pl.BlockSpec((bm, qw), lambda r: (r, 0)),
            pl.BlockSpec((bm, width - qw), lambda r: (r, 0)),
        ],
        out_shape=[
            jax.ShapeDtypeStruct((rows, d), BF),
            jax.ShapeDtypeStruct((rows, qw), BF),
            jax.ShapeDtypeStruct((rows, width - qw), BF),
        ],
        cost_estimate=pl.CostEstimate(
            flops=2 * rows * d * width, bytes_accessed=4 * rows * d + 2 * d * width, transcendentals=rows
        ),
        compiler_params=pltpu.CompilerParams(vmem_limit_bytes=40 << 20),
        name="norm_qkv",
    )(x, gain, w, cos, sin)


class Plan:
    def __init__(self, total, group, wide):
        self.total, self.group, self.wide = total, group, wide
        self.chunk = total // (2 * group)
        self.cw = self.chunk // wide
        self.rows = 2 * self.chunk


def build_keys(plan, kv_ref, kf_ref, kx, vx):
    cw = plan.cw
    lane = lax.broadcasted_iota(jnp.int32, (cw, 128), 1)
    ones = jnp.where(lane < 3, 1.0, 0.0).astype(BF)

    def fill(c, carry):
        late = c >= plan.group
        owner = jnp.where(late, 2 * plan.group - 1 - c, c)
        for w in range(plan.wide):
            src = pl.multiple_of(owner * plan.rows + w * 2 * cw + jnp.where(late, cw, 0), cw)
            dst = pl.multiple_of(c * plan.chunk + w * cw, cw)
            kv = kv_ref[pl.ds(src, cw), :]
            kx[pl.ds(dst, cw), :] = jnp.where(lane < HD, kv, kf_ref[pl.ds(dst, cw), :])
            vx[pl.ds(dst, cw), :] = jnp.where(lane < HD, ones, kv)
        return carry

    lax.fori_loop(0, 2 * plan.group, fill, 0)


def split_heads(block, heads, low):
    tiles = []
    for h in range(heads):
        tile = block[:, (h // 2) * 128 : (h // 2 + 1) * 128]
        if (h % 2 == 0) != low:
            tile = pltpu.roll(tile, HD, 1)
        tiles.append(tile)
    return tiles


def join_heads(tiles, low):
    rows = tiles[0].shape[0]
    lane = lax.broadcasted_iota(jnp.int32, (rows, 128), 1)
    pairs = []
    for h in range(0, len(tiles), 2):
        first, second = tiles[h], tiles[h + 1]
        if low:
            second = pltpu.roll(second, HD, 1)
        else:
            first = pltpu.roll(first, HD, 1)
        pairs.append(jnp.where(lane < HD, first, second))
    return jnp.concatenate(pairs, axis=1)


def block_place(plan, s_ref):
    block = pl.program_id(1)
    w, late = block // 2, block % 2 == 1
    c = jnp.where(late, 2 * plan.group - 1 - s_ref[0], s_ref[0])
    return w, c


def forward_kernel(plan, heads, s_ref, q_ref, kv_ref, kf_ref, o_ref, qe_ref, kx, vx):
    cw, chunk = plan.cw, plan.chunk

    @pl.when(pl.program_id(1) == 0)
    def _():
        build_keys(plan, kv_ref, kf_ref, kx, vx)

    w, c = block_place(plan, s_ref)
    lane = lax.broadcasted_iota(jnp.int32, (cw, 128), 1)
    token = c * chunk + w * cw + lax.broadcasted_iota(jnp.int32, (cw, 128), 0)
    segment = (token >= s_ref[1]).astype(jnp.int32) + (token >= s_ref[2]).astype(jnp.int32)
    mark = jnp.where(lane == HD + segment, 1.0, 0.0)
    tiles = split_heads(q_ref[...].astype(F32), heads, True)
    q32 = jnp.concatenate([jnp.where(lane < HD, t, mark) for t in tiles], axis=0)
    q = q32.astype(BF)
    rows = heads * cw

    def step(j, carry, diagonal=False):
        top, acc = carry
        at = pl.ds(pl.multiple_of(j * chunk, chunk), chunk)
        s = lax.dot_general(q, kx[at, :], NT, preferred_element_type=F32)
        if diagonal:
            row = lax.broadcasted_iota(jnp.int32, (rows, chunk), 0) % cw + w * cw
            col = lax.broadcasted_iota(jnp.int32, (rows, chunk), 1)
            s = jnp.where(col <= row, s, NEG)
        new = jnp.maximum(top, jnp.max(s, axis=1, keepdims=True))
        p = jnp.exp(s - new).astype(BF)
        acc = acc * jnp.exp(top - new) + jnp.dot(p, vx[at, :], preferred_element_type=F32)
        return new, acc

    start = (jnp.full((rows, 1), NEG, F32), jnp.zeros((rows, 128), F32))
    carry = lax.fori_loop(0, c, step, start)
    top, acc = step(c, carry, True)
    total = acc[:, 0:1]
    out = acc / total
    o_ref[...] = join_heads([out[h * cw : (h + 1) * cw] for h in range(heads)], False).astype(BF)
    first, second, third = pieces_of(-(top + jnp.log(total)))
    wide_lane = lax.broadcasted_iota(jnp.int32, (rows, 128), 1)
    qe = jnp.where(wide_lane == HD + 3, first, q32)
    qe = jnp.where(wide_lane == HD + 4, second, qe)
    qe = jnp.where(wide_lane == HD + 5, third, qe)
    qe_ref[0, 0] = qe.astype(BF)


def forward_call(plan, scalars, q, kv, kf, kv_heads, heads):
    rows = plan.rows
    blocks = rows // plan.cw
    total = plan.total
    pairs = kv_heads * heads * total * rows // 2
    return pl.pallas_call(
        functools.partial(forward_kernel, plan, heads),
        grid_spec=pltpu.PrefetchScalarGridSpec(
            num_scalar_prefetch=1,
            grid=(kv_heads, blocks),
            in_specs=[
                pl.BlockSpec((plan.cw, heads * HD), lambda g, b, s: (b, g)),
                pl.BlockSpec((total, 128), lambda g, b, s: (0, g)),
                pl.BlockSpec((total, 128), lambda g, b, s: (0, 0)),
            ],
            out_specs=[
                pl.BlockSpec((plan.cw, heads * HD), lambda g, b, s: (b, g)),
                pl.BlockSpec((1, 1, heads * plan.cw, 128), lambda g, b, s: (g, b, 0, 0)),
            ],
            scratch_shapes=[pltpu.VMEM((total, 128), BF), pltpu.VMEM((total, 128), BF)],
        ),
        out_shape=[
            jax.ShapeDtypeStruct(q.shape, BF),
            jax.ShapeDtypeStruct((kv_heads, blocks, heads * plan.cw, 128), BF),
        ],
        cost_estimate=pl.CostEstimate(
            flops=8 * pairs * HD, bytes_accessed=8 * total * 128, transcendentals=pairs
        ),
        compiler_params=pltpu.CompilerParams(vmem_limit_bytes=48 << 20),
        name="attention_forward",
    )(scalars, q, kv, kf)


def backward_kernel(
    plan, heads, s_ref, qe_ref, kv_ref, kf_ref, o_ref, do_ref, dq_ref, dkv_ref, kx, vx, total
):
    cw, chunk = plan.cw, plan.chunk

    @pl.when(pl.program_id(1) == 0)
    def _():
        build_keys(plan, kv_ref, kf_ref, kx, vx)
        total[...] = jnp.zeros_like(total)

    w, c = block_place(plan, s_ref)
    rows = heads * cw
    lane = lax.broadcasted_iota(jnp.int32, (cw, 128), 1)
    o = split_heads(o_ref[...].astype(F32), heads, False)
    do = split_heads(do_ref[...].astype(F32), heads, False)
    marked = []
    for one, grad in zip(o, do):
        clean = jnp.where(lane >= HD, grad, 0.0)
        first, second, third = pieces_of(-jnp.sum(one * clean, axis=1, keepdims=True))
        tile = jnp.where(lane == 0, first, clean)
        tile = jnp.where(lane == 1, second, tile)
        marked.append(jnp.where(lane == 2, third, tile))
    dox32 = jnp.concatenate(marked, axis=0)
    wide_lane = lax.broadcasted_iota(jnp.int32, (rows, 128), 1)
    dox = dox32.astype(BF)
    do_clean = jnp.where(wide_lane >= HD, dox32, 0.0).astype(BF)
    q = qe_ref[0, 0]
    q_clean = jnp.where(wide_lane < HD, q.astype(F32), 0.0).astype(BF)

    def step(j, dq, diagonal=False):
        at = pl.ds(pl.multiple_of(j * chunk, chunk), chunk)
        key = kx[at, :]
        s = lax.dot_general(key, q, NT, preferred_element_type=F32)
        if diagonal:
            row = lax.broadcasted_iota(jnp.int32, (chunk, rows), 1) % cw + w * cw
            col = lax.broadcasted_iota(jnp.int32, (chunk, rows), 0)
            s = jnp.where(col <= row, s, NEG)
        p = jnp.exp(s)
        dp = lax.dot_general(vx[at, :], dox, NT, preferred_element_type=F32)
        ds = (p * dp).astype(BF)
        total[at, :] += jnp.dot(ds, q_clean, preferred_element_type=F32) + jnp.dot(
            p.astype(BF), do_clean, preferred_element_type=F32
        )
        return dq + lax.dot_general(ds, key, TN, preferred_element_type=F32)

    dq = lax.fori_loop(0, c, step, jnp.zeros((rows, 128), F32))
    dq = step(c, dq, True) * (HD ** -0.5)
    dq_ref[...] = join_heads([dq[h * cw : (h + 1) * cw] for h in range(heads)], True)

    @pl.when(pl.program_id(1) == pl.num_programs(1) - 1)
    def _():
        def put(c, carry):
            late = c >= plan.group
            owner = jnp.where(late, 2 * plan.group - 1 - c, c)
            for w in range(plan.wide):
                dst = pl.multiple_of(owner * plan.rows + w * 2 * cw + jnp.where(late, cw, 0), cw)
                src = pl.multiple_of(c * chunk + w * cw, cw)
                dkv_ref[pl.ds(dst, cw), :] = total[pl.ds(src, cw), :].astype(BF)
            return carry

        lax.fori_loop(0, 2 * plan.group, put, 0)


def backward_call(plan, scalars, qe, kv, kf, o, do, kv_heads, heads):
    rows = plan.rows
    blocks = rows // plan.cw
    total = plan.total
    pairs = kv_heads * heads * total * rows // 2
    return pl.pallas_call(
        functools.partial(backward_kernel, plan, heads),
        grid_spec=pltpu.PrefetchScalarGridSpec(
            num_scalar_prefetch=1,
            grid=(kv_heads, blocks),
            in_specs=[
                pl.BlockSpec((1, 1, heads * plan.cw, 128), lambda g, b, s: (g, b, 0, 0)),
                pl.BlockSpec((total, 128), lambda g, b, s: (0, g)),
                pl.BlockSpec((total, 128), lambda g, b, s: (0, 0)),
                pl.BlockSpec((plan.cw, heads * HD), lambda g, b, s: (b, g)),
                pl.BlockSpec((plan.cw, heads * HD), lambda g, b, s: (b, g)),
            ],
            out_specs=[
                pl.BlockSpec((plan.cw, heads * HD), lambda g, b, s: (b, g)),
                pl.BlockSpec((total, 128), lambda g, b, s: (0, g)),
            ],
            scratch_shapes=[
                pltpu.VMEM((total, 128), BF),
                pltpu.VMEM((total, 128), BF),
                pltpu.VMEM((total, 128), F32),
            ],
        ),
        out_shape=[
            jax.ShapeDtypeStruct(o.shape, F32),
            jax.ShapeDtypeStruct((total, kv_heads * 128), BF),
        ],
        cost_estimate=pl.CostEstimate(
            flops=20 * pairs * HD, bytes_accessed=8 * total * 128, transcendentals=pairs
        ),
        compiler_params=pltpu.CompilerParams(vmem_limit_bytes=56 << 20),
        name="attention_backward",
    )(scalars, qe, kv, kf, o, do)


def half_of(weight, seq_index, seq_count):
    part = weight.shape[0] // seq_count
    return lax.dynamic_slice_in_dim(weight, seq_index * part, part, 0)


def body(
    tokens, attn_gain, w_query, w_key, w_value, w_out, ffn_gain, w_gate, w_up, w_down,
    segment_ids, token_mask, out_grad,
):
    seq_count = lax.axis_size("seq")
    narrow = lax.axis_size("narrow")
    wide = lax.axis_size("wide")
    group = seq_count * narrow
    seq_index = lax.axis_index("seq")
    narrow_index = lax.axis_index("narrow")
    wide_index = lax.axis_index("wide")
    index = seq_index * narrow + narrow_index
    total = segment_ids.shape[0]
    plan = Plan(total, group, wide)
    chunk, cw, rows = plan.chunk, plan.cw, plan.rows
    own = rows // wide
    d_part = tokens.shape[1]
    d = d_part * narrow
    qw = w_query.shape[1]
    kw = w_key.shape[1]
    kv_heads = kw // HD
    heads = qw // kw
    ff = w_gate.shape[1]

    start_one = jnp.sum((segment_ids < 1).astype(jnp.int32))
    start_two = jnp.sum((segment_ids < 2).astype(jnp.int32))
    scalars = jnp.stack([index, start_one, start_two]).astype(jnp.int32)

    def to_rows(values):
        parts = values.reshape(group, chunk, d_part)
        parts = jnp.where(seq_index == 1, parts[::-1], parts)
        got = lax.all_to_all(parts, SN, 0, 0, tiled=True)
        got = got.reshape(2, narrow, wide, cw, d_part)
        return jnp.transpose(got, (2, 0, 3, 1, 4)).reshape(rows, d)

    def from_rows(values):
        parts = values.astype(BF).reshape(2, cw, narrow, d_part)
        parts = jnp.transpose(parts, (0, 2, 1, 3)).reshape(group, cw, d_part)
        got = lax.all_to_all(parts, SN, 0, 0, tiled=True)
        every = lax.all_gather(got, "wide", axis=0)
        every = jnp.where(seq_index == 1, every[:, ::-1], every)
        return jnp.transpose(every, (1, 0, 2, 3)).reshape(group * chunk, d_part)

    def gather_weight(weight):
        return lax.all_gather(half_of(weight, seq_index, seq_count), NS, axis=0, tiled=True)

    def scatter_grad(grad):
        mine = lax.psum_scatter(grad.astype(BF), NS, scatter_dimension=0, tiled=True)
        return lax.all_gather(mine, "seq", axis=0, tiled=True).astype(F32)

    def wide_scatter(values):
        return lax.psum_scatter(values.astype(BF), "wide", scatter_dimension=0, tiled=True).astype(F32)

    def wide_gather(values):
        return lax.all_gather(values, "wide", axis=0, tiled=True)

    def own_rows(values):
        return lax.dynamic_slice_in_dim(values, wide_index * own, own, 0)

    x_rows = to_rows(tokens)
    w_kv = jnp.concatenate(
        [w_key.reshape(d_part, kv_heads, 1, HD), w_value.reshape(d_part, kv_heads, 1, HD)], axis=2
    ).reshape(d_part, 2 * kw)
    w_qkv = gather_weight(jnp.concatenate([w_query, w_kv], axis=1))
    gains = lax.all_gather(jnp.stack([attn_gain, ffn_gain]), "narrow", axis=1, tiled=True)
    gain_one, gain_two = gains[0:1], gains[1:2]

    row = jnp.arange(rows, dtype=jnp.int32)
    row_chunk = jnp.where((row // cw) % 2 == 1, 2 * group - 1 - index, index)
    row_token = row_chunk * chunk + (row // (2 * cw)) * cw + row % cw
    row_start = jnp.where(row_token >= start_two, start_two, jnp.where(row_token >= start_one, start_one, 0))
    row_pos = (row_token - row_start).astype(F32)
    frequency = THETA ** (-2.0 * jnp.arange(HD // 2, dtype=F32) / HD)
    angles = row_pos[:, None] * jnp.tile(frequency, 4)[None, :]
    cos, sin = jnp.cos(angles), jnp.sin(angles)

    h_one, q, kv = qkv_call(x_rows, gain_one, w_qkv, cos, sin, qw)
    kv_all = lax.all_gather(kv, SN, axis=0, tiled=True)

    lane = jnp.arange(128, dtype=jnp.int32)[None, :]
    closed = (segment_ids[:, None] != lane - HD) | (token_mask[:, None] != 1)
    kf = jnp.where((lane >= HD) & (lane < HD + 3) & closed, NEG, 0.0)
    kf = jnp.where((lane >= HD + 3) & (lane < HD + 6), 1.0, kf).astype(BF)

    o, qe = forward_call(plan, scalars, q, kv_all, kf, kv_heads, heads)

    w_o = gather_weight(w_out).reshape(narrow, qw, d_part)
    w_gu = gather_weight(jnp.concatenate([w_gate, w_up], axis=1))
    w_dn = gather_weight(w_down).reshape(narrow, ff, d_part)

    def times_split(left, weight):
        out = lax.dot_general(left, weight, (((1,), (1,)), ((), ())), preferred_element_type=F32)
        return out.reshape(left.shape[0], d)

    def times_split_back(left, weight):
        left = left.reshape(left.shape[0], narrow, d_part)
        return lax.dot_general(left, weight, (((1, 2), (0, 2)), ((), ())), preferred_element_type=F32)

    x_own = own_rows(x_rows).astype(F32)
    x2 = x_own + wide_scatter(times_split(o, w_o))
    r2 = lax.rsqrt(jnp.mean(x2 * x2, axis=1, keepdims=True) + EPS)
    z2 = x2 * r2
    h_two = wide_gather((z2 * gain_two).astype(BF))
    gate = jnp.dot(h_two, w_gu[:, :ff], preferred_element_type=F32)
    up = jnp.dot(h_two, w_gu[:, ff:], preferred_element_type=F32)
    sig = jax.nn.sigmoid(gate)
    act = (gate * sig * up).astype(BF)
    result = from_rows(x2 + wide_scatter(times_split(act, w_dn)))

    row_valid = lax.dynamic_slice_in_dim(token_mask, seq_index * (group * chunk), group * chunk, 0)
    g_rows = to_rows(jnp.where(row_valid[:, None] == 1, out_grad, jnp.zeros_like(out_grad)))
    d_act = times_split_back(g_rows, w_dn)
    d_gate = d_act * up * sig * (1.0 + gate * (1.0 - sig))
    d_up = d_act * gate * sig
    dgu = jnp.concatenate([d_gate, d_up], axis=1).astype(BF)
    dh2 = wide_scatter(lax.dot_general(dgu, w_gu, NT, preferred_element_type=F32))
    grad_gain_two = jnp.sum(dh2 * z2, axis=0)
    dz2 = dh2 * gain_two
    dx2 = own_rows(g_rows).astype(F32) + r2 * (dz2 - z2 * jnp.mean(dz2 * z2, axis=1, keepdims=True))
    db = wide_gather(dx2.astype(BF))
    do = times_split_back(db, w_o).astype(BF)
    dq, dkv = backward_call(plan, scalars, qe, kv_all, kf, o, do, kv_heads, heads)
    dkv = lax.psum_scatter(dkv, SN, scatter_dimension=0, tiled=True).astype(F32)

    def turn_back(values):
        left, right = jnp.roll(values, -(HD // 2), 1), jnp.roll(values, HD // 2, 1)
        lanes = jnp.arange(values.shape[1])[None, :]
        turned = jnp.where(lanes % HD < HD // 2, -left, right)
        copies = values.shape[1] // 128
        return values * jnp.tile(cos, (1, copies)) - turned * jnp.tile(sin, (1, copies))

    is_value = (jnp.arange(2 * kw) % 128 >= HD)[None, :]
    dqkv = jnp.concatenate([turn_back(dq), jnp.where(is_value, dkv, turn_back(dkv))], axis=1).astype(BF)
    dh1 = wide_scatter(lax.dot_general(dqkv, w_qkv, NT, preferred_element_type=F32))
    r1 = lax.rsqrt(jnp.mean(x_own * x_own, axis=1, keepdims=True) + EPS)
    z1 = x_own * r1
    grad_gain_one = jnp.sum(dh1 * z1, axis=0)
    dz1 = dh1 * gain_one
    dx = dx2 + r1 * (dz1 - z1 * jnp.mean(dz1 * z1, axis=1, keepdims=True))
    input_grad = from_rows(dx).astype(F32)

    def tn(left, right):
        return lax.dot_general(left, right, TN, preferred_element_type=F32)

    grad_gu = scatter_grad(tn(h_two, dgu))
    grad_dn = scatter_grad(
        jnp.transpose(tn(act, g_rows).astype(BF).reshape(ff, narrow, d_part), (1, 0, 2)).reshape(narrow * ff, d_part)
    )
    grad_o = scatter_grad(
        jnp.transpose(tn(o, db).astype(BF).reshape(qw, narrow, d_part), (1, 0, 2)).reshape(narrow * qw, d_part)
    )
    grad_qkv = scatter_grad(tn(h_one, dqkv))
    gain_grads = lax.psum(jnp.stack([grad_gain_one, grad_gain_two]), ("seq", "narrow", "wide"))
    gain_grads = lax.dynamic_slice_in_dim(gain_grads, narrow_index * d_part, d_part, 1)
    grad_kv = grad_qkv[:, qw:].reshape(d_part, kv_heads, 2, HD)
    return (
        result,
        input_grad,
        gain_grads[0],
        grad_qkv[:, :qw],
        grad_kv[:, :, 0].reshape(d_part, kw),
        grad_kv[:, :, 1].reshape(d_part, kw),
        grad_o,
        gain_grads[1],
        grad_gu[:, :ff],
        grad_gu[:, ff:],
        grad_dn,
    )


def solution(mesh):
    width_in, width_out = P("narrow", "wide"), P("wide", "narrow")
    acts = P("seq", "narrow")
    return jax.shard_map(
        body,
        mesh=mesh,
        in_specs=(
            acts, P("narrow"), width_in, width_in, width_in, width_out, P("narrow"),
            width_in, width_in, width_out, P(), P(), acts,
        ),
        out_specs=(
            acts, acts, P("narrow"), width_in, width_in, width_in, width_out, P("narrow"),
            width_in, width_in, width_out,
        ),
        check_vma=False,
    )
```

```python
import functools

import jax
import jax.numpy as jnp
from jax import lax
from jax.experimental import pallas as pl
from jax.experimental.pallas import tpu as pltpu
from jax.sharding import PartitionSpec as P

HD = 64
EPS = 1e-05
THETA = 500000.0
NEG = -1e30
SN = ("seq", "narrow")
NS = ("narrow", "seq")
BF = jnp.bfloat16
F32 = jnp.float32
NT = (((1,), (1,)), ((), ()))
TN = (((0,), (0,)), ((), ()))


def pieces_of(value):
    first = value.astype(BF).astype(F32)
    second = (value - first).astype(BF).astype(F32)
    third = (value - first - second).astype(BF).astype(F32)
    return first, second, third


class Plan:
    def __init__(self, total, group, wide):
        self.total, self.group, self.wide = total, group, wide
        self.chunk = total // (2 * group)
        self.cw = self.chunk // wide
        self.rows = 2 * self.chunk
        self.own = 2 * self.cw


def block_of(plan, s_ref, r):
    return lax.rem(s_ref[3] + r, plan.wide)


def near_of(plan, z, p):
    side = jnp.minimum(z, plan.wide - 1 - z)
    both = jnp.where(lax.rem(p, 2) == 1, z + (p + 1) // 2, z - p // 2)
    one = jnp.where(z <= plan.wide - 1 - z, z + p - side, z - p + side)
    return jnp.where(p <= 2 * side, both, one)


def turn(values, sign):
    width = values.shape[1]
    lane = lax.broadcasted_iota(jnp.int32, values.shape, 1)
    left, right = pltpu.roll(values, width - HD // 2, 1), pltpu.roll(values, HD // 2, 1)
    return jnp.where(lane % HD < HD // 2, -sign * left, sign * right)


def widen(table, width):
    return jnp.concatenate([table] * (width // 128), axis=1) if width > 128 else table


def qkv_kernel(plan, qw, s_ref, x_ref, gain_ref, w_ref, cos_ref, sin_ref, h_ref, q_ref, kv_ref, own_ref, x_scr):
    narrow = plan.group // 2
    part = x_ref.shape[3]
    for half in range(2):
        for n in range(narrow):
            x_scr[half * plan.cw : (half + 1) * plan.cw, n * part : (n + 1) * part] = x_ref[
                s_ref[0] ^ (half * narrow + n), 0
            ]
    low = x_scr[...]

    @pl.when(pl.program_id(0) == 0)
    def _():
        own_ref[...] = low

    x = low.astype(F32)
    mean = jnp.mean(x * x, axis=1, keepdims=True)
    h = (x * lax.rsqrt(mean + EPS) * gain_ref[...]).astype(BF)
    h_ref[...] = h
    t = jnp.dot(h, w_ref[...], preferred_element_type=F32)
    width = t.shape[1]
    lane = lax.broadcasted_iota(jnp.int32, t.shape, 1)
    plain = (lane >= qw) & (lane % 128 >= HD)
    out = jnp.where(plain, t, t * widen(cos_ref[...], width) + turn(t, 1.0) * widen(sin_ref[...], width))
    q_ref[...] = (out[:, :qw] * (HD ** -0.5)).astype(BF)
    kv_ref[...] = out[:, qw:].astype(BF)


def qkv_call(plan, scalars, x, gain, w, cos, sin, qw):
    part = x.shape[3]
    d = part * plan.group // 2
    width = w.shape[1]
    rows, bm = plan.rows, plan.own
    return pl.pallas_call(
        functools.partial(qkv_kernel, plan, qw),
        grid_spec=pltpu.PrefetchScalarGridSpec(
            num_scalar_prefetch=1,
            grid=(plan.wide,),
            in_specs=[
                pl.BlockSpec((plan.group, 1, plan.cw, part), lambda r, s: (0, block_of(plan, s, r), 0, 0)),
                pl.BlockSpec((1, d), lambda r, s: (0, 0)),
                pl.BlockSpec((d, width), lambda r, s: (0, 0)),
                pl.BlockSpec((bm, 128), lambda r, s: (r, 0)),
                pl.BlockSpec((bm, 128), lambda r, s: (r, 0)),
            ],
            out_specs=[
                pl.BlockSpec((bm, d), lambda r, s: (r, 0)),
                pl.BlockSpec((bm, qw), lambda r, s: (r, 0)),
                pl.BlockSpec((bm, width - qw), lambda r, s: (r, 0)),
                pl.BlockSpec((bm, d), lambda r, s: (0, 0)),
            ],
            scratch_shapes=[pltpu.VMEM((bm, d), BF)],
        ),
        out_shape=[
            jax.ShapeDtypeStruct((rows, d), BF),
            jax.ShapeDtypeStruct((rows, qw), BF),
            jax.ShapeDtypeStruct((rows, width - qw), BF),
            jax.ShapeDtypeStruct((bm, d), BF),
        ],
        cost_estimate=pl.CostEstimate(
            flops=2 * rows * d * width, bytes_accessed=4 * rows * d + 2 * d * width, transcendentals=rows
        ),
        compiler_params=pltpu.CompilerParams(vmem_limit_bytes=40 << 20),
        name="norm_qkv",
    )(scalars, x, gain, w, cos, sin)


def keys_kernel(plan, s_ref, kv_ref, kf_ref, kx_ref, vx_ref):
    cw, group = plan.cw, plan.group
    lane = lax.broadcasted_iota(jnp.int32, (cw, 128), 1)
    ones = jnp.where(lane < 3, 1.0, 0.0).astype(BF)

    @pl.loop(0, 2 * group)
    def _(c):
        late = c >= group
        owner = jnp.where(late, 2 * group - 1 - c, c)
        for r in range(plan.wide):
            at = pl.ds(pl.multiple_of(c * plan.chunk + block_of(plan, s_ref, r) * cw, cw), cw)
            kv = kv_ref[s_ref[0] ^ owner, r, jnp.where(late, 1, 0)]
            kx_ref[0, at, :] = jnp.where(lane < HD, kv, kf_ref[at, :])
            vx_ref[0, at, :] = jnp.where(lane < HD, ones, kv)


def keys_call(plan, scalars, kv, kf, kv_heads):
    group, total = plan.group, plan.total
    kv = kv.reshape(group, plan.wide, 2, plan.cw, kv_heads * 128)
    out = pl.BlockSpec((1, total, 128), lambda g, s: (g, 0, 0))
    return pl.pallas_call(
        functools.partial(keys_kernel, plan),
        grid_spec=pltpu.PrefetchScalarGridSpec(
            num_scalar_prefetch=1,
            grid=(kv_heads,),
            in_specs=[
                pl.BlockSpec((group, plan.wide, 2, plan.cw, 128), lambda g, s: (0, 0, 0, 0, g)),
                pl.BlockSpec((total, 128), lambda g, s: (0, 0)),
            ],
            out_specs=[out, out],
        ),
        out_shape=[jax.ShapeDtypeStruct((kv_heads, total, 128), BF)] * 2,
        cost_estimate=pl.CostEstimate(
            flops=kv_heads * total * 128, bytes_accessed=8 * kv_heads * total * 128, transcendentals=0
        ),
        compiler_params=pltpu.CompilerParams(vmem_limit_bytes=40 << 20),
        name="keys",
    )(scalars, kv, kf)


def split_heads(block, heads, low):
    tiles = []
    for h in range(heads):
        tile = block[:, (h // 2) * 128 : (h // 2 + 1) * 128]
        if (h % 2 == 0) != low:
            tile = pltpu.roll(tile, HD, 1)
        tiles.append(tile)
    return tiles


def join_heads(tiles, low):
    rows = tiles[0].shape[0]
    lane = lax.broadcasted_iota(jnp.int32, (rows, 128), 1)
    pairs = []
    for h in range(0, len(tiles), 2):
        first, second = tiles[h], tiles[h + 1]
        if low:
            second = pltpu.roll(second, HD, 1)
        else:
            first = pltpu.roll(first, HD, 1)
        pairs.append(jnp.where(lane < HD, first, second))
    return jnp.concatenate(pairs, axis=1)


def chunk_of(plan, s_ref, half):
    return jnp.where(half == 1, 2 * plan.group - 1 - s_ref[0], s_ref[0])


def forward_kernel(plan, heads, r, s_ref, q_ref, kx, vx, o_ref, qe_ref):
    cw, chunk = plan.cw, plan.chunk
    w, c = block_of(plan, s_ref, r), chunk_of(plan, s_ref, pl.program_id(1))
    lane = lax.broadcasted_iota(jnp.int32, (cw, 128), 1)
    token = c * chunk + w * cw + lax.broadcasted_iota(jnp.int32, (cw, 128), 0)
    segment = (token >= s_ref[1]).astype(jnp.int32) + (token >= s_ref[2]).astype(jnp.int32)
    mark = jnp.where(lane == HD + segment, 1.0, 0.0)
    tiles = split_heads(q_ref[...].astype(F32), heads, True)
    q32 = jnp.concatenate([jnp.where(lane < HD, t, mark) for t in tiles], axis=0)
    q = q32.astype(BF)
    rows = heads * cw

    def step(j, carry, diagonal=False):
        top, acc = carry
        at = pl.ds(pl.multiple_of(j * chunk, chunk), chunk)
        s = lax.dot_general(q, kx[0, at, :], NT, preferred_element_type=F32)
        if diagonal:
            row = lax.broadcasted_iota(jnp.int32, (rows, chunk), 0) % cw + w * cw
            col = lax.broadcasted_iota(jnp.int32, (rows, chunk), 1)
            s = jnp.where(col <= row, s, NEG)
        new = jnp.maximum(top, jnp.max(s, axis=1, keepdims=True))
        p = jnp.exp(s - new).astype(BF)
        acc = acc * jnp.exp(top - new) + jnp.dot(p, vx[0, at, :], preferred_element_type=F32)
        return new, acc

    start = (jnp.full((rows, 1), NEG, F32), jnp.zeros((rows, 128), F32))
    carry = lax.fori_loop(0, c, step, start)
    top, acc = step(c, carry, True)
    total = acc[:, 0:1]
    out = acc / total
    o_ref[...] = join_heads([out[h * cw : (h + 1) * cw] for h in range(heads)], False).astype(BF)
    first, second, third = pieces_of(-(top + jnp.log(total)))
    wide_lane = lax.broadcasted_iota(jnp.int32, (rows, 128), 1)
    qe = jnp.where(wide_lane == HD + 3, first, q32)
    qe = jnp.where(wide_lane == HD + 4, second, qe)
    qe = jnp.where(wide_lane == HD + 5, third, qe)
    qe_ref[0, 0] = qe.astype(BF)


def forward_call(plan, scalars, q, kx, vx, kv_heads, heads, r):
    total, cw = plan.total, plan.cw
    pairs = kv_heads * heads * total * plan.own // 2
    keys = pl.BlockSpec((1, total, 128), lambda g, b, s: (g, 0, 0))
    return pl.pallas_call(
        functools.partial(forward_kernel, plan, heads, r),
        grid_spec=pltpu.PrefetchScalarGridSpec(
            num_scalar_prefetch=1,
            grid=(kv_heads, 2),
            in_specs=[pl.BlockSpec((cw, heads * HD), lambda g, b, s: (2 * r + b, g)), keys, keys],
            out_specs=[
                pl.BlockSpec((cw, heads * HD), lambda g, b, s: (b, g)),
                pl.BlockSpec((1, 1, heads * cw, 128), lambda g, b, s: (g, b, 0, 0)),
            ],
        ),
        out_shape=[
            jax.ShapeDtypeStruct((plan.own, q.shape[1]), BF),
            jax.ShapeDtypeStruct((kv_heads, 2, heads * cw, 128), BF),
        ],
        cost_estimate=pl.CostEstimate(
            flops=16 * pairs * HD, bytes_accessed=8 * total * 128, transcendentals=pairs
        ),
        compiler_params=pltpu.CompilerParams(vmem_limit_bytes=48 << 20),
        name="attention_forward",
    )(scalars, q, kx, vx)


def backward_kernel(plan, heads, r, first_call, s_ref, qe_ref, kx, vx, o_ref, do_ref, cos_ref, sin_ref, *refs):
    dq_ref, total = refs[-2:]
    cw, chunk = plan.cw, plan.chunk
    half = pl.program_id(0)

    @pl.when(half == 0)
    def _():
        total[...] = jnp.zeros_like(total) if first_call else refs[0][...]

    w, c = block_of(plan, s_ref, r), chunk_of(plan, s_ref, half)
    rows = heads * cw
    lane = lax.broadcasted_iota(jnp.int32, (cw, 128), 1)
    o = split_heads(o_ref[...].astype(F32), heads, False)
    do = split_heads(do_ref[...].astype(F32), heads, False)
    marked = []
    for one, grad in zip(o, do):
        clean = jnp.where(lane >= HD, grad, 0.0)
        first, second, third = pieces_of(-jnp.sum(one * clean, axis=1, keepdims=True))
        tile = jnp.where(lane == 0, first, clean)
        tile = jnp.where(lane == 1, second, tile)
        marked.append(jnp.where(lane == 2, third, tile))
    dox32 = jnp.concatenate(marked, axis=0)
    wide_lane = lax.broadcasted_iota(jnp.int32, (rows, 128), 1)
    dox = dox32.astype(BF)
    do_clean = jnp.where(wide_lane >= HD, dox32, 0.0).astype(BF)
    q = qe_ref[0, 0]
    q_clean = jnp.where(wide_lane < HD, q.astype(F32), 0.0).astype(BF)

    def step(j, dq, diagonal=False):
        at = pl.ds(pl.multiple_of(j * chunk, chunk), chunk)
        key = kx[0, at, :]
        s = lax.dot_general(key, q, NT, preferred_element_type=F32)
        if diagonal:
            row = lax.broadcasted_iota(jnp.int32, (chunk, rows), 1) % cw + w * cw
            col = lax.broadcasted_iota(jnp.int32, (chunk, rows), 0)
            s = jnp.where(col <= row, s, NEG)
        p = jnp.exp(s)
        dp = lax.dot_general(vx[0, at, :], dox, NT, preferred_element_type=F32)
        ds = (p * dp).astype(BF)
        total[at, :] += jnp.dot(ds, q_clean, preferred_element_type=F32) + jnp.dot(
            p.astype(BF), do_clean, preferred_element_type=F32
        )
        return dq + lax.dot_general(ds, key, TN, preferred_element_type=F32)

    dq = lax.fori_loop(0, c, step, jnp.zeros((rows, 128), F32))
    dq = step(c, dq, True) * (HD ** -0.5)
    dq = join_heads([dq[h * cw : (h + 1) * cw] for h in range(heads)], True)
    width = dq.shape[1]
    dq = dq * widen(cos_ref[...], width) + turn(dq, -1.0) * widen(sin_ref[...], width)
    dq_ref[...] = dq.astype(BF)


def backward_call(plan, scalars, qe, kx, vx, o, do, cos, sin, heads, r, g, before):
    total, cw = plan.total, plan.cw
    pairs = heads * total * plan.own // 2
    once = pl.Buffered(1)
    keys = pl.BlockSpec((1, total, 128), lambda b, s: (g, 0, 0), pipeline_mode=once)
    some = pl.BlockSpec((cw, heads * HD), lambda b, s: (b, g))
    table = pl.BlockSpec((cw, 128), lambda b, s: (2 * r + b, 0))
    sums = pl.BlockSpec((total, 128), lambda b, s: (0, 0), pipeline_mode=once)
    operands = [scalars, qe, kx, vx, o, do, cos, sin]
    in_specs = [
        pl.BlockSpec((1, 1, heads * cw, 128), lambda b, s: (g, b, 0, 0)),
        keys, keys, some, some, table, table,
    ]
    aliases = {}
    if before is not None:
        operands.append(before)
        in_specs.append(sums)
        aliases = {8: 1}
    return pl.pallas_call(
        functools.partial(backward_kernel, plan, heads, r, before is None),
        grid_spec=pltpu.PrefetchScalarGridSpec(
            num_scalar_prefetch=1,
            grid=(2,),
            in_specs=in_specs,
            out_specs=[pl.BlockSpec((cw, heads * HD), lambda b, s: (b, 0)), sums],
        ),
        out_shape=[
            jax.ShapeDtypeStruct((plan.own, heads * HD), BF),
            jax.ShapeDtypeStruct((total, 128), F32),
        ],
        input_output_aliases=aliases,
        cost_estimate=pl.CostEstimate(
            flops=36 * pairs * HD, bytes_accessed=12 * total * 128, transcendentals=pairs
        ),
        compiler_params=pltpu.CompilerParams(vmem_limit_bytes=56 << 20),
        name="attention_backward",
    )(*operands)


def rows_kernel(plan, s_ref, x_ref, out_ref):
    narrow = plan.group // 2
    part = x_ref.shape[3]
    for half in range(2):
        for n in range(narrow):
            out_ref[half * plan.cw : (half + 1) * plan.cw, n * part : (n + 1) * part] = x_ref[
                s_ref[0] ^ (half * narrow + n), 0
            ]


def rows_call(plan, scalars, x):
    part = x.shape[3]
    d = part * plan.group // 2
    return pl.pallas_call(
        functools.partial(rows_kernel, plan),
        grid_spec=pltpu.PrefetchScalarGridSpec(
            num_scalar_prefetch=1,
            grid=(plan.wide,),
            in_specs=[
                pl.BlockSpec((plan.group, 1, plan.cw, part), lambda p, s: (0, near_of(plan, s[3], p), 0, 0))
            ],
            out_specs=pl.BlockSpec((plan.own, d), lambda p, s: (p, 0)),
        ),
        out_shape=jax.ShapeDtypeStruct((plan.rows, d), x.dtype),
        cost_estimate=pl.CostEstimate(flops=x.size, bytes_accessed=4 * x.size, transcendentals=0),
        compiler_params=pltpu.CompilerParams(vmem_limit_bytes=40 << 20),
        name="rows",
    )(scalars, x)


MESH = pl.DeviceIdType.MESH


def greet(partners):
    barrier = pltpu.get_barrier_semaphore()
    for partner in partners:
        pl.semaphore_signal(barrier, inc=1, device_id=partner, device_id_type=MESH)
    pl.semaphore_wait(barrier, len(partners))


def along_wide(plan, r):
    return {"wide": lax.rem(lax.axis_index("wide") + r + plan.wide, plan.wide)}


def push(src, dst, send, recv, device):
    return pltpu.make_async_remote_copy(
        src_ref=src, dst_ref=dst, send_sem=send, recv_sem=recv, device_id=device, device_id_type=MESH
    )


def ffn_kernel(
    plan, x2_ref, gain_ref, g_ref, wg_ref, wu_ref, wd_ref,
    act_ref, dg_ref, du_ref, h_out, dn_ref, dx_ref, gain_out,
    h_buf, in_buf, out_buf, dn_acc, dh_acc, own_dh, own_g, ag_send, ag_recv, rs_send, rs_recv,
):
    wide, narrow = plan.wide, plan.group // 2
    own, d = x2_ref.shape
    part = d // narrow
    piece, step = pl.program_id(0), pl.program_id(1)
    last = pl.num_programs(1) - 1
    tall = min(32, own)

    z = lax.axis_index("wide")
    owner = near_of(plan, z, piece)

    def share(p):
        return push(h_buf.at[z], h_buf.at[z], ag_send.at[p], ag_recv.at[z], {"wide": near_of(plan, z, p)})

    def give(device):
        return push(out_buf.at[device], in_buf.at[z], rs_send.at[device], rs_recv.at[z], {"wide": device})

    @pl.when((piece == 0) & (step == 0))
    def _():
        greet([along_wide(plan, r) for r in range(1, wide)])

        @pl.loop(0, own // tall)
        def _(b):
            at = pl.ds(pl.multiple_of(b * tall, tall), tall)
            x2 = x2_ref[at, :]
            scale = lax.rsqrt(jnp.mean(x2 * x2, axis=1, keepdims=True) + EPS)
            h_buf[z, at, :] = (x2 * scale * gain_ref[...]).astype(BF)

        share(1).start()
        if wide > 2:
            share(2).start()
        own_g[...] = g_ref[...]

    for p in range(3, wide):
        @pl.when((piece == min(p - 3, wide - 1)) & (step == last))
        def _():
            share(p).start()

    @pl.when((piece > 0) & (step == 0))
    def _():
        push(h_buf.at[z], h_buf.at[owner], ag_send.at[0], ag_recv.at[owner], {"wide": owner}).wait_recv()

    @pl.when(step == 0)
    def _():
        h_out[...] = h_buf[owner]

    h = h_buf[owner]
    wg, wu = wg_ref[...], wu_ref[...]
    gate = jnp.dot(h, wg, preferred_element_type=F32)
    up = jnp.dot(h, wu, preferred_element_type=F32)
    d_act = jnp.zeros_like(gate)
    for n in range(narrow):
        d_act += lax.dot_general(
            g_ref[:, n * part : (n + 1) * part], wd_ref[n], NT, preferred_element_type=F32
        )
    sig = jax.nn.sigmoid(gate)
    silu = gate * sig
    act = (silu * up).astype(BF)
    dg = (d_act * up * sig * (1.0 + gate * (1.0 - sig))).astype(BF)
    du = (d_act * silu).astype(BF)
    act_ref[...] = act
    dg_ref[...] = dg
    du_ref[...] = du
    dh = lax.dot_general(dg, wg, NT, preferred_element_type=F32) + lax.dot_general(
        du, wu, NT, preferred_element_type=F32
    )

    @pl.when(step == 0)
    def _():
        dh_acc[...] = dh

    @pl.when(step > 0)
    def _():
        dh_acc[...] += dh

    for n in range(narrow):
        at = slice(n * part, (n + 1) * part)
        down = jnp.dot(act, wd_ref[n], preferred_element_type=F32)

        @pl.when(step == 0)
        def _():
            dn_acc[:, at] = down

        @pl.when(step > 0)
        def _():
            dn_acc[:, at] += down

    @pl.when(step == last)
    def _():
        dn_ref[0] = dn_acc[...].astype(BF)

    @pl.when((step == last) & (piece == 0))
    def _():
        own_dh[...] = dh_acc[...]

    @pl.when((step == last) & (piece > 0))
    def _():
        out_buf[owner] = dh_acc[...].astype(BF)
        give(owner).start()

    @pl.when((step == last) & (piece == wide - 1))
    def _():
        for p in range(1, wide):
            other = near_of(plan, z, p)
            push(out_buf.at[z], in_buf.at[other], rs_send.at[z], rs_recv.at[other], {"wide": other}).wait_recv()
        gain_out[...] = jnp.zeros_like(gain_out)

        @pl.loop(0, own // tall)
        def _(b):
            at = pl.ds(pl.multiple_of(b * tall, tall), tall)
            dh2 = own_dh[at, :]
            for p in range(1, wide):
                dh2 = dh2 + in_buf[near_of(plan, z, p), at, :].astype(F32)
            x2 = x2_ref[at, :]
            scale = lax.rsqrt(jnp.mean(x2 * x2, axis=1, keepdims=True) + EPS)
            z2 = x2 * scale
            gain_out[...] += jnp.sum(dh2 * z2, axis=0, keepdims=True)
            dz2 = dh2 * gain_ref[...]
            inner = jnp.mean(dz2 * z2, axis=1, keepdims=True)
            dx_ref[at, :] = own_g[at, :].astype(F32) + scale * (dz2 - z2 * inner)

        for p in range(1, wide):
            share(p).wait_send()
            give(near_of(plan, z, p)).wait_send()


def ffn_call(plan, x2, gain, g_rows, w_gu, w_dn):
    own, d = x2.shape
    wide, rows = plan.wide, plan.rows
    narrow, ff, part = w_dn.shape
    tile = min(512, ff)
    tiles = ff // tile
    fixed = lambda shape: pl.BlockSpec(shape, lambda p, f: (0,) * len(shape), pipeline_mode=pl.Buffered(1))
    tall = pl.BlockSpec((own, tile), lambda p, f: (p, f))
    hidden = jax.ShapeDtypeStruct((rows, ff), BF)
    buffer = pltpu.VMEM((wide, own, d), BF)
    sems = pltpu.SemaphoreType.DMA((wide,))
    return pl.pallas_call(
        functools.partial(ffn_kernel, plan),
        grid=(wide, tiles),
        in_specs=[
            fixed((own, d)),
            fixed((1, d)),
            pl.BlockSpec((own, d), lambda p, f: (p, 0)),
            pl.BlockSpec((d, tile), lambda p, f: (0, f)),
            pl.BlockSpec((d, tile), lambda p, f: (0, tiles + f)),
            pl.BlockSpec((narrow, tile, part), lambda p, f: (0, f, 0)),
        ],
        out_specs=[
            tall, tall, tall,
            pl.BlockSpec((own, d), lambda p, f: (p, 0)),
            pl.BlockSpec((1, own, d), lambda p, f: (p, 0, 0)),
            fixed((own, d)),
            fixed((1, d)),
        ],
        out_shape=[
            hidden, hidden, hidden,
            jax.ShapeDtypeStruct((rows, d), BF),
            jax.ShapeDtypeStruct((wide, own, d), BF),
            jax.ShapeDtypeStruct((own, d), F32),
            jax.ShapeDtypeStruct((1, d), F32),
        ],
        scratch_shapes=[
            buffer, buffer, buffer,
            pltpu.VMEM((own, d), F32), pltpu.VMEM((own, d), F32), pltpu.VMEM((own, d), F32),
            pltpu.VMEM((own, d), BF),
            sems, sems, sems, sems,
        ],
        cost_estimate=pl.CostEstimate(
            flops=16 * rows * d * ff, bytes_accessed=6 * d * ff + 12 * rows * d, transcendentals=rows * ff
        ),
        compiler_params=pltpu.CompilerParams(
            vmem_limit_bytes=58 << 20, collective_id=1, has_side_effects=True
        ),
        name="feed_forward",
    )(x2, gain, g_rows, w_gu, w_gu, w_dn)


def tail_kernel(
    plan, kv_heads, *refs
):
    sums_ref = refs[:kv_heads]
    (
        dh_ref, term_ref, gain2_ref, dx2_ref, x_ref, gain_ref, wkv_ref, cos_ref, sin_ref,
        dkv_ref, got_ref, gain_out,
        swap_out, swap_in, low, near_in, mine, head_in, dh_acc, dx_low, every, term_in,
        gain_part, gain_in, gain_sum, gain_all,
        swap_sem, near_send, near_recv, head_send, head_recv, part_send, part_recv,
        right_send, right_recv, left_send, left_recv, own_sem, term_sem,
        gain_send, gain_recv, gain2_send, gain2_recv,
    ) = refs[kv_heads:]
    group, wide, chunk, cw, own = plan.group, plan.wide, plan.chunk, plan.cw, plan.own
    narrow = group // 2
    part = dx_low.shape[1] // narrow
    seq, me, z = lax.axis_index("seq"), lax.axis_index("narrow"), lax.axis_index("wide")
    index = seq * narrow + me

    def member(k):
        other = lax.rem(index + k + group, group)
        return {"seq": other // narrow, "narrow": lax.rem(other, narrow)}

    sibling = {"seq": 1 - seq}
    greet([member(k) for k in range(1, group)] + [along_wide(plan, r) for r in range(1, wide)])

    def place(owner_seq, half, n):
        quarter = owner_seq if half == 0 else 3 - owner_seq
        return (quarter * narrow + (n if half == 0 else narrow - 1 - n)) * chunk

    @pl.loop(0, narrow)
    def _(n):
        for g in range(kv_heads):
            for half in range(2):
                at = pl.ds(pl.multiple_of(place(1 - seq, half, n), chunk), chunk)
                swap_out[n, g, half] = sums_ref[g][at, :].astype(BF)

    swap = push(swap_out, swap_in, swap_sem.at[0], swap_sem.at[1], sibling)
    swap.start()
    term = push(term_ref, term_in, term_sem.at[0], term_sem.at[1], along_wide(plan, -1))
    term.start()
    swap.wait_recv()

    @pl.loop(0, narrow)
    def _(n):
        for g in range(kv_heads):
            for half in range(2):
                at = pl.ds(pl.multiple_of(place(seq, half, n), chunk), chunk)
                low[n, g, half] = (sums_ref[g][at, :] + swap_in[n, g, half].astype(F32)).astype(BF)

    def near(k):
        other = lax.rem(me + k, narrow)
        return push(low.at[other], near_in.at[k], near_send.at[k], near_recv.at[k], {"narrow": other})

    for k in range(1, narrow):
        near(k).start()
    for k in range(1, narrow):
        near(k).wait_recv()

    lane = lax.broadcasted_iota(jnp.int32, (cw, 128), 1)
    for r in range(wide):
        block = lax.rem(z + r, wide)
        at = pl.ds(pl.multiple_of(block * cw, cw), cw)
        for half in range(2):
            rows = slice((2 * r + half) * cw, (2 * r + half + 1) * cw)
            for g in range(kv_heads):
                total = low[me, g, half, at, :].astype(F32)
                for k in range(1, narrow):
                    total = total + near_in[k, g, half, at, :].astype(F32)
                back = total * cos_ref[rows, :] + turn(total, -1.0) * sin_ref[rows, :]
                value = jnp.where(lane < HD, back, total).astype(BF)
                mine[r, half * cw : (half + 1) * cw, g * 128 : (g + 1) * 128] = value
                dkv_ref[rows, g * 128 : (g + 1) * 128] = value

    def heads_to(r):
        return push(mine.at[r], head_in.at[r], head_send.at[r], head_recv.at[r], along_wide(plan, r))

    for r in range(1, wide):
        heads_to(r).start()
    head_in[0] = mine[0]
    tile = min(512, part)
    for r in range(wide):
        if r > 0:
            heads_to(r).wait_recv()

        @pl.loop(0, dh_acc.shape[1] // tile)
        def _(b):
            at = pl.ds(pl.multiple_of(b * tile, tile), tile)
            more = lax.dot_general(head_in[r], wkv_ref[r, at, :], NT, preferred_element_type=F32)
            dh_acc[:, at] = (dh_ref[:, at] if r == 0 else dh_acc[:, at]) + more

    term.wait_recv()
    gain_part[0:1, :] = jnp.zeros_like(gain2_ref[...])
    gain_part[1:2, :] = gain2_ref[...]
    tall = min(32, own)

    @pl.loop(0, own // tall)
    def _(b):
        at = pl.ds(pl.multiple_of(b * tall, tall), tall)
        dh1 = dh_acc[at, :] + term_in[at, :].astype(F32)
        x = x_ref[at, :].astype(F32)
        scale = lax.rsqrt(jnp.mean(x * x, axis=1, keepdims=True) + EPS)
        z1 = x * scale
        gain_part[0:1, :] += jnp.sum(dh1 * z1, axis=0, keepdims=True)
        dz1 = dh1 * gain_ref[...]
        inner = jnp.mean(dz1 * z1, axis=1, keepdims=True)
        dx_low[at, :] = (dx2_ref[at, :] + scale * (dz1 - z1 * inner)).astype(BF)

    def slab(other):
        rows = pl.ds(pl.multiple_of((other // narrow) * cw, cw), cw)
        return dx_low.at[rows, pl.ds(pl.multiple_of(lax.rem(other, narrow) * part, part), part)]

    def parts_to(k):
        other = lax.rem(index + k, group)
        return push(slab(other), every.at[0, index], part_send.at[k], part_recv.at[k], member(k))

    def parts_from(k):
        other = lax.rem(index - k + group, group)
        return push(slab(index), every.at[0, other], part_send.at[k], part_recv.at[k], member(k))

    def columns(other):
        return gain_part.at[:, pl.ds(pl.multiple_of(lax.rem(other, narrow) * part, part), part)]

    def gain_to(k):
        other = lax.rem(index + k, group)
        return push(columns(other), gain_in.at[k], gain_send.at[k], gain_recv.at[k], member(k))

    for k in range(1, group):
        parts_to(k).start()
    for k in range(1, group):
        gain_to(k).start()
    stay = pltpu.make_async_copy(slab(index), every.at[0, index], own_sem)
    stay.start()
    stay.wait()
    for k in range(1, group):
        parts_from(k).wait_recv()
    for k in range(1, group):
        gain_to(k).wait_recv()
    gain = gain_part[:, pl.ds(pl.multiple_of(me * part, part), part)]
    for k in range(1, group):
        gain = gain + gain_in[k]
    gain_sum[...] = gain

    def gain_on(r):
        return push(gain_sum, gain_all.at[r], gain2_send.at[r], gain2_recv.at[r], along_wide(plan, r))

    for r in range(1, wide):
        gain_on(r).start()

    def to_right(h):
        return push(
            every.at[(wide - h) % wide], every.at[wide - 1 - h], right_send.at[h], right_recv.at[h], along_wide(plan, 1)
        )

    def to_left(h):
        return push(every.at[h], every.at[h + 1], left_send.at[h], left_recv.at[h], along_wide(plan, -1))

    for h in range(wide - 1):
        @pl.when((z <= wide - 2) & (z >= h))
        def _():
            to_right(h).start()

        @pl.when((z >= 1) & (z + h <= wide - 1))
        def _():
            to_left(h).start()

        @pl.when(z >= h + 1)
        def _():
            to_right(h).wait_recv()

        @pl.when(z + h + 1 <= wide - 1)
        def _():
            to_left(h).wait_recv()

    for h in range(wide - 1):
        @pl.when((z <= wide - 2) & (z >= h))
        def _():
            to_right(h).wait_send()

        @pl.when((z >= 1) & (z + h <= wide - 1))
        def _():
            to_left(h).wait_send()

    got_ref[...] = every[...]
    gain = gain_sum[...]
    for r in range(1, wide):
        gain_on(r).wait_recv()
        gain = gain + gain_all[r]
    gain_out[...] = gain
    for r in range(1, wide):
        gain_on(r).wait_send()
    for k in range(1, group):
        gain_to(k).wait_send()
    term.wait_send()
    swap.wait_send()
    for k in range(1, narrow):
        near(k).wait_send()
    for r in range(1, wide):
        heads_to(r).wait_send()
    for k in range(1, group):
        parts_to(k).wait_send()


def tail_call(plan, sums, dh, term, gain2, dx2, x, gain, w_kv, cos, sin):
    kv_heads = len(sums)
    own, d = dh.shape
    group, wide, chunk, cw = plan.group, plan.wide, plan.chunk, plan.cw
    narrow = group // 2
    part = d // narrow
    dma = pltpu.SemaphoreType.DMA
    quarter = pltpu.VMEM((narrow, kv_heads, 2, chunk, 128), BF)
    whole = pl.BlockSpec(memory_space=pltpu.VMEM)
    return pl.pallas_call(
        functools.partial(tail_kernel, plan, kv_heads),
        in_specs=[whole] * (kv_heads + 9),
        out_specs=[whole] * 3,
        out_shape=[
            jax.ShapeDtypeStruct((plan.rows, kv_heads * 128), BF),
            jax.ShapeDtypeStruct((wide, group, cw, part), BF),
            jax.ShapeDtypeStruct((2, part), F32),
        ],
        scratch_shapes=[
            quarter, quarter, quarter, quarter,
            pltpu.VMEM((wide, own, kv_heads * 128), BF),
            pltpu.VMEM((wide, own, kv_heads * 128), BF),
            pltpu.VMEM((own, d), F32),
            pltpu.VMEM((own, d), BF),
            pltpu.VMEM((wide, group, cw, part), BF),
            pltpu.VMEM((own, d), BF),
            pltpu.VMEM((2, d), F32),
            pltpu.VMEM((group, 2, part), F32),
            pltpu.VMEM((2, part), F32),
            pltpu.VMEM((wide, 2, part), F32),
            dma((2,)), dma((narrow,)), dma((narrow,)), dma((wide,)), dma((wide,)), dma((group,)), dma((group,)),
            dma((wide,)), dma((wide,)), dma((wide,)), dma((wide,)), dma(()), dma((2,)),
            dma((group,)), dma((group,)), dma((wide,)), dma((wide,)),
        ],
        cost_estimate=pl.CostEstimate(
            flops=200 * own * d * wide * kv_heads * 128,
            bytes_accessed=4 * kv_heads * plan.total * 128,
            transcendentals=0,
        ),
        compiler_params=pltpu.CompilerParams(
            vmem_limit_bytes=58 << 20, collective_id=2, has_side_effects=True
        ),
        name="input_gradient",
    )(*sums, dh, term, gain2, dx2, x, gain, w_kv, cos, sin)


def assemble_kernel(plan, crossed, s_ref, in_ref, out_ref):
    group = plan.group
    for l in range(group):
        owner = jnp.where(s_ref[0] >= group // 2, group - 1 - l, l)
        out_ref[l, 0] = in_ref[0, s_ref[0] ^ owner if crossed else owner].astype(out_ref.dtype)


def assemble_call(plan, scalars, values, dtype, crossed):
    wide, group, cw, part = values.shape
    out = pl.pallas_call(
        functools.partial(assemble_kernel, plan, crossed),
        grid_spec=pltpu.PrefetchScalarGridSpec(
            num_scalar_prefetch=1,
            grid=(wide,),
            in_specs=[pl.BlockSpec((1, group, cw, part), lambda r, s: (r, 0, 0, 0))],
            out_specs=[pl.BlockSpec((group, 1, cw, part), lambda r, s: (0, block_of(plan, s, r), 0, 0))],
        ),
        out_shape=[jax.ShapeDtypeStruct((group, wide, cw, part), dtype)],
        cost_estimate=pl.CostEstimate(flops=values.size, bytes_accessed=6 * values.size, transcendentals=0),
        compiler_params=pltpu.CompilerParams(vmem_limit_bytes=40 << 20),
        name="assemble",
    )(scalars, values)[0]
    return out.reshape(group * wide * cw, part)


def half_of(weight, seq_index, seq_count):
    part = weight.shape[0] // seq_count
    return lax.dynamic_slice_in_dim(weight, seq_index * part, part, 0)


def body(
    tokens, attn_gain, w_query, w_key, w_value, w_out, ffn_gain, w_gate, w_up, w_down,
    segment_ids, token_mask, out_grad,
):
    seq_count = lax.axis_size("seq")
    narrow = lax.axis_size("narrow")
    wide = lax.axis_size("wide")
    group = seq_count * narrow
    seq_index = lax.axis_index("seq")
    narrow_index = lax.axis_index("narrow")
    wide_index = lax.axis_index("wide")
    index = seq_index * narrow + narrow_index
    total = segment_ids.shape[0]
    plan = Plan(total, group, wide)
    chunk, cw, rows, own = plan.chunk, plan.cw, plan.rows, plan.own
    d_part = tokens.shape[1]
    d = d_part * narrow
    qw = w_query.shape[1]
    kw = w_key.shape[1]
    kv_heads = kw // HD
    heads = qw // kw
    ff = w_gate.shape[1]
    pieces = range(wide)

    start_one = jnp.sum((segment_ids < 1).astype(jnp.int32))
    start_two = jnp.sum((segment_ids < 2).astype(jnp.int32))
    scalars = jnp.stack([index, start_one, start_two, wide_index]).astype(jnp.int32)

    def swap(values, axes, k, size):
        return values if k == 0 else lax.ppermute(values, axes, [(a, a ^ k) for a in range(size)])

    def exchange(parts):
        sent = [lax.dynamic_index_in_dim(parts, index ^ k, 0, keepdims=False) for k in range(group)]
        return jnp.stack([swap(part, SN, k, group) for k, part in enumerate(sent)])

    def to_rows(values):
        parts = values.reshape(group, wide, cw, d_part)
        return exchange(jnp.where(seq_index == 1, parts[::-1], parts))

    def send(values, r):
        return values if r == 0 else lax.ppermute(values, "wide", [(a, (a + r) % wide) for a in pieces])

    def fetch(values, r):
        return send(values, (wide - r) % wide)

    def wide_total(parts):
        out = parts[0]
        for r in range(1, len(parts)):
            out = out + send(parts[r].astype(BF), r).astype(F32)
        return out

    def from_rows(values, dtype):
        parts = values.astype(BF).reshape(2, cw, narrow, d_part)
        parts = jnp.transpose(parts, (0, 2, 1, 3)).reshape(group, cw, d_part)
        got = exchange(parts)
        return assemble_call(plan, scalars, jnp.stack([fetch(got, r) for r in pieces]), dtype, True)

    def gather_weight(weight):
        return lax.all_gather(half_of(weight, seq_index, seq_count), NS, axis=0, tiled=True)

    def scatter_grad(grad):
        mine = lax.psum_scatter(grad.astype(BF), NS, scatter_dimension=0, tiled=True)
        return lax.all_gather(mine, "seq", axis=0, tiled=True).astype(F32)

    def after(values, *others):
        return lax.optimization_barrier((values, *others))[0]

    x_parts = to_rows(tokens)
    w_kv = jnp.concatenate(
        [w_key.reshape(d_part, kv_heads, 1, HD), w_value.reshape(d_part, kv_heads, 1, HD)], axis=2
    ).reshape(d_part, 2 * kw)
    w_qkv = gather_weight(jnp.concatenate([w_query, w_kv], axis=1))
    gains = jnp.stack([attn_gain, ffn_gain])
    gains = jnp.stack([swap(gains, "narrow", k, narrow) for k in range(narrow)])
    order = narrow_index ^ jnp.arange(narrow)
    gains = jnp.sum(jnp.where((order[:, None] == jnp.arange(narrow)[None, :])[:, :, None, None], gains[None], 0.0), axis=1)
    gains = jnp.transpose(gains, (1, 0, 2)).reshape(2, d)
    gain_one, gain_two = gains[0:1], gains[1:2]

    row = jnp.arange(rows, dtype=jnp.int32)
    row_chunk = jnp.where((row // cw) % 2 == 1, 2 * group - 1 - index, index)
    row_block = (row // own + wide_index) % wide
    row_token = row_chunk * chunk + row_block * cw + row % cw
    row_start = jnp.where(row_token >= start_two, start_two, jnp.where(row_token >= start_one, start_one, 0))
    row_pos = (row_token - row_start).astype(F32)
    frequency = THETA ** (-2.0 * jnp.arange(HD // 2, dtype=F32) / HD)
    angles = row_pos[:, None] * jnp.tile(frequency, 4)[None, :]
    cos, sin = jnp.cos(angles), jnp.sin(angles)

    h_one, q, kv, x_low = qkv_call(plan, scalars, x_parts, gain_one, w_qkv, cos, sin, qw)
    near = [swap(kv, "narrow", k, narrow) for k in range(narrow)]
    far = [swap(part, "seq", 1, seq_count) for part in near]
    kv_all = jnp.concatenate(near + far, axis=0)

    lane = jnp.arange(128, dtype=jnp.int32)[None, :]
    closed = (segment_ids[:, None] != lane - HD) | (token_mask[:, None] != 1)
    kf = jnp.where((lane >= HD) & (lane < HD + 3) & closed, NEG, 0.0)
    kf = jnp.where((lane >= HD + 3) & (lane < HD + 6), 1.0, kf).astype(BF)
    kx, vx = keys_call(plan, scalars, kv_all, kf, kv_heads)

    w_o = jnp.transpose(gather_weight(after(w_out, x_parts)).reshape(narrow, qw, d_part), (1, 0, 2)).reshape(qw, d)
    w_gu = gather_weight(after(jnp.concatenate([w_gate, w_up], axis=1), x_parts))
    w_dn = gather_weight(after(w_down, x_parts)).reshape(narrow, ff, d_part)
    row_valid = lax.dynamic_slice_in_dim(token_mask, seq_index * (group * chunk), group * chunk, 0)
    g_low = jnp.where(row_valid[:, None] == 1, out_grad, jnp.zeros_like(out_grad))
    g_parts = to_rows(after(g_low, kv_all))
    g_rows = rows_call(plan, scalars, g_parts)

    far_first = sorted(pieces, key=lambda r: (r == 0, -min(r, wide - r)))
    near_first = sorted(pieces, key=lambda r: min(r, wide - r))
    o, qe, attn = [None] * wide, [None] * wide, [None] * wide
    for r in far_first:
        o[r], qe[r] = forward_call(plan, scalars, q, kx, vx, kv_heads, heads, r)
        attn[r] = jnp.dot(o[r], w_o, preferred_element_type=F32)
    x_own = x_low.astype(F32)
    x2 = x_own + wide_total(attn)

    act, d_gate, d_up, h_all, down, dx2, grad_gain_two = ffn_call(plan, x2, gain_two, g_rows, w_gu, w_dn)

    db_own = dx2.astype(BF)
    db = [fetch(db_own, r) for r in pieces]
    sums = [None] * kv_heads
    dq, terms = [None] * wide, [None] * wide
    w_q = w_qkv[:, :qw]
    w_k = w_qkv[:, qw:]
    for r in pieces:
        do = lax.dot_general(db[r], w_o, NT, preferred_element_type=F32).astype(BF)
        parts = []
        for g in range(kv_heads):
            part, sums[g] = backward_call(
                plan, scalars, qe[r], kx, vx, o[r], do, cos, sin, heads, r, g, sums[g]
            )
            parts.append(part)
        dq[r] = jnp.concatenate(parts, axis=1)
        terms[r] = lax.dot_general(dq[r], w_q, NT, preferred_element_type=F32)
    dh1 = wide_total(terms[:-1])

    down = after(down, *db)
    slot = [jnp.argmax(near_of(plan, wide_index, jnp.arange(wide)) == (wide_index + r) % wide) for r in pieces]
    down = [lax.dynamic_index_in_dim(down, slot[r], 0, keepdims=False) for r in pieces]
    result = from_rows(x2 + wide_total([down[0].astype(F32)] + down[1:]), BF)

    w_k_all = jnp.stack([send(w_k, r) for r in pieces])
    sums[0] = after(sums[0], result)
    dkv, got, gain_grads = tail_call(
        plan, sums, dh1, terms[-1].astype(BF), grad_gain_two, dx2, x_low, gain_one, w_k_all, cos, sin
    )
    input_grad = assemble_call(plan, scalars, got, F32, False)

    def tn(left, right):
        return lax.dot_general(left, right, TN, preferred_element_type=F32).astype(BF)

    def tn_split(left, right):
        return jnp.concatenate([tn(left, right[:, n * d_part : (n + 1) * d_part]) for n in range(narrow)], axis=0)

    grad_gu = scatter_grad(jnp.concatenate([tn(h_all, d_gate), tn(h_all, d_up)], axis=1))
    grad_dn = scatter_grad(tn_split(act, g_rows))
    grad_o = scatter_grad(tn_split(jnp.concatenate(o, axis=0), jnp.concatenate(db, axis=0)))
    grad_qkv = scatter_grad(tn(h_one, jnp.concatenate([jnp.concatenate(dq, axis=0), dkv], axis=1)))
    grad_kv = grad_qkv[:, qw:].reshape(d_part, kv_heads, 2, HD)
    return (
        result,
        input_grad,
        gain_grads[0],
        grad_qkv[:, :qw],
        grad_kv[:, :, 0].reshape(d_part, kw),
        grad_kv[:, :, 1].reshape(d_part, kw),
        grad_o,
        gain_grads[1],
        grad_gu[:, :ff],
        grad_gu[:, ff:],
        grad_dn,
    )


def solution(mesh):
    width_in, width_out = P("narrow", "wide"), P("wide", "narrow")
    acts = P("seq", "narrow")
    return jax.shard_map(
        body,
        mesh=mesh,
        in_specs=(
            acts, P("narrow"), width_in, width_in, width_in, width_out, P("narrow"),
            width_in, width_in, width_out, P(), P(), acts,
        ),
        out_specs=(
            acts, acts, P("narrow"), width_in, width_in, width_in, width_out, P("narrow"),
            width_in, width_in, width_out,
        ),
        check_vma=False,
    )
```

```python
import functools

import jax
import jax.numpy as jnp
from jax import lax
from jax.experimental import pallas as pl
from jax.experimental.pallas import tpu as pltpu
from jax.sharding import PartitionSpec as P

HD = 64
EPS = 1e-05
THETA = 500000.0
NEG = -1e30
SN = ("seq", "narrow")
NS = ("narrow", "seq")
BF = jnp.bfloat16
F32 = jnp.float32
NT = (((1,), (1,)), ((), ()))
TN = (((0,), (0,)), ((), ()))


def pieces_of(value):
    first = value.astype(BF).astype(F32)
    second = (value - first).astype(BF).astype(F32)
    third = (value - first - second).astype(BF).astype(F32)
    return first, second, third


class Plan:
    def __init__(self, total, group, wide):
        self.total, self.group, self.wide = total, group, wide
        self.chunk = total // (2 * group)
        self.cw = self.chunk // wide
        self.rows = 2 * self.chunk
        self.own = 2 * self.cw


def block_of(plan, s_ref, r):
    return lax.rem(s_ref[3] + r, plan.wide)


def near_of(plan, z, p):
    side = jnp.minimum(z, plan.wide - 1 - z)
    both = jnp.where(lax.rem(p, 2) == 1, z + (p + 1) // 2, z - p // 2)
    one = jnp.where(z <= plan.wide - 1 - z, z + p - side, z - p + side)
    return jnp.where(p <= 2 * side, both, one)


def turn(values, sign):
    width = values.shape[1]
    lane = lax.broadcasted_iota(jnp.int32, values.shape, 1)
    left, right = pltpu.roll(values, width - HD // 2, 1), pltpu.roll(values, HD // 2, 1)
    return jnp.where(lane % HD < HD // 2, -sign * left, sign * right)


def widen(table, width):
    return jnp.concatenate([table] * (width // 128), axis=1) if width > 128 else table


def qkv_kernel(plan, qw, s_ref, x_ref, gain_ref, w_ref, cos_ref, sin_ref, h_ref, q_ref, kv_ref, own_ref, x_scr):
    narrow = plan.group // 2
    part = x_ref.shape[3]
    for half in range(2):
        for n in range(narrow):
            x_scr[half * plan.cw : (half + 1) * plan.cw, n * part : (n + 1) * part] = x_ref[
                s_ref[0] ^ (half * narrow + n), 0
            ]
    low = x_scr[...]

    @pl.when(pl.program_id(0) == 0)
    def _():
        own_ref[...] = low

    x = low.astype(F32)
    mean = jnp.mean(x * x, axis=1, keepdims=True)
    h = (x * lax.rsqrt(mean + EPS) * gain_ref[...]).astype(BF)
    h_ref[...] = h
    t = jnp.dot(h, w_ref[...], preferred_element_type=F32)
    width = t.shape[1]
    lane = lax.broadcasted_iota(jnp.int32, t.shape, 1)
    plain = (lane >= qw) & (lane % 128 >= HD)
    out = jnp.where(plain, t, t * widen(cos_ref[...], width) + turn(t, 1.0) * widen(sin_ref[...], width))
    q_ref[...] = (out[:, :qw] * (HD ** -0.5)).astype(BF)
    kv_ref[...] = out[:, qw:].astype(BF)


def qkv_call(plan, scalars, x, gain, w, cos, sin, qw):
    part = x.shape[3]
    d = part * plan.group // 2
    width = w.shape[1]
    rows, bm = plan.rows, plan.own
    return pl.pallas_call(
        functools.partial(qkv_kernel, plan, qw),
        grid_spec=pltpu.PrefetchScalarGridSpec(
            num_scalar_prefetch=1,
            grid=(plan.wide,),
            in_specs=[
                pl.BlockSpec((plan.group, 1, plan.cw, part), lambda r, s: (0, block_of(plan, s, r), 0, 0)),
                pl.BlockSpec((1, d), lambda r, s: (0, 0)),
                pl.BlockSpec((d, width), lambda r, s: (0, 0)),
                pl.BlockSpec((bm, 128), lambda r, s: (r, 0)),
                pl.BlockSpec((bm, 128), lambda r, s: (r, 0)),
            ],
            out_specs=[
                pl.BlockSpec((bm, d), lambda r, s: (r, 0)),
                pl.BlockSpec((bm, qw), lambda r, s: (r, 0)),
                pl.BlockSpec((bm, width - qw), lambda r, s: (r, 0)),
                pl.BlockSpec((bm, d), lambda r, s: (0, 0)),
            ],
            scratch_shapes=[pltpu.VMEM((bm, d), BF)],
        ),
        out_shape=[
            jax.ShapeDtypeStruct((rows, d), BF),
            jax.ShapeDtypeStruct((rows, qw), BF),
            jax.ShapeDtypeStruct((rows, width - qw), BF),
            jax.ShapeDtypeStruct((bm, d), BF),
        ],
        cost_estimate=pl.CostEstimate(
            flops=2 * rows * d * width, bytes_accessed=4 * rows * d + 2 * d * width, transcendentals=rows
        ),
        compiler_params=pltpu.CompilerParams(vmem_limit_bytes=40 << 20),
        name="norm_qkv",
    )(scalars, x, gain, w, cos, sin)


def keys_kernel(plan, s_ref, kv_ref, kf_ref, kx_ref, vx_ref):
    cw, group = plan.cw, plan.group
    lane = lax.broadcasted_iota(jnp.int32, (cw, 128), 1)
    ones = jnp.where(lane < 3, 1.0, 0.0).astype(BF)

    @pl.loop(0, 2 * group)
    def _(c):
        late = c >= group
        owner = jnp.where(late, 2 * group - 1 - c, c)
        for r in range(plan.wide):
            at = pl.ds(pl.multiple_of(c * plan.chunk + block_of(plan, s_ref, r) * cw, cw), cw)
            kv = kv_ref[s_ref[0] ^ owner, r, jnp.where(late, 1, 0)]
            kx_ref[0, at, :] = jnp.where(lane < HD, kv, kf_ref[at, :])
            vx_ref[0, at, :] = jnp.where(lane < HD, ones, kv)


def keys_call(plan, scalars, kv, kf, kv_heads):
    group, total = plan.group, plan.total
    kv = kv.reshape(group, plan.wide, 2, plan.cw, kv_heads * 128)
    out = pl.BlockSpec((1, total, 128), lambda g, s: (g, 0, 0))
    return pl.pallas_call(
        functools.partial(keys_kernel, plan),
        grid_spec=pltpu.PrefetchScalarGridSpec(
            num_scalar_prefetch=1,
            grid=(kv_heads,),
            in_specs=[
                pl.BlockSpec((group, plan.wide, 2, plan.cw, 128), lambda g, s: (0, 0, 0, 0, g)),
                pl.BlockSpec((total, 128), lambda g, s: (0, 0)),
            ],
            out_specs=[out, out],
        ),
        out_shape=[jax.ShapeDtypeStruct((kv_heads, total, 128), BF)] * 2,
        cost_estimate=pl.CostEstimate(
            flops=kv_heads * total * 128, bytes_accessed=8 * kv_heads * total * 128, transcendentals=0
        ),
        compiler_params=pltpu.CompilerParams(vmem_limit_bytes=40 << 20),
        name="keys",
    )(scalars, kv, kf)


def split_heads(block, heads, low):
    tiles = []
    for h in range(heads):
        tile = block[:, (h // 2) * 128 : (h // 2 + 1) * 128]
        if (h % 2 == 0) != low:
            tile = pltpu.roll(tile, HD, 1)
        tiles.append(tile)
    return tiles


def join_heads(tiles, low):
    rows = tiles[0].shape[0]
    lane = lax.broadcasted_iota(jnp.int32, (rows, 128), 1)
    pairs = []
    for h in range(0, len(tiles), 2):
        first, second = tiles[h], tiles[h + 1]
        if low:
            second = pltpu.roll(second, HD, 1)
        else:
            first = pltpu.roll(first, HD, 1)
        pairs.append(jnp.where(lane < HD, first, second))
    return jnp.concatenate(pairs, axis=1)


def chunk_of(plan, s_ref, half):
    return jnp.where(half == 1, 2 * plan.group - 1 - s_ref[0], s_ref[0])


def forward_kernel(plan, heads, r, s_ref, q_ref, kx, vx, o_ref, qe_ref):
    cw, chunk = plan.cw, plan.chunk
    w, c = block_of(plan, s_ref, r), chunk_of(plan, s_ref, pl.program_id(1))
    lane = lax.broadcasted_iota(jnp.int32, (cw, 128), 1)
    token = c * chunk + w * cw + lax.broadcasted_iota(jnp.int32, (cw, 128), 0)
    segment = (token >= s_ref[1]).astype(jnp.int32) + (token >= s_ref[2]).astype(jnp.int32)
    mark = jnp.where(lane == HD + segment, 1.0, 0.0)
    tiles = split_heads(q_ref[...].astype(F32), heads, True)
    q32 = jnp.concatenate([jnp.where(lane < HD, t, mark) for t in tiles], axis=0)
    q = q32.astype(BF)
    rows = heads * cw

    def step(j, carry, diagonal=False):
        top, acc = carry
        at = pl.ds(pl.multiple_of(j * chunk, chunk), chunk)
        s = lax.dot_general(q, kx[0, at, :], NT, preferred_element_type=F32)
        if diagonal:
            row = lax.broadcasted_iota(jnp.int32, (rows, chunk), 0) % cw + w * cw
            col = lax.broadcasted_iota(jnp.int32, (rows, chunk), 1)
            s = jnp.where(col <= row, s, NEG)
        new = jnp.maximum(top, jnp.max(s, axis=1, keepdims=True))
        p = jnp.exp(s - new).astype(BF)
        acc = acc * jnp.exp(top - new) + jnp.dot(p, vx[0, at, :], preferred_element_type=F32)
        return new, acc

    start = (jnp.full((rows, 1), NEG, F32), jnp.zeros((rows, 128), F32))
    carry = lax.fori_loop(0, c, step, start)
    top, acc = step(c, carry, True)
    total = acc[:, 0:1]
    out = acc / total
    o_ref[...] = join_heads([out[h * cw : (h + 1) * cw] for h in range(heads)], False).astype(BF)
    first, second, third = pieces_of(-(top + jnp.log(total)))
    wide_lane = lax.broadcasted_iota(jnp.int32, (rows, 128), 1)
    qe = jnp.where(wide_lane == HD + 3, first, q32)
    qe = jnp.where(wide_lane == HD + 4, second, qe)
    qe = jnp.where(wide_lane == HD + 5, third, qe)
    qe_ref[0, 0] = qe.astype(BF)


def forward_call(plan, scalars, q, kx, vx, kv_heads, heads, r):
    total, cw = plan.total, plan.cw
    pairs = kv_heads * heads * total * plan.own // 2
    keys = pl.BlockSpec((1, total, 128), lambda g, b, s: (g, 0, 0))
    return pl.pallas_call(
        functools.partial(forward_kernel, plan, heads, r),
        grid_spec=pltpu.PrefetchScalarGridSpec(
            num_scalar_prefetch=1,
            grid=(kv_heads, 2),
            in_specs=[pl.BlockSpec((cw, heads * HD), lambda g, b, s: (2 * r + b, g)), keys, keys],
            out_specs=[
                pl.BlockSpec((cw, heads * HD), lambda g, b, s: (b, g)),
                pl.BlockSpec((1, 1, heads * cw, 128), lambda g, b, s: (g, b, 0, 0)),
            ],
        ),
        out_shape=[
            jax.ShapeDtypeStruct((plan.own, q.shape[1]), BF),
            jax.ShapeDtypeStruct((kv_heads, 2, heads * cw, 128), BF),
        ],
        cost_estimate=pl.CostEstimate(
            flops=16 * pairs * HD, bytes_accessed=8 * total * 128, transcendentals=pairs
        ),
        compiler_params=pltpu.CompilerParams(vmem_limit_bytes=48 << 20),
        name="attention_forward",
    )(scalars, q, kx, vx)


def rows_kernel(plan, s_ref, x_ref, out_ref):
    narrow = plan.group // 2
    part = x_ref.shape[3]
    for half in range(2):
        for n in range(narrow):
            out_ref[half * plan.cw : (half + 1) * plan.cw, n * part : (n + 1) * part] = x_ref[
                s_ref[0] ^ (half * narrow + n), 0
            ]


def rows_call(plan, scalars, x):
    part = x.shape[3]
    d = part * plan.group // 2
    return pl.pallas_call(
        functools.partial(rows_kernel, plan),
        grid_spec=pltpu.PrefetchScalarGridSpec(
            num_scalar_prefetch=1,
            grid=(plan.wide,),
            in_specs=[
                pl.BlockSpec((plan.group, 1, plan.cw, part), lambda p, s: (0, near_of(plan, s[3], p), 0, 0))
            ],
            out_specs=pl.BlockSpec((plan.own, d), lambda p, s: (p, 0)),
        ),
        out_shape=jax.ShapeDtypeStruct((plan.rows, d), x.dtype),
        cost_estimate=pl.CostEstimate(flops=x.size, bytes_accessed=4 * x.size, transcendentals=0),
        compiler_params=pltpu.CompilerParams(vmem_limit_bytes=40 << 20),
        name="rows",
    )(scalars, x)


MESH = pl.DeviceIdType.MESH


def greet(partners):
    barrier = pltpu.get_barrier_semaphore()
    for partner in partners:
        pl.semaphore_signal(barrier, inc=1, device_id=partner, device_id_type=MESH)
    pl.semaphore_wait(barrier, len(partners))


def along_wide(plan, r):
    return {"wide": lax.rem(lax.axis_index("wide") + r + plan.wide, plan.wide)}


def push(src, dst, send, recv, device):
    return pltpu.make_async_remote_copy(
        src_ref=src, dst_ref=dst, send_sem=send, recv_sem=recv, device_id=device, device_id_type=MESH
    )


class Chain:
    def __init__(self, plan, buf, sems):
        self.wide, self.buf, self.sems = plan.wide, buf, sems
        self.z = lax.axis_index("wide")

    def copy(self, slot, h, way):
        send, recv = (self.sems[0], self.sems[1]) if way > 0 else (self.sems[2], self.sems[3])
        return push(self.buf.at[slot], self.buf.at[slot], send.at[h], recv.at[h], {"wide": self.z + way})

    def sends(self, h, way):
        z, last = self.z, self.wide - 1
        return (z >= h - 1) & (z < last) if way > 0 else (z + h - 1 <= last) & (z > 0)

    def go(self, h):
        for way in (1, -1):
            @pl.when(self.sends(h, way))
            def _():
                self.copy(self.z - way * (h - 1), h, way).start()

    def arrive(self, h):
        for way in (1, -1):
            @pl.when(self.z >= h if way > 0 else self.z + h <= self.wide - 1)
            def _():
                slot = self.z - way * h
                send, recv = (self.sems[0], self.sems[1]) if way > 0 else (self.sems[2], self.sems[3])
                push(self.buf.at[slot], self.buf.at[slot], send.at[h], recv.at[h], {"wide": slot}).wait_recv()

    def finish(self):
        for h in range(1, self.wide):
            for way in (1, -1):
                @pl.when(self.sends(h, way))
                def _():
                    self.copy(self.z - way * (h - 1), h, way).wait_send()


def ffn_kernel(
    plan, x2_ref, gain_ref, g_ref, wg_ref, wu_ref, wd_ref,
    act_ref, dg_ref, du_ref, h_out, dn_ref, dx_ref, gain_out,
    h_buf, in_buf, out_buf, dn_acc, dh_acc, own_dh, own_g, rs_send, rs_recv, *chain_sems
):
    wide, narrow = plan.wide, plan.group // 2
    own, d = x2_ref.shape
    part = d // narrow
    piece, step = pl.program_id(0), pl.program_id(1)
    last = pl.num_programs(1) - 1
    tall = min(32, own)

    z = lax.axis_index("wide")
    owner = near_of(plan, z, piece)

    chain = Chain(plan, h_buf, chain_sems)

    def give(device):
        return push(out_buf.at[device], in_buf.at[z], rs_send.at[device], rs_recv.at[z], {"wide": device})

    @pl.when((piece == 0) & (step == 0))
    def _():
        greet([along_wide(plan, r) for r in range(1, wide)])

        @pl.loop(0, own // tall)
        def _(b):
            at = pl.ds(pl.multiple_of(b * tall, tall), tall)
            x2 = x2_ref[at, :]
            scale = lax.rsqrt(jnp.mean(x2 * x2, axis=1, keepdims=True) + EPS)
            h_buf[z, at, :] = (x2 * scale * gain_ref[...]).astype(BF)

        chain.go(1)
        own_g[...] = g_ref[...]

    for h in range(1, wide):
        @pl.when((piece == h) & (step == 0))
        def _():
            chain.arrive(h)
            if h + 1 < wide:
                chain.go(h + 1)

    @pl.when(step == 0)
    def _():
        h_out[...] = h_buf[owner]

    h = h_buf[owner]
    wg, wu = wg_ref[...], wu_ref[...]
    gate = jnp.dot(h, wg, preferred_element_type=F32)
    up = jnp.dot(h, wu, preferred_element_type=F32)
    d_act = jnp.zeros_like(gate)
    for n in range(narrow):
        d_act += lax.dot_general(
            g_ref[:, n * part : (n + 1) * part], wd_ref[n], NT, preferred_element_type=F32
        )
    sig = jax.nn.sigmoid(gate)
    silu = gate * sig
    act = (silu * up).astype(BF)
    dg = (d_act * up * sig * (1.0 + gate * (1.0 - sig))).astype(BF)
    du = (d_act * silu).astype(BF)
    act_ref[...] = act
    dg_ref[...] = dg
    du_ref[...] = du
    dh = lax.dot_general(dg, wg, NT, preferred_element_type=F32) + lax.dot_general(
        du, wu, NT, preferred_element_type=F32
    )

    @pl.when(step == 0)
    def _():
        dh_acc[...] = dh

    @pl.when(step > 0)
    def _():
        dh_acc[...] += dh

    for n in range(narrow):
        at = slice(n * part, (n + 1) * part)
        down = jnp.dot(act, wd_ref[n], preferred_element_type=F32)

        @pl.when(step == 0)
        def _():
            dn_acc[:, at] = down

        @pl.when(step > 0)
        def _():
            dn_acc[:, at] += down

    @pl.when(step == last)
    def _():
        dn_ref[0] = dn_acc[...].astype(BF)

    @pl.when((step == last) & (piece == 0))
    def _():
        own_dh[...] = dh_acc[...]

    @pl.when((step == last) & (piece > 0))
    def _():
        out_buf[owner] = dh_acc[...].astype(BF)
        give(owner).start()

    @pl.when((step == last) & (piece == wide - 1))
    def _():
        for p in range(1, wide):
            other = near_of(plan, z, p)
            push(out_buf.at[z], in_buf.at[other], rs_send.at[z], rs_recv.at[other], {"wide": other}).wait_recv()
        gain_out[...] = jnp.zeros_like(gain_out)

        @pl.loop(0, own // tall)
        def _(b):
            at = pl.ds(pl.multiple_of(b * tall, tall), tall)
            dh2 = own_dh[at, :]
            for p in range(1, wide):
                dh2 = dh2 + in_buf[near_of(plan, z, p), at, :].astype(F32)
            x2 = x2_ref[at, :]
            scale = lax.rsqrt(jnp.mean(x2 * x2, axis=1, keepdims=True) + EPS)
            z2 = x2 * scale
            gain_out[...] += jnp.sum(dh2 * z2, axis=0, keepdims=True)
            dz2 = dh2 * gain_ref[...]
            inner = jnp.mean(dz2 * z2, axis=1, keepdims=True)
            dx_ref[at, :] = own_g[at, :].astype(F32) + scale * (dz2 - z2 * inner)

        chain.finish()
        for p in range(1, wide):
            give(near_of(plan, z, p)).wait_send()


def ffn_call(plan, x2, gain, g_rows, w_gu, w_dn):
    own, d = x2.shape
    wide, rows = plan.wide, plan.rows
    narrow, ff, part = w_dn.shape
    tile = min(512, ff)
    tiles = ff // tile
    fixed = lambda shape: pl.BlockSpec(shape, lambda p, f: (0,) * len(shape), pipeline_mode=pl.Buffered(1))
    tall = pl.BlockSpec((own, tile), lambda p, f: (p, f))
    hidden = jax.ShapeDtypeStruct((rows, ff), BF)
    buffer = pltpu.VMEM((wide, own, d), BF)
    sems = pltpu.SemaphoreType.DMA((wide,))
    return pl.pallas_call(
        functools.partial(ffn_kernel, plan),
        grid=(wide, tiles),
        in_specs=[
            fixed((own, d)),
            fixed((1, d)),
            pl.BlockSpec((own, d), lambda p, f: (p, 0)),
            pl.BlockSpec((d, tile), lambda p, f: (0, f)),
            pl.BlockSpec((d, tile), lambda p, f: (0, tiles + f)),
            pl.BlockSpec((narrow, tile, part), lambda p, f: (0, f, 0)),
        ],
        out_specs=[
            tall, tall, tall,
            pl.BlockSpec((own, d), lambda p, f: (p, 0)),
            pl.BlockSpec((1, own, d), lambda p, f: (p, 0, 0)),
            fixed((own, d)),
            fixed((1, d)),
        ],
        out_shape=[
            hidden, hidden, hidden,
            jax.ShapeDtypeStruct((rows, d), BF),
            jax.ShapeDtypeStruct((wide, own, d), BF),
            jax.ShapeDtypeStruct((own, d), F32),
            jax.ShapeDtypeStruct((1, d), F32),
        ],
        scratch_shapes=[
            buffer, buffer, buffer,
            pltpu.VMEM((own, d), F32), pltpu.VMEM((own, d), F32), pltpu.VMEM((own, d), F32),
            pltpu.VMEM((own, d), BF),
            sems, sems, sems, sems, sems, sems,
        ],
        cost_estimate=pl.CostEstimate(
            flops=16 * rows * d * ff, bytes_accessed=6 * d * ff + 12 * rows * d, transcendentals=rows * ff
        ),
        compiler_params=pltpu.CompilerParams(
            vmem_limit_bytes=58 << 20, collective_id=1, has_side_effects=True
        ),
        name="feed_forward",
    )(x2, gain, g_rows, w_gu, w_gu, w_dn)


def backward_kernel(
    plan, kv_heads, heads, dx2_ref, qe_ref, kx, vx, o_ref, wo_ref, wq_ref, cos_ref, sin_ref, dn_ref,
    dq_ref, sums, dh_ref, db_out, dn_got,
    db_buf, in_buf, out_buf, term_acc, rs_send, rs_recv, dn_send, dn_recv, out_sem, *chain_sems
):
    wide, cw, chunk, own = plan.wide, plan.cw, plan.chunk, plan.own
    rows = heads * cw
    width = heads * HD
    z = lax.axis_index("wide")
    index = lax.axis_index("seq") * lax.axis_size("narrow") + lax.axis_index("narrow")
    unit, g = pl.program_id(0), pl.program_id(1)
    last_unit, last_g = 2 * wide - 1, kv_heads - 1
    place = jnp.where(unit == 0, 0, jnp.where(unit == last_unit, 1, unit + 1))
    piece, half = place // 2, lax.rem(place, 2)
    w = near_of(plan, z, piece)
    r = lax.rem(w - z + wide, wide)
    c = jnp.where(half == 1, 2 * plan.group - 1 - index, index)
    chain = Chain(plan, db_buf, chain_sems)
    low_rows = pl.ds(pl.multiple_of(half * cw, cw), cw)

    def give(device):
        return push(out_buf.at[device], in_buf.at[z], rs_send.at[device], rs_recv.at[z], {"wide": device})

    def give_down(p):
        device = near_of(plan, z, p)
        slot = lax.rem(z - device + wide, wide)
        return push(dn_ref.at[p], dn_got.at[slot], dn_send.at[p], dn_recv.at[slot], {"wide": device})

    def keep(p):
        device = near_of(plan, z, p)
        slot = lax.rem(device - z + wide, wide)
        return pltpu.make_async_copy(db_buf.at[device], db_out.at[slot], out_sem.at[p])

    @pl.when((unit == 0) & (g == 0))
    def _():
        db_buf[z] = dx2_ref[...].astype(BF)
        greet([along_wide(plan, k) for k in range(1, wide)])
        chain.go(1)
        keep(0).start()

        @pl.loop(0, kv_heads * plan.total // chunk)
        def _(b):
            at = pl.ds(pl.multiple_of(lax.rem(b, plan.total // chunk) * chunk, chunk), chunk)
            sums[b // (plan.total // chunk), at, :] = jnp.zeros((chunk, 128), F32)

    for h in range(1, wide):
        @pl.when((unit == 2 * h - 1) & (g == 0))
        def _():
            chain.arrive(h)
            if h + 1 < wide:
                chain.go(h + 1)

        @pl.when((unit == 2 * h - 2) & (g == last_g))
        def _():
            give_down(h).start()

        @pl.when((unit == 2 * h - 1) & (g == last_g))
        def _():
            keep(h).start()

    lane = lax.broadcasted_iota(jnp.int32, (cw, 128), 1)
    columns = pl.ds(pl.multiple_of(g * width, width), width)
    grad = lax.dot_general(db_buf[w, low_rows, :], wo_ref[g], NT, preferred_element_type=F32)
    do = split_heads(grad.astype(BF).astype(F32), heads, False)
    o = split_heads(o_ref[r, low_rows, columns].astype(F32), heads, False)
    marked = []
    for one, other in zip(o, do):
        clean = jnp.where(lane >= HD, other, 0.0)
        first, second, third = pieces_of(-jnp.sum(one * clean, axis=1, keepdims=True))
        tile = jnp.where(lane == 0, first, clean)
        tile = jnp.where(lane == 1, second, tile)
        marked.append(jnp.where(lane == 2, third, tile))
    dox32 = jnp.concatenate(marked, axis=0)
    wide_lane = lax.broadcasted_iota(jnp.int32, (rows, 128), 1)
    dox = dox32.astype(BF)
    do_clean = jnp.where(wide_lane >= HD, dox32, 0.0).astype(BF)
    q = qe_ref[r, g, half]
    q_clean = jnp.where(wide_lane < HD, q.astype(F32), 0.0).astype(BF)

    def step(j, dq, diagonal=False):
        at = pl.ds(pl.multiple_of(j * chunk, chunk), chunk)
        key = kx[g, at, :]
        s = lax.dot_general(key, q, NT, preferred_element_type=F32)
        if diagonal:
            row = lax.broadcasted_iota(jnp.int32, (chunk, rows), 1) % cw + w * cw
            col = lax.broadcasted_iota(jnp.int32, (chunk, rows), 0)
            s = jnp.where(col <= row, s, NEG)
        p = jnp.exp(s)
        dp = lax.dot_general(vx[g, at, :], dox, NT, preferred_element_type=F32)
        ds = (p * dp).astype(BF)
        sums[g, at, :] += jnp.dot(ds, q_clean, preferred_element_type=F32) + jnp.dot(
            p.astype(BF), do_clean, preferred_element_type=F32
        )
        return dq + lax.dot_general(ds, key, TN, preferred_element_type=F32)

    dq = lax.fori_loop(0, c, step, jnp.zeros((rows, 128), F32))
    dq = step(c, dq, True) * (HD ** -0.5)
    dq = join_heads([dq[h * cw : (h + 1) * cw] for h in range(heads)], True)
    at = pl.ds(pl.multiple_of(r * own + half * cw, cw), cw)
    dq = dq * widen(cos_ref[at, :], width) + turn(dq, -1.0) * widen(sin_ref[at, :], width)
    dq = dq.astype(BF)
    dq_ref[at, columns] = dq

    term = lax.dot_general(dq, wq_ref[:, columns], NT, preferred_element_type=F32)

    @pl.when(g == 0)
    def _():
        term_acc[...] = term

    @pl.when(g > 0)
    def _():
        term_acc[...] += term

    @pl.when((g == last_g) & (piece == 0))
    def _():
        dh_ref[low_rows, :] = term_acc[...]

    @pl.when((g == last_g) & (piece > 0))
    def _():
        out_buf[w, low_rows, :] = term_acc[...].astype(BF)

    @pl.when((g == last_g) & (piece > 0) & (half == 1))
    def _():
        give(w).start()

    @pl.when((unit == last_unit) & (g == last_g))
    def _():
        for p in range(1, wide):
            other = near_of(plan, z, p)
            push(out_buf.at[z], in_buf.at[other], rs_send.at[z], rs_recv.at[other], {"wide": other}).wait_recv()
        tall = min(32, own)

        @pl.loop(0, own // tall)
        def _(b):
            at = pl.ds(pl.multiple_of(b * tall, tall), tall)
            total = dh_ref[at, :]
            for p in range(1, wide):
                total = total + in_buf[near_of(plan, z, p), at, :].astype(F32)
            dh_ref[at, :] = total

        chain.finish()
        for p in range(wide):
            keep(p).wait()
        for p in range(1, wide):
            other = near_of(plan, z, p)
            slot = lax.rem(other - z + wide, wide)
            push(dn_ref.at[p], dn_got.at[slot], dn_send.at[p], dn_recv.at[slot], {"wide": other}).wait_recv()
            give(other).wait_send()
            give_down(p).wait_send()


def backward_call(plan, dx2, qe, kx, vx, o, w_o, w_q, cos, sin, down, heads):
    kv_heads, total, _ = kx.shape
    own, d = dx2.shape
    wide, rows, cw = plan.wide, plan.rows, plan.cw
    qw = w_q.shape[1]
    pairs = kv_heads * heads * total * rows // 2
    fixed = lambda a: pl.BlockSpec(a.shape, lambda u, g: (0,) * a.ndim, pipeline_mode=pl.Buffered(1))
    hbm = pl.BlockSpec(memory_space=pl.ANY)
    given = [dx2, qe, kx, vx, o, w_o.reshape(kv_heads, heads * HD, d), w_q, cos, sin]
    outs = [
        jax.ShapeDtypeStruct((rows, qw), BF),
        jax.ShapeDtypeStruct((kv_heads, total, 128), F32),
        jax.ShapeDtypeStruct((own, d), F32),
    ]
    pieces = jax.ShapeDtypeStruct((wide, own, d), BF)
    buffer = pltpu.VMEM((wide, own, d), BF)
    sems = pltpu.SemaphoreType.DMA((wide,))
    return pl.pallas_call(
        functools.partial(backward_kernel, plan, kv_heads, heads),
        grid=(2 * wide, kv_heads),
        in_specs=[fixed(a) for a in given] + [hbm],
        out_specs=[fixed(a) for a in outs] + [hbm, hbm],
        out_shape=outs + [pieces, pieces],
        scratch_shapes=[buffer, buffer, buffer, pltpu.VMEM((cw, d), F32)] + [sems] * 9,
        cost_estimate=pl.CostEstimate(
            flops=36 * pairs * HD, bytes_accessed=12 * kv_heads * total * 128, transcendentals=pairs
        ),
        compiler_params=pltpu.CompilerParams(
            vmem_limit_bytes=60 << 20, collective_id=3, has_side_effects=True
        ),
        name="attention_backward",
    )(*given, down)


def tail_kernel(
    plan, kv_heads, sums_ref, h_ref, res_ref, dh_ref, gain2_ref, dx2_ref, x_ref, gain_ref, wkv_ref,
    cos_ref, sin_ref, res_out, got_out, gain_out, kv_out,
    swap_out, swap_in, low, near_in, dkv, head_in, dh_acc, dx_low, every, results,
    gain_part, gain_in, gain_sum, gain_all, kv_part, kv_in,
    swap_sem, near_send, near_recv, head_send, head_recv, part_send, part_recv,
    res_send, res_recv, gain_send, gain_recv, gain2_send, gain2_recv, kv_send, kv_recv, own_sem, *chain_sems
):
    group, wide, chunk, cw, own = plan.group, plan.wide, plan.chunk, plan.cw, plan.own
    narrow = group // 2
    part = dx_low.shape[1] // narrow
    seq, me, z = lax.axis_index("seq"), lax.axis_index("narrow"), lax.axis_index("wide")
    index = seq * narrow + me
    res_chain = Chain(plan, results, chain_sems[:4])
    dx_chain = Chain(plan, every, chain_sems[4:])

    def device(k):
        return lax.rem(index + k + group, group)

    def member(k):
        return {"seq": device(k) // narrow, "narrow": lax.rem(device(k), narrow)}

    greet([member(k) for k in range(1, group)] + [along_wide(plan, r) for r in range(1, wide)])

    def slab(ref, other):
        rows = pl.ds(pl.multiple_of((other // narrow) * cw, cw), cw)
        return ref.at[rows, pl.ds(pl.multiple_of(lax.rem(other, narrow) * part, part), part)]

    class Parts:
        def __init__(self, ref, slots, send, recv, stay):
            self.ref, self.slots, self.send, self.recv = ref, slots, send, recv
            self.stay = pltpu.make_async_copy(slab(ref, index), slots.at[z, index], stay)

        def to(self, k):
            return push(slab(self.ref, device(k)), self.slots.at[z, index], self.send.at[k], self.recv.at[k], member(k))

        def start(self):
            for k in range(1, group):
                self.to(k).start()
            self.stay.start()

        def wait(self):
            self.stay.wait()
            for k in range(1, group):
                other = device(-k)
                push(
                    slab(self.ref, index), self.slots.at[z, other], self.send.at[k], self.recv.at[k], member(k)
                ).wait_recv()

        def sent(self):
            for k in range(1, group):
                self.to(k).wait_send()

    def place(owner_seq, half, n):
        quarter = owner_seq if half == 0 else 3 - owner_seq
        return pl.ds(
            pl.multiple_of((quarter * narrow + (n if half == 0 else narrow - 1 - n)) * chunk, chunk), chunk
        )

    @pl.loop(0, narrow)
    def _(n):
        for g in range(kv_heads):
            for half in range(2):
                swap_out[n, g, half] = sums_ref[g, place(1 - seq, half, n), :].astype(BF)

    swap = push(swap_out, swap_in, swap_sem.at[0], swap_sem.at[1], {"seq": 1 - seq})
    swap.start()
    res_parts = Parts(res_ref, results, res_send, res_recv, own_sem.at[0])
    res_parts.start()
    swap.wait_recv()

    @pl.loop(0, narrow)
    def _(n):
        for g in range(kv_heads):
            for half in range(2):
                total = sums_ref[g, place(seq, half, n), :] + swap_in[n, g, half].astype(F32)
                low[n, g, half] = total.astype(BF)

    def near(k):
        other = lax.rem(me + k, narrow)
        return push(low.at[other], near_in.at[k], near_send.at[k], near_recv.at[k], {"narrow": other})

    for k in range(1, narrow):
        near(k).start()
    res_parts.wait()
    res_chain.go(1)
    for k in range(1, narrow):
        near(k).wait_recv()

    lane = lax.broadcasted_iota(jnp.int32, (cw, 128), 1)
    for r in range(wide):
        at = pl.ds(pl.multiple_of(lax.rem(z + r, wide) * cw, cw), cw)
        for half in range(2):
            rows = slice((2 * r + half) * cw, (2 * r + half + 1) * cw)
            for g in range(kv_heads):
                total = low[me, g, half, at, :].astype(F32)
                for k in range(1, narrow):
                    total = total + near_in[k, g, half, at, :].astype(F32)
                back = total * cos_ref[rows, :] + turn(total, -1.0) * sin_ref[rows, :]
                dkv[rows, g * 128 : (g + 1) * 128] = jnp.where(lane < HD, back, total).astype(BF)

    def heads_to(r):
        mine = dkv.at[pl.ds(r * own, own)]
        return push(mine, head_in.at[r], head_send.at[r], head_recv.at[r], along_wide(plan, r))

    for r in range(1, wide):
        heads_to(r).start()

    for n in range(narrow):
        columns = slice(n * part, (n + 1) * part)
        kv_part[n] = lax.dot_general(dkv[...], h_ref[:, columns], TN, preferred_element_type=F32).astype(BF)

    def kv_to(k):
        return push(kv_part.at[lax.rem(device(k), narrow)], kv_in.at[k], kv_send.at[k], kv_recv.at[k], member(k))

    for k in range(1, group):
        kv_to(k).start()
    if wide > 1:
        res_chain.arrive(1)
    if wide > 2:
        res_chain.go(2)

    tile = min(512, part)
    for r in range(wide):
        if r > 0:
            heads_to(r).wait_recv()
        mine = dkv[0:own] if r == 0 else head_in[r]

        @pl.loop(0, dh_acc.shape[1] // tile)
        def _(b):
            at = pl.ds(pl.multiple_of(b * tile, tile), tile)
            more = lax.dot_general(mine, wkv_ref[r, at, :], NT, preferred_element_type=F32)
            dh_acc[:, at] = (dh_ref[:, at] if r == 0 else dh_acc[:, at]) + more

    gain_part[0:1, :] = jnp.zeros_like(gain2_ref[...])
    gain_part[1:2, :] = gain2_ref[...]
    tall = min(32, own)

    @pl.loop(0, own // tall)
    def _(b):
        at = pl.ds(pl.multiple_of(b * tall, tall), tall)
        dh1 = dh_acc[at, :]
        x = x_ref[at, :].astype(F32)
        scale = lax.rsqrt(jnp.mean(x * x, axis=1, keepdims=True) + EPS)
        z1 = x * scale
        gain_part[0:1, :] += jnp.sum(dh1 * z1, axis=0, keepdims=True)
        dz1 = dh1 * gain_ref[...]
        inner = jnp.mean(dz1 * z1, axis=1, keepdims=True)
        dx_low[at, :] = (dx2_ref[at, :] + scale * (dz1 - z1 * inner)).astype(BF)

    dx_parts = Parts(dx_low, every, part_send, part_recv, own_sem.at[1])
    dx_parts.start()

    def gain_to(k):
        columns = pl.ds(pl.multiple_of(lax.rem(device(k), narrow) * part, part), part)
        return push(gain_part.at[:, columns], gain_in.at[k], gain_send.at[k], gain_recv.at[k], member(k))

    for k in range(1, group):
        gain_to(k).start()
    for h in range(2, wide):
        res_chain.arrive(h)
        if h + 1 < wide:
            res_chain.go(h + 1)
    dx_parts.wait()
    dx_chain.go(1)

    gain = gain_part[:, pl.ds(pl.multiple_of(me * part, part), part)]
    for k in range(1, group):
        gain_to(k).wait_recv()
        gain = gain + gain_in[k]
    gain_sum[...] = gain

    def gain_on(r):
        return push(gain_sum, gain_all.at[r], gain2_send.at[r], gain2_recv.at[r], along_wide(plan, r))

    for r in range(1, wide):
        gain_on(r).start()
    for k in range(1, group):
        kv_to(k).wait_recv()
    res_keep = pltpu.make_async_copy(results, res_out, own_sem.at[2])
    res_keep.start()
    kv_out[...] = kv_part[me].astype(F32)
    for k in range(1, group):
        kv_out[...] += kv_in[k].astype(F32)
    gain = gain_sum[...]
    for r in range(1, wide):
        gain_on(r).wait_recv()
        gain = gain + gain_all[r]
    gain_out[...] = gain
    for h in range(1, wide):
        dx_chain.arrive(h)
        if h + 1 < wide:
            dx_chain.go(h + 1)
    got_keep = pltpu.make_async_copy(every, got_out, own_sem.at[3])
    got_keep.start()

    res_chain.finish()
    dx_chain.finish()
    swap.wait_send()
    for k in range(1, narrow):
        near(k).wait_send()
    for r in range(1, wide):
        heads_to(r).wait_send()
        gain_on(r).wait_send()
    res_parts.sent()
    dx_parts.sent()
    for k in range(1, group):
        gain_to(k).wait_send()
        kv_to(k).wait_send()
    res_keep.wait()
    got_keep.wait()


def tail_call(plan, sums, h, res, dh, gain2, dx2, x, gain, w_kv, cos, sin):
    kv_heads = sums.shape[0]
    own, d = dh.shape
    group, wide, chunk, cw = plan.group, plan.wide, plan.chunk, plan.cw
    narrow = group // 2
    part = d // narrow
    kv_width = kv_heads * 128
    dma = pltpu.SemaphoreType.DMA
    quarter = pltpu.VMEM((narrow, kv_heads, 2, chunk, 128), BF)
    slots = (wide, group, cw, part)
    given = [sums, h, res, dh, gain2, dx2, x, gain, w_kv, cos, sin]
    whole = pl.BlockSpec(memory_space=pltpu.VMEM)
    hbm = pl.BlockSpec(memory_space=pl.ANY)
    return pl.pallas_call(
        functools.partial(tail_kernel, plan, kv_heads),
        in_specs=[whole] * len(given),
        out_specs=[hbm, hbm, whole, whole],
        out_shape=[
            jax.ShapeDtypeStruct(slots, BF),
            jax.ShapeDtypeStruct(slots, BF),
            jax.ShapeDtypeStruct((2, part), F32),
            jax.ShapeDtypeStruct((kv_width, part), F32),
        ],
        scratch_shapes=[
            quarter, quarter, quarter, quarter,
            pltpu.VMEM((plan.rows, kv_width), BF),
            pltpu.VMEM((wide, own, kv_width), BF),
            pltpu.VMEM((own, d), F32),
            pltpu.VMEM((own, d), BF),
            pltpu.VMEM(slots, BF),
            pltpu.VMEM(slots, BF),
            pltpu.VMEM((2, d), F32),
            pltpu.VMEM((group, 2, part), F32),
            pltpu.VMEM((2, part), F32),
            pltpu.VMEM((wide, 2, part), F32),
            pltpu.VMEM((narrow, kv_width, part), BF),
            pltpu.VMEM((group, kv_width, part), BF),
            dma((2,)), dma((narrow,)), dma((narrow,)), dma((wide,)), dma((wide,)), dma((group,)), dma((group,)),
            dma((group,)), dma((group,)), dma((group,)), dma((group,)), dma((wide,)), dma((wide,)),
            dma((group,)), dma((group,)), dma((4,)),
        ] + [dma((wide,))] * 8,
        cost_estimate=pl.CostEstimate(
            flops=200 * own * d * wide * kv_width, bytes_accessed=4 * sums.size, transcendentals=0
        ),
        compiler_params=pltpu.CompilerParams(
            vmem_limit_bytes=60 << 20, collective_id=2, has_side_effects=True
        ),
        name="input_gradient",
    )(*given)


def assemble_kernel(plan, s_ref, in_ref, out_ref):
    group = plan.group
    for l in range(group):
        owner = jnp.where(s_ref[0] >= group // 2, group - 1 - l, l)
        out_ref[l, 0] = in_ref[0, owner].astype(out_ref.dtype)


def assemble_call(plan, scalars, values, dtype):
    wide, group, cw, part = values.shape
    out = pl.pallas_call(
        functools.partial(assemble_kernel, plan),
        grid_spec=pltpu.PrefetchScalarGridSpec(
            num_scalar_prefetch=1,
            grid=(wide,),
            in_specs=[pl.BlockSpec((1, group, cw, part), lambda w, s: (w, 0, 0, 0))],
            out_specs=[pl.BlockSpec((group, 1, cw, part), lambda w, s: (0, w, 0, 0))],
        ),
        out_shape=[jax.ShapeDtypeStruct((group, wide, cw, part), dtype)],
        cost_estimate=pl.CostEstimate(flops=values.size, bytes_accessed=6 * values.size, transcendentals=0),
        compiler_params=pltpu.CompilerParams(vmem_limit_bytes=40 << 20),
        name="assemble",
    )(scalars, values)[0]
    return out.reshape(group * wide * cw, part)


def half_of(weight, seq_index, seq_count):
    part = weight.shape[0] // seq_count
    return lax.dynamic_slice_in_dim(weight, seq_index * part, part, 0)


def body(
    tokens, attn_gain, w_query, w_key, w_value, w_out, ffn_gain, w_gate, w_up, w_down,
    segment_ids, token_mask, out_grad,
):
    seq_count = lax.axis_size("seq")
    narrow = lax.axis_size("narrow")
    wide = lax.axis_size("wide")
    group = seq_count * narrow
    seq_index = lax.axis_index("seq")
    narrow_index = lax.axis_index("narrow")
    wide_index = lax.axis_index("wide")
    index = seq_index * narrow + narrow_index
    total = segment_ids.shape[0]
    plan = Plan(total, group, wide)
    chunk, cw, rows, own = plan.chunk, plan.cw, plan.rows, plan.own
    d_part = tokens.shape[1]
    d = d_part * narrow
    qw = w_query.shape[1]
    kw = w_key.shape[1]
    kv_heads = kw // HD
    heads = qw // kw
    ff = w_gate.shape[1]
    pieces = range(wide)

    start_one = jnp.sum((segment_ids < 1).astype(jnp.int32))
    start_two = jnp.sum((segment_ids < 2).astype(jnp.int32))
    scalars = jnp.stack([index, start_one, start_two, wide_index]).astype(jnp.int32)

    def swap(values, axes, k, size):
        return values if k == 0 else lax.ppermute(values, axes, [(a, a ^ k) for a in range(size)])

    def exchange(parts):
        sent = [lax.dynamic_index_in_dim(parts, index ^ k, 0, keepdims=False) for k in range(group)]
        return jnp.stack([swap(part, SN, k, group) for k, part in enumerate(sent)])

    def to_rows(values):
        parts = values.reshape(group, wide, cw, d_part)
        return exchange(jnp.where(seq_index == 1, parts[::-1], parts))

    def send(values, r):
        return values if r == 0 else lax.ppermute(values, "wide", [(a, (a + r) % wide) for a in pieces])

    def wide_total(parts):
        out = parts[0]
        for r in range(1, len(parts)):
            out = out + send(parts[r].astype(BF), r).astype(F32)
        return out

    def gather_weight(weight):
        return lax.all_gather(half_of(weight, seq_index, seq_count), NS, axis=0, tiled=True)

    def scatter_grad(grad):
        mine = lax.psum_scatter(grad.astype(BF), NS, scatter_dimension=0, tiled=True)
        return lax.all_gather(mine, "seq", axis=0, tiled=True).astype(F32)

    def after(values, *others):
        return lax.optimization_barrier((values, *others))[0]

    x_parts = to_rows(tokens)
    w_kv = jnp.concatenate(
        [w_key.reshape(d_part, kv_heads, 1, HD), w_value.reshape(d_part, kv_heads, 1, HD)], axis=2
    ).reshape(d_part, 2 * kw)
    w_qkv = gather_weight(jnp.concatenate([w_query, w_kv], axis=1))
    gains = jnp.stack([attn_gain, ffn_gain])
    gains = jnp.stack([swap(gains, "narrow", k, narrow) for k in range(narrow)])
    order = narrow_index ^ jnp.arange(narrow)
    gains = jnp.sum(jnp.where((order[:, None] == jnp.arange(narrow)[None, :])[:, :, None, None], gains[None], 0.0), axis=1)
    gains = jnp.transpose(gains, (1, 0, 2)).reshape(2, d)
    gain_one, gain_two = gains[0:1], gains[1:2]

    row = jnp.arange(rows, dtype=jnp.int32)
    row_chunk = jnp.where((row // cw) % 2 == 1, 2 * group - 1 - index, index)
    row_block = (row // own + wide_index) % wide
    row_token = row_chunk * chunk + row_block * cw + row % cw
    row_start = jnp.where(row_token >= start_two, start_two, jnp.where(row_token >= start_one, start_one, 0))
    row_pos = (row_token - row_start).astype(F32)
    frequency = THETA ** (-2.0 * jnp.arange(HD // 2, dtype=F32) / HD)
    angles = row_pos[:, None] * jnp.tile(frequency, 4)[None, :]
    cos, sin = jnp.cos(angles), jnp.sin(angles)

    h_one, q, kv, x_low = qkv_call(plan, scalars, x_parts, gain_one, w_qkv, cos, sin, qw)
    near = [swap(kv, "narrow", k, narrow) for k in range(narrow)]
    far = [swap(part, "seq", 1, seq_count) for part in near]
    kv_all = jnp.concatenate(near + far, axis=0)

    lane = jnp.arange(128, dtype=jnp.int32)[None, :]
    closed = (segment_ids[:, None] != lane - HD) | (token_mask[:, None] != 1)
    kf = jnp.where((lane >= HD) & (lane < HD + 3) & closed, NEG, 0.0)
    kf = jnp.where((lane >= HD + 3) & (lane < HD + 6), 1.0, kf).astype(BF)
    kx, vx = keys_call(plan, scalars, kv_all, kf, kv_heads)

    w_o = jnp.transpose(gather_weight(after(w_out, x_parts)).reshape(narrow, qw, d_part), (1, 0, 2)).reshape(qw, d)
    w_gu = gather_weight(after(jnp.concatenate([w_gate, w_up], axis=1), x_parts))
    w_dn = gather_weight(after(w_down, x_parts)).reshape(narrow, ff, d_part)
    row_valid = lax.dynamic_slice_in_dim(token_mask, seq_index * (group * chunk), group * chunk, 0)
    g_low = jnp.where(row_valid[:, None] == 1, out_grad, jnp.zeros_like(out_grad))
    g_parts = to_rows(after(g_low, kv_all))
    g_rows = rows_call(plan, scalars, g_parts)

    far_first = sorted(pieces, key=lambda r: (r == 0, -min(r, wide - r)))
    o, qe, attn = [None] * wide, [None] * wide, [None] * wide
    for r in far_first:
        o[r], qe[r] = forward_call(plan, scalars, q, kx, vx, kv_heads, heads, r)
        attn[r] = jnp.dot(o[r], w_o, preferred_element_type=F32)
    x_own = x_low.astype(F32)
    x2 = x_own + wide_total(attn)

    act, d_gate, d_up, h_all, down, dx2, grad_gain_two = ffn_call(plan, x2, gain_two, g_rows, w_gu, w_dn)

    o = jnp.stack(o)
    w_q, w_kv = w_qkv[:, :qw], w_qkv[:, qw:]
    dq, sums, dh1, db, down_in = backward_call(
        plan, dx2, jnp.stack(qe), kx, vx, o, w_o, w_q, cos, sin, down, heads
    )
    result = x2 + down[0].astype(F32)
    for r in range(1, wide):
        result = result + down_in[r].astype(F32)

    w_kv = jnp.stack([send(w_kv, r) for r in pieces])
    result, input_grad, gain_grads, grad_kv = tail_call(
        plan, sums, h_one, result.astype(BF), dh1, grad_gain_two, dx2, x_low, gain_one, w_kv, cos, sin
    )
    result = assemble_call(plan, scalars, result, BF)
    input_grad = assemble_call(plan, scalars, input_grad, F32)

    def tn(left, right):
        return lax.dot_general(left, right, TN, preferred_element_type=F32).astype(BF)

    def tn_split(left, right):
        return jnp.concatenate([tn(left, right[:, n * d_part : (n + 1) * d_part]) for n in range(narrow)], axis=0)

    grad_gu = scatter_grad(jnp.concatenate([tn(h_all, d_gate), tn(h_all, d_up)], axis=1))
    grad_dn = scatter_grad(tn_split(act, g_rows))
    grad_o = scatter_grad(tn_split(o.reshape(rows, qw), db.reshape(rows, d)))
    grad_q = scatter_grad(tn(h_one, dq))
    grad_kv = jnp.transpose(grad_kv.reshape(kv_heads, 2, HD, d_part), (3, 0, 1, 2))
    return (
        result,
        input_grad,
        gain_grads[0],
        grad_q,
        grad_kv[:, :, 0].reshape(d_part, kw),
        grad_kv[:, :, 1].reshape(d_part, kw),
        grad_o,
        gain_grads[1],
        grad_gu[:, :ff],
        grad_gu[:, ff:],
        grad_dn,
    )


def solution(mesh):
    width_in, width_out = P("narrow", "wide"), P("wide", "narrow")
    acts = P("seq", "narrow")
    return jax.shard_map(
        body,
        mesh=mesh,
        in_specs=(
            acts, P("narrow"), width_in, width_in, width_in, width_out, P("narrow"),
            width_in, width_in, width_out, P(), P(), acts,
        ),
        out_specs=(
            acts, acts, P("narrow"), width_in, width_in, width_in, width_out, P("narrow"),
            width_in, width_in, width_out,
        ),
        check_vma=False,
    )
```

```python
import functools

import jax
import jax.numpy as jnp
from jax import lax
from jax.experimental import pallas as pl
from jax.experimental.pallas import tpu as pltpu
from jax.sharding import PartitionSpec as P

HD = 64
EPS = 1e-05
THETA = 500000.0
NEG = -1e30
SN = ("seq", "narrow")
NS = ("narrow", "seq")
BF = jnp.bfloat16
F32 = jnp.float32
NT = (((1,), (1,)), ((), ()))
TN = (((0,), (0,)), ((), ()))


def pieces_of(value):
    first = value.astype(BF).astype(F32)
    second = (value - first).astype(BF).astype(F32)
    third = (value - first - second).astype(BF).astype(F32)
    return first, second, third


class Plan:
    def __init__(self, total, group, wide):
        self.total, self.group, self.wide = total, group, wide
        self.chunk = total // (2 * group)
        self.cw = self.chunk // wide
        self.rows = 2 * self.chunk
        self.own = 2 * self.cw


def near_of(plan, z, p):
    side = jnp.minimum(z, plan.wide - 1 - z)
    both = jnp.where(lax.rem(p, 2) == 1, z + (p + 1) // 2, z - p // 2)
    one = jnp.where(z <= plan.wide - 1 - z, z + p - side, z - p + side)
    return jnp.where(p <= 2 * side, both, one)


def turn(values, sign):
    width = values.shape[1]
    lane = lax.broadcasted_iota(jnp.int32, values.shape, 1)
    left, right = pltpu.roll(values, width - HD // 2, 1), pltpu.roll(values, HD // 2, 1)
    return jnp.where(lane % HD < HD // 2, -sign * left, sign * right)


def widen(table, width):
    return jnp.concatenate([table] * (width // 128), axis=1) if width > 128 else table


MESH = pl.DeviceIdType.MESH


def greet(partners):
    barrier = pltpu.get_barrier_semaphore()
    for partner in partners:
        pl.semaphore_signal(barrier, inc=1, device_id=partner, device_id_type=MESH)
    pl.semaphore_wait(barrier, len(partners))


def along_wide(plan, r):
    return {"wide": lax.rem(lax.axis_index("wide") + r + plan.wide, plan.wide)}


def push(src, dst, send, recv, device):
    return pltpu.make_async_remote_copy(
        src_ref=src, dst_ref=dst, send_sem=send, recv_sem=recv, device_id=device, device_id_type=MESH
    )


class Chain:
    def __init__(self, plan, buf, sems):
        self.wide, self.buf, self.sems = plan.wide, buf, sems
        self.z = lax.axis_index("wide")

    def copy(self, slot, h, way):
        send, recv = (self.sems[0], self.sems[1]) if way > 0 else (self.sems[2], self.sems[3])
        return push(self.buf.at[slot], self.buf.at[slot], send.at[h], recv.at[h], {"wide": self.z + way})

    def sends(self, h, way):
        z, last = self.z, self.wide - 1
        return (z >= h - 1) & (z < last) if way > 0 else (z + h - 1 <= last) & (z > 0)

    def go(self, h):
        for way in (1, -1):
            @pl.when(self.sends(h, way))
            def _():
                self.copy(self.z - way * (h - 1), h, way).start()

    def arrive(self, h):
        for way in (1, -1):
            @pl.when(self.z >= h if way > 0 else self.z + h <= self.wide - 1)
            def _():
                slot = self.z - way * h
                send, recv = (self.sems[0], self.sems[1]) if way > 0 else (self.sems[2], self.sems[3])
                push(self.buf.at[slot], self.buf.at[slot], send.at[h], recv.at[h], {"wide": slot}).wait_recv()

    def finish(self):
        for h in range(1, self.wide):
            for way in (1, -1):
                @pl.when(self.sends(h, way))
                def _():
                    self.copy(self.z - way * (h - 1), h, way).wait_send()


class Group:
    def __init__(self, plan):
        self.size, self.narrow = plan.group, plan.group // 2
        self.seq, self.me = lax.axis_index("seq"), lax.axis_index("narrow")
        self.index = self.seq * self.narrow + self.me
        self.sibling = {"seq": 1 - self.seq}

    def device(self, k):
        return lax.rem(self.index + k + self.size, self.size)

    def member(self, k):
        return {"seq": self.device(k) // self.narrow, "narrow": lax.rem(self.device(k), self.narrow)}

    def beside(self, k):
        return lax.rem(self.me + k + self.narrow, self.narrow)


def head_kernel(
    plan, kv_heads, qw, x_ref, g_ref, w_ref, gains_ref, cos_ref, sin_ref, kf_ref,
    h_out, q_out, own_out, kx, vx, w_out, gains_out, g_out, side_out,
    x_buf, side_buf, side_send, side_recv, w_buf, kv_buf, g_buf, gain_buf,
    x_send, x_recv, x_stay, w_send, w_recv, w_on_send, w_on_recv, gain_send, gain_recv,
    g_send, g_recv, kv_send, kv_recv, kv_on_send, kv_on_recv, keep_sem, *chain_sems
):
    group, wide, chunk, cw, own = plan.group, plan.wide, plan.chunk, plan.cw, plan.own
    team = Group(plan)
    narrow, seq, me = team.narrow, team.seq, team.me
    z = lax.axis_index("wide")
    part = x_ref.shape[3]
    d = part * narrow
    width = w_ref.shape[1]
    fold = part // 2
    chain = Chain(plan, g_buf, chain_sems)
    greet([team.member(k) for k in range(1, group)] + [along_wide(plan, r) for r in range(1, wide)])

    def spot(ref, slot, source):
        rows = pl.ds(pl.multiple_of((source // narrow) * cw, cw), cw)
        return ref.at[slot, rows, pl.ds(pl.multiple_of(lax.rem(source, narrow) * part, part), part)]

    def chunk_for(device):
        return jnp.where(seq == 0, device, group - 1 - device)

    def x_to(r, k):
        src = x_ref.at[chunk_for(team.device(k)), lax.rem(z + r, wide)]
        return push(src, spot(x_buf, r, team.index), x_send.at[r, k], x_recv.at[r, k], team.member(k))

    def x_from(r, k):
        src = x_ref.at[0, 0]
        return push(src, spot(x_buf, r, team.device(-k)), x_send.at[r, k], x_recv.at[r, k], team.member(k))

    def x_own(r):
        src = x_ref.at[chunk_for(team.index), lax.rem(z + r, wide)]
        return pltpu.make_async_copy(src, spot(x_buf, r, team.index), x_stay.at[r])

    def x_start(r):
        for k in range(1, group):
            x_to(r, k).start()
        x_own(r).start()

    def g_to(k):
        src = g_ref.at[chunk_for(team.device(k))]
        return push(src, spot(g_buf, z, team.index), g_send.at[k], g_recv.at[k], team.member(k))

    def w_rows(n, core):
        return w_buf.at[pl.ds(pl.multiple_of(n * part + core * fold, fold), fold)]

    def w_to(k):
        src = w_ref.at[pl.ds(pl.multiple_of(seq * fold, fold), fold)]
        return push(src, w_rows(me, seq), w_send.at[k], w_recv.at[k], {"narrow": team.beside(k)})

    def w_from(k):
        n = team.beside(-k)
        return push(w_rows(n, seq), w_rows(n, seq), w_send.at[k], w_recv.at[k], {"narrow": n})

    def w_on(k, core):
        n = team.beside(-k)
        return push(w_rows(n, core), w_rows(n, core), w_on_send.at[k], w_on_recv.at[k], team.sibling)

    def side_to(r, slot):
        mine = w_ref.at[:, qw:]
        return push(mine, side_buf.at[slot], side_send.at[r], side_recv.at[r], along_wide(plan, r))

    def gain_to(k, slot):
        return push(gains_ref, gain_buf.at[slot], gain_send.at[k], gain_recv.at[k], {"narrow": team.beside(k)})

    for k in range(1, group):
        g_to(k).start()
    g_stay = pltpu.make_async_copy(g_ref.at[chunk_for(team.index)], spot(g_buf, z, team.index), keep_sem.at[0])
    g_stay.start()
    for k in range(1, narrow):
        w_to(k).start()
        gain_to(k, me).start()
    x_start(0)
    if wide > 1:
        x_start(1)
    for r in range(1, wide):
        side_to(r, z).start()
    side_buf[z] = w_ref[:, qw:]
    w_buf[pl.ds(pl.multiple_of(me * part, part), part), :] = w_ref[...]
    gain_buf[me] = gains_ref[...]
    for k in range(1, narrow):
        w_from(k).wait_recv()
        w_on(k, seq).start()
    g_stay.wait()
    for k in range(1, group):
        push(
            g_ref.at[0], spot(g_buf, z, team.device(-k)), g_send.at[k], g_recv.at[k], team.member(k)
        ).wait_recv()
    chain.go(1)
    for k in range(1, narrow):
        gain_to(k, team.beside(-k)).wait_recv()
        w_on(k, 1 - seq).wait_recv()
    gain_one = jnp.concatenate([gain_buf[n, 0:1] for n in range(narrow)], axis=1)
    gains_out[...] = gain_buf[...]
    w_keep = pltpu.make_async_copy(w_buf, w_out, keep_sem.at[1])
    w_keep.start()

    def kv_rows(core, n, r):
        return kv_buf.at[core, n, pl.ds(pl.multiple_of(r * own, own), own)]

    def kv_to(r, k):
        mine = kv_rows(seq, me, r)
        return push(mine, mine, kv_send.at[r, k], kv_recv.at[r, k], {"narrow": team.beside(k)})

    def kv_from(r, k):
        theirs = kv_rows(seq, team.beside(-k), r)
        return push(theirs, theirs, kv_send.at[r, k], kv_recv.at[r, k], {"narrow": team.beside(k)})

    def kv_on(k, core):
        slot = kv_buf.at[core, team.beside(-k)]
        return push(slot, slot, kv_on_send.at[k], kv_on_recv.at[k], team.sibling)

    @pl.loop(0, wide)
    def _(r):
        x_own(r).wait()
        for k in range(1, group):
            x_from(r, k).wait_recv()
        for later in range(2, wide):
            @pl.when(r == later - 2)
            def _():
                x_start(later)
        at = pl.ds(pl.multiple_of(r * own, own), own)
        low = x_buf[r]
        x = low.astype(F32)
        mean = jnp.mean(x * x, axis=1, keepdims=True)
        h = (x * lax.rsqrt(mean + EPS) * gain_one).astype(BF)
        h_out[at, :] = h
        t = jnp.dot(h, w_buf[...], preferred_element_type=F32)
        lane = lax.broadcasted_iota(jnp.int32, t.shape, 1)
        plain = (lane >= qw) & (lane % 128 >= HD)
        out = t * widen(cos_ref[at, :], width) + turn(t, 1.0) * widen(sin_ref[at, :], width)
        out = jnp.where(plain, t, out)
        q_out[at, :] = (out[:, :qw] * (HD ** -0.5)).astype(BF)
        kv_buf[seq, me, at, :] = out[:, qw:].astype(BF)
        for k in range(1, narrow):
            kv_to(r, k).start()

        @pl.when(r == min(1, wide - 1))
        def _():
            chain.arrive(1)
            if wide > 2:
                chain.go(2)

    kv_on(0, seq).start()
    own_out[...] = x_buf[0]
    if wide > 2:
        chain.arrive(2)
    if wide > 3:
        chain.go(3)
    for k in range(1, narrow):
        for r in range(wide):
            kv_from(r, k).wait_recv()
        kv_on(k, seq).start()
    for k in range(narrow):
        kv_on(k, 1 - seq).wait_recv()

    feature = lax.broadcasted_iota(jnp.int32, (cw, 128), 1)
    ones = jnp.where(feature < 3, 1.0, 0.0).astype(BF)

    @pl.loop(0, 2 * group)
    def _(c):
        late = c >= group
        owner = jnp.where(late, 2 * group - 1 - c, c)
        for r in range(wide):
            at = pl.ds(pl.multiple_of(c * chunk + lax.rem(z + r, wide) * cw, cw), cw)
            source = pl.ds(pl.multiple_of(r * own + jnp.where(late, cw, 0), cw), cw)
            for g in range(kv_heads):
                kv = kv_buf[owner // narrow, lax.rem(owner, narrow), source, g * 128 : (g + 1) * 128]
                kx[g, at, :] = jnp.where(feature < HD, kv, kf_ref[at, :])
                vx[g, at, :] = jnp.where(feature < HD, ones, kv)

    for h in range(3, wide):
        chain.arrive(h)
        if h + 1 < wide:
            chain.go(h + 1)
    for r in range(1, wide):
        side_to(r, lax.rem(z - r + wide, wide)).wait_recv()
        side_to(r, z).wait_send()
    side_out[...] = side_buf[...]
    keep = [
        pltpu.make_async_copy(g_buf.at[near_of(plan, z, p)], g_out.at[p], keep_sem.at[2 + p]) for p in range(wide)
    ]
    for copy in keep:
        copy.start()
    chain.finish()
    for k in range(1, narrow):
        w_to(k).wait_send()
        w_on(k, seq).wait_send()
        gain_to(k, me).wait_send()
        for r in range(wide):
            kv_to(r, k).wait_send()
    for k in range(narrow):
        kv_on(k, seq).wait_send()
    for k in range(1, group):
        g_to(k).wait_send()
        for r in range(wide):
            x_to(r, k).wait_send()
    w_keep.wait()
    for copy in keep:
        copy.wait()


def head_call(plan, x, g, w, gains, cos, sin, kf, qw, kv_heads):
    group, wide, cw, part = x.shape
    narrow = group // 2
    d = part * narrow
    width = w.shape[1]
    rows, own, total = plan.rows, plan.own, plan.total
    dma = pltpu.SemaphoreType.DMA
    whole = pl.BlockSpec(memory_space=pltpu.VMEM)
    hbm = pl.BlockSpec(memory_space=pl.ANY)
    keys = jax.ShapeDtypeStruct((kv_heads, total, 128), BF)
    return pl.pallas_call(
        functools.partial(head_kernel, plan, kv_heads, qw),
        in_specs=[hbm, hbm] + [whole] * 5,
        out_specs=[whole] * 5 + [hbm, whole, hbm, whole],
        out_shape=[
            jax.ShapeDtypeStruct((rows, d), BF),
            jax.ShapeDtypeStruct((rows, qw), BF),
            jax.ShapeDtypeStruct((own, d), BF),
            keys,
            keys,
            jax.ShapeDtypeStruct((d, width), BF),
            jax.ShapeDtypeStruct((narrow, 2, part), F32),
            jax.ShapeDtypeStruct((wide, own, d), BF),
            jax.ShapeDtypeStruct((wide, part, width - qw), BF),
        ],
        scratch_shapes=[
            pltpu.VMEM((wide, own, d), BF),
            pltpu.VMEM((wide, part, width - qw), BF),
            dma((wide,)), dma((wide,)),
            pltpu.VMEM((d, width), BF),
            pltpu.VMEM((2, narrow, rows, width - qw), BF),
            pltpu.VMEM((wide, own, d), BF),
            pltpu.VMEM((narrow, 2, part), F32),
            dma((wide, group)), dma((wide, group)), dma((wide,)),
            dma((narrow,)), dma((narrow,)), dma((narrow,)), dma((narrow,)), dma((narrow,)), dma((narrow,)),
            dma((group,)), dma((group,)),
            dma((wide, narrow)), dma((wide, narrow)), dma((narrow,)), dma((narrow,)),
            dma((2 + wide,)),
        ] + [dma((wide,))] * 4,
        cost_estimate=pl.CostEstimate(
            flops=60 * rows * d * width, bytes_accessed=8 * rows * d + 2 * d * width, transcendentals=rows
        ),
        compiler_params=pltpu.CompilerParams(
            vmem_limit_bytes=60 << 20, collective_id=4, has_side_effects=True
        ),
        name="head",
    )(x, g, w, gains, cos, sin, kf)


def split_heads(block, heads, low):
    tiles = []
    for h in range(heads):
        tile = block[:, (h // 2) * 128 : (h // 2 + 1) * 128]
        if (h % 2 == 0) != low:
            tile = pltpu.roll(tile, HD, 1)
        tiles.append(tile)
    return tiles


def join_heads(tiles, low):
    rows = tiles[0].shape[0]
    lane = lax.broadcasted_iota(jnp.int32, (rows, 128), 1)
    pairs = []
    for h in range(0, len(tiles), 2):
        first, second = tiles[h], tiles[h + 1]
        if low:
            second = pltpu.roll(second, HD, 1)
        else:
            first = pltpu.roll(first, HD, 1)
        pairs.append(jnp.where(lane < HD, first, second))
    return jnp.concatenate(pairs, axis=1)


def forward_kernel(
    plan, kv_heads, heads, s_ref, q_ref, kx, vx, wo_ref, x_ref, o_ref, qe_ref, x2_ref,
    in_buf, out_buf, term_acc, rs_send, rs_recv,
):
    wide, cw, chunk, own = plan.wide, plan.cw, plan.chunk, plan.own
    rows, width = heads * cw, heads * HD
    z = lax.axis_index("wide")
    index = lax.axis_index("seq") * lax.axis_size("narrow") + lax.axis_index("narrow")
    unit, g = pl.program_id(0), pl.program_id(1)
    last_g = kv_heads - 1
    piece, half = wide - 1 - unit // 2, lax.rem(unit, 2)
    w = near_of(plan, z, piece)
    r = lax.rem(w - z + wide, wide)
    c = jnp.where(half == 1, 2 * plan.group - 1 - index, index)
    low_rows = pl.ds(pl.multiple_of(half * cw, cw), cw)
    columns = pl.ds(pl.multiple_of(g * width, width), width)

    def give(device):
        return push(out_buf.at[device], in_buf.at[z], rs_send.at[device], rs_recv.at[z], {"wide": device})

    @pl.when((unit == 0) & (g == 0))
    def _():
        greet([along_wide(plan, k) for k in range(1, wide)])

    lane = lax.broadcasted_iota(jnp.int32, (cw, 128), 1)
    token = c * chunk + w * cw + lax.broadcasted_iota(jnp.int32, (cw, 128), 0)
    segment = (token >= s_ref[0]).astype(jnp.int32) + (token >= s_ref[1]).astype(jnp.int32)
    mark = jnp.where(lane == HD + segment, 1.0, 0.0)
    block = q_ref[pl.ds(pl.multiple_of(r * own + half * cw, cw), cw), columns]
    tiles = split_heads(block.astype(F32), heads, True)
    q32 = jnp.concatenate([jnp.where(lane < HD, t, mark) for t in tiles], axis=0)
    q = q32.astype(BF)

    def step(j, carry, diagonal=False):
        top, acc = carry
        at = pl.ds(pl.multiple_of(j * chunk, chunk), chunk)
        s = lax.dot_general(q, kx[g, at, :], NT, preferred_element_type=F32)
        if diagonal:
            row = lax.broadcasted_iota(jnp.int32, (rows, chunk), 0) % cw + w * cw
            col = lax.broadcasted_iota(jnp.int32, (rows, chunk), 1)
            s = jnp.where(col <= row, s, NEG)
        new = jnp.maximum(top, jnp.max(s, axis=1, keepdims=True))
        p = jnp.exp(s - new).astype(BF)
        acc = acc * jnp.exp(top - new) + jnp.dot(p, vx[g, at, :], preferred_element_type=F32)
        return new, acc

    start = (jnp.full((rows, 1), NEG, F32), jnp.zeros((rows, 128), F32))
    carry = lax.fori_loop(0, c, step, start)
    top, acc = step(c, carry, True)
    total = acc[:, 0:1]
    out = acc / total
    out = join_heads([out[h * cw : (h + 1) * cw] for h in range(heads)], False).astype(BF)
    o_ref[w, low_rows, columns] = out
    first, second, third = pieces_of(-(top + jnp.log(total)))
    wide_lane = lax.broadcasted_iota(jnp.int32, (rows, 128), 1)
    qe = jnp.where(wide_lane == HD + 3, first, q32)
    qe = jnp.where(wide_lane == HD + 4, second, qe)
    qe = jnp.where(wide_lane == HD + 5, third, qe)
    qe_ref[r, g, half] = qe.astype(BF)

    term = jnp.dot(out, wo_ref[g], preferred_element_type=F32)

    @pl.when(g == 0)
    def _():
        term_acc[...] = term

    @pl.when(g > 0)
    def _():
        term_acc[...] += term

    @pl.when((g == last_g) & (piece == 0))
    def _():
        x2_ref[low_rows, :] = x_ref[low_rows, :].astype(F32) + term_acc[...]

    @pl.when((g == last_g) & (piece > 0))
    def _():
        out_buf[w, low_rows, :] = term_acc[...].astype(BF)

    @pl.when((g == last_g) & (piece > 0) & (half == 1))
    def _():
        give(w).start()

    @pl.when((unit == 2 * wide - 1) & (g == last_g))
    def _():
        for p in range(1, wide):
            other = near_of(plan, z, p)
            push(out_buf.at[z], in_buf.at[other], rs_send.at[z], rs_recv.at[other], {"wide": other}).wait_recv()
        tall = min(32, own)

        @pl.loop(0, own // tall)
        def _(b):
            at = pl.ds(pl.multiple_of(b * tall, tall), tall)
            total = x2_ref[at, :]
            for p in range(1, wide):
                total = total + in_buf[near_of(plan, z, p), at, :].astype(F32)
            x2_ref[at, :] = total

        for p in range(1, wide):
            give(near_of(plan, z, p)).wait_send()


def forward_call(plan, starts, q, kx, vx, w_o, x, heads):
    kv_heads, total, _ = kx.shape
    own, d = x.shape
    wide, rows, cw = plan.wide, plan.rows, plan.cw
    qw = q.shape[1]
    pairs = kv_heads * heads * total * rows // 2
    fixed = lambda a: pl.BlockSpec(a.shape, lambda u, g: (0,) * a.ndim, pipeline_mode=pl.Buffered(1))
    given = [q, kx, vx, w_o, x]
    outs = [
        jax.ShapeDtypeStruct((wide, own, qw), BF),
        jax.ShapeDtypeStruct((wide, kv_heads, 2, heads * cw, 128), BF),
        jax.ShapeDtypeStruct((own, d), F32),
    ]
    buffer = pltpu.VMEM((wide, own, d), BF)
    sems = pltpu.SemaphoreType.DMA((wide,))
    return pl.pallas_call(
        functools.partial(forward_kernel, plan, kv_heads, heads),
        grid=(2 * wide, kv_heads),
        in_specs=[pl.BlockSpec(memory_space=pltpu.SMEM)] + [fixed(a) for a in given],
        out_specs=[fixed(a) for a in outs],
        out_shape=outs,
        scratch_shapes=[buffer, buffer, pltpu.VMEM((cw, d), F32), sems, sems],
        cost_estimate=pl.CostEstimate(
            flops=16 * pairs * HD, bytes_accessed=8 * kv_heads * total * 128, transcendentals=pairs
        ),
        compiler_params=pltpu.CompilerParams(
            vmem_limit_bytes=56 << 20, collective_id=5, has_side_effects=True
        ),
        name="attention_forward",
    )(starts, *given)


def ffn_kernel(
    plan, x2_ref, gain_ref, g_ref, wg_ref, wu_ref, wd_ref,
    act_ref, dg_ref, du_ref, h_out, dn_ref, dx_ref, gain_out,
    h_buf, in_buf, out_buf, dn_acc, dh_acc, own_dh, own_g, rs_send, rs_recv, *chain_sems
):
    wide, narrow = plan.wide, plan.group // 2
    own, d = x2_ref.shape
    part = d // narrow
    piece, step = pl.program_id(0), pl.program_id(1)
    last = pl.num_programs(1) - 1
    tall = min(32, own)

    z = lax.axis_index("wide")
    owner = near_of(plan, z, piece)

    chain = Chain(plan, h_buf, chain_sems)

    def give(device):
        return push(out_buf.at[device], in_buf.at[z], rs_send.at[device], rs_recv.at[z], {"wide": device})

    @pl.when((piece == 0) & (step == 0))
    def _():
        greet([along_wide(plan, r) for r in range(1, wide)])

        @pl.loop(0, own // tall)
        def _(b):
            at = pl.ds(pl.multiple_of(b * tall, tall), tall)
            x2 = x2_ref[at, :]
            scale = lax.rsqrt(jnp.mean(x2 * x2, axis=1, keepdims=True) + EPS)
            h_buf[z, at, :] = (x2 * scale * gain_ref[...]).astype(BF)

        chain.go(1)
        own_g[...] = g_ref[...]

    for h in range(1, wide):
        @pl.when((piece == h) & (step == 0))
        def _():
            chain.arrive(h)
            if h + 1 < wide:
                chain.go(h + 1)

    @pl.when(step == 0)
    def _():
        h_out[...] = h_buf[owner]

    h = h_buf[owner]
    wg, wu = wg_ref[...], wu_ref[...]
    gate = jnp.dot(h, wg, preferred_element_type=F32)
    up = jnp.dot(h, wu, preferred_element_type=F32)
    d_act = jnp.zeros_like(gate)
    for n in range(narrow):
        d_act += lax.dot_general(
            g_ref[:, n * part : (n + 1) * part], wd_ref[n], NT, preferred_element_type=F32
        )
    sig = jax.nn.sigmoid(gate)
    silu = gate * sig
    act = (silu * up).astype(BF)
    dg = (d_act * up * sig * (1.0 + gate * (1.0 - sig))).astype(BF)
    du = (d_act * silu).astype(BF)
    act_ref[...] = act
    dg_ref[...] = dg
    du_ref[...] = du
    dh = lax.dot_general(dg, wg, NT, preferred_element_type=F32) + lax.dot_general(
        du, wu, NT, preferred_element_type=F32
    )

    @pl.when(step == 0)
    def _():
        dh_acc[...] = dh

    @pl.when(step > 0)
    def _():
        dh_acc[...] += dh

    for n in range(narrow):
        at = slice(n * part, (n + 1) * part)
        down = jnp.dot(act, wd_ref[n], preferred_element_type=F32)

        @pl.when(step == 0)
        def _():
            dn_acc[:, at] = down

        @pl.when(step > 0)
        def _():
            dn_acc[:, at] += down

    @pl.when(step == last)
    def _():
        dn_ref[0] = dn_acc[...].astype(BF)

    @pl.when((step == last) & (piece == 0))
    def _():
        own_dh[...] = dh_acc[...]

    @pl.when((step == last) & (piece > 0))
    def _():
        out_buf[owner] = dh_acc[...].astype(BF)
        give(owner).start()

    @pl.when((step == last) & (piece == wide - 1))
    def _():
        for p in range(1, wide):
            other = near_of(plan, z, p)
            push(out_buf.at[z], in_buf.at[other], rs_send.at[z], rs_recv.at[other], {"wide": other}).wait_recv()
        gain_out[...] = jnp.zeros_like(gain_out)

        @pl.loop(0, own // tall)
        def _(b):
            at = pl.ds(pl.multiple_of(b * tall, tall), tall)
            dh2 = own_dh[at, :]
            for p in range(1, wide):
                dh2 = dh2 + in_buf[near_of(plan, z, p), at, :].astype(F32)
            x2 = x2_ref[at, :]
            scale = lax.rsqrt(jnp.mean(x2 * x2, axis=1, keepdims=True) + EPS)
            z2 = x2 * scale
            gain_out[...] += jnp.sum(dh2 * z2, axis=0, keepdims=True)
            dz2 = dh2 * gain_ref[...]
            inner = jnp.mean(dz2 * z2, axis=1, keepdims=True)
            dx_ref[at, :] = own_g[at, :].astype(F32) + scale * (dz2 - z2 * inner)

        chain.finish()
        for p in range(1, wide):
            give(near_of(plan, z, p)).wait_send()


def ffn_call(plan, x2, gain, g_rows, w_gu, w_dn):
    own, d = x2.shape
    wide, rows = plan.wide, plan.rows
    narrow, ff, part = w_dn.shape
    tile = min(512, ff)
    tiles = ff // tile
    fixed = lambda shape: pl.BlockSpec(shape, lambda p, f: (0,) * len(shape), pipeline_mode=pl.Buffered(1))
    tall = pl.BlockSpec((own, tile), lambda p, f: (p, f))
    hidden = jax.ShapeDtypeStruct((rows, ff), BF)
    buffer = pltpu.VMEM((wide, own, d), BF)
    sems = pltpu.SemaphoreType.DMA((wide,))
    return pl.pallas_call(
        functools.partial(ffn_kernel, plan),
        grid=(wide, tiles),
        in_specs=[
            fixed((own, d)),
            fixed((1, d)),
            pl.BlockSpec((own, d), lambda p, f: (p, 0)),
            pl.BlockSpec((d, tile), lambda p, f: (0, f)),
            pl.BlockSpec((d, tile), lambda p, f: (0, tiles + f)),
            pl.BlockSpec((narrow, tile, part), lambda p, f: (0, f, 0)),
        ],
        out_specs=[
            tall, tall, tall,
            pl.BlockSpec((own, d), lambda p, f: (p, 0)),
            pl.BlockSpec((1, own, d), lambda p, f: (p, 0, 0)),
            fixed((own, d)),
            fixed((1, d)),
        ],
        out_shape=[
            hidden, hidden, hidden,
            jax.ShapeDtypeStruct((rows, d), BF),
            jax.ShapeDtypeStruct((wide, own, d), BF),
            jax.ShapeDtypeStruct((own, d), F32),
            jax.ShapeDtypeStruct((1, d), F32),
        ],
        scratch_shapes=[
            buffer, buffer, buffer,
            pltpu.VMEM((own, d), F32), pltpu.VMEM((own, d), F32), pltpu.VMEM((own, d), F32),
            pltpu.VMEM((own, d), BF),
            sems, sems, sems, sems, sems, sems,
        ],
        cost_estimate=pl.CostEstimate(
            flops=16 * rows * d * ff, bytes_accessed=6 * d * ff + 12 * rows * d, transcendentals=rows * ff
        ),
        compiler_params=pltpu.CompilerParams(
            vmem_limit_bytes=58 << 20, collective_id=1, has_side_effects=True
        ),
        name="feed_forward",
    )(x2, gain, g_rows, w_gu, w_gu, w_dn)


def weights_kernel(
    plan, tiles, dx2_ref, act_ref, h_ref, g_ref, dg_ref, du_ref, dn_out, gate_out, up_out, db_out,
    db_buf, keep_sem, *chain_sems
):
    wide = plan.wide
    step = pl.program_id(0)
    last = pl.num_programs(0) - 1
    chain = Chain(plan, db_buf, chain_sems)
    keep = pltpu.make_async_copy(db_buf, db_out, keep_sem)

    @pl.when(step == 0)
    def _():
        db_buf[lax.axis_index("wide")] = dx2_ref[...].astype(BF)
        greet([along_wide(plan, k) for k in range(1, wide)])
        chain.go(1)

    @pl.when(step < tiles)
    def _():
        narrow, _, part = dn_out.shape
        for n in range(narrow):
            dn_out[n] = lax.dot_general(
                act_ref[...], g_ref[:, n * part : (n + 1) * part], TN, preferred_element_type=F32
            ).astype(BF)

    @pl.when((step >= tiles) & (step < 2 * tiles))
    def _():
        gate_out[...] = lax.dot_general(h_ref[...], dg_ref[...], TN, preferred_element_type=F32).astype(BF)

    @pl.when(step >= 2 * tiles)
    def _():
        up_out[...] = lax.dot_general(h_ref[...], du_ref[...], TN, preferred_element_type=F32).astype(BF)

    for h in range(1, wide):
        @pl.when(step == min(last, (2 * h - 1) * tiles + tiles // 2))
        def _():
            chain.arrive(h)
            if h + 1 < wide:
                chain.go(h + 1)

    @pl.when(step == last)
    def _():
        keep.start()
        chain.finish()
        keep.wait()


def weights_call(plan, dx2, act, h, g, d_gate, d_up):
    own, d = dx2.shape
    rows, ff = act.shape
    wide, narrow = plan.wide, plan.group // 2
    part = d // narrow
    tiles = 4
    ff_tile, d_tile = ff // tiles, d // tiles
    fixed = lambda a: pl.BlockSpec(a.shape, lambda s: (0,) * a.ndim, pipeline_mode=pl.Buffered(1))
    first = lambda s: jnp.minimum(s, tiles - 1)
    second = lambda s: jnp.clip(s - tiles, 0, tiles - 1)
    third = lambda s: jnp.clip(s - 2 * tiles, 0, tiles - 1)
    both = lambda s: jnp.where(s < 2 * tiles, second(s), third(s))
    sems = pltpu.SemaphoreType.DMA((wide,))
    return pl.pallas_call(
        functools.partial(weights_kernel, plan, tiles),
        grid=(3 * tiles,),
        in_specs=[
            fixed(dx2),
            pl.BlockSpec((rows, ff_tile), lambda s: (0, first(s))),
            pl.BlockSpec((rows, d_tile), lambda s: (0, both(s))),
            fixed(g), fixed(d_gate), fixed(d_up),
        ],
        out_specs=[
            pl.BlockSpec((narrow, ff_tile, part), lambda s: (0, first(s), 0)),
            pl.BlockSpec((d_tile, ff), lambda s: (second(s), 0)),
            pl.BlockSpec((d_tile, ff), lambda s: (third(s), 0)),
            pl.BlockSpec(memory_space=pl.ANY),
        ],
        out_shape=[
            jax.ShapeDtypeStruct((narrow, ff, part), BF),
            jax.ShapeDtypeStruct((d, ff), BF),
            jax.ShapeDtypeStruct((d, ff), BF),
            jax.ShapeDtypeStruct((wide, own, d), BF),
        ],
        scratch_shapes=[pltpu.VMEM((wide, own, d), BF), pltpu.SemaphoreType.DMA] + [sems] * 4,
        cost_estimate=pl.CostEstimate(
            flops=10 * rows * d * ff, bytes_accessed=20 * rows * d, transcendentals=0
        ),
        compiler_params=pltpu.CompilerParams(
            vmem_limit_bytes=56 << 20, collective_id=6, has_side_effects=True
        ),
        name="weight_gradients",
    )(dx2, act, h, g, d_gate, d_up)


def backward_kernel(
    plan, kv_heads, heads, db_ref, qe_ref, kx, vx, o_ref, wo_ref, wq_ref, cos_ref, sin_ref, dn_ref,
    dq_ref, sums, dh_ref, dn_got, in_buf, out_buf, term_acc, rs_send, rs_recv, dn_send, dn_recv
):
    wide, cw, chunk, own = plan.wide, plan.cw, plan.chunk, plan.own
    rows = heads * cw
    width = heads * HD
    z = lax.axis_index("wide")
    index = lax.axis_index("seq") * lax.axis_size("narrow") + lax.axis_index("narrow")
    unit, g = pl.program_id(0), pl.program_id(1)
    last_unit, last_g = 2 * wide - 1, kv_heads - 1
    piece, half = wide - 1 - unit // 2, lax.rem(unit, 2)
    w = near_of(plan, z, piece)
    r = lax.rem(w - z + wide, wide)
    c = jnp.where(half == 1, 2 * plan.group - 1 - index, index)
    low_rows = pl.ds(pl.multiple_of(half * cw, cw), cw)

    def give(device):
        return push(out_buf.at[device], in_buf.at[z], rs_send.at[device], rs_recv.at[z], {"wide": device})

    def give_down(p):
        device = near_of(plan, z, p)
        slot = lax.rem(z - device + wide, wide)
        return push(dn_ref.at[p], dn_got.at[slot], dn_send.at[p], dn_recv.at[slot], {"wide": device})

    @pl.when((unit == 0) & (g == 0))
    def _():
        greet([along_wide(plan, k) for k in range(1, wide)])

        @pl.loop(0, kv_heads * plan.total // chunk)
        def _(b):
            at = pl.ds(pl.multiple_of(lax.rem(b, plan.total // chunk) * chunk, chunk), chunk)
            sums[b // (plan.total // chunk), at, :] = jnp.zeros((chunk, 128), F32)

    for p in range(1, wide):
        @pl.when((unit == wide - 1 - p) & (g == last_g))
        def _():
            give_down(p).start()

    lane = lax.broadcasted_iota(jnp.int32, (cw, 128), 1)
    columns = pl.ds(pl.multiple_of(g * width, width), width)
    grad = lax.dot_general(db_ref[w, low_rows, :], wo_ref[g], NT, preferred_element_type=F32)
    do = split_heads(grad.astype(BF).astype(F32), heads, False)
    o = split_heads(o_ref[w, low_rows, columns].astype(F32), heads, False)
    marked = []
    for one, other in zip(o, do):
        clean = jnp.where(lane >= HD, other, 0.0)
        first, second, third = pieces_of(-jnp.sum(one * clean, axis=1, keepdims=True))
        tile = jnp.where(lane == 0, first, clean)
        tile = jnp.where(lane == 1, second, tile)
        marked.append(jnp.where(lane == 2, third, tile))
    dox32 = jnp.concatenate(marked, axis=0)
    wide_lane = lax.broadcasted_iota(jnp.int32, (rows, 128), 1)
    dox = dox32.astype(BF)
    do_clean = jnp.where(wide_lane >= HD, dox32, 0.0).astype(BF)
    q = qe_ref[r, g, half]
    q_clean = jnp.where(wide_lane < HD, q.astype(F32), 0.0).astype(BF)

    def step(j, dq, diagonal=False):
        at = pl.ds(pl.multiple_of(j * chunk, chunk), chunk)
        key = kx[g, at, :]
        s = lax.dot_general(key, q, NT, preferred_element_type=F32)
        if diagonal:
            row = lax.broadcasted_iota(jnp.int32, (chunk, rows), 1) % cw + w * cw
            col = lax.broadcasted_iota(jnp.int32, (chunk, rows), 0)
            s = jnp.where(col <= row, s, NEG)
        p = jnp.exp(s)
        dp = lax.dot_general(vx[g, at, :], dox, NT, preferred_element_type=F32)
        ds = (p * dp).astype(BF)
        sums[g, at, :] += jnp.dot(ds, q_clean, preferred_element_type=F32) + jnp.dot(
            p.astype(BF), do_clean, preferred_element_type=F32
        )
        return dq + lax.dot_general(ds, key, TN, preferred_element_type=F32)

    dq = lax.fori_loop(0, c, step, jnp.zeros((rows, 128), F32))
    dq = step(c, dq, True) * (HD ** -0.5)
    dq = join_heads([dq[h * cw : (h + 1) * cw] for h in range(heads)], True)
    at = pl.ds(pl.multiple_of(r * own + half * cw, cw), cw)
    dq = dq * widen(cos_ref[at, :], width) + turn(dq, -1.0) * widen(sin_ref[at, :], width)
    dq = dq.astype(BF)
    dq_ref[at, columns] = dq

    term = lax.dot_general(dq, wq_ref[:, columns], NT, preferred_element_type=F32)

    @pl.when(g == 0)
    def _():
        term_acc[...] = term

    @pl.when(g > 0)
    def _():
        term_acc[...] += term

    @pl.when((g == last_g) & (piece == 0))
    def _():
        dh_ref[low_rows, :] = term_acc[...]

    @pl.when((g == last_g) & (piece > 0))
    def _():
        out_buf[w, low_rows, :] = term_acc[...].astype(BF)

    @pl.when((g == last_g) & (piece > 0) & (half == 1))
    def _():
        give(w).start()

    @pl.when((unit == last_unit) & (g == last_g))
    def _():
        for p in range(1, wide):
            other = near_of(plan, z, p)
            push(out_buf.at[z], in_buf.at[other], rs_send.at[z], rs_recv.at[other], {"wide": other}).wait_recv()
        tall = min(32, own)

        @pl.loop(0, own // tall)
        def _(b):
            at = pl.ds(pl.multiple_of(b * tall, tall), tall)
            total = dh_ref[at, :]
            for p in range(1, wide):
                total = total + in_buf[near_of(plan, z, p), at, :].astype(F32)
            dh_ref[at, :] = total

        for p in range(1, wide):
            other = near_of(plan, z, p)
            slot = lax.rem(other - z + wide, wide)
            push(dn_ref.at[p], dn_got.at[slot], dn_send.at[p], dn_recv.at[slot], {"wide": other}).wait_recv()
            give(other).wait_send()
            give_down(p).wait_send()


def backward_call(plan, db, qe, kx, vx, o, w_o, w_qkv, cos, sin, down, heads):
    kv_heads, total, _ = kx.shape
    _, own, d = db.shape
    wide, rows, cw = plan.wide, plan.rows, plan.cw
    qw = o.shape[2]
    pairs = kv_heads * heads * total * rows // 2
    fixed = lambda a: pl.BlockSpec(a.shape, lambda u, g: (0,) * a.ndim, pipeline_mode=pl.Buffered(1))
    hbm = pl.BlockSpec(memory_space=pl.ANY)
    given = [db, qe, kx, vx, o, w_o, w_qkv, cos, sin]
    outs = [
        jax.ShapeDtypeStruct((rows, qw), BF),
        jax.ShapeDtypeStruct((kv_heads, total, 128), F32),
        jax.ShapeDtypeStruct((own, d), F32),
    ]
    pieces = jax.ShapeDtypeStruct((wide, own, d), BF)
    buffer = pltpu.VMEM((wide, own, d), BF)
    sems = pltpu.SemaphoreType.DMA((wide,))
    return pl.pallas_call(
        functools.partial(backward_kernel, plan, kv_heads, heads),
        grid=(2 * wide, kv_heads),
        in_specs=[fixed(a) for a in given[:6]]
        + [pl.BlockSpec((d, qw), lambda u, g: (0, 0), pipeline_mode=pl.Buffered(1)), fixed(cos), fixed(sin), hbm],
        out_specs=[fixed(a) for a in outs] + [hbm],
        out_shape=outs + [pieces],
        scratch_shapes=[buffer, buffer, pltpu.VMEM((cw, d), F32)] + [sems] * 4,
        cost_estimate=pl.CostEstimate(
            flops=36 * pairs * HD, bytes_accessed=12 * kv_heads * total * 128, transcendentals=pairs
        ),
        compiler_params=pltpu.CompilerParams(
            vmem_limit_bytes=60 << 20, collective_id=3, has_side_effects=True
        ),
        name="attention_backward",
    )(*given, down)


def tail_kernel(
    plan, kv_heads, sums_ref, h_ref, res_ref, dh_ref, gain2_ref, dx2_ref, x_ref, gain_ref, wkv_ref,
    cos_ref, sin_ref, res_out, got_out, gain_out, kv_out,
    swap_out, swap_in, low, near_in, dkv, head_in, dh_acc, dx_low, every, results,
    gain_part, gain_in, gain_sum, gain_all, kv_part, kv_in,
    swap_sem, near_send, near_recv, head_send, head_recv, part_send, part_recv,
    res_send, res_recv, gain_send, gain_recv, gain2_send, gain2_recv, kv_send, kv_recv, own_sem, *chain_sems
):
    group, wide, chunk, cw, own = plan.group, plan.wide, plan.chunk, plan.cw, plan.own
    narrow = group // 2
    part = dx_low.shape[1] // narrow
    seq, me, z = lax.axis_index("seq"), lax.axis_index("narrow"), lax.axis_index("wide")
    index = seq * narrow + me
    res_chain = Chain(plan, results, chain_sems[:4])
    dx_chain = Chain(plan, every, chain_sems[4:])

    def device(k):
        return lax.rem(index + k + group, group)

    def member(k):
        return {"seq": device(k) // narrow, "narrow": lax.rem(device(k), narrow)}

    greet([member(k) for k in range(1, group)] + [along_wide(plan, r) for r in range(1, wide)])

    def slab(ref, other):
        rows = pl.ds(pl.multiple_of((other // narrow) * cw, cw), cw)
        return ref.at[rows, pl.ds(pl.multiple_of(lax.rem(other, narrow) * part, part), part)]

    class Parts:
        def __init__(self, ref, slots, send, recv, stay):
            self.ref, self.slots, self.send, self.recv = ref, slots, send, recv
            self.stay = pltpu.make_async_copy(slab(ref, index), slots.at[z, index], stay)

        def to(self, k):
            return push(slab(self.ref, device(k)), self.slots.at[z, index], self.send.at[k], self.recv.at[k], member(k))

        def start(self):
            for k in range(1, group):
                self.to(k).start()
            self.stay.start()

        def wait(self):
            self.stay.wait()
            for k in range(1, group):
                other = device(-k)
                push(
                    slab(self.ref, index), self.slots.at[z, other], self.send.at[k], self.recv.at[k], member(k)
                ).wait_recv()

        def sent(self):
            for k in range(1, group):
                self.to(k).wait_send()

    def place(owner_seq, half, n):
        quarter = owner_seq if half == 0 else 3 - owner_seq
        return pl.ds(
            pl.multiple_of((quarter * narrow + (n if half == 0 else narrow - 1 - n)) * chunk, chunk), chunk
        )

    @pl.loop(0, narrow)
    def _(n):
        for g in range(kv_heads):
            for half in range(2):
                swap_out[n, g, half] = sums_ref[g, place(1 - seq, half, n), :].astype(BF)

    swap = push(swap_out, swap_in, swap_sem.at[0], swap_sem.at[1], {"seq": 1 - seq})
    swap.start()
    res_parts = Parts(res_ref, results, res_send, res_recv, own_sem.at[0])
    res_parts.start()
    swap.wait_recv()

    @pl.loop(0, narrow)
    def _(n):
        for g in range(kv_heads):
            for half in range(2):
                total = sums_ref[g, place(seq, half, n), :] + swap_in[n, g, half].astype(F32)
                low[n, g, half] = total.astype(BF)

    def near(k):
        other = lax.rem(me + k, narrow)
        return push(low.at[other], near_in.at[k], near_send.at[k], near_recv.at[k], {"narrow": other})

    for k in range(1, narrow):
        near(k).start()
    res_parts.wait()
    res_chain.go(1)
    for k in range(1, narrow):
        near(k).wait_recv()

    lane = lax.broadcasted_iota(jnp.int32, (cw, 128), 1)
    for r in range(wide):
        at = pl.ds(pl.multiple_of(lax.rem(z + r, wide) * cw, cw), cw)
        for half in range(2):
            rows = slice((2 * r + half) * cw, (2 * r + half + 1) * cw)
            for g in range(kv_heads):
                total = low[me, g, half, at, :].astype(F32)
                for k in range(1, narrow):
                    total = total + near_in[k, g, half, at, :].astype(F32)
                back = total * cos_ref[rows, :] + turn(total, -1.0) * sin_ref[rows, :]
                dkv[rows, g * 128 : (g + 1) * 128] = jnp.where(lane < HD, back, total).astype(BF)

    def heads_to(r):
        mine = dkv.at[pl.ds(r * own, own)]
        return push(mine, head_in.at[r], head_send.at[r], head_recv.at[r], along_wide(plan, r))

    for r in range(1, wide):
        heads_to(r).start()

    for n in range(narrow):
        columns = slice(n * part, (n + 1) * part)
        kv_part[n] = lax.dot_general(dkv[...], h_ref[:, columns], TN, preferred_element_type=F32).astype(BF)

    def kv_to(k):
        return push(kv_part.at[lax.rem(device(k), narrow)], kv_in.at[k], kv_send.at[k], kv_recv.at[k], member(k))

    for k in range(1, group):
        kv_to(k).start()
    if wide > 1:
        res_chain.arrive(1)
    if wide > 2:
        res_chain.go(2)

    tile = min(512, part)
    for r in range(wide):
        if r > 0:
            heads_to(r).wait_recv()
        mine = dkv[0:own] if r == 0 else head_in[r]

        @pl.loop(0, dh_acc.shape[1] // tile)
        def _(b):
            at = pl.ds(pl.multiple_of(b * tile, tile), tile)
            more = lax.dot_general(mine, wkv_ref[lax.rem(z - r + wide, wide), at, :], NT, preferred_element_type=F32)
            dh_acc[:, at] = (dh_ref[:, at] if r == 0 else dh_acc[:, at]) + more

    gain_part[0:1, :] = jnp.zeros_like(gain2_ref[...])
    gain_part[1:2, :] = gain2_ref[...]
    tall = min(32, own)

    @pl.loop(0, own // tall)
    def _(b):
        at = pl.ds(pl.multiple_of(b * tall, tall), tall)
        dh1 = dh_acc[at, :]
        x = x_ref[at, :].astype(F32)
        scale = lax.rsqrt(jnp.mean(x * x, axis=1, keepdims=True) + EPS)
        z1 = x * scale
        gain_part[0:1, :] += jnp.sum(dh1 * z1, axis=0, keepdims=True)
        dz1 = dh1 * gain_ref[...]
        inner = jnp.mean(dz1 * z1, axis=1, keepdims=True)
        dx_low[at, :] = (dx2_ref[at, :] + scale * (dz1 - z1 * inner)).astype(BF)

    dx_parts = Parts(dx_low, every, part_send, part_recv, own_sem.at[1])
    dx_parts.start()

    def gain_to(k):
        columns = pl.ds(pl.multiple_of(lax.rem(device(k), narrow) * part, part), part)
        return push(gain_part.at[:, columns], gain_in.at[k], gain_send.at[k], gain_recv.at[k], member(k))

    for k in range(1, group):
        gain_to(k).start()
    for h in range(2, wide):
        res_chain.arrive(h)
        if h + 1 < wide:
            res_chain.go(h + 1)
    dx_parts.wait()
    dx_chain.go(1)

    gain = gain_part[:, pl.ds(pl.multiple_of(me * part, part), part)]
    for k in range(1, group):
        gain_to(k).wait_recv()
        gain = gain + gain_in[k]
    gain_sum[...] = gain

    def gain_on(r):
        return push(gain_sum, gain_all.at[r], gain2_send.at[r], gain2_recv.at[r], along_wide(plan, r))

    for r in range(1, wide):
        gain_on(r).start()
    for k in range(1, group):
        kv_to(k).wait_recv()
    res_keep = pltpu.make_async_copy(results, res_out, own_sem.at[2])
    res_keep.start()
    kv_out[...] = kv_part[me].astype(F32)
    for k in range(1, group):
        kv_out[...] += kv_in[k].astype(F32)
    gain = gain_sum[...]
    for r in range(1, wide):
        gain_on(r).wait_recv()
        gain = gain + gain_all[r]
    gain_out[...] = gain
    for h in range(1, wide):
        dx_chain.arrive(h)
        if h + 1 < wide:
            dx_chain.go(h + 1)
    got_keep = pltpu.make_async_copy(every, got_out, own_sem.at[3])
    got_keep.start()

    res_chain.finish()
    dx_chain.finish()
    swap.wait_send()
    for k in range(1, narrow):
        near(k).wait_send()
    for r in range(1, wide):
        heads_to(r).wait_send()
        gain_on(r).wait_send()
    res_parts.sent()
    dx_parts.sent()
    for k in range(1, group):
        gain_to(k).wait_send()
        kv_to(k).wait_send()
    res_keep.wait()
    got_keep.wait()


def tail_call(plan, sums, h, res, dh, gain2, dx2, x, gain, w_kv, cos, sin):
    kv_heads = sums.shape[0]
    own, d = dh.shape
    group, wide, chunk, cw = plan.group, plan.wide, plan.chunk, plan.cw
    narrow = group // 2
    part = d // narrow
    kv_width = kv_heads * 128
    dma = pltpu.SemaphoreType.DMA
    quarter = pltpu.VMEM((narrow, kv_heads, 2, chunk, 128), BF)
    slots = (wide, group, cw, part)
    given = [sums, h, res, dh, gain2, dx2, x, gain, w_kv, cos, sin]
    whole = pl.BlockSpec(memory_space=pltpu.VMEM)
    hbm = pl.BlockSpec(memory_space=pl.ANY)
    return pl.pallas_call(
        functools.partial(tail_kernel, plan, kv_heads),
        in_specs=[whole] * len(given),
        out_specs=[hbm, hbm, whole, whole],
        out_shape=[
            jax.ShapeDtypeStruct(slots, BF),
            jax.ShapeDtypeStruct(slots, BF),
            jax.ShapeDtypeStruct((2, part), F32),
            jax.ShapeDtypeStruct((kv_width, part), F32),
        ],
        scratch_shapes=[
            quarter, quarter, quarter, quarter,
            pltpu.VMEM((plan.rows, kv_width), BF),
            pltpu.VMEM((wide, own, kv_width), BF),
            pltpu.VMEM((own, d), F32),
            pltpu.VMEM((own, d), BF),
            pltpu.VMEM(slots, BF),
            pltpu.VMEM(slots, BF),
            pltpu.VMEM((2, d), F32),
            pltpu.VMEM((group, 2, part), F32),
            pltpu.VMEM((2, part), F32),
            pltpu.VMEM((wide, 2, part), F32),
            pltpu.VMEM((narrow, kv_width, part), BF),
            pltpu.VMEM((group, kv_width, part), BF),
            dma((2,)), dma((narrow,)), dma((narrow,)), dma((wide,)), dma((wide,)), dma((group,)), dma((group,)),
            dma((group,)), dma((group,)), dma((group,)), dma((group,)), dma((wide,)), dma((wide,)),
            dma((group,)), dma((group,)), dma((4,)),
        ] + [dma((wide,))] * 8,
        cost_estimate=pl.CostEstimate(
            flops=200 * own * d * wide * kv_width, bytes_accessed=4 * sums.size, transcendentals=0
        ),
        compiler_params=pltpu.CompilerParams(
            vmem_limit_bytes=60 << 20, collective_id=2, has_side_effects=True
        ),
        name="input_gradient",
    )(*given)


def assemble_kernel(plan, s_ref, in_ref, out_ref):
    group = plan.group
    for l in range(group):
        owner = jnp.where(s_ref[0] >= group // 2, group - 1 - l, l)
        out_ref[l, 0] = in_ref[0, owner].astype(out_ref.dtype)


def assemble_call(plan, scalars, values, dtype):
    wide, group, cw, part = values.shape
    out = pl.pallas_call(
        functools.partial(assemble_kernel, plan),
        grid_spec=pltpu.PrefetchScalarGridSpec(
            num_scalar_prefetch=1,
            grid=(wide,),
            in_specs=[pl.BlockSpec((1, group, cw, part), lambda w, s: (w, 0, 0, 0))],
            out_specs=[pl.BlockSpec((group, 1, cw, part), lambda w, s: (0, w, 0, 0))],
        ),
        out_shape=[jax.ShapeDtypeStruct((group, wide, cw, part), dtype)],
        cost_estimate=pl.CostEstimate(flops=values.size, bytes_accessed=6 * values.size, transcendentals=0),
        compiler_params=pltpu.CompilerParams(vmem_limit_bytes=40 << 20),
        name="assemble",
    )(scalars, values)[0]
    return out.reshape(group * wide * cw, part)


def half_of(weight, seq_index, seq_count):
    part = weight.shape[0] // seq_count
    return lax.dynamic_slice_in_dim(weight, seq_index * part, part, 0)


def body(
    tokens, attn_gain, w_query, w_key, w_value, w_out, ffn_gain, w_gate, w_up, w_down,
    segment_ids, token_mask, out_grad,
):
    seq_count = lax.axis_size("seq")
    narrow = lax.axis_size("narrow")
    wide = lax.axis_size("wide")
    group = seq_count * narrow
    seq_index = lax.axis_index("seq")
    narrow_index = lax.axis_index("narrow")
    wide_index = lax.axis_index("wide")
    index = seq_index * narrow + narrow_index
    total = segment_ids.shape[0]
    plan = Plan(total, group, wide)
    chunk, cw, rows, own = plan.chunk, plan.cw, plan.rows, plan.own
    d_part = tokens.shape[1]
    d = d_part * narrow
    qw = w_query.shape[1]
    kw = w_key.shape[1]
    kv_heads = kw // HD
    heads = qw // kw
    ff = w_gate.shape[1]

    start_one = jnp.sum((segment_ids < 1).astype(jnp.int32))
    start_two = jnp.sum((segment_ids < 2).astype(jnp.int32))
    starts = jnp.stack([start_one, start_two])
    scalars = jnp.reshape(index, (1,)).astype(jnp.int32)

    def gather_weight(weight):
        return lax.all_gather(half_of(weight, seq_index, seq_count), NS, axis=0, tiled=True)

    def scatter_grad(grad):
        mine = lax.psum_scatter(grad.astype(BF), NS, scatter_dimension=0, tiled=True)
        return lax.all_gather(mine, "seq", axis=0, tiled=True).astype(F32)

    def after(values, *others):
        return lax.optimization_barrier((values, *others))[0]

    w_kv = jnp.concatenate(
        [w_key.reshape(d_part, kv_heads, 1, HD), w_value.reshape(d_part, kv_heads, 1, HD)], axis=2
    ).reshape(d_part, 2 * kw)

    row = jnp.arange(rows, dtype=jnp.int32)
    row_chunk = jnp.where((row // cw) % 2 == 1, 2 * group - 1 - index, index)
    row_block = (row // own + wide_index) % wide
    row_token = row_chunk * chunk + row_block * cw + row % cw
    row_start = jnp.where(row_token >= start_two, start_two, jnp.where(row_token >= start_one, start_one, 0))
    row_pos = (row_token - row_start).astype(F32)
    frequency = THETA ** (-2.0 * jnp.arange(HD // 2, dtype=F32) / HD)
    angles = row_pos[:, None] * jnp.tile(frequency, 4)[None, :]
    cos, sin = jnp.cos(angles), jnp.sin(angles)

    lane = jnp.arange(128, dtype=jnp.int32)[None, :]
    closed = (segment_ids[:, None] != lane - HD) | (token_mask[:, None] != 1)
    kf = jnp.where((lane >= HD) & (lane < HD + 3) & closed, NEG, 0.0)
    kf = jnp.where((lane >= HD + 3) & (lane < HD + 6), 1.0, kf).astype(BF)

    mask = lax.dynamic_slice_in_dim(token_mask, seq_index * (group * chunk), group * chunk, 0)
    g_part = lax.dynamic_index_in_dim(out_grad.reshape(group, wide, cw, d_part), wide_index, 1, keepdims=False)
    mask = lax.dynamic_index_in_dim(mask.reshape(group, wide, cw), wide_index, 1, keepdims=False)
    g_part = jnp.where(mask[:, :, None] == 1, g_part, jnp.zeros_like(g_part))

    w_o = jnp.transpose(gather_weight(w_out).reshape(narrow, kv_heads, heads * HD, d_part), (1, 2, 0, 3))
    w_o = w_o.reshape(kv_heads, heads * HD, d)
    h_one, q, x_low, kx, vx, w_qkv, gains, g_rows, w_kv = head_call(
        plan, tokens.reshape(group, wide, cw, d_part), g_part, jnp.concatenate([w_query, w_kv], axis=1),
        jnp.stack([attn_gain, ffn_gain]), cos, sin, kf, qw, kv_heads
    )
    gains = jnp.transpose(gains, (1, 0, 2)).reshape(2, d)
    gain_one, gain_two = gains[0:1], gains[1:2]
    g_rows = g_rows.reshape(rows, d)

    w_gu = gather_weight(after(jnp.concatenate([w_gate, w_up], axis=1), q))
    w_dn = gather_weight(after(w_down, q)).reshape(narrow, ff, d_part)
    o, qe, x2 = forward_call(plan, starts, q, kx, vx, w_o, x_low, heads)
    w_kv = jnp.transpose(w_kv.reshape(wide, seq_count, d_part // seq_count, 2 * kw), (1, 0, 2, 3))
    w_kv = lax.dynamic_index_in_dim(w_kv, seq_index, 0, keepdims=False).reshape(-1, 2 * kw)
    w_kv = lax.all_gather(after(w_kv, o), NS, axis=0, tiled=True)
    w_kv = w_kv.reshape(group, wide, d_part // seq_count, 2 * kw)
    w_kv = jnp.transpose(w_kv, (1, 0, 2, 3)).reshape(wide, d, 2 * kw)

    act, d_gate, d_up, h_all, down, dx2, grad_gain_two = ffn_call(plan, x2, gain_two, g_rows, w_gu, w_dn)

    act = after(act, w_kv)
    grad_dn, grad_gate, grad_up, db = weights_call(plan, dx2, act, h_all, g_rows, d_gate, d_up)
    dq, sums, dh1, down_in = backward_call(
        plan, db, qe, kx, vx, o, w_o, w_qkv, cos, sin, down, heads
    )
    result = x2 + down[0].astype(F32)
    for r in range(1, wide):
        result = result + down_in[r].astype(F32)

    result, input_grad, gain_grads, grad_kv = tail_call(
        plan, sums, h_one, result.astype(BF), dh1, grad_gain_two, dx2, x_low, gain_one, w_kv, cos, sin
    )
    result = assemble_call(plan, scalars, result, BF)
    input_grad = assemble_call(plan, scalars, input_grad, F32)

    def tn(left, right):
        return lax.dot_general(left, right, TN, preferred_element_type=F32).astype(BF)

    def tn_split(left, right):
        return jnp.concatenate([tn(left, right[:, n * d_part : (n + 1) * d_part]) for n in range(narrow)], axis=0)

    grad_dn = scatter_grad(grad_dn.reshape(narrow * ff, d_part))
    grad_gate = scatter_grad(grad_gate)
    grad_up = scatter_grad(grad_up)
    grad_o = scatter_grad(tn_split(o.reshape(rows, qw), db.reshape(rows, d)))
    grad_q = scatter_grad(tn(h_one, dq))
    grad_kv = jnp.transpose(grad_kv.reshape(kv_heads, 2, HD, d_part), (3, 0, 1, 2))
    return (
        result,
        input_grad,
        gain_grads[0],
        grad_q,
        grad_kv[:, :, 0].reshape(d_part, kw),
        grad_kv[:, :, 1].reshape(d_part, kw),
        grad_o,
        gain_grads[1],
        grad_gate,
        grad_up,
        grad_dn,
    )


def solution(mesh):
    width_in, width_out = P("narrow", "wide"), P("wide", "narrow")
    acts = P("seq", "narrow")
    return jax.shard_map(
        body,
        mesh=mesh,
        in_specs=(
            acts, P("narrow"), width_in, width_in, width_in, width_out, P("narrow"),
            width_in, width_in, width_out, P(), P(), acts,
        ),
        out_specs=(
            acts, acts, P("narrow"), width_in, width_in, width_in, width_out, P("narrow"),
            width_in, width_in, width_out,
        ),
        check_vma=False,
    )
```

```python
import functools

import jax
import jax.numpy as jnp
from jax import lax
from jax.experimental import pallas as pl
from jax.experimental.pallas import tpu as pltpu
from jax.sharding import PartitionSpec as P

HD = 64
EPS = 1e-05
THETA = 500000.0
NEG = -1e30
SN = ("seq", "narrow")
NS = ("narrow", "seq")
BF = jnp.bfloat16
F32 = jnp.float32
NT = (((1,), (1,)), ((), ()))
TN = (((0,), (0,)), ((), ()))


def pieces_of(value):
    first = value.astype(BF).astype(F32)
    second = (value - first).astype(BF).astype(F32)
    third = (value - first - second).astype(BF).astype(F32)
    return first, second, third


class Plan:
    def __init__(self, total, group, wide):
        self.total, self.group, self.wide = total, group, wide
        self.chunk = total // (2 * group)
        self.cw = self.chunk // wide
        self.rows = 2 * self.chunk
        self.own = 2 * self.cw


def near_of(plan, z, p):
    side = jnp.minimum(z, plan.wide - 1 - z)
    both = jnp.where(lax.rem(p, 2) == 1, z + (p + 1) // 2, z - p // 2)
    one = jnp.where(z <= plan.wide - 1 - z, z + p - side, z - p + side)
    return jnp.where(p <= 2 * side, both, one)


def turn(values, sign):
    width = values.shape[1]
    lane = lax.broadcasted_iota(jnp.int32, values.shape, 1)
    left, right = pltpu.roll(values, width - HD // 2, 1), pltpu.roll(values, HD // 2, 1)
    return jnp.where(lane % HD < HD // 2, -sign * left, sign * right)


def widen(table, width):
    return jnp.concatenate([table] * (width // 128), axis=1) if width > 128 else table


MESH = pl.DeviceIdType.MESH


def greet(partners):
    barrier = pltpu.get_barrier_semaphore()
    for partner in partners:
        pl.semaphore_signal(barrier, inc=1, device_id=partner, device_id_type=MESH)
    pl.semaphore_wait(barrier, len(partners))


def along_wide(plan, r):
    return {"wide": lax.rem(lax.axis_index("wide") + r + plan.wide, plan.wide)}


def push(src, dst, send, recv, device):
    return pltpu.make_async_remote_copy(
        src_ref=src, dst_ref=dst, send_sem=send, recv_sem=recv, device_id=device, device_id_type=MESH
    )


class Chain:
    def __init__(self, plan, buf, sems):
        self.wide, self.buf, self.sems = plan.wide, buf, sems
        self.z = lax.axis_index("wide")

    def copy(self, slot, h, way):
        send, recv = (self.sems[0], self.sems[1]) if way > 0 else (self.sems[2], self.sems[3])
        return push(self.buf.at[slot], self.buf.at[slot], send.at[h], recv.at[h], {"wide": self.z + way})

    def sends(self, h, way):
        z, last = self.z, self.wide - 1
        return (z >= h - 1) & (z < last) if way > 0 else (z + h - 1 <= last) & (z > 0)

    def go(self, h):
        for way in (1, -1):
            @pl.when(self.sends(h, way))
            def _():
                self.copy(self.z - way * (h - 1), h, way).start()

    def arrive(self, h):
        for way in (1, -1):
            @pl.when(self.z >= h if way > 0 else self.z + h <= self.wide - 1)
            def _():
                slot = self.z - way * h
                send, recv = (self.sems[0], self.sems[1]) if way > 0 else (self.sems[2], self.sems[3])
                push(self.buf.at[slot], self.buf.at[slot], send.at[h], recv.at[h], {"wide": slot}).wait_recv()

    def finish(self):
        for h in range(1, self.wide):
            for way in (1, -1):
                @pl.when(self.sends(h, way))
                def _():
                    self.copy(self.z - way * (h - 1), h, way).wait_send()


class Group:
    def __init__(self, plan):
        self.size, self.narrow = plan.group, plan.group // 2
        self.seq, self.me = lax.axis_index("seq"), lax.axis_index("narrow")
        self.index = self.seq * self.narrow + self.me
        self.sibling = {"seq": 1 - self.seq}

    def device(self, k):
        return lax.rem(self.index + k + self.size, self.size)

    def member(self, k):
        return {"seq": self.device(k) // self.narrow, "narrow": lax.rem(self.device(k), self.narrow)}

    def beside(self, k):
        return lax.rem(self.me + k + self.narrow, self.narrow)


class Parts:
    def __init__(self, plan, team, ref, slots, send, recv, stay):
        self.plan, self.team, self.ref, self.send, self.recv = plan, team, ref, send, recv
        self.slots = slots.at[lax.axis_index("wide")]
        self.part = ref.shape[1] // team.narrow
        self.stay = pltpu.make_async_copy(self.slab(team.index), self.slots.at[team.index], stay)

    def slab(self, other):
        cw, narrow, part = self.plan.cw, self.team.narrow, self.part
        rows = pl.ds(pl.multiple_of((other // narrow) * cw, cw), cw)
        return self.ref.at[rows, pl.ds(pl.multiple_of(lax.rem(other, narrow) * part, part), part)]

    def to(self, k):
        team = self.team
        src = self.slab(team.device(k))
        return push(src, self.slots.at[team.index], self.send.at[k], self.recv.at[k], team.member(k))

    def start(self):
        for k in range(1, self.team.size):
            self.to(k).start()
        self.stay.start()

    def wait(self):
        team = self.team
        self.stay.wait()
        for k in range(1, team.size):
            src = self.slab(team.index)
            push(src, self.slots.at[team.device(-k)], self.send.at[k], self.recv.at[k], team.member(k)).wait_recv()

    def sent(self):
        for k in range(1, self.team.size):
            self.to(k).wait_send()


class Sums:
    def __init__(self, plan, terms, right, left, sems):
        self.wide, self.terms, self.sums, self.sems = plan.wide, terms, (right, left), sems
        self.z = lax.axis_index("wide")
        self.side = jnp.minimum(self.z, plan.wide - 1 - self.z)

    def term(self, h, way):
        return jnp.where(h <= self.side, 2 * h - 1 if way > 0 else 2 * h, self.side + h)

    def sends(self, t, way):
        h = self.wide - t
        return self.z + h <= self.wide - 1 if way > 0 else self.z >= h

    def first(self, way):
        return self.z == (0 if way > 0 else self.wide - 1)

    def copy(self, src, t, way):
        buf = self.sums[0 if way > 0 else 1]
        send, recv = self.sems[:2] if way > 0 else self.sems[2:]
        return push(src, buf.at[t], send.at[t], recv.at[t], {"wide": self.z + way})

    def came(self, t, way):
        buf = self.sums[0 if way > 0 else 1]
        send, recv = self.sems[:2] if way > 0 else self.sems[2:]
        push(buf.at[t], buf.at[t], send.at[t], recv.at[t], {"wide": self.z - way}).wait_recv()

    def go(self, t):
        for way in (1, -1):
            term = self.term(self.wide - t, way)

            @pl.when(self.sends(t, way) & self.first(way))
            def _():
                self.copy(self.terms.at[term], t, way).start()

            if t > 1:
                @pl.when(self.sends(t, way) & jnp.logical_not(self.first(way)))
                def _():
                    self.came(t - 1, way)
                    buf = self.sums[0 if way > 0 else 1]
                    tall = min(32, buf.shape[1])

                    @pl.loop(0, buf.shape[1] // tall)
                    def _(b):
                        at = pl.ds(pl.multiple_of(b * tall, tall), tall)
                        total = buf[t - 1, at, :].astype(F32) + self.terms[term, at, :].astype(F32)
                        buf[t - 1, at, :] = total.astype(BF)

                    self.copy(buf.at[t - 1], t, way).start()

    def finish(self):
        for way in (1, -1):
            @pl.when(jnp.logical_not(self.first(way)))
            def _():
                self.came(self.wide - 1, way)

        for t in range(1, self.wide):
            for way in (1, -1):
                @pl.when(self.sends(t, way))
                def _():
                    self.copy(self.terms.at[0], t, way).wait_send()

    def total(self, own, at):
        out = own
        for way in (1, -1):
            sums = self.sums[0 if way > 0 else 1][self.wide - 1, at, :].astype(F32)
            out = out + jnp.where(self.first(way), 0.0, sums)
        return out


def head_kernel(
    plan, kv_heads, qw, x_ref, g_ref, w_ref, gains_ref, cos_ref, sin_ref, kf_ref,
    h_out, q_out, own_out, kx, vx, w_out, gains_out, g_out, side_out,
    x_buf, side_buf, side_send, side_recv, w_buf, kv_buf, g_buf, gain_buf,
    x_send, x_recv, x_stay, w_send, w_recv, w_on_send, w_on_recv, gain_send, gain_recv,
    g_send, g_recv, kv_send, kv_recv, kv_on_send, kv_on_recv, keep_sem, *chain_sems
):
    group, wide, chunk, cw, own = plan.group, plan.wide, plan.chunk, plan.cw, plan.own
    team = Group(plan)
    narrow, seq, me = team.narrow, team.seq, team.me
    z = lax.axis_index("wide")
    part = x_ref.shape[3]
    d = part * narrow
    width = w_ref.shape[1]
    fold = part // 2
    chain = Chain(plan, g_buf, chain_sems)
    greet([team.member(k) for k in range(1, group)] + [along_wide(plan, r) for r in range(1, wide)])

    def spot(ref, slot, source):
        rows = pl.ds(pl.multiple_of((source // narrow) * cw, cw), cw)
        return ref.at[slot, rows, pl.ds(pl.multiple_of(lax.rem(source, narrow) * part, part), part)]

    def chunk_for(device):
        return jnp.where(seq == 0, device, group - 1 - device)

    def x_to(r, k):
        src = x_ref.at[chunk_for(team.device(k)), lax.rem(z + r, wide)]
        return push(src, spot(x_buf, r, team.index), x_send.at[r, k], x_recv.at[r, k], team.member(k))

    def x_from(r, k):
        src = x_ref.at[0, 0]
        return push(src, spot(x_buf, r, team.device(-k)), x_send.at[r, k], x_recv.at[r, k], team.member(k))

    def x_own(r):
        src = x_ref.at[chunk_for(team.index), lax.rem(z + r, wide)]
        return pltpu.make_async_copy(src, spot(x_buf, r, team.index), x_stay.at[r])

    def x_start(r):
        for k in range(1, group):
            x_to(r, k).start()
        x_own(r).start()

    def g_to(k):
        src = g_ref.at[chunk_for(team.device(k))]
        return push(src, spot(g_buf, z, team.index), g_send.at[k], g_recv.at[k], team.member(k))

    def w_rows(n, core):
        return w_buf.at[pl.ds(pl.multiple_of(n * part + core * fold, fold), fold)]

    def w_to(k):
        src = w_ref.at[pl.ds(pl.multiple_of(seq * fold, fold), fold)]
        return push(src, w_rows(me, seq), w_send.at[k], w_recv.at[k], {"narrow": team.beside(k)})

    def w_from(k):
        n = team.beside(-k)
        return push(w_rows(n, seq), w_rows(n, seq), w_send.at[k], w_recv.at[k], {"narrow": n})

    def w_on(k, core):
        n = team.beside(-k)
        return push(w_rows(n, core), w_rows(n, core), w_on_send.at[k], w_on_recv.at[k], team.sibling)

    def side_to(r, slot):
        mine = w_ref.at[:, qw:]
        return push(mine, side_buf.at[slot], side_send.at[r], side_recv.at[r], along_wide(plan, r))

    def gain_to(k, slot):
        return push(gains_ref, gain_buf.at[slot], gain_send.at[k], gain_recv.at[k], {"narrow": team.beside(k)})

    for k in range(1, group):
        g_to(k).start()
    g_stay = pltpu.make_async_copy(g_ref.at[chunk_for(team.index)], spot(g_buf, z, team.index), keep_sem.at[0])
    g_stay.start()
    for k in range(1, narrow):
        w_to(k).start()
        gain_to(k, me).start()
    x_start(0)
    if wide > 1:
        x_start(1)
    for r in range(1, wide):
        side_to(r, z).start()
    side_buf[z] = w_ref[:, qw:]
    w_buf[pl.ds(pl.multiple_of(me * part, part), part), :] = w_ref[...]
    gain_buf[me] = gains_ref[...]
    for k in range(1, narrow):
        w_from(k).wait_recv()
        w_on(k, seq).start()
    g_stay.wait()
    for k in range(1, group):
        push(
            g_ref.at[0], spot(g_buf, z, team.device(-k)), g_send.at[k], g_recv.at[k], team.member(k)
        ).wait_recv()
    chain.go(1)
    for k in range(1, narrow):
        gain_to(k, team.beside(-k)).wait_recv()
        w_on(k, 1 - seq).wait_recv()
    gain_one = jnp.concatenate([gain_buf[n, 0:1] for n in range(narrow)], axis=1)
    gains_out[...] = gain_buf[...]
    w_keep = pltpu.make_async_copy(w_buf, w_out, keep_sem.at[1])
    w_keep.start()

    def kv_rows(core, n, r):
        return kv_buf.at[core, n, pl.ds(pl.multiple_of(r * own, own), own)]

    def kv_to(r, k):
        mine = kv_rows(seq, me, r)
        return push(mine, mine, kv_send.at[r, k], kv_recv.at[r, k], {"narrow": team.beside(k)})

    def kv_from(r, k):
        theirs = kv_rows(seq, team.beside(-k), r)
        return push(theirs, theirs, kv_send.at[r, k], kv_recv.at[r, k], {"narrow": team.beside(k)})

    def kv_on(k, core):
        slot = kv_buf.at[core, team.beside(-k)]
        return push(slot, slot, kv_on_send.at[k], kv_on_recv.at[k], team.sibling)

    @pl.loop(0, wide)
    def _(r):
        x_own(r).wait()
        for k in range(1, group):
            x_from(r, k).wait_recv()
        for later in range(2, wide):
            @pl.when(r == later - 2)
            def _():
                x_start(later)
        at = pl.ds(pl.multiple_of(r * own, own), own)
        low = x_buf[r]
        x = low.astype(F32)
        mean = jnp.mean(x * x, axis=1, keepdims=True)
        h = (x * lax.rsqrt(mean + EPS) * gain_one).astype(BF)
        h_out[at, :] = h
        t = jnp.dot(h, w_buf[...], preferred_element_type=F32)
        lane = lax.broadcasted_iota(jnp.int32, t.shape, 1)
        plain = (lane >= qw) & (lane % 128 >= HD)
        out = t * widen(cos_ref[at, :], width) + turn(t, 1.0) * widen(sin_ref[at, :], width)
        out = jnp.where(plain, t, out)
        q_out[at, :] = (out[:, :qw] * (HD ** -0.5)).astype(BF)
        kv_buf[seq, me, at, :] = out[:, qw:].astype(BF)
        for k in range(1, narrow):
            kv_to(r, k).start()

        @pl.when(r == min(1, wide - 1))
        def _():
            chain.arrive(1)
            if wide > 2:
                chain.go(2)

    kv_on(0, seq).start()
    own_out[...] = x_buf[0]
    if wide > 2:
        chain.arrive(2)
    if wide > 3:
        chain.go(3)
    for k in range(1, narrow):
        for r in range(wide):
            kv_from(r, k).wait_recv()
        kv_on(k, seq).start()
    for k in range(narrow):
        kv_on(k, 1 - seq).wait_recv()

    feature = lax.broadcasted_iota(jnp.int32, (cw, 128), 1)
    ones = jnp.where(feature < 3, 1.0, 0.0).astype(BF)

    @pl.loop(0, 2 * group)
    def _(c):
        late = c >= group
        owner = jnp.where(late, 2 * group - 1 - c, c)
        for r in range(wide):
            at = pl.ds(pl.multiple_of(c * chunk + lax.rem(z + r, wide) * cw, cw), cw)
            source = pl.ds(pl.multiple_of(r * own + jnp.where(late, cw, 0), cw), cw)
            for g in range(kv_heads):
                kv = kv_buf[owner // narrow, lax.rem(owner, narrow), source, g * 128 : (g + 1) * 128]
                kx[g, at, :] = jnp.where(feature < HD, kv, kf_ref[at, :])
                vx[g, at, :] = jnp.where(feature < HD, ones, kv)

    for h in range(3, wide):
        chain.arrive(h)
        if h + 1 < wide:
            chain.go(h + 1)
    for r in range(1, wide):
        side_to(r, lax.rem(z - r + wide, wide)).wait_recv()
        side_to(r, z).wait_send()
    side_out[...] = side_buf[...]
    keep = [
        pltpu.make_async_copy(g_buf.at[near_of(plan, z, p)], g_out.at[p], keep_sem.at[2 + p]) for p in range(wide)
    ]
    for copy in keep:
        copy.start()
    chain.finish()
    for k in range(1, narrow):
        w_to(k).wait_send()
        w_on(k, seq).wait_send()
        gain_to(k, me).wait_send()
        for r in range(wide):
            kv_to(r, k).wait_send()
    for k in range(narrow):
        kv_on(k, seq).wait_send()
    for k in range(1, group):
        g_to(k).wait_send()
        for r in range(wide):
            x_to(r, k).wait_send()
    w_keep.wait()
    for copy in keep:
        copy.wait()


def head_call(plan, x, g, w, gains, cos, sin, kf, qw, kv_heads):
    group, wide, cw, part = x.shape
    narrow = group // 2
    d = part * narrow
    width = w.shape[1]
    rows, own, total = plan.rows, plan.own, plan.total
    dma = pltpu.SemaphoreType.DMA
    whole = pl.BlockSpec(memory_space=pltpu.VMEM)
    hbm = pl.BlockSpec(memory_space=pl.ANY)
    keys = jax.ShapeDtypeStruct((kv_heads, total, 128), BF)
    return pl.pallas_call(
        functools.partial(head_kernel, plan, kv_heads, qw),
        in_specs=[hbm, hbm] + [whole] * 5,
        out_specs=[whole] * 5 + [hbm, whole, hbm, whole],
        out_shape=[
            jax.ShapeDtypeStruct((rows, d), BF),
            jax.ShapeDtypeStruct((rows, qw), BF),
            jax.ShapeDtypeStruct((own, d), BF),
            keys,
            keys,
            jax.ShapeDtypeStruct((d, width), BF),
            jax.ShapeDtypeStruct((narrow, 2, part), F32),
            jax.ShapeDtypeStruct((wide, own, d), BF),
            jax.ShapeDtypeStruct((wide, part, width - qw), BF),
        ],
        scratch_shapes=[
            pltpu.VMEM((wide, own, d), BF),
            pltpu.VMEM((wide, part, width - qw), BF),
            dma((wide,)), dma((wide,)),
            pltpu.VMEM((d, width), BF),
            pltpu.VMEM((2, narrow, rows, width - qw), BF),
            pltpu.VMEM((wide, own, d), BF),
            pltpu.VMEM((narrow, 2, part), F32),
            dma((wide, group)), dma((wide, group)), dma((wide,)),
            dma((narrow,)), dma((narrow,)), dma((narrow,)), dma((narrow,)), dma((narrow,)), dma((narrow,)),
            dma((group,)), dma((group,)),
            dma((wide, narrow)), dma((wide, narrow)), dma((narrow,)), dma((narrow,)),
            dma((2 + wide,)),
        ] + [dma((wide,))] * 4,
        cost_estimate=pl.CostEstimate(
            flops=60 * rows * d * width, bytes_accessed=8 * rows * d + 2 * d * width, transcendentals=rows
        ),
        compiler_params=pltpu.CompilerParams(
            vmem_limit_bytes=60 << 20, collective_id=4, has_side_effects=True
        ),
        name="head",
    )(x, g, w, gains, cos, sin, kf)


def split_heads(block, heads, low):
    tiles = []
    for h in range(heads):
        tile = block[:, (h // 2) * 128 : (h // 2 + 1) * 128]
        if (h % 2 == 0) != low:
            tile = pltpu.roll(tile, HD, 1)
        tiles.append(tile)
    return tiles


def join_heads(tiles, low):
    rows = tiles[0].shape[0]
    lane = lax.broadcasted_iota(jnp.int32, (rows, 128), 1)
    pairs = []
    for h in range(0, len(tiles), 2):
        first, second = tiles[h], tiles[h + 1]
        if low:
            second = pltpu.roll(second, HD, 1)
        else:
            first = pltpu.roll(first, HD, 1)
        pairs.append(jnp.where(lane < HD, first, second))
    return jnp.concatenate(pairs, axis=1)


def forward_kernel(
    plan, kv_heads, heads, s_ref, q_ref, kx, vx, wo_ref, x_ref, o_ref, qe_ref, x2_ref,
    terms, right, left, term_acc, *sems
):
    wide, cw, chunk, own = plan.wide, plan.cw, plan.chunk, plan.own
    rows, width = heads * cw, heads * HD
    z = lax.axis_index("wide")
    index = lax.axis_index("seq") * lax.axis_size("narrow") + lax.axis_index("narrow")
    unit, g = pl.program_id(0), pl.program_id(1)
    last_g = kv_heads - 1
    piece, half = wide - 1 - unit // 2, lax.rem(unit, 2)
    w = near_of(plan, z, piece)
    r = lax.rem(w - z + wide, wide)
    c = jnp.where(half == 1, 2 * plan.group - 1 - index, index)
    low_rows = pl.ds(pl.multiple_of(half * cw, cw), cw)
    columns = pl.ds(pl.multiple_of(g * width, width), width)

    attn = Sums(plan, terms, right, left, sems)

    @pl.when((unit == 0) & (g == 0))
    def _():
        greet([along_wide(plan, k) for k in range(1, wide)])

    lane = lax.broadcasted_iota(jnp.int32, (cw, 128), 1)
    token = c * chunk + w * cw + lax.broadcasted_iota(jnp.int32, (cw, 128), 0)
    segment = (token >= s_ref[0]).astype(jnp.int32) + (token >= s_ref[1]).astype(jnp.int32)
    mark = jnp.where(lane == HD + segment, 1.0, 0.0)
    block = q_ref[pl.ds(pl.multiple_of(r * own + half * cw, cw), cw), columns]
    tiles = split_heads(block.astype(F32), heads, True)
    q32 = jnp.concatenate([jnp.where(lane < HD, t, mark) for t in tiles], axis=0)
    q = q32.astype(BF)

    def step(j, carry, diagonal=False):
        top, acc = carry
        at = pl.ds(pl.multiple_of(j * chunk, chunk), chunk)
        s = lax.dot_general(q, kx[g, at, :], NT, preferred_element_type=F32)
        if diagonal:
            row = lax.broadcasted_iota(jnp.int32, (rows, chunk), 0) % cw + w * cw
            col = lax.broadcasted_iota(jnp.int32, (rows, chunk), 1)
            s = jnp.where(col <= row, s, NEG)
        new = jnp.maximum(top, jnp.max(s, axis=1, keepdims=True))
        p = jnp.exp(s - new).astype(BF)
        acc = acc * jnp.exp(top - new) + jnp.dot(p, vx[g, at, :], preferred_element_type=F32)
        return new, acc

    start = (jnp.full((rows, 1), NEG, F32), jnp.zeros((rows, 128), F32))
    carry = lax.fori_loop(0, c, step, start)
    top, acc = step(c, carry, True)
    total = acc[:, 0:1]
    out = acc / total
    out = join_heads([out[h * cw : (h + 1) * cw] for h in range(heads)], False).astype(BF)
    o_ref[w, low_rows, columns] = out
    first, second, third = pieces_of(-(top + jnp.log(total)))
    wide_lane = lax.broadcasted_iota(jnp.int32, (rows, 128), 1)
    qe = jnp.where(wide_lane == HD + 3, first, q32)
    qe = jnp.where(wide_lane == HD + 4, second, qe)
    qe = jnp.where(wide_lane == HD + 5, third, qe)
    qe_ref[r, g, half] = qe.astype(BF)

    term = jnp.dot(out, wo_ref[g], preferred_element_type=F32)

    @pl.when(g == 0)
    def _():
        term_acc[...] = term

    @pl.when(g > 0)
    def _():
        term_acc[...] += term

    @pl.when((g == last_g) & (piece == 0))
    def _():
        x2_ref[low_rows, :] = x_ref[low_rows, :].astype(F32) + term_acc[...]

    @pl.when((g == last_g) & (piece > 0))
    def _():
        terms[piece, low_rows, :] = term_acc[...].astype(BF)

    for t in range(1, wide):
        @pl.when((g == last_g) & (unit == 2 * t - 1))
        def _():
            attn.go(t)

    @pl.when((unit == 2 * wide - 1) & (g == last_g))
    def _():
        attn.finish()
        tall = min(32, own)

        @pl.loop(0, own // tall)
        def _(b):
            at = pl.ds(pl.multiple_of(b * tall, tall), tall)
            x2_ref[at, :] = attn.total(x2_ref[at, :], at)


def forward_call(plan, starts, q, kx, vx, w_o, x, heads):
    kv_heads, total, _ = kx.shape
    own, d = x.shape
    wide, rows, cw = plan.wide, plan.rows, plan.cw
    qw = q.shape[1]
    pairs = kv_heads * heads * total * rows // 2
    fixed = lambda a: pl.BlockSpec(a.shape, lambda u, g: (0,) * a.ndim, pipeline_mode=pl.Buffered(1))
    given = [q, kx, vx, w_o, x]
    outs = [
        jax.ShapeDtypeStruct((wide, own, qw), BF),
        jax.ShapeDtypeStruct((wide, kv_heads, 2, heads * cw, 128), BF),
        jax.ShapeDtypeStruct((own, d), F32),
    ]
    buffer = pltpu.VMEM((wide, own, d), BF)
    sems = pltpu.SemaphoreType.DMA((wide,))
    return pl.pallas_call(
        functools.partial(forward_kernel, plan, kv_heads, heads),
        grid=(2 * wide, kv_heads),
        in_specs=[pl.BlockSpec(memory_space=pltpu.SMEM)] + [fixed(a) for a in given],
        out_specs=[fixed(a) for a in outs],
        out_shape=outs,
        scratch_shapes=[buffer] * 3 + [pltpu.VMEM((cw, d), F32)] + [sems] * 4,
        cost_estimate=pl.CostEstimate(
            flops=16 * pairs * HD, bytes_accessed=8 * kv_heads * total * 128, transcendentals=pairs
        ),
        compiler_params=pltpu.CompilerParams(
            vmem_limit_bytes=56 << 20, collective_id=5, has_side_effects=True
        ),
        name="attention_forward",
    )(starts, *given)


def ffn_kernel(
    plan, x2_ref, gain_ref, g_ref, wg_ref, wu_ref, wd_ref,
    act_ref, dg_ref, du_ref, h_out, dn_ref, dx_ref, gain_out,
    h_buf, in_buf, out_buf, dn_acc, dh_acc, own_dh, own_g, rs_send, rs_recv, *chain_sems
):
    wide, narrow = plan.wide, plan.group // 2
    own, d = x2_ref.shape
    part = d // narrow
    piece, step = pl.program_id(0), pl.program_id(1)
    last = pl.num_programs(1) - 1
    tall = min(32, own)

    z = lax.axis_index("wide")
    owner = near_of(plan, z, piece)

    chain = Chain(plan, h_buf, chain_sems)

    def give(device):
        return push(out_buf.at[device], in_buf.at[z], rs_send.at[device], rs_recv.at[z], {"wide": device})

    @pl.when((piece == 0) & (step == 0))
    def _():
        greet([along_wide(plan, r) for r in range(1, wide)])

        @pl.loop(0, own // tall)
        def _(b):
            at = pl.ds(pl.multiple_of(b * tall, tall), tall)
            x2 = x2_ref[at, :]
            scale = lax.rsqrt(jnp.mean(x2 * x2, axis=1, keepdims=True) + EPS)
            h_buf[z, at, :] = (x2 * scale * gain_ref[...]).astype(BF)

        chain.go(1)
        own_g[...] = g_ref[...]

    for h in range(1, wide):
        @pl.when((piece == h) & (step == 0))
        def _():
            chain.arrive(h)
            if h + 1 < wide:
                chain.go(h + 1)

    @pl.when(step == 0)
    def _():
        h_out[...] = h_buf[owner]

    h = h_buf[owner]
    wg, wu = wg_ref[...], wu_ref[...]
    gate = jnp.dot(h, wg, preferred_element_type=F32)
    up = jnp.dot(h, wu, preferred_element_type=F32)
    d_act = jnp.zeros_like(gate)
    for n in range(narrow):
        d_act += lax.dot_general(
            g_ref[:, n * part : (n + 1) * part], wd_ref[n], NT, preferred_element_type=F32
        )
    sig = jax.nn.sigmoid(gate)
    silu = gate * sig
    act = (silu * up).astype(BF)
    dg = (d_act * up * sig * (1.0 + gate * (1.0 - sig))).astype(BF)
    du = (d_act * silu).astype(BF)
    act_ref[...] = act
    dg_ref[...] = dg
    du_ref[...] = du
    dh = lax.dot_general(dg, wg, NT, preferred_element_type=F32) + lax.dot_general(
        du, wu, NT, preferred_element_type=F32
    )

    @pl.when(step == 0)
    def _():
        dh_acc[...] = dh

    @pl.when(step > 0)
    def _():
        dh_acc[...] += dh

    for n in range(narrow):
        at = slice(n * part, (n + 1) * part)
        down = jnp.dot(act, wd_ref[n], preferred_element_type=F32)

        @pl.when(step == 0)
        def _():
            dn_acc[:, at] = down

        @pl.when(step > 0)
        def _():
            dn_acc[:, at] += down

    @pl.when(step == last)
    def _():
        dn_ref[0] = dn_acc[...].astype(BF)

    @pl.when((step == last) & (piece == 0))
    def _():
        own_dh[...] = dh_acc[...]

    @pl.when((step == last) & (piece > 0))
    def _():
        out_buf[owner] = dh_acc[...].astype(BF)
        give(owner).start()

    @pl.when((step == last) & (piece == wide - 1))
    def _():
        for p in range(1, wide):
            other = near_of(plan, z, p)
            push(out_buf.at[z], in_buf.at[other], rs_send.at[z], rs_recv.at[other], {"wide": other}).wait_recv()
        gain_out[...] = jnp.zeros_like(gain_out)

        @pl.loop(0, own // tall)
        def _(b):
            at = pl.ds(pl.multiple_of(b * tall, tall), tall)
            dh2 = own_dh[at, :]
            for p in range(1, wide):
                dh2 = dh2 + in_buf[near_of(plan, z, p), at, :].astype(F32)
            x2 = x2_ref[at, :]
            scale = lax.rsqrt(jnp.mean(x2 * x2, axis=1, keepdims=True) + EPS)
            z2 = x2 * scale
            gain_out[...] += jnp.sum(dh2 * z2, axis=0, keepdims=True)
            dz2 = dh2 * gain_ref[...]
            inner = jnp.mean(dz2 * z2, axis=1, keepdims=True)
            dx_ref[at, :] = own_g[at, :].astype(F32) + scale * (dz2 - z2 * inner)

        chain.finish()
        for p in range(1, wide):
            give(near_of(plan, z, p)).wait_send()


def ffn_call(plan, x2, gain, g_rows, w_gu, w_dn):
    own, d = x2.shape
    wide, rows = plan.wide, plan.rows
    narrow, ff, part = w_dn.shape
    tile = min(512, ff)
    tiles = ff // tile
    fixed = lambda shape: pl.BlockSpec(shape, lambda p, f: (0,) * len(shape), pipeline_mode=pl.Buffered(1))
    tall = pl.BlockSpec((own, tile), lambda p, f: (p, f))
    hidden = jax.ShapeDtypeStruct((rows, ff), BF)
    buffer = pltpu.VMEM((wide, own, d), BF)
    sems = pltpu.SemaphoreType.DMA((wide,))
    return pl.pallas_call(
        functools.partial(ffn_kernel, plan),
        grid=(wide, tiles),
        in_specs=[
            fixed((own, d)),
            fixed((1, d)),
            pl.BlockSpec((own, d), lambda p, f: (p, 0)),
            pl.BlockSpec((d, tile), lambda p, f: (0, f)),
            pl.BlockSpec((d, tile), lambda p, f: (0, tiles + f)),
            pl.BlockSpec((narrow, tile, part), lambda p, f: (0, f, 0)),
        ],
        out_specs=[
            tall, tall, tall,
            pl.BlockSpec((own, d), lambda p, f: (p, 0)),
            pl.BlockSpec((1, own, d), lambda p, f: (p, 0, 0)),
            fixed((own, d)),
            fixed((1, d)),
        ],
        out_shape=[
            hidden, hidden, hidden,
            jax.ShapeDtypeStruct((rows, d), BF),
            jax.ShapeDtypeStruct((wide, own, d), BF),
            jax.ShapeDtypeStruct((own, d), F32),
            jax.ShapeDtypeStruct((1, d), F32),
        ],
        scratch_shapes=[
            buffer, buffer, buffer,
            pltpu.VMEM((own, d), F32), pltpu.VMEM((own, d), F32), pltpu.VMEM((own, d), F32),
            pltpu.VMEM((own, d), BF),
            sems, sems, sems, sems, sems, sems,
        ],
        cost_estimate=pl.CostEstimate(
            flops=16 * rows * d * ff, bytes_accessed=6 * d * ff + 12 * rows * d, transcendentals=rows * ff
        ),
        compiler_params=pltpu.CompilerParams(
            vmem_limit_bytes=58 << 20, collective_id=1, has_side_effects=True
        ),
        name="feed_forward",
    )(x2, gain, g_rows, w_gu, w_gu, w_dn)


def weights_kernel(
    plan, tiles, dx2_ref, act_ref, h_ref, g_ref, dg_ref, du_ref, down_ref, x2_ref,
    dn_out, gate_out, up_out, db_out, res_out,
    db_buf, right, left, keep_sem, *sems
):
    wide = plan.wide
    step = pl.program_id(0)
    last = pl.num_programs(0) - 1
    chain = Chain(plan, db_buf, sems[:4])
    down = Sums(plan, down_ref, right, left, sems[4:])
    keep = pltpu.make_async_copy(db_buf, db_out, keep_sem)

    @pl.when(step == 0)
    def _():
        db_buf[lax.axis_index("wide")] = dx2_ref[...].astype(BF)
        greet([along_wide(plan, k) for k in range(1, wide)])
        chain.go(1)

    @pl.when(step < tiles)
    def _():
        narrow, _, part = dn_out.shape
        for n in range(narrow):
            dn_out[n] = lax.dot_general(
                act_ref[...], g_ref[:, n * part : (n + 1) * part], TN, preferred_element_type=F32
            ).astype(BF)

    @pl.when((step >= tiles) & (step < 2 * tiles))
    def _():
        gate_out[...] = lax.dot_general(h_ref[...], dg_ref[...], TN, preferred_element_type=F32).astype(BF)

    @pl.when(step >= 2 * tiles)
    def _():
        up_out[...] = lax.dot_general(h_ref[...], du_ref[...], TN, preferred_element_type=F32).astype(BF)

    for h in range(1, wide):
        @pl.when(step == min(last, (2 * h - 1) * tiles + tiles // 2))
        def _():
            chain.arrive(h)
            if h + 1 < wide:
                chain.go(h + 1)
            down.go(h)

    @pl.when(step == last)
    def _():
        keep.start()
        down.finish()
        tall = min(32, x2_ref.shape[0])

        @pl.loop(0, x2_ref.shape[0] // tall)
        def _(b):
            at = pl.ds(pl.multiple_of(b * tall, tall), tall)
            res_out[at, :] = down.total(x2_ref[at, :] + down_ref[0, at, :].astype(F32), at).astype(BF)

        chain.finish()
        keep.wait()


def weights_call(plan, dx2, act, h, g, d_gate, d_up, down, x2):
    own, d = dx2.shape
    rows, ff = act.shape
    wide, narrow = plan.wide, plan.group // 2
    part = d // narrow
    tiles = 4
    ff_tile, d_tile = ff // tiles, d // tiles
    fixed = lambda a: pl.BlockSpec(a.shape, lambda s: (0,) * a.ndim, pipeline_mode=pl.Buffered(1))
    first = lambda s: jnp.minimum(s, tiles - 1)
    second = lambda s: jnp.clip(s - tiles, 0, tiles - 1)
    third = lambda s: jnp.clip(s - 2 * tiles, 0, tiles - 1)
    both = lambda s: jnp.where(s < 2 * tiles, second(s), third(s))
    sems = pltpu.SemaphoreType.DMA((wide,))
    return pl.pallas_call(
        functools.partial(weights_kernel, plan, tiles),
        grid=(3 * tiles,),
        in_specs=[
            fixed(dx2),
            pl.BlockSpec((rows, ff_tile), lambda s: (0, first(s))),
            pl.BlockSpec((rows, d_tile), lambda s: (0, both(s))),
            fixed(g), fixed(d_gate), fixed(d_up), fixed(down), fixed(x2),
        ],
        out_specs=[
            pl.BlockSpec((narrow, ff_tile, part), lambda s: (0, first(s), 0)),
            pl.BlockSpec((d_tile, ff), lambda s: (second(s), 0)),
            pl.BlockSpec((d_tile, ff), lambda s: (third(s), 0)),
            pl.BlockSpec(memory_space=pl.ANY),
            pl.BlockSpec((own, d), lambda s: (0, 0), pipeline_mode=pl.Buffered(1)),
        ],
        out_shape=[
            jax.ShapeDtypeStruct((narrow, ff, part), BF),
            jax.ShapeDtypeStruct((d, ff), BF),
            jax.ShapeDtypeStruct((d, ff), BF),
            jax.ShapeDtypeStruct((wide, own, d), BF),
            jax.ShapeDtypeStruct((own, d), BF),
        ],
        scratch_shapes=[pltpu.VMEM((wide, own, d), BF)] * 3 + [pltpu.SemaphoreType.DMA] + [sems] * 8,
        cost_estimate=pl.CostEstimate(
            flops=10 * rows * d * ff, bytes_accessed=20 * rows * d, transcendentals=0
        ),
        compiler_params=pltpu.CompilerParams(
            vmem_limit_bytes=60 << 20, collective_id=6, has_side_effects=True
        ),
        name="weight_gradients",
    )(dx2, act, h, g, d_gate, d_up, down, x2)


def backward_kernel(
    plan, kv_heads, heads, db_ref, qe_ref, kx, vx, o_ref, wo_ref, wq_ref, cos_ref, sin_ref, res_ref,
    dq_ref, sums, dh_ref, res_out, terms, right, left, term_acc, results,
    part_send, part_recv, keep_sem, *sems
):
    wide, cw, chunk, own = plan.wide, plan.cw, plan.chunk, plan.own
    rows = heads * cw
    width = heads * HD
    z = lax.axis_index("wide")
    team = Group(plan)
    index = team.index
    chain = Chain(plan, results, sems[:4])
    back = Sums(plan, terms, right, left, sems[4:])
    parts = Parts(plan, team, res_ref, results, part_send, part_recv, keep_sem.at[0])
    unit, g = pl.program_id(0), pl.program_id(1)
    last_unit, last_g = 2 * wide - 1, kv_heads - 1
    piece, half = wide - 1 - unit // 2, lax.rem(unit, 2)
    w = near_of(plan, z, piece)
    r = lax.rem(w - z + wide, wide)
    c = jnp.where(half == 1, 2 * plan.group - 1 - index, index)
    low_rows = pl.ds(pl.multiple_of(half * cw, cw), cw)

    @pl.when((unit == 0) & (g == 0))
    def _():
        others = [team.member(k) for k in range(1, plan.group)]
        greet(others + [along_wide(plan, k) for k in range(1, wide)])
        parts.start()

        @pl.loop(0, kv_heads * plan.total // chunk)
        def _(b):
            at = pl.ds(pl.multiple_of(lax.rem(b, plan.total // chunk) * chunk, chunk), chunk)
            sums[b // (plan.total // chunk), at, :] = jnp.zeros((chunk, 128), F32)

    @pl.when((unit == 1) & (g == last_g))
    def _():
        parts.wait()
        chain.go(1)

    for h in range(1, wide):
        late = {1: (3, 0), 2: (4, last_g), 3: (6, 0)}.get(h, (min(h + 3, last_unit), last_g))

        @pl.when((unit == late[0]) & (g == late[1]))
        def _():
            chain.arrive(h)
            if h + 1 < wide:
                chain.go(h + 1)

    lane = lax.broadcasted_iota(jnp.int32, (cw, 128), 1)
    columns = pl.ds(pl.multiple_of(g * width, width), width)
    grad = lax.dot_general(db_ref[w, low_rows, :], wo_ref[g], NT, preferred_element_type=F32)
    do = split_heads(grad.astype(BF).astype(F32), heads, False)
    o = split_heads(o_ref[w, low_rows, columns].astype(F32), heads, False)
    marked = []
    for one, other in zip(o, do):
        clean = jnp.where(lane >= HD, other, 0.0)
        first, second, third = pieces_of(-jnp.sum(one * clean, axis=1, keepdims=True))
        tile = jnp.where(lane == 0, first, clean)
        tile = jnp.where(lane == 1, second, tile)
        marked.append(jnp.where(lane == 2, third, tile))
    dox32 = jnp.concatenate(marked, axis=0)
    wide_lane = lax.broadcasted_iota(jnp.int32, (rows, 128), 1)
    dox = dox32.astype(BF)
    do_clean = jnp.where(wide_lane >= HD, dox32, 0.0).astype(BF)
    q = qe_ref[r, g, half]
    q_clean = jnp.where(wide_lane < HD, q.astype(F32), 0.0).astype(BF)

    def step(j, dq, diagonal=False):
        at = pl.ds(pl.multiple_of(j * chunk, chunk), chunk)
        key = kx[g, at, :]
        s = lax.dot_general(key, q, NT, preferred_element_type=F32)
        if diagonal:
            row = lax.broadcasted_iota(jnp.int32, (chunk, rows), 1) % cw + w * cw
            col = lax.broadcasted_iota(jnp.int32, (chunk, rows), 0)
            s = jnp.where(col <= row, s, NEG)
        p = jnp.exp(s)
        dp = lax.dot_general(vx[g, at, :], dox, NT, preferred_element_type=F32)
        ds = (p * dp).astype(BF)
        sums[g, at, :] += jnp.dot(ds, q_clean, preferred_element_type=F32) + jnp.dot(
            p.astype(BF), do_clean, preferred_element_type=F32
        )
        return dq + lax.dot_general(ds, key, TN, preferred_element_type=F32)

    dq = lax.fori_loop(0, c, step, jnp.zeros((rows, 128), F32))
    dq = step(c, dq, True) * (HD ** -0.5)
    dq = join_heads([dq[h * cw : (h + 1) * cw] for h in range(heads)], True)
    at = pl.ds(pl.multiple_of(r * own + half * cw, cw), cw)
    dq = dq * widen(cos_ref[at, :], width) + turn(dq, -1.0) * widen(sin_ref[at, :], width)
    dq = dq.astype(BF)
    dq_ref[at, columns] = dq

    term = lax.dot_general(dq, wq_ref[:, columns], NT, preferred_element_type=F32)

    @pl.when(g == 0)
    def _():
        term_acc[...] = term

    @pl.when(g > 0)
    def _():
        term_acc[...] += term

    @pl.when((g == last_g) & (piece == 0))
    def _():
        dh_ref[low_rows, :] = term_acc[...]

    @pl.when((g == last_g) & (piece > 0))
    def _():
        terms[piece, low_rows, :] = term_acc[...].astype(BF)

    for t in range(1, wide):
        @pl.when((g == last_g) & (unit == 2 * t - 1))
        def _():
            back.go(t)

    @pl.when((unit == last_unit) & (g == last_g))
    def _():
        keep = pltpu.make_async_copy(results, res_out, keep_sem.at[1])
        keep.start()
        back.finish()
        tall = min(32, own)

        @pl.loop(0, own // tall)
        def _(b):
            at = pl.ds(pl.multiple_of(b * tall, tall), tall)
            dh_ref[at, :] = back.total(dh_ref[at, :], at)

        chain.finish()
        parts.sent()
        keep.wait()


def backward_call(plan, db, qe, kx, vx, o, w_o, w_qkv, cos, sin, res, heads):
    kv_heads, total, _ = kx.shape
    _, own, d = db.shape
    wide, rows, cw = plan.wide, plan.rows, plan.cw
    qw = o.shape[2]
    pairs = kv_heads * heads * total * rows // 2
    fixed = lambda a: pl.BlockSpec(a.shape, lambda u, g: (0,) * a.ndim, pipeline_mode=pl.Buffered(1))
    hbm = pl.BlockSpec(memory_space=pl.ANY)
    given = [db, qe, kx, vx, o, w_o, w_qkv, cos, sin]
    outs = [
        jax.ShapeDtypeStruct((rows, qw), BF),
        jax.ShapeDtypeStruct((kv_heads, total, 128), F32),
        jax.ShapeDtypeStruct((own, d), F32),
    ]
    slots = (wide, plan.group, cw, d // (plan.group // 2))
    buffer = pltpu.VMEM((wide, own, d), BF)
    sems = pltpu.SemaphoreType.DMA((wide,))
    return pl.pallas_call(
        functools.partial(backward_kernel, plan, kv_heads, heads),
        grid=(2 * wide, kv_heads),
        in_specs=[fixed(a) for a in given[:6]]
        + [pl.BlockSpec((d, qw), lambda u, g: (0, 0), pipeline_mode=pl.Buffered(1)), fixed(cos), fixed(sin), fixed(res)],
        out_specs=[fixed(a) for a in outs] + [hbm],
        out_shape=outs + [jax.ShapeDtypeStruct(slots, BF)],
        scratch_shapes=[buffer] * 3 + [pltpu.VMEM((cw, d), F32), pltpu.VMEM(slots, BF)]
        + [pltpu.SemaphoreType.DMA((plan.group,))] * 2 + [pltpu.SemaphoreType.DMA((2,))] + [sems] * 8,
        cost_estimate=pl.CostEstimate(
            flops=36 * pairs * HD, bytes_accessed=12 * kv_heads * total * 128, transcendentals=pairs
        ),
        compiler_params=pltpu.CompilerParams(
            vmem_limit_bytes=60 << 20, collective_id=3, has_side_effects=True
        ),
        name="attention_backward",
    )(*given, res)


def tail_kernel(
    plan, kv_heads, sums_ref, h_ref, dh_ref, gain2_ref, dx2_ref, x_ref, gain_ref, wkv_ref,
    cos_ref, sin_ref, got_out, gain_out, kv_out,
    swap_out, swap_in, low, near_in, dkv, head_in, dh_acc, dx_low, every,
    gain_part, gain_in, gain_sum, gain_all, kv_part, kv_in,
    swap_sem, near_send, near_recv, head_send, head_recv, part_send, part_recv,
    gain_send, gain_recv, gain2_send, gain2_recv, kv_send, kv_recv, own_sem, *chain_sems
):
    group, wide, chunk, cw, own = plan.group, plan.wide, plan.chunk, plan.cw, plan.own
    narrow = group // 2
    part = dx_low.shape[1] // narrow
    team = Group(plan)
    seq, me, z = team.seq, team.me, lax.axis_index("wide")
    device, member = team.device, team.member
    dx_chain = Chain(plan, every, chain_sems)

    greet([member(k) for k in range(1, group)] + [along_wide(plan, r) for r in range(1, wide)])

    def place(owner_seq, half, n):
        quarter = owner_seq if half == 0 else 3 - owner_seq
        return pl.ds(
            pl.multiple_of((quarter * narrow + (n if half == 0 else narrow - 1 - n)) * chunk, chunk), chunk
        )

    @pl.loop(0, narrow)
    def _(n):
        for g in range(kv_heads):
            for half in range(2):
                swap_out[n, g, half] = sums_ref[g, place(1 - seq, half, n), :].astype(BF)

    swap = push(swap_out, swap_in, swap_sem.at[0], swap_sem.at[1], {"seq": 1 - seq})
    swap.start()
    swap.wait_recv()

    @pl.loop(0, narrow)
    def _(n):
        for g in range(kv_heads):
            for half in range(2):
                total = sums_ref[g, place(seq, half, n), :] + swap_in[n, g, half].astype(F32)
                low[n, g, half] = total.astype(BF)

    def near(k):
        other = lax.rem(me + k, narrow)
        return push(low.at[other], near_in.at[k], near_send.at[k], near_recv.at[k], {"narrow": other})

    for k in range(1, narrow):
        near(k).start()
    for k in range(1, narrow):
        near(k).wait_recv()

    lane = lax.broadcasted_iota(jnp.int32, (cw, 128), 1)
    for r in range(wide):
        at = pl.ds(pl.multiple_of(lax.rem(z + r, wide) * cw, cw), cw)
        for half in range(2):
            rows = slice((2 * r + half) * cw, (2 * r + half + 1) * cw)
            for g in range(kv_heads):
                total = low[me, g, half, at, :].astype(F32)
                for k in range(1, narrow):
                    total = total + near_in[k, g, half, at, :].astype(F32)
                back = total * cos_ref[rows, :] + turn(total, -1.0) * sin_ref[rows, :]
                dkv[rows, g * 128 : (g + 1) * 128] = jnp.where(lane < HD, back, total).astype(BF)

    def heads_to(r):
        mine = dkv.at[pl.ds(r * own, own)]
        return push(mine, head_in.at[r], head_send.at[r], head_recv.at[r], along_wide(plan, r))

    for r in range(1, wide):
        heads_to(r).start()

    for n in range(narrow):
        columns = slice(n * part, (n + 1) * part)
        kv_part[n] = lax.dot_general(dkv[...], h_ref[:, columns], TN, preferred_element_type=F32).astype(BF)

    def kv_to(k):
        return push(kv_part.at[lax.rem(device(k), narrow)], kv_in.at[k], kv_send.at[k], kv_recv.at[k], member(k))

    for k in range(1, group):
        kv_to(k).start()

    tile = min(512, part)
    for r in range(wide):
        if r > 0:
            heads_to(r).wait_recv()
        mine = dkv[0:own] if r == 0 else head_in[r]

        @pl.loop(0, dh_acc.shape[1] // tile)
        def _(b):
            at = pl.ds(pl.multiple_of(b * tile, tile), tile)
            more = lax.dot_general(mine, wkv_ref[lax.rem(z - r + wide, wide), at, :], NT, preferred_element_type=F32)
            dh_acc[:, at] = (dh_ref[:, at] if r == 0 else dh_acc[:, at]) + more

    gain_part[0:1, :] = jnp.zeros_like(gain2_ref[...])
    gain_part[1:2, :] = gain2_ref[...]
    tall = min(32, own)

    @pl.loop(0, own // tall)
    def _(b):
        at = pl.ds(pl.multiple_of(b * tall, tall), tall)
        dh1 = dh_acc[at, :]
        x = x_ref[at, :].astype(F32)
        scale = lax.rsqrt(jnp.mean(x * x, axis=1, keepdims=True) + EPS)
        z1 = x * scale
        gain_part[0:1, :] += jnp.sum(dh1 * z1, axis=0, keepdims=True)
        dz1 = dh1 * gain_ref[...]
        inner = jnp.mean(dz1 * z1, axis=1, keepdims=True)
        dx_low[at, :] = (dx2_ref[at, :] + scale * (dz1 - z1 * inner)).astype(BF)

    dx_parts = Parts(plan, team, dx_low, every, part_send, part_recv, own_sem.at[0])
    dx_parts.start()

    def gain_to(k):
        columns = pl.ds(pl.multiple_of(lax.rem(device(k), narrow) * part, part), part)
        return push(gain_part.at[:, columns], gain_in.at[k], gain_send.at[k], gain_recv.at[k], member(k))

    for k in range(1, group):
        gain_to(k).start()
    dx_parts.wait()
    dx_chain.go(1)

    gain = gain_part[:, pl.ds(pl.multiple_of(me * part, part), part)]
    for k in range(1, group):
        gain_to(k).wait_recv()
        gain = gain + gain_in[k]
    gain_sum[...] = gain

    def gain_on(r):
        return push(gain_sum, gain_all.at[r], gain2_send.at[r], gain2_recv.at[r], along_wide(plan, r))

    for r in range(1, wide):
        gain_on(r).start()
    for k in range(1, group):
        kv_to(k).wait_recv()
    kv_out[...] = kv_part[me].astype(F32)
    for k in range(1, group):
        kv_out[...] += kv_in[k].astype(F32)
    gain = gain_sum[...]
    for r in range(1, wide):
        gain_on(r).wait_recv()
        gain = gain + gain_all[r]
    gain_out[...] = gain
    for h in range(1, wide):
        dx_chain.arrive(h)
        if h + 1 < wide:
            dx_chain.go(h + 1)
    got_keep = pltpu.make_async_copy(every, got_out, own_sem.at[1])
    got_keep.start()

    dx_chain.finish()
    swap.wait_send()
    for k in range(1, narrow):
        near(k).wait_send()
    for r in range(1, wide):
        heads_to(r).wait_send()
        gain_on(r).wait_send()
    dx_parts.sent()
    for k in range(1, group):
        gain_to(k).wait_send()
        kv_to(k).wait_send()
    got_keep.wait()


def tail_call(plan, sums, h, dh, gain2, dx2, x, gain, w_kv, cos, sin):
    kv_heads = sums.shape[0]
    own, d = dh.shape
    group, wide, chunk, cw = plan.group, plan.wide, plan.chunk, plan.cw
    narrow = group // 2
    part = d // narrow
    kv_width = kv_heads * 128
    dma = pltpu.SemaphoreType.DMA
    quarter = pltpu.VMEM((narrow, kv_heads, 2, chunk, 128), BF)
    slots = (wide, group, cw, part)
    given = [sums, h, dh, gain2, dx2, x, gain, w_kv, cos, sin]
    whole = pl.BlockSpec(memory_space=pltpu.VMEM)
    hbm = pl.BlockSpec(memory_space=pl.ANY)
    return pl.pallas_call(
        functools.partial(tail_kernel, plan, kv_heads),
        in_specs=[whole] * len(given),
        out_specs=[hbm, whole, whole],
        out_shape=[
            jax.ShapeDtypeStruct(slots, BF),
            jax.ShapeDtypeStruct((2, part), F32),
            jax.ShapeDtypeStruct((kv_width, part), F32),
        ],
        scratch_shapes=[
            quarter, quarter, quarter, quarter,
            pltpu.VMEM((plan.rows, kv_width), BF),
            pltpu.VMEM((wide, own, kv_width), BF),
            pltpu.VMEM((own, d), F32),
            pltpu.VMEM((own, d), BF),
            pltpu.VMEM(slots, BF),
            pltpu.VMEM((2, d), F32),
            pltpu.VMEM((group, 2, part), F32),
            pltpu.VMEM((2, part), F32),
            pltpu.VMEM((wide, 2, part), F32),
            pltpu.VMEM((narrow, kv_width, part), BF),
            pltpu.VMEM((group, kv_width, part), BF),
            dma((2,)), dma((narrow,)), dma((narrow,)), dma((wide,)), dma((wide,)), dma((group,)), dma((group,)),
            dma((group,)), dma((group,)), dma((wide,)), dma((wide,)),
            dma((group,)), dma((group,)), dma((2,)),
        ] + [dma((wide,))] * 4,
        cost_estimate=pl.CostEstimate(
            flops=200 * own * d * wide * kv_width, bytes_accessed=4 * sums.size, transcendentals=0
        ),
        compiler_params=pltpu.CompilerParams(
            vmem_limit_bytes=60 << 20, collective_id=2, has_side_effects=True
        ),
        name="input_gradient",
    )(*given)


def assemble_kernel(plan, s_ref, in_ref, out_ref):
    group = plan.group
    for l in range(group):
        owner = jnp.where(s_ref[0] >= group // 2, group - 1 - l, l)
        out_ref[l, 0] = in_ref[0, owner].astype(out_ref.dtype)


def assemble_call(plan, scalars, values, dtype):
    wide, group, cw, part = values.shape
    out = pl.pallas_call(
        functools.partial(assemble_kernel, plan),
        grid_spec=pltpu.PrefetchScalarGridSpec(
            num_scalar_prefetch=1,
            grid=(wide,),
            in_specs=[pl.BlockSpec((1, group, cw, part), lambda w, s: (w, 0, 0, 0))],
            out_specs=[pl.BlockSpec((group, 1, cw, part), lambda w, s: (0, w, 0, 0))],
        ),
        out_shape=[jax.ShapeDtypeStruct((group, wide, cw, part), dtype)],
        cost_estimate=pl.CostEstimate(flops=values.size, bytes_accessed=6 * values.size, transcendentals=0),
        compiler_params=pltpu.CompilerParams(vmem_limit_bytes=40 << 20),
        name="assemble",
    )(scalars, values)[0]
    return out.reshape(group * wide * cw, part)


def half_of(weight, seq_index, seq_count):
    part = weight.shape[0] // seq_count
    return lax.dynamic_slice_in_dim(weight, seq_index * part, part, 0)


def body(
    tokens, attn_gain, w_query, w_key, w_value, w_out, ffn_gain, w_gate, w_up, w_down,
    segment_ids, token_mask, out_grad,
):
    seq_count = lax.axis_size("seq")
    narrow = lax.axis_size("narrow")
    wide = lax.axis_size("wide")
    group = seq_count * narrow
    seq_index = lax.axis_index("seq")
    narrow_index = lax.axis_index("narrow")
    wide_index = lax.axis_index("wide")
    index = seq_index * narrow + narrow_index
    total = segment_ids.shape[0]
    plan = Plan(total, group, wide)
    chunk, cw, rows, own = plan.chunk, plan.cw, plan.rows, plan.own
    d_part = tokens.shape[1]
    d = d_part * narrow
    qw = w_query.shape[1]
    kw = w_key.shape[1]
    kv_heads = kw // HD
    heads = qw // kw
    ff = w_gate.shape[1]

    start_one = jnp.sum((segment_ids < 1).astype(jnp.int32))
    start_two = jnp.sum((segment_ids < 2).astype(jnp.int32))
    starts = jnp.stack([start_one, start_two])
    scalars = jnp.reshape(index, (1,)).astype(jnp.int32)

    def gather_weight(weight):
        return lax.all_gather(half_of(weight, seq_index, seq_count), NS, axis=0, tiled=True)

    def scatter_grad(grad):
        mine = lax.psum_scatter(grad.astype(BF), NS, scatter_dimension=0, tiled=True)
        return lax.all_gather(mine, "seq", axis=0, tiled=True).astype(F32)

    def after(values, *others):
        return lax.optimization_barrier((values, *others))[0]

    w_kv = jnp.concatenate(
        [w_key.reshape(d_part, kv_heads, 1, HD), w_value.reshape(d_part, kv_heads, 1, HD)], axis=2
    ).reshape(d_part, 2 * kw)

    row = jnp.arange(rows, dtype=jnp.int32)
    row_chunk = jnp.where((row // cw) % 2 == 1, 2 * group - 1 - index, index)
    row_block = (row // own + wide_index) % wide
    row_token = row_chunk * chunk + row_block * cw + row % cw
    row_start = jnp.where(row_token >= start_two, start_two, jnp.where(row_token >= start_one, start_one, 0))
    row_pos = (row_token - row_start).astype(F32)
    frequency = THETA ** (-2.0 * jnp.arange(HD // 2, dtype=F32) / HD)
    angles = row_pos[:, None] * jnp.tile(frequency, 4)[None, :]
    cos, sin = jnp.cos(angles), jnp.sin(angles)

    lane = jnp.arange(128, dtype=jnp.int32)[None, :]
    closed = (segment_ids[:, None] != lane - HD) | (token_mask[:, None] != 1)
    kf = jnp.where((lane >= HD) & (lane < HD + 3) & closed, NEG, 0.0)
    kf = jnp.where((lane >= HD + 3) & (lane < HD + 6), 1.0, kf).astype(BF)

    mask = lax.dynamic_slice_in_dim(token_mask, seq_index * (group * chunk), group * chunk, 0)
    g_part = lax.dynamic_index_in_dim(out_grad.reshape(group, wide, cw, d_part), wide_index, 1, keepdims=False)
    mask = lax.dynamic_index_in_dim(mask.reshape(group, wide, cw), wide_index, 1, keepdims=False)
    g_part = jnp.where(mask[:, :, None] == 1, g_part, jnp.zeros_like(g_part))

    w_o = jnp.transpose(gather_weight(w_out).reshape(narrow, kv_heads, heads * HD, d_part), (1, 2, 0, 3))
    w_o = w_o.reshape(kv_heads, heads * HD, d)
    h_one, q, x_low, kx, vx, w_qkv, gains, g_rows, w_kv = head_call(
        plan, tokens.reshape(group, wide, cw, d_part), g_part, jnp.concatenate([w_query, w_kv], axis=1),
        jnp.stack([attn_gain, ffn_gain]), cos, sin, kf, qw, kv_heads
    )
    gains = jnp.transpose(gains, (1, 0, 2)).reshape(2, d)
    gain_one, gain_two = gains[0:1], gains[1:2]
    g_rows = g_rows.reshape(rows, d)

    w_gu = gather_weight(after(jnp.concatenate([w_gate, w_up], axis=1), q))
    w_dn = gather_weight(after(w_down, q)).reshape(narrow, ff, d_part)
    o, qe, x2 = forward_call(plan, starts, q, kx, vx, w_o, x_low, heads)
    w_kv = jnp.transpose(w_kv.reshape(wide, seq_count, d_part // seq_count, 2 * kw), (1, 0, 2, 3))
    w_kv = lax.dynamic_index_in_dim(w_kv, seq_index, 0, keepdims=False).reshape(-1, 2 * kw)
    w_kv = lax.all_gather(after(w_kv, o, w_dn, w_gu), NS, axis=0, tiled=True)
    w_kv = w_kv.reshape(group, wide, d_part // seq_count, 2 * kw)
    w_kv = jnp.transpose(w_kv, (1, 0, 2, 3)).reshape(wide, d, 2 * kw)

    act, d_gate, d_up, h_all, down, dx2, grad_gain_two = ffn_call(plan, x2, gain_two, g_rows, w_gu, w_dn)

    act = after(act, w_kv)
    grad_dn, grad_gate, grad_up, db, result = weights_call(
        plan, dx2, act, h_all, g_rows, d_gate, d_up, down, x2
    )
    dq, sums, dh1, result = backward_call(plan, db, qe, kx, vx, o, w_o, w_qkv, cos, sin, result, heads)

    input_grad, gain_grads, grad_kv = tail_call(
        plan, sums, h_one, dh1, grad_gain_two, dx2, x_low, gain_one, w_kv, cos, sin
    )
    result = assemble_call(plan, scalars, result, BF)
    input_grad = assemble_call(plan, scalars, input_grad, F32)

    def tn(left, right):
        return lax.dot_general(left, right, TN, preferred_element_type=F32).astype(BF)

    def tn_split(left, right):
        return jnp.concatenate([tn(left, right[:, n * d_part : (n + 1) * d_part]) for n in range(narrow)], axis=0)

    grad_dn = scatter_grad(grad_dn.reshape(narrow * ff, d_part))
    grad_gate = scatter_grad(grad_gate)
    grad_up = scatter_grad(grad_up)
    grad_o = scatter_grad(tn_split(o.reshape(rows, qw), db.reshape(rows, d)))
    grad_q = scatter_grad(tn(h_one, dq))
    grad_kv = jnp.transpose(grad_kv.reshape(kv_heads, 2, HD, d_part), (3, 0, 1, 2))
    return (
        result,
        input_grad,
        gain_grads[0],
        grad_q,
        grad_kv[:, :, 0].reshape(d_part, kw),
        grad_kv[:, :, 1].reshape(d_part, kw),
        grad_o,
        gain_grads[1],
        grad_gate,
        grad_up,
        grad_dn,
    )


def solution(mesh):
    width_in, width_out = P("narrow", "wide"), P("wide", "narrow")
    acts = P("seq", "narrow")
    return jax.shard_map(
        body,
        mesh=mesh,
        in_specs=(
            acts, P("narrow"), width_in, width_in, width_in, width_out, P("narrow"),
            width_in, width_in, width_out, P(), P(), acts,
        ),
        out_specs=(
            acts, acts, P("narrow"), width_in, width_in, width_in, width_out, P("narrow"),
            width_in, width_in, width_out,
        ),
        check_vma=False,
    )
```

```python
import functools

import jax
import jax.numpy as jnp
from jax import lax
from jax.experimental import pallas as pl
from jax.experimental.pallas import tpu as pltpu
from jax.sharding import PartitionSpec as P

HD = 64
EPS = 1e-05
THETA = 500000.0
NEG = -1e30
SN = ("seq", "narrow")
NS = ("narrow", "seq")
BF = jnp.bfloat16
F32 = jnp.float32
NT = (((1,), (1,)), ((), ()))
TN = (((0,), (0,)), ((), ()))


def pieces_of(value):
    first = value.astype(BF).astype(F32)
    second = (value - first).astype(BF).astype(F32)
    third = (value - first - second).astype(BF).astype(F32)
    return first, second, third


class Plan:
    def __init__(self, total, group, wide):
        self.total, self.group, self.wide = total, group, wide
        self.chunk = total // (2 * group)
        self.cw = self.chunk // wide
        self.rows = 2 * self.chunk
        self.own = 2 * self.cw


def near_of(plan, z, p):
    side = jnp.minimum(z, plan.wide - 1 - z)
    both = jnp.where(lax.rem(p, 2) == 1, z + (p + 1) // 2, z - p // 2)
    one = jnp.where(z <= plan.wide - 1 - z, z + p - side, z - p + side)
    return jnp.where(p <= 2 * side, both, one)


def turn(values, sign):
    width = values.shape[1]
    lane = lax.broadcasted_iota(jnp.int32, values.shape, 1)
    left, right = pltpu.roll(values, width - HD // 2, 1), pltpu.roll(values, HD // 2, 1)
    return jnp.where(lane % HD < HD // 2, -sign * left, sign * right)


def widen(table, width):
    return jnp.concatenate([table] * (width // 128), axis=1) if width > 128 else table


MESH = pl.DeviceIdType.MESH


def greet(partners):
    barrier = pltpu.get_barrier_semaphore()
    for partner in partners:
        pl.semaphore_signal(barrier, inc=1, device_id=partner, device_id_type=MESH)
    pl.semaphore_wait(barrier, len(partners))


def along_wide(plan, r):
    return {"wide": lax.rem(lax.axis_index("wide") + r + plan.wide, plan.wide)}


def push(src, dst, send, recv, device):
    return pltpu.make_async_remote_copy(
        src_ref=src, dst_ref=dst, send_sem=send, recv_sem=recv, device_id=device, device_id_type=MESH
    )


class Chain:
    def __init__(self, plan, buf, sems):
        self.wide, self.buf, self.sems = plan.wide, buf, sems
        self.z = lax.axis_index("wide")

    def copy(self, slot, h, way):
        send, recv = (self.sems[0], self.sems[1]) if way > 0 else (self.sems[2], self.sems[3])
        return push(self.buf.at[slot], self.buf.at[slot], send.at[h], recv.at[h], {"wide": self.z + way})

    def sends(self, h, way):
        z, last = self.z, self.wide - 1
        return (z >= h - 1) & (z < last) if way > 0 else (z + h - 1 <= last) & (z > 0)

    def go(self, h):
        for way in (1, -1):
            @pl.when(self.sends(h, way))
            def _():
                self.copy(self.z - way * (h - 1), h, way).start()

    def arrive(self, h):
        for way in (1, -1):
            @pl.when(self.z >= h if way > 0 else self.z + h <= self.wide - 1)
            def _():
                slot = self.z - way * h
                send, recv = (self.sems[0], self.sems[1]) if way > 0 else (self.sems[2], self.sems[3])
                push(self.buf.at[slot], self.buf.at[slot], send.at[h], recv.at[h], {"wide": slot}).wait_recv()

    def finish(self):
        for h in range(1, self.wide):
            for way in (1, -1):
                @pl.when(self.sends(h, way))
                def _():
                    self.copy(self.z - way * (h - 1), h, way).wait_send()


class Group:
    def __init__(self, plan):
        self.size, self.narrow = plan.group, plan.group // 2
        self.seq, self.me = lax.axis_index("seq"), lax.axis_index("narrow")
        self.index = self.seq * self.narrow + self.me
        self.sibling = {"seq": 1 - self.seq}

    def device(self, k):
        return lax.rem(self.index + k + self.size, self.size)

    def member(self, k):
        return {"seq": self.device(k) // self.narrow, "narrow": lax.rem(self.device(k), self.narrow)}

    def beside(self, k):
        return lax.rem(self.me + k + self.narrow, self.narrow)


class Parts:
    def __init__(self, plan, team, ref, slots, send, recv, stay):
        self.plan, self.team, self.ref, self.send, self.recv = plan, team, ref, send, recv
        self.slots = slots.at[lax.axis_index("wide")]
        self.part = ref.shape[1] // team.narrow
        self.stay = pltpu.make_async_copy(self.slab(team.index), self.slots.at[team.index], stay)

    def slab(self, other):
        cw, narrow, part = self.plan.cw, self.team.narrow, self.part
        rows = pl.ds(pl.multiple_of((other // narrow) * cw, cw), cw)
        return self.ref.at[rows, pl.ds(pl.multiple_of(lax.rem(other, narrow) * part, part), part)]

    def to(self, k):
        team = self.team
        src = self.slab(team.device(k))
        return push(src, self.slots.at[team.index], self.send.at[k], self.recv.at[k], team.member(k))

    def start(self):
        for k in range(1, self.team.size):
            self.to(k).start()
        self.stay.start()

    def wait(self):
        team = self.team
        self.stay.wait()
        for k in range(1, team.size):
            src = self.slab(team.index)
            push(src, self.slots.at[team.device(-k)], self.send.at[k], self.recv.at[k], team.member(k)).wait_recv()

    def sent(self):
        for k in range(1, self.team.size):
            self.to(k).wait_send()


class Sums:
    def __init__(self, plan, terms, right, left, sems):
        self.wide, self.terms, self.sums, self.sems = plan.wide, terms, (right, left), sems
        self.z = lax.axis_index("wide")
        self.side = jnp.minimum(self.z, plan.wide - 1 - self.z)

    def term(self, h, way):
        return jnp.where(h <= self.side, 2 * h - 1 if way > 0 else 2 * h, self.side + h)

    def sends(self, t, way):
        h = self.wide - t
        return self.z + h <= self.wide - 1 if way > 0 else self.z >= h

    def first(self, way):
        return self.z == (0 if way > 0 else self.wide - 1)

    def copy(self, src, t, way):
        buf = self.sums[0 if way > 0 else 1]
        send, recv = self.sems[:2] if way > 0 else self.sems[2:]
        return push(src, buf.at[t], send.at[t], recv.at[t], {"wide": self.z + way})

    def came(self, t, way):
        buf = self.sums[0 if way > 0 else 1]
        send, recv = self.sems[:2] if way > 0 else self.sems[2:]
        push(buf.at[t], buf.at[t], send.at[t], recv.at[t], {"wide": self.z - way}).wait_recv()

    def go(self, t):
        for way in (1, -1):
            term = self.term(self.wide - t, way)

            @pl.when(self.sends(t, way) & self.first(way))
            def _():
                self.copy(self.terms.at[term], t, way).start()

            if t > 1:
                @pl.when(self.sends(t, way) & jnp.logical_not(self.first(way)))
                def _():
                    self.came(t - 1, way)
                    buf = self.sums[0 if way > 0 else 1]
                    tall = min(32, buf.shape[1])

                    @pl.loop(0, buf.shape[1] // tall)
                    def _(b):
                        at = pl.ds(pl.multiple_of(b * tall, tall), tall)
                        total = buf[t - 1, at, :].astype(F32) + self.terms[term, at, :].astype(F32)
                        buf[t - 1, at, :] = total.astype(BF)

                    self.copy(buf.at[t - 1], t, way).start()

    def finish(self):
        for way in (1, -1):
            @pl.when(jnp.logical_not(self.first(way)))
            def _():
                self.came(self.wide - 1, way)

        for t in range(1, self.wide):
            for way in (1, -1):
                @pl.when(self.sends(t, way))
                def _():
                    self.copy(self.terms.at[0], t, way).wait_send()

    def total(self, own, at):
        out = own
        for way in (1, -1):
            sums = self.sums[0 if way > 0 else 1][self.wide - 1, at, :].astype(F32)
            out = out + jnp.where(self.first(way), 0.0, sums)
        return out


class WeightSum:
    def __init__(self, team, part, came, mine, near, last, out, send, recv):
        self.team, self.part, self.came, self.mine, self.near = team, part, came, mine, near
        self.last, self.out, self.send, self.recv = last, out, send, recv
        self.size = part.shape[1] // 2

    def half(self, core):
        return pl.ds(pl.multiple_of(core * self.size, self.size), self.size)

    def swap(self):
        other = self.part.at[:, self.half(1 - self.team.seq)]
        return push(other, self.came, self.send.at[0], self.recv.at[0], self.team.sibling)

    def give(self, k):
        other = self.team.beside(k)
        return push(self.mine.at[other], self.near.at[k], self.send.at[k], self.recv.at[k], {"narrow": other})

    def back(self):
        at = self.team.narrow
        return push(self.last.at[0], self.last.at[1], self.send.at[at], self.recv.at[at], self.team.sibling)

    def first(self):
        self.swap().start()

    def second(self):
        self.swap().wait_recv()
        for n in range(self.team.narrow):
            own = self.part[n, self.half(self.team.seq), :].astype(F32)
            self.mine[n] = (own + self.came[n].astype(F32)).astype(BF)
        for k in range(1, self.team.narrow):
            self.give(k).start()

    def third(self):
        total = self.mine[self.team.me].astype(F32)
        for k in range(1, self.team.narrow):
            self.give(k).wait_recv()
            total = total + self.near[k].astype(F32)
        self.last[0] = total.astype(BF)
        self.back().start()
        self.out[self.half(self.team.seq), :] = self.last[0].astype(F32)

    def fourth(self):
        self.back().wait_recv()
        self.out[self.half(1 - self.team.seq), :] = self.last[1].astype(F32)

    def sent(self):
        self.swap().wait_send()
        self.back().wait_send()
        for k in range(1, self.team.narrow):
            self.give(k).wait_send()


def head_kernel(
    plan, kv_heads, qw, x_ref, g_ref, w_ref, gains_ref, cos_ref, sin_ref, marks_ref,
    h_out, q_out, own_out, kx, vx, w_out, gains_out, g_out, side_out,
    x_buf, marks, side_buf, side_send, side_recv, w_buf, kv_buf, g_buf, gain_buf,
    x_send, x_recv, x_stay, w_send, w_recv, w_on_send, w_on_recv, gain_send, gain_recv,
    g_send, g_recv, kv_send, kv_recv, kv_on_send, kv_on_recv, keep_sem, *chain_sems
):
    group, wide, chunk, cw, own = plan.group, plan.wide, plan.chunk, plan.cw, plan.own
    team = Group(plan)
    narrow, seq, me = team.narrow, team.seq, team.me
    z = lax.axis_index("wide")
    part = x_ref.shape[3]
    d = part * narrow
    width = w_ref.shape[1]
    fold = part // 2
    chain = Chain(plan, g_buf, chain_sems)
    greet([team.member(k) for k in range(1, group)] + [along_wide(plan, r) for r in range(1, wide)])

    def spot(ref, slot, source):
        rows = pl.ds(pl.multiple_of((source // narrow) * cw, cw), cw)
        return ref.at[slot, rows, pl.ds(pl.multiple_of(lax.rem(source, narrow) * part, part), part)]

    def chunk_for(device):
        return jnp.where(seq == 0, device, group - 1 - device)

    def x_to(r, k):
        src = x_ref.at[chunk_for(team.device(k)), lax.rem(z + r, wide)]
        return push(src, spot(x_buf, r, team.index), x_send.at[r, k], x_recv.at[r, k], team.member(k))

    def x_from(r, k):
        src = x_ref.at[0, 0]
        return push(src, spot(x_buf, r, team.device(-k)), x_send.at[r, k], x_recv.at[r, k], team.member(k))

    def x_own(r):
        src = x_ref.at[chunk_for(team.index), lax.rem(z + r, wide)]
        return pltpu.make_async_copy(src, spot(x_buf, r, team.index), x_stay.at[r])

    def x_start(r):
        for k in range(1, group):
            x_to(r, k).start()
        x_own(r).start()

    def g_to(k):
        src = g_ref.at[chunk_for(team.device(k))]
        return push(src, spot(g_buf, z, team.index), g_send.at[k], g_recv.at[k], team.member(k))

    def w_rows(n, core):
        return w_buf.at[pl.ds(pl.multiple_of(n * part + core * fold, fold), fold)]

    def w_to(k):
        src = w_ref.at[pl.ds(pl.multiple_of(seq * fold, fold), fold)]
        return push(src, w_rows(me, seq), w_send.at[k], w_recv.at[k], {"narrow": team.beside(k)})

    def w_from(k):
        n = team.beside(-k)
        return push(w_rows(n, seq), w_rows(n, seq), w_send.at[k], w_recv.at[k], {"narrow": n})

    def w_on(k, core):
        n = team.beside(-k)
        return push(w_rows(n, core), w_rows(n, core), w_on_send.at[k], w_on_recv.at[k], team.sibling)

    def side_to(r, slot):
        mine = w_ref.at[:, qw:]
        return push(mine, side_buf.at[slot], side_send.at[r], side_recv.at[r], along_wide(plan, r))

    def gain_to(k, slot):
        return push(gains_ref, gain_buf.at[slot], gain_send.at[k], gain_recv.at[k], {"narrow": team.beside(k)})

    for k in range(1, group):
        g_to(k).start()
    g_stay = pltpu.make_async_copy(g_ref.at[chunk_for(team.index)], spot(g_buf, z, team.index), keep_sem.at[0])
    g_stay.start()
    for k in range(1, narrow):
        w_to(k).start()
        gain_to(k, me).start()
    x_start(0)
    if wide > 1:
        x_start(1)
    for r in range(1, wide):
        side_to(r, z).start()
    side_buf[z] = w_ref[:, qw:]
    w_buf[pl.ds(pl.multiple_of(me * part, part), part), :] = w_ref[...]
    gain_buf[me] = gains_ref[...]
    for k in range(1, narrow):
        w_from(k).wait_recv()
        w_on(k, seq).start()
    g_stay.wait()
    for k in range(1, group):
        push(
            g_ref.at[0], spot(g_buf, z, team.device(-k)), g_send.at[k], g_recv.at[k], team.member(k)
        ).wait_recv()
    chain.go(1)
    for k in range(1, narrow):
        gain_to(k, team.beside(-k)).wait_recv()
        w_on(k, 1 - seq).wait_recv()
    gain_one = jnp.concatenate([gain_buf[n, 0:1] for n in range(narrow)], axis=1)
    gains_out[...] = gain_buf[...]
    w_keep = pltpu.make_async_copy(w_buf, w_out, keep_sem.at[1])
    w_keep.start()

    def kv_rows(core, n, r):
        return kv_buf.at[core, n, pl.ds(pl.multiple_of(r * own, own), own)]

    def kv_to(r, k):
        mine = kv_rows(seq, me, r)
        return push(mine, mine, kv_send.at[r, k], kv_recv.at[r, k], {"narrow": team.beside(k)})

    def kv_from(r, k):
        theirs = kv_rows(seq, team.beside(-k), r)
        return push(theirs, theirs, kv_send.at[r, k], kv_recv.at[r, k], {"narrow": team.beside(k)})

    def kv_on(k, core):
        slot = kv_buf.at[core, team.beside(-k)]
        return push(slot, slot, kv_on_send.at[k], kv_on_recv.at[k], team.sibling)

    @pl.loop(0, wide)
    def _(r):
        x_own(r).wait()
        for k in range(1, group):
            x_from(r, k).wait_recv()
        for later in range(2, wide):
            @pl.when(r == later - 2)
            def _():
                x_start(later)
        at = pl.ds(pl.multiple_of(r * own, own), own)
        low = x_buf[r]
        x = low.astype(F32)
        mean = jnp.mean(x * x, axis=1, keepdims=True)
        h = (x * lax.rsqrt(mean + EPS) * gain_one).astype(BF)
        h_out[at, :] = h
        t = jnp.dot(h, w_buf[...], preferred_element_type=F32)
        lane = lax.broadcasted_iota(jnp.int32, t.shape, 1)
        plain = (lane >= qw) & (lane % 128 >= HD)
        out = t * widen(cos_ref[at, :], width) + turn(t, 1.0) * widen(sin_ref[at, :], width)
        out = jnp.where(plain, t, out)
        q_out[at, :] = (out[:, :qw] * (HD ** -0.5)).astype(BF)
        kv_buf[seq, me, at, :] = out[:, qw:].astype(BF)
        for k in range(1, narrow):
            kv_to(r, k).start()

        @pl.when(r == min(1, wide - 1))
        def _():
            chain.arrive(1)
            if wide > 2:
                chain.go(2)

    kv_on(0, seq).start()
    own_out[...] = x_buf[0]
    if wide > 2:
        chain.arrive(2)
    if wide > 3:
        chain.go(3)
    for k in range(1, narrow):
        for r in range(wide):
            kv_from(r, k).wait_recv()
        kv_on(k, seq).start()
    for k in range(narrow):
        kv_on(k, 1 - seq).wait_recv()

    feature = lax.broadcasted_iota(jnp.int32, (cw, 128), 1)
    ones = jnp.where(feature < 3, 1.0, 0.0).astype(BF)
    spread = lax.broadcasted_iota(jnp.int32, (marks_ref.shape[0], 128), 0) + HD
    target = lax.broadcasted_iota(jnp.int32, (marks_ref.shape[0], 128), 1)
    spread = jnp.where(spread == target, 1.0, 0.0).astype(BF)

    @pl.loop(0, 2 * group)
    def _(c):
        columns = pl.ds(pl.multiple_of(c * chunk, chunk), chunk)
        marks[...] = lax.dot_general(marks_ref[:, columns], spread, TN, preferred_element_type=F32).astype(BF)
        late = c >= group
        owner = jnp.where(late, 2 * group - 1 - c, c)
        for r in range(wide):
            block = pl.ds(pl.multiple_of(lax.rem(z + r, wide) * cw, cw), cw)
            at = pl.ds(pl.multiple_of(c * chunk + lax.rem(z + r, wide) * cw, cw), cw)
            source = pl.ds(pl.multiple_of(r * own + jnp.where(late, cw, 0), cw), cw)
            for g in range(kv_heads):
                kv = kv_buf[owner // narrow, lax.rem(owner, narrow), source, g * 128 : (g + 1) * 128]
                kx[g, at, :] = jnp.where(feature < HD, kv, marks[block, :])
                vx[g, at, :] = jnp.where(feature < HD, ones, kv)

    for h in range(3, wide):
        chain.arrive(h)
        if h + 1 < wide:
            chain.go(h + 1)
    for r in range(1, wide):
        side_to(r, lax.rem(z - r + wide, wide)).wait_recv()
        side_to(r, z).wait_send()
    side_out[...] = side_buf[...]
    keep = [
        pltpu.make_async_copy(g_buf.at[near_of(plan, z, p)], g_out.at[p], keep_sem.at[2 + p]) for p in range(wide)
    ]
    for copy in keep:
        copy.start()
    chain.finish()
    for k in range(1, narrow):
        w_to(k).wait_send()
        w_on(k, seq).wait_send()
        gain_to(k, me).wait_send()
        for r in range(wide):
            kv_to(r, k).wait_send()
    for k in range(narrow):
        kv_on(k, seq).wait_send()
    for k in range(1, group):
        g_to(k).wait_send()
        for r in range(wide):
            x_to(r, k).wait_send()
    w_keep.wait()
    for copy in keep:
        copy.wait()


def head_call(plan, x, g, w, gains, cos, sin, marks, qw, kv_heads):
    group, wide, cw, part = x.shape
    narrow = group // 2
    d = part * narrow
    width = w.shape[1]
    rows, own, total = plan.rows, plan.own, plan.total
    dma = pltpu.SemaphoreType.DMA
    whole = pl.BlockSpec(memory_space=pltpu.VMEM)
    hbm = pl.BlockSpec(memory_space=pl.ANY)
    keys = jax.ShapeDtypeStruct((kv_heads, total, 128), BF)
    return pl.pallas_call(
        functools.partial(head_kernel, plan, kv_heads, qw),
        in_specs=[hbm, hbm] + [whole] * 5,
        out_specs=[whole] * 5 + [hbm, whole, hbm, whole],
        out_shape=[
            jax.ShapeDtypeStruct((rows, d), BF),
            jax.ShapeDtypeStruct((rows, qw), BF),
            jax.ShapeDtypeStruct((own, d), BF),
            keys,
            keys,
            jax.ShapeDtypeStruct((d, width), BF),
            jax.ShapeDtypeStruct((narrow, 2, part), F32),
            jax.ShapeDtypeStruct((wide, own, d), BF),
            jax.ShapeDtypeStruct((wide, part, width - qw), BF),
        ],
        scratch_shapes=[
            pltpu.VMEM((wide, own, d), BF),
            pltpu.VMEM((plan.chunk, 128), BF),
            pltpu.VMEM((wide, part, width - qw), BF),
            dma((wide,)), dma((wide,)),
            pltpu.VMEM((d, width), BF),
            pltpu.VMEM((2, narrow, rows, width - qw), BF),
            pltpu.VMEM((wide, own, d), BF),
            pltpu.VMEM((narrow, 2, part), F32),
            dma((wide, group)), dma((wide, group)), dma((wide,)),
            dma((narrow,)), dma((narrow,)), dma((narrow,)), dma((narrow,)), dma((narrow,)), dma((narrow,)),
            dma((group,)), dma((group,)),
            dma((wide, narrow)), dma((wide, narrow)), dma((narrow,)), dma((narrow,)),
            dma((2 + wide,)),
        ] + [dma((wide,))] * 4,
        cost_estimate=pl.CostEstimate(
            flops=60 * rows * d * width, bytes_accessed=8 * rows * d + 2 * d * width, transcendentals=rows
        ),
        compiler_params=pltpu.CompilerParams(
            vmem_limit_bytes=60 << 20, collective_id=4, has_side_effects=True
        ),
        name="head",
    )(x, g, w, gains, cos, sin, marks)


def split_heads(block, heads, low):
    tiles = []
    for h in range(heads):
        tile = block[:, (h // 2) * 128 : (h // 2 + 1) * 128]
        if (h % 2 == 0) != low:
            tile = pltpu.roll(tile, HD, 1)
        tiles.append(tile)
    return tiles


def join_heads(tiles, low):
    rows = tiles[0].shape[0]
    lane = lax.broadcasted_iota(jnp.int32, (rows, 128), 1)
    pairs = []
    for h in range(0, len(tiles), 2):
        first, second = tiles[h], tiles[h + 1]
        if low:
            second = pltpu.roll(second, HD, 1)
        else:
            first = pltpu.roll(first, HD, 1)
        pairs.append(jnp.where(lane < HD, first, second))
    return jnp.concatenate(pairs, axis=1)


def forward_kernel(
    plan, kv_heads, heads, s_ref, q_ref, kx, vx, wo_ref, x_ref, wd_ref, o_ref, qe_ref, x2_ref, wd_out,
    terms, right, left, term_acc, wd_send, wd_recv, wd_on_send, wd_on_recv, wd_keep, *sems
):
    wide, cw, chunk, own = plan.wide, plan.cw, plan.chunk, plan.own
    rows, width = heads * cw, heads * HD
    z = lax.axis_index("wide")
    team = Group(plan)
    index = team.index
    unit, g = pl.program_id(0), pl.program_id(1)
    last_g = kv_heads - 1
    piece, half = wide - 1 - unit // 2, lax.rem(unit, 2)
    w = near_of(plan, z, piece)
    r = lax.rem(w - z + wide, wide)
    c = jnp.where(half == 1, 2 * plan.group - 1 - index, index)
    low_rows = pl.ds(pl.multiple_of(half * cw, cw), cw)
    columns = pl.ds(pl.multiple_of(g * width, width), width)

    attn = Sums(plan, terms, right, left, sems)

    def out_rows(n):
        return pl.ds(pl.multiple_of((n * kv_heads + g) * width, width), width)

    fold = wd_ref.shape[0] // 2

    def wd_rows(n, core):
        return wd_out.at[n, pl.ds(pl.multiple_of(core * fold, fold), fold)]

    def wd_to(k):
        mine = wd_ref.at[pl.ds(pl.multiple_of(team.seq * fold, fold), fold)]
        return push(mine, wd_rows(team.me, team.seq), wd_send.at[k], wd_recv.at[k], {"narrow": team.beside(k)})

    def wd_from(k):
        theirs = wd_rows(team.beside(-k), team.seq)
        return push(theirs, theirs, wd_send.at[k], wd_recv.at[k], {"narrow": team.beside(k)})

    def wd_on(k, core):
        rows_of = wd_rows(team.beside(-k), core)
        return push(rows_of, rows_of, wd_on_send.at[k], wd_on_recv.at[k], team.sibling)

    wd_own = pltpu.make_async_copy(wd_ref, wd_out.at[team.me], wd_keep)

    @pl.when((unit == 0) & (g == 0))
    def _():
        others = [team.member(k) for k in range(1, plan.group)]
        greet(others + [along_wide(plan, k) for k in range(1, wide)])
        for k in range(1, team.narrow):
            wd_to(k).start()
        wd_own.start()

    for k in range(1, team.narrow):
        @pl.when((unit == 2 * wide - (3 if k == 1 else 2)) & (g == 0))
        def _():
            wd_from(k).wait_recv()
            wd_on(k, team.seq).start()

    lane = lax.broadcasted_iota(jnp.int32, (cw, 128), 1)
    token = c * chunk + w * cw + lax.broadcasted_iota(jnp.int32, (cw, 128), 0)
    segment = (token >= s_ref[0]).astype(jnp.int32) + (token >= s_ref[1]).astype(jnp.int32)
    mark = jnp.where(lane == HD + segment, 1.0, 0.0)
    block = q_ref[pl.ds(pl.multiple_of(r * own + half * cw, cw), cw), columns]
    tiles = split_heads(block.astype(F32), heads, True)
    q32 = jnp.concatenate([jnp.where(lane < HD, t, mark) for t in tiles], axis=0)
    q = q32.astype(BF)

    def step(j, carry, diagonal=False):
        top, acc = carry
        at = pl.ds(pl.multiple_of(j * chunk, chunk), chunk)
        s = lax.dot_general(q, kx[g, at, :], NT, preferred_element_type=F32)
        if diagonal:
            row = lax.broadcasted_iota(jnp.int32, (rows, chunk), 0) % cw + w * cw
            col = lax.broadcasted_iota(jnp.int32, (rows, chunk), 1)
            s = jnp.where(col <= row, s, NEG)
        new = jnp.maximum(top, jnp.max(s, axis=1, keepdims=True))
        p = jnp.exp(s - new).astype(BF)
        acc = acc * jnp.exp(top - new) + jnp.dot(p, vx[g, at, :], preferred_element_type=F32)
        return new, acc

    start = (jnp.full((rows, 1), NEG, F32), jnp.zeros((rows, 128), F32))
    carry = lax.fori_loop(0, c, step, start)
    top, acc = step(c, carry, True)
    total = acc[:, 0:1]
    out = acc / total
    out = join_heads([out[h * cw : (h + 1) * cw] for h in range(heads)], False).astype(BF)
    o_ref[w, low_rows, columns] = out
    first, second, third = pieces_of(-(top + jnp.log(total)))
    wide_lane = lax.broadcasted_iota(jnp.int32, (rows, 128), 1)
    qe = jnp.where(wide_lane == HD + 3, first, q32)
    qe = jnp.where(wide_lane == HD + 4, second, qe)
    qe = jnp.where(wide_lane == HD + 5, third, qe)
    qe_ref[r, g, half] = qe.astype(BF)

    term = jnp.concatenate(
        [jnp.dot(out, wo_ref[out_rows(n), :], preferred_element_type=F32) for n in range(plan.group // 2)], axis=1
    )

    @pl.when(g == 0)
    def _():
        term_acc[...] = term

    @pl.when(g > 0)
    def _():
        term_acc[...] += term

    @pl.when((g == last_g) & (piece == 0))
    def _():
        x2_ref[low_rows, :] = x_ref[low_rows, :].astype(F32) + term_acc[...]

    @pl.when((g == last_g) & (piece > 0))
    def _():
        terms[piece, low_rows, :] = term_acc[...].astype(BF)

    for t in range(1, wide):
        @pl.when((g == last_g) & (unit == 2 * t - 1))
        def _():
            attn.go(t)

    @pl.when((unit == 2 * wide - 1) & (g == last_g))
    def _():
        attn.finish()
        tall = min(32, own)

        @pl.loop(0, own // tall)
        def _(b):
            at = pl.ds(pl.multiple_of(b * tall, tall), tall)
            x2_ref[at, :] = attn.total(x2_ref[at, :], at)

        wd_own.wait()
        for k in range(1, team.narrow):
            wd_on(k, 1 - team.seq).wait_recv()
            wd_to(k).wait_send()
            wd_on(k, team.seq).wait_send()


def forward_call(plan, starts, q, kx, vx, w_o, x, w_down, heads):
    kv_heads, total, _ = kx.shape
    own, d = x.shape
    wide, rows, cw = plan.wide, plan.rows, plan.cw
    qw = q.shape[1]
    pairs = kv_heads * heads * total * rows // 2
    fixed = lambda a: pl.BlockSpec(a.shape, lambda u, g: (0,) * a.ndim, pipeline_mode=pl.Buffered(1))
    given = [q, kx, vx, w_o, x]
    outs = [
        jax.ShapeDtypeStruct((wide, own, qw), BF),
        jax.ShapeDtypeStruct((wide, kv_heads, 2, heads * cw, 128), BF),
        jax.ShapeDtypeStruct((own, d), F32),
    ]
    buffer = pltpu.VMEM((wide, own, d), BF)
    sems = pltpu.SemaphoreType.DMA((wide,))
    return pl.pallas_call(
        functools.partial(forward_kernel, plan, kv_heads, heads),
        grid=(2 * wide, kv_heads),
        in_specs=[pl.BlockSpec(memory_space=pltpu.SMEM)] + [fixed(a) for a in given]
        + [pl.BlockSpec(memory_space=pl.ANY)],
        out_specs=[fixed(a) for a in outs] + [pl.BlockSpec(memory_space=pl.ANY)],
        out_shape=outs + [jax.ShapeDtypeStruct((plan.group // 2, *w_down.shape), BF)],
        scratch_shapes=[buffer] * 3 + [pltpu.VMEM((cw, d), F32)]
        + [pltpu.SemaphoreType.DMA((plan.group // 2,))] * 4 + [pltpu.SemaphoreType.DMA] + [sems] * 4,
        cost_estimate=pl.CostEstimate(
            flops=16 * pairs * HD, bytes_accessed=8 * kv_heads * total * 128, transcendentals=pairs
        ),
        compiler_params=pltpu.CompilerParams(
            vmem_limit_bytes=56 << 20, collective_id=5, has_side_effects=True
        ),
        name="attention_forward",
    )(starts, *given, w_down)


def ffn_kernel(
    plan, x2_ref, gain_ref, g_ref, wg_ref, wu_ref, wd_ref,
    dg_ref, du_ref, h_out, dn_ref, dx_ref, gain_out, grad_out,
    h_buf, in_buf, out_buf, dn_acc, dh_acc, own_dh, act_buf, g_buf, grad_buf, rs_send, rs_recv, grad_sem, *chain_sems
):
    wide, narrow = plan.wide, plan.group // 2
    own, d = x2_ref.shape
    part = d // narrow
    piece, step = pl.program_id(0), pl.program_id(1)
    last = pl.num_programs(1) - 1
    tall = min(32, own)

    z = lax.axis_index("wide")
    owner = near_of(plan, z, piece)

    chain = Chain(plan, h_buf, chain_sems)

    def give(device):
        return push(out_buf.at[device], in_buf.at[z], rs_send.at[device], rs_recv.at[z], {"wide": device})

    @pl.when((piece == 0) & (step == 0))
    def _():
        greet([along_wide(plan, r) for r in range(1, wide)])

        @pl.loop(0, own // tall)
        def _(b):
            at = pl.ds(pl.multiple_of(b * tall, tall), tall)
            x2 = x2_ref[at, :]
            scale = lax.rsqrt(jnp.mean(x2 * x2, axis=1, keepdims=True) + EPS)
            h_buf[z, at, :] = (x2 * scale * gain_ref[...]).astype(BF)

        chain.go(1)

    for h in range(1, wide):
        @pl.when((piece == h) & (step == 0))
        def _():
            chain.arrive(h)
            if h + 1 < wide:
                chain.go(h + 1)

    @pl.when(step == 0)
    def _():
        h_out[...] = h_buf[owner]
        g_buf[pl.ds(pl.multiple_of(piece * own, own), own), :] = g_ref[...]

    h = h_buf[owner]
    wg, wu = wg_ref[...], wu_ref[...]
    gate = jnp.dot(h, wg, preferred_element_type=F32)
    up = jnp.dot(h, wu, preferred_element_type=F32)
    d_act = jnp.zeros_like(gate)
    for n in range(narrow):
        d_act += lax.dot_general(
            g_ref[:, n * part : (n + 1) * part], wd_ref[n], NT, preferred_element_type=F32
        )
    sig = jax.nn.sigmoid(gate)
    silu = gate * sig
    act = (silu * up).astype(BF)
    dg = (d_act * up * sig * (1.0 + gate * (1.0 - sig))).astype(BF)
    du = (d_act * silu).astype(BF)
    tile = act.shape[1]
    act_buf[pl.ds(pl.multiple_of(piece * own, own), own), pl.ds(pl.multiple_of(step * tile, tile), tile)] = act
    dg_ref[...] = dg
    du_ref[...] = du
    dh = lax.dot_general(dg, wg, NT, preferred_element_type=F32) + lax.dot_general(
        du, wu, NT, preferred_element_type=F32
    )

    @pl.when(step == 0)
    def _():
        dh_acc[...] = dh

    @pl.when(step > 0)
    def _():
        dh_acc[...] += dh

    for n in range(narrow):
        at = slice(n * part, (n + 1) * part)
        down = jnp.dot(act, wd_ref[n], preferred_element_type=F32)

        @pl.when(step == 0)
        def _():
            dn_acc[:, at] = down

        @pl.when(step > 0)
        def _():
            dn_acc[:, at] += down

    @pl.when(step == last)
    def _():
        dn_ref[0] = dn_acc[...].astype(BF)

    @pl.when((step == last) & (piece == 0))
    def _():
        own_dh[...] = dh_acc[...]

    @pl.when((step == last) & (piece > 0))
    def _():
        out_buf[owner] = dh_acc[...].astype(BF)
        give(owner).start()

    @pl.when((step == last) & (piece == wide - 1))
    def _():
        @pl.loop(0, last + 1)
        def _(t):
            at = pl.ds(pl.multiple_of(t * tile, tile), tile)
            keep = pltpu.make_async_copy(grad_buf, grad_out.at[:, at, :], grad_sem)

            @pl.when(t > 0)
            def _():
                keep.wait()

            for n in range(narrow):
                grad_buf[n] = lax.dot_general(
                    act_buf[:, at], g_buf[:, n * part : (n + 1) * part], TN, preferred_element_type=F32
                ).astype(BF)
            keep.start()

        for p in range(1, wide):
            other = near_of(plan, z, p)
            push(out_buf.at[z], in_buf.at[other], rs_send.at[z], rs_recv.at[other], {"wide": other}).wait_recv()
        gain_out[...] = jnp.zeros_like(gain_out)

        @pl.loop(0, own // tall)
        def _(b):
            at = pl.ds(pl.multiple_of(b * tall, tall), tall)
            dh2 = own_dh[at, :]
            for p in range(1, wide):
                dh2 = dh2 + in_buf[near_of(plan, z, p), at, :].astype(F32)
            x2 = x2_ref[at, :]
            scale = lax.rsqrt(jnp.mean(x2 * x2, axis=1, keepdims=True) + EPS)
            z2 = x2 * scale
            gain_out[...] += jnp.sum(dh2 * z2, axis=0, keepdims=True)
            dz2 = dh2 * gain_ref[...]
            inner = jnp.mean(dz2 * z2, axis=1, keepdims=True)
            dx_ref[at, :] = g_buf[at, :].astype(F32) + scale * (dz2 - z2 * inner)

        chain.finish()
        for p in range(1, wide):
            give(near_of(plan, z, p)).wait_send()
        pltpu.make_async_copy(grad_buf, grad_out.at[:, pl.ds(0, tile), :], grad_sem).wait()


def ffn_call(plan, x2, gain, g_rows, w_gu, w_dn):
    own, d = x2.shape
    wide, rows = plan.wide, plan.rows
    narrow, ff, part = w_dn.shape
    tile = min(512, ff)
    tiles = ff // tile
    fixed = lambda shape: pl.BlockSpec(shape, lambda p, f: (0,) * len(shape), pipeline_mode=pl.Buffered(1))
    tall = pl.BlockSpec((own, tile), lambda p, f: (p, f))
    hidden = jax.ShapeDtypeStruct((rows, ff), BF)
    buffer = pltpu.VMEM((wide, own, d), BF)
    sems = pltpu.SemaphoreType.DMA((wide,))
    return pl.pallas_call(
        functools.partial(ffn_kernel, plan),
        grid=(wide, tiles),
        in_specs=[
            fixed((own, d)),
            fixed((1, d)),
            pl.BlockSpec((own, d), lambda p, f: (p, 0)),
            pl.BlockSpec((d, tile), lambda p, f: (0, f)),
            pl.BlockSpec((d, tile), lambda p, f: (0, tiles + f)),
            pl.BlockSpec((narrow, tile, part), lambda p, f: (0, f, 0)),
        ],
        out_specs=[
            tall, tall,
            pl.BlockSpec((own, d), lambda p, f: (p, 0)),
            pl.BlockSpec((1, own, d), lambda p, f: (p, 0, 0)),
            fixed((own, d)),
            fixed((1, d)),
            pl.BlockSpec(memory_space=pl.ANY),
        ],
        out_shape=[
            hidden, hidden,
            jax.ShapeDtypeStruct((rows, d), BF),
            jax.ShapeDtypeStruct((wide, own, d), BF),
            jax.ShapeDtypeStruct((own, d), F32),
            jax.ShapeDtypeStruct((1, d), F32),
            jax.ShapeDtypeStruct((narrow, ff, part), BF),
        ],
        scratch_shapes=[
            buffer, buffer, buffer,
            pltpu.VMEM((own, d), F32), pltpu.VMEM((own, d), F32), pltpu.VMEM((own, d), F32),
            pltpu.VMEM((rows, ff), BF), pltpu.VMEM((rows, d), BF), pltpu.VMEM((narrow, tile, part), BF),
            sems, sems, pltpu.SemaphoreType.DMA, sems, sems, sems, sems,
        ],
        cost_estimate=pl.CostEstimate(
            flops=16 * rows * d * ff, bytes_accessed=6 * d * ff + 12 * rows * d, transcendentals=rows * ff
        ),
        compiler_params=pltpu.CompilerParams(
            vmem_limit_bytes=60 << 20, collective_id=1, has_side_effects=True
        ),
        name="feed_forward",
    )(x2, gain, g_rows, w_gu, w_gu, w_dn)


def weights_kernel(
    plan, tiles, dx2_ref, h_ref, dg_ref, du_ref, down_ref, x2_ref,
    gate_out, up_out, db_out, res_out,
    db_buf, right, left, keep_sem, *sems
):
    wide = plan.wide
    step = pl.program_id(0)
    last = pl.num_programs(0) - 1
    chain = Chain(plan, db_buf, sems[:4])
    down = Sums(plan, down_ref, right, left, sems[4:])
    keep = pltpu.make_async_copy(db_buf, db_out, keep_sem)

    @pl.when(step == 0)
    def _():
        db_buf[lax.axis_index("wide")] = dx2_ref[...].astype(BF)
        greet([along_wide(plan, k) for k in range(1, wide)])
        chain.go(1)

    @pl.when(step < tiles)
    def _():
        gate_out[...] = lax.dot_general(h_ref[...], dg_ref[...], TN, preferred_element_type=F32).astype(BF)

    @pl.when(step >= tiles)
    def _():
        up_out[...] = lax.dot_general(h_ref[...], du_ref[...], TN, preferred_element_type=F32).astype(BF)

    for h in range(1, wide):
        @pl.when(step == min(last, h * (tiles + 1) - 1))
        def _():
            chain.arrive(h)
            if h + 1 < wide:
                chain.go(h + 1)
            down.go(h)

    @pl.when(step == last)
    def _():
        keep.start()
        down.finish()
        tall = min(32, x2_ref.shape[0])

        @pl.loop(0, x2_ref.shape[0] // tall)
        def _(b):
            at = pl.ds(pl.multiple_of(b * tall, tall), tall)
            res_out[at, :] = down.total(x2_ref[at, :] + down_ref[0, at, :].astype(F32), at).astype(BF)

        chain.finish()
        keep.wait()


def weights_call(plan, dx2, h, d_gate, d_up, down, x2):
    own, d = dx2.shape
    rows, ff = d_gate.shape
    wide = plan.wide
    tiles = 4
    d_tile = d // tiles
    fixed = lambda a: pl.BlockSpec(a.shape, lambda s: (0,) * a.ndim, pipeline_mode=pl.Buffered(1))
    first = lambda s: jnp.minimum(s, tiles - 1)
    second = lambda s: jnp.clip(s - tiles, 0, tiles - 1)
    sems = pltpu.SemaphoreType.DMA((wide,))
    return pl.pallas_call(
        functools.partial(weights_kernel, plan, tiles),
        grid=(2 * tiles,),
        in_specs=[
            fixed(dx2),
            pl.BlockSpec((rows, d_tile), lambda s: (0, lax.rem(s, tiles))),
            fixed(d_gate), fixed(d_up), fixed(down), fixed(x2),
        ],
        out_specs=[
            pl.BlockSpec((d_tile, ff), lambda s: (first(s), 0)),
            pl.BlockSpec((d_tile, ff), lambda s: (second(s), 0)),
            pl.BlockSpec(memory_space=pl.ANY),
            pl.BlockSpec((own, d), lambda s: (0, 0), pipeline_mode=pl.Buffered(1)),
        ],
        out_shape=[
            jax.ShapeDtypeStruct((d, ff), BF),
            jax.ShapeDtypeStruct((d, ff), BF),
            jax.ShapeDtypeStruct((wide, own, d), BF),
            jax.ShapeDtypeStruct((own, d), BF),
        ],
        scratch_shapes=[pltpu.VMEM((wide, own, d), BF)] * 3 + [pltpu.SemaphoreType.DMA] + [sems] * 8,
        cost_estimate=pl.CostEstimate(
            flops=8 * rows * d * ff, bytes_accessed=20 * rows * d, transcendentals=0
        ),
        compiler_params=pltpu.CompilerParams(
            vmem_limit_bytes=60 << 20, collective_id=6, has_side_effects=True
        ),
        name="weight_gradients",
    )(dx2, h, d_gate, d_up, down, x2)


def backward_kernel(
    plan, kv_heads, heads, db_ref, qe_ref, kx, vx, o_ref, wo_ref, wq_ref, cos_ref, sin_ref, res_ref,
    dq_ref, sums, dh_ref, res_out, terms, right, left, term_acc, results,
    part_send, part_recv, keep_sem, *sems
):
    wide, cw, chunk, own = plan.wide, plan.cw, plan.chunk, plan.own
    rows = heads * cw
    width = heads * HD
    z = lax.axis_index("wide")
    team = Group(plan)
    index = team.index
    chain = Chain(plan, results, sems[:4])
    back = Sums(plan, terms, right, left, sems[4:])
    parts = Parts(plan, team, res_ref, results, part_send, part_recv, keep_sem.at[0])
    unit, g = pl.program_id(0), pl.program_id(1)
    last_unit, last_g = 2 * wide - 1, kv_heads - 1
    piece, half = wide - 1 - unit // 2, lax.rem(unit, 2)
    w = near_of(plan, z, piece)
    r = lax.rem(w - z + wide, wide)
    c = jnp.where(half == 1, 2 * plan.group - 1 - index, index)
    low_rows = pl.ds(pl.multiple_of(half * cw, cw), cw)

    @pl.when((unit == 0) & (g == 0))
    def _():
        others = [team.member(k) for k in range(1, plan.group)]
        greet(others + [along_wide(plan, k) for k in range(1, wide)])
        parts.start()

        @pl.loop(0, kv_heads * plan.total // chunk)
        def _(b):
            at = pl.ds(pl.multiple_of(lax.rem(b, plan.total // chunk) * chunk, chunk), chunk)
            sums[b // (plan.total // chunk), at, :] = jnp.zeros((chunk, 128), F32)

    @pl.when((unit == 1) & (g == last_g))
    def _():
        parts.wait()
        chain.go(1)

    for h in range(1, wide):
        late = {1: (3, 0), 2: (4, last_g), 3: (6, 0)}.get(h, (min(h + 3, last_unit), last_g))

        @pl.when((unit == late[0]) & (g == late[1]))
        def _():
            chain.arrive(h)
            if h + 1 < wide:
                chain.go(h + 1)

    lane = lax.broadcasted_iota(jnp.int32, (cw, 128), 1)
    columns = pl.ds(pl.multiple_of(g * width, width), width)
    part = wo_ref.shape[1]
    grad = jnp.zeros((cw, width), F32)
    for n in range(team.narrow):
        out_rows = pl.ds(pl.multiple_of((n * kv_heads + g) * width, width), width)
        grad += lax.dot_general(
            db_ref[w, low_rows, n * part : (n + 1) * part], wo_ref[out_rows, :], NT, preferred_element_type=F32
        )
    do = split_heads(grad.astype(BF).astype(F32), heads, False)
    o = split_heads(o_ref[w, low_rows, columns].astype(F32), heads, False)
    marked = []
    for one, other in zip(o, do):
        clean = jnp.where(lane >= HD, other, 0.0)
        first, second, third = pieces_of(-jnp.sum(one * clean, axis=1, keepdims=True))
        tile = jnp.where(lane == 0, first, clean)
        tile = jnp.where(lane == 1, second, tile)
        marked.append(jnp.where(lane == 2, third, tile))
    dox32 = jnp.concatenate(marked, axis=0)
    wide_lane = lax.broadcasted_iota(jnp.int32, (rows, 128), 1)
    dox = dox32.astype(BF)
    do_clean = jnp.where(wide_lane >= HD, dox32, 0.0).astype(BF)
    q = qe_ref[r, g, half]
    q_clean = jnp.where(wide_lane < HD, q.astype(F32), 0.0).astype(BF)

    def step(j, dq, diagonal=False):
        at = pl.ds(pl.multiple_of(j * chunk, chunk), chunk)
        key = kx[g, at, :]
        s = lax.dot_general(key, q, NT, preferred_element_type=F32)
        if diagonal:
            row = lax.broadcasted_iota(jnp.int32, (chunk, rows), 1) % cw + w * cw
            col = lax.broadcasted_iota(jnp.int32, (chunk, rows), 0)
            s = jnp.where(col <= row, s, NEG)
        p = jnp.exp(s)
        dp = lax.dot_general(vx[g, at, :], dox, NT, preferred_element_type=F32)
        ds = (p * dp).astype(BF)
        sums[g, at, :] += jnp.dot(ds, q_clean, preferred_element_type=F32) + jnp.dot(
            p.astype(BF), do_clean, preferred_element_type=F32
        )
        return dq + lax.dot_general(ds, key, TN, preferred_element_type=F32)

    dq = lax.fori_loop(0, c, step, jnp.zeros((rows, 128), F32))
    dq = step(c, dq, True) * (HD ** -0.5)
    dq = join_heads([dq[h * cw : (h + 1) * cw] for h in range(heads)], True)
    at = pl.ds(pl.multiple_of(r * own + half * cw, cw), cw)
    dq = dq * widen(cos_ref[at, :], width) + turn(dq, -1.0) * widen(sin_ref[at, :], width)
    dq = dq.astype(BF)
    dq_ref[at, columns] = dq

    term = lax.dot_general(dq, wq_ref[:, columns], NT, preferred_element_type=F32)

    @pl.when(g == 0)
    def _():
        term_acc[...] = term

    @pl.when(g > 0)
    def _():
        term_acc[...] += term

    @pl.when((g == last_g) & (piece == 0))
    def _():
        dh_ref[low_rows, :] = term_acc[...]

    @pl.when((g == last_g) & (piece > 0))
    def _():
        terms[piece, low_rows, :] = term_acc[...].astype(BF)

    for t in range(1, wide):
        @pl.when((g == last_g) & (unit == 2 * t - 1))
        def _():
            back.go(t)

    @pl.when((unit == last_unit) & (g == last_g))
    def _():
        keep = pltpu.make_async_copy(results, res_out, keep_sem.at[1])
        keep.start()
        back.finish()
        tall = min(32, own)

        @pl.loop(0, own // tall)
        def _(b):
            at = pl.ds(pl.multiple_of(b * tall, tall), tall)
            dh_ref[at, :] = back.total(dh_ref[at, :], at)

        chain.finish()
        parts.sent()
        keep.wait()


def backward_call(plan, db, qe, kx, vx, o, w_o, w_qkv, cos, sin, res, heads):
    kv_heads, total, _ = kx.shape
    _, own, d = db.shape
    wide, rows, cw = plan.wide, plan.rows, plan.cw
    qw = o.shape[2]
    pairs = kv_heads * heads * total * rows // 2
    fixed = lambda a: pl.BlockSpec(a.shape, lambda u, g: (0,) * a.ndim, pipeline_mode=pl.Buffered(1))
    hbm = pl.BlockSpec(memory_space=pl.ANY)
    given = [db, qe, kx, vx, o, w_o, w_qkv, cos, sin]
    outs = [
        jax.ShapeDtypeStruct((rows, qw), BF),
        jax.ShapeDtypeStruct((kv_heads, total, 128), F32),
        jax.ShapeDtypeStruct((own, d), F32),
    ]
    slots = (wide, plan.group, cw, d // (plan.group // 2))
    buffer = pltpu.VMEM((wide, own, d), BF)
    sems = pltpu.SemaphoreType.DMA((wide,))
    return pl.pallas_call(
        functools.partial(backward_kernel, plan, kv_heads, heads),
        grid=(2 * wide, kv_heads),
        in_specs=[fixed(a) for a in given[:6]]
        + [pl.BlockSpec((d, qw), lambda u, g: (0, 0), pipeline_mode=pl.Buffered(1)), fixed(cos), fixed(sin), fixed(res)],
        out_specs=[fixed(a) for a in outs] + [hbm],
        out_shape=outs + [jax.ShapeDtypeStruct(slots, BF)],
        scratch_shapes=[buffer] * 3 + [pltpu.VMEM((cw, d), F32), pltpu.VMEM(slots, BF)]
        + [pltpu.SemaphoreType.DMA((plan.group,))] * 2 + [pltpu.SemaphoreType.DMA((2,))] + [sems] * 8,
        cost_estimate=pl.CostEstimate(
            flops=36 * pairs * HD, bytes_accessed=12 * kv_heads * total * 128, transcendentals=pairs
        ),
        compiler_params=pltpu.CompilerParams(
            vmem_limit_bytes=60 << 20, collective_id=3, has_side_effects=True
        ),
        name="attention_backward",
    )(*given, res)


def tail_kernel(
    plan, kv_heads, sums_ref, h_hbm, dh_ref, gain2_ref, dx2_ref, x_ref, gain_ref, wkv_hbm,
    cos_ref, sin_ref, dq_ref, o_ref, db_hbm, got_out, gain_out, kv_out, q_out, o_out,
    h_ref, wkv_ref, db_buf, swap_out, swap_in, low, near_in, dkv, head_in, dh_acc, dx_low, every,
    gain_part, gain_in, gain_sum, gain_all,
    swap_sem, near_send, near_recv, head_send, head_recv, part_send, part_recv,
    gain_send, gain_recv, gain2_send, gain2_recv, own_sem, *more
):
    group, wide, chunk, cw, own = plan.group, plan.wide, plan.chunk, plan.cw, plan.own
    narrow = group // 2
    part = dx_low.shape[1] // narrow
    team = Group(plan)
    seq, me, z = team.seq, team.me, lax.axis_index("wide")
    device, member = team.device, team.member
    dx_chain = Chain(plan, every, more[:4])
    q_sum = WeightSum(team, *more[4:9], q_out, *more[9:11])
    kv_sum = WeightSum(team, *more[11:16], kv_out, *more[16:18])
    o_sum = WeightSum(team, *more[18:23], o_out, *more[23:25])
    q_part, kv_part, o_part = q_sum.part, kv_sum.part, o_sum.part

    greet([member(k) for k in range(1, group)] + [along_wide(plan, r) for r in range(1, wide)])

    def place(owner_seq, half, n):
        quarter = owner_seq if half == 0 else 3 - owner_seq
        return pl.ds(
            pl.multiple_of((quarter * narrow + (n if half == 0 else narrow - 1 - n)) * chunk, chunk), chunk
        )

    load_h = pltpu.make_async_copy(h_hbm, h_ref, own_sem.at[2])
    load_w = pltpu.make_async_copy(wkv_hbm, wkv_ref, own_sem.at[3])
    load_h.start()
    load_w.start()

    def swap(g):
        return push(swap_out.at[g], swap_in.at[g], swap_sem.at[0, g], swap_sem.at[1, g], team.sibling)

    def near(k, g):
        other = team.beside(k)
        return push(low.at[g, other], near_in.at[g, k], near_send.at[g, k], near_recv.at[g, k], {"narrow": other})

    def heads_to(r, g):
        columns = slice(g * 128, (g + 1) * 128)
        mine = dkv.at[r * own : (r + 1) * own, columns]
        return push(mine, head_in.at[r, :, columns], head_send.at[r, g], head_recv.at[r, g], along_wide(plan, r))

    for g in range(kv_heads):
        @pl.loop(0, narrow)
        def _(n):
            for half in range(2):
                swap_out[g, n, half] = sums_ref[g, place(1 - seq, half, n), :].astype(BF)

        swap(g).start()

    load_h.wait()
    for n in range(narrow):
        columns = slice(n * part, (n + 1) * part)
        q_part[n] = lax.dot_general(h_ref[:, columns], dq_ref[...], TN, preferred_element_type=F32).astype(BF)
    q_sum.first()

    for g in range(kv_heads):
        swap(g).wait_recv()

        @pl.loop(0, narrow)
        def _(n):
            for half in range(2):
                total = sums_ref[g, place(seq, half, n), :] + swap_in[g, n, half].astype(F32)
                low[g, n, half] = total.astype(BF)

        for k in range(1, narrow):
            near(k, g).start()

    lane = lax.broadcasted_iota(jnp.int32, (cw, 128), 1)
    for g in range(kv_heads):
        for k in range(1, narrow):
            near(k, g).wait_recv()
        for r in range(wide):
            at = pl.ds(pl.multiple_of(lax.rem(z + r, wide) * cw, cw), cw)
            for half in range(2):
                rows = slice((2 * r + half) * cw, (2 * r + half + 1) * cw)
                total = low[g, me, half, at, :].astype(F32)
                for k in range(1, narrow):
                    total = total + near_in[g, k, half, at, :].astype(F32)
                back = total * cos_ref[rows, :] + turn(total, -1.0) * sin_ref[rows, :]
                dkv[rows, g * 128 : (g + 1) * 128] = jnp.where(lane < HD, back, total).astype(BF)
        for r in range(1, wide):
            heads_to(r, g).start()

    q_sum.second()

    for n in range(narrow):
        columns = slice(n * part, (n + 1) * part)
        kv_part[n] = lax.dot_general(dkv[...], h_ref[:, columns], TN, preferred_element_type=F32).astype(BF)
    kv_sum.first()

    tile = part // 2
    load_w.wait()
    for r in range(wide):
        if r > 0:
            for g in range(kv_heads):
                heads_to(r, g).wait_recv()
        mine = dkv[0:own] if r == 0 else head_in[r]
        source = lax.rem(z - r + wide, wide)

        for b in range(group):
            at = slice(b * tile, (b + 1) * tile)
            more = lax.dot_general(mine, wkv_ref[b, source], NT, preferred_element_type=F32)
            dh_acc[:, at] = (dh_ref[:, at] if r == 0 else dh_acc[:, at]) + more

    gain_part[0:1, :] = jnp.zeros_like(gain2_ref[...])
    gain_part[1:2, :] = gain2_ref[...]
    tall = min(32, own)

    @pl.loop(0, own // tall)
    def _(b):
        at = pl.ds(pl.multiple_of(b * tall, tall), tall)
        dh1 = dh_acc[at, :]
        x = x_ref[at, :].astype(F32)
        scale = lax.rsqrt(jnp.mean(x * x, axis=1, keepdims=True) + EPS)
        z1 = x * scale
        gain_part[0:1, :] += jnp.sum(dh1 * z1, axis=0, keepdims=True)
        dz1 = dh1 * gain_ref[...]
        inner = jnp.mean(dz1 * z1, axis=1, keepdims=True)
        dx_low[at, :] = (dx2_ref[at, :] + scale * (dz1 - z1 * inner)).astype(BF)

    dx_parts = Parts(plan, team, dx_low, every, part_send, part_recv, own_sem.at[0])
    dx_parts.start()

    def gain_to(k):
        columns = pl.ds(pl.multiple_of(lax.rem(device(k), narrow) * part, part), part)
        return push(gain_part.at[:, columns], gain_in.at[k], gain_send.at[k], gain_recv.at[k], member(k))

    for k in range(1, group):
        gain_to(k).start()
    dx_parts.wait()
    dx_chain.go(1)
    kv_sum.second()

    rows = o_ref.shape[0] * o_ref.shape[1]
    for n in range(narrow):
        load = pltpu.make_async_copy(db_hbm.at[:, :, n * part : (n + 1) * part], db_buf, own_sem.at[4])
        load.start()
        load.wait()
        o_part[n] = lax.dot_general(
            o_ref[...].reshape(rows, -1), db_buf[...].reshape(rows, part), TN, preferred_element_type=F32
        ).astype(BF)
    o_sum.first()
    q_sum.third()

    gain = gain_part[:, pl.ds(pl.multiple_of(me * part, part), part)]
    for k in range(1, group):
        gain_to(k).wait_recv()
        gain = gain + gain_in[k]
    gain_sum[...] = gain

    def gain_on(r):
        return push(gain_sum, gain_all.at[r], gain2_send.at[r], gain2_recv.at[r], along_wide(plan, r))

    for r in range(1, wide):
        gain_on(r).start()
    dx_chain.arrive(1)
    if wide > 2:
        dx_chain.go(2)
    o_sum.second()
    kv_sum.third()
    q_sum.fourth()
    gain = gain_sum[...]
    for r in range(1, wide):
        gain_on(r).wait_recv()
        gain = gain + gain_all[r]
    gain_out[...] = gain
    for h in range(2, wide):
        dx_chain.arrive(h)
        if h + 1 < wide:
            dx_chain.go(h + 1)
        if h == 2:
            o_sum.third()
            kv_sum.fourth()
    o_sum.fourth()
    got_keep = pltpu.make_async_copy(every, got_out, own_sem.at[1])
    got_keep.start()

    dx_chain.finish()
    for g in range(kv_heads):
        swap(g).wait_send()
        for k in range(1, narrow):
            near(k, g).wait_send()
        for r in range(1, wide):
            heads_to(r, g).wait_send()
    for r in range(1, wide):
        gain_on(r).wait_send()
    dx_parts.sent()
    for k in range(1, group):
        gain_to(k).wait_send()
    for one in (q_sum, kv_sum, o_sum):
        one.sent()
    got_keep.wait()


def tail_call(plan, sums, h, dh, gain2, dx2, x, gain, w_kv, cos, sin, dq, o, db):
    kv_heads = sums.shape[0]
    own, d = dh.shape
    group, wide, chunk, cw = plan.group, plan.wide, plan.chunk, plan.cw
    narrow = group // 2
    part = d // narrow
    kv_width = kv_heads * 128
    dma = pltpu.SemaphoreType.DMA
    quarter = pltpu.VMEM((kv_heads, narrow, 2, chunk, 128), BF)
    slots = (wide, group, cw, part)

    def weight(height, across):
        half = pltpu.VMEM((narrow, height // 2, across), BF)
        ends = pltpu.VMEM((2, height // 2, across), BF)
        return [pltpu.VMEM((narrow, height, across), BF), half, half, half, ends] + [dma((narrow + 1,))] * 2

    given = [sums, h, dh, gain2, dx2, x, gain, w_kv, cos, sin, dq, o, db]
    qw = dq.shape[1]
    whole = pl.BlockSpec(memory_space=pltpu.VMEM)
    hbm = pl.BlockSpec(memory_space=pl.ANY)
    return pl.pallas_call(
        functools.partial(tail_kernel, plan, kv_heads),
        in_specs=[hbm if i in (1, 7, 12) else whole for i in range(len(given))],
        out_specs=[hbm] + [whole] * 4,
        out_shape=[
            jax.ShapeDtypeStruct(slots, BF),
            jax.ShapeDtypeStruct((2, part), F32),
            jax.ShapeDtypeStruct((kv_width, part), F32),
            jax.ShapeDtypeStruct((part, qw), F32),
            jax.ShapeDtypeStruct((qw, part), F32),
        ],
        scratch_shapes=[
            pltpu.VMEM(h.shape, BF), pltpu.VMEM(w_kv.shape, BF), pltpu.VMEM((wide, own, part), BF),
            quarter, quarter, quarter, quarter,
            pltpu.VMEM((plan.rows, kv_width), BF),
            pltpu.VMEM((wide, own, kv_width), BF),
            pltpu.VMEM((own, d), F32),
            pltpu.VMEM((own, d), BF),
            pltpu.VMEM(slots, BF),
            pltpu.VMEM((2, d), F32),
            pltpu.VMEM((group, 2, part), F32),
            pltpu.VMEM((2, part), F32),
            pltpu.VMEM((wide, 2, part), F32),
            dma((2, kv_heads)), dma((kv_heads, narrow)), dma((kv_heads, narrow)),
            dma((wide, kv_heads)), dma((wide, kv_heads)), dma((group,)), dma((group,)),
            dma((group,)), dma((group,)), dma((wide,)), dma((wide,)),
            dma((5,)),
        ] + [dma((wide,))] * 4 + weight(part, qw) + weight(kv_width, part) + weight(qw, part),
        cost_estimate=pl.CostEstimate(
            flops=200 * own * d * wide * kv_width, bytes_accessed=4 * sums.size, transcendentals=0
        ),
        compiler_params=pltpu.CompilerParams(
            vmem_limit_bytes=60 << 20, collective_id=2, has_side_effects=True
        ),
        name="input_gradient",
    )(*given)


def assemble_kernel(plan, s_ref, in_ref, out_ref):
    group = plan.group
    for l in range(group):
        owner = jnp.where(s_ref[0] >= group // 2, group - 1 - l, l)
        out_ref[l, 0] = in_ref[0, owner].astype(out_ref.dtype)


def assemble_call(plan, scalars, values, dtype):
    wide, group, cw, part = values.shape
    out = pl.pallas_call(
        functools.partial(assemble_kernel, plan),
        grid_spec=pltpu.PrefetchScalarGridSpec(
            num_scalar_prefetch=1,
            grid=(wide,),
            in_specs=[pl.BlockSpec((1, group, cw, part), lambda w, s: (w, 0, 0, 0))],
            out_specs=[pl.BlockSpec((group, 1, cw, part), lambda w, s: (0, w, 0, 0))],
        ),
        out_shape=[jax.ShapeDtypeStruct((group, wide, cw, part), dtype)],
        cost_estimate=pl.CostEstimate(flops=values.size, bytes_accessed=6 * values.size, transcendentals=0),
        compiler_params=pltpu.CompilerParams(vmem_limit_bytes=40 << 20),
        name="assemble",
    )(scalars, values)[0]
    return out.reshape(group * wide * cw, part)


def half_of(weight, seq_index, seq_count):
    part = weight.shape[0] // seq_count
    return lax.dynamic_slice_in_dim(weight, seq_index * part, part, 0)


def body(
    tokens, attn_gain, w_query, w_key, w_value, w_out, ffn_gain, w_gate, w_up, w_down,
    segment_ids, token_mask, out_grad,
):
    seq_count = lax.axis_size("seq")
    narrow = lax.axis_size("narrow")
    wide = lax.axis_size("wide")
    group = seq_count * narrow
    seq_index = lax.axis_index("seq")
    narrow_index = lax.axis_index("narrow")
    wide_index = lax.axis_index("wide")
    index = seq_index * narrow + narrow_index
    total = segment_ids.shape[0]
    plan = Plan(total, group, wide)
    chunk, cw, rows, own = plan.chunk, plan.cw, plan.rows, plan.own
    d_part = tokens.shape[1]
    d = d_part * narrow
    qw = w_query.shape[1]
    kw = w_key.shape[1]
    kv_heads = kw // HD
    heads = qw // kw
    ff = w_gate.shape[1]

    start_one = jnp.sum((segment_ids < 1).astype(jnp.int32))
    start_two = jnp.sum((segment_ids < 2).astype(jnp.int32))
    starts = jnp.stack([start_one, start_two])
    scalars = jnp.reshape(index, (1,)).astype(jnp.int32)

    def gather_weight(weight):
        return lax.all_gather(half_of(weight, seq_index, seq_count), NS, axis=0, tiled=True)

    def scatter_grad(grad, *others):
        mine = after(lax.psum_scatter(grad.astype(BF), NS, scatter_dimension=0, tiled=True), *others)
        return lax.all_gather(mine, "seq", axis=0, tiled=True).astype(F32)

    def after(values, *others):
        return lax.optimization_barrier((values, *others))[0]

    w_kv = jnp.concatenate(
        [w_key.reshape(d_part, kv_heads, 1, HD), w_value.reshape(d_part, kv_heads, 1, HD)], axis=2
    ).reshape(d_part, 2 * kw)

    row = jnp.arange(rows, dtype=jnp.int32)
    row_chunk = jnp.where((row // cw) % 2 == 1, 2 * group - 1 - index, index)
    row_block = (row // own + wide_index) % wide
    row_token = row_chunk * chunk + row_block * cw + row % cw
    row_start = jnp.where(row_token >= start_two, start_two, jnp.where(row_token >= start_one, start_one, 0))
    row_pos = (row_token - row_start).astype(F32)
    frequency = THETA ** (-2.0 * jnp.arange(HD // 2, dtype=F32) / HD)
    angles = row_pos[:, None] * jnp.tile(frequency, 4)[None, :]
    cos, sin = jnp.cos(angles), jnp.sin(angles)

    feature = jnp.arange(16, dtype=jnp.int32)[:, None]
    closed = (segment_ids[None, :] != feature) | (token_mask[None, :] != 1)
    marks = jnp.where((feature < 3) & closed, NEG, jnp.where((feature >= 3) & (feature < 6), 1.0, 0.0)).astype(BF)

    mask = lax.dynamic_slice_in_dim(token_mask, seq_index * (group * chunk), group * chunk, 0)
    g_part = lax.dynamic_index_in_dim(out_grad.reshape(group, wide, cw, d_part), wide_index, 1, keepdims=False)
    mask = lax.dynamic_index_in_dim(mask.reshape(group, wide, cw), wide_index, 1, keepdims=False)
    g_part = jnp.where(mask[:, :, None] == 1, g_part, jnp.zeros_like(g_part))

    w_o = gather_weight(w_out)
    h_one, q, x_low, kx, vx, w_qkv, gains, g_rows, w_kv = head_call(
        plan, tokens.reshape(group, wide, cw, d_part), g_part, jnp.concatenate([w_query, w_kv], axis=1),
        jnp.stack([attn_gain, ffn_gain]), cos, sin, marks, qw, kv_heads
    )
    gains = jnp.transpose(gains, (1, 0, 2)).reshape(2, d)
    gain_one, gain_two = gains[0:1], gains[1:2]
    g_rows = g_rows.reshape(rows, d)

    w_gu = gather_weight(after(jnp.concatenate([w_gate, w_up], axis=1), q))
    o, qe, x2, w_dn = forward_call(plan, starts, q, kx, vx, w_o, x_low, w_down, heads)
    w_kv = jnp.transpose(w_kv.reshape(wide, seq_count, d_part // seq_count, 2 * kw), (1, 0, 2, 3))
    w_kv = lax.dynamic_index_in_dim(w_kv, seq_index, 0, keepdims=False).reshape(-1, 2 * kw)
    w_kv = lax.all_gather(after(w_kv, o, w_gu), NS, axis=0, tiled=True)
    w_kv = w_kv.reshape(group, wide, d_part // seq_count, 2 * kw)

    d_gate, d_up, h_all, down, dx2, grad_gain_two, grad_dn = ffn_call(plan, x2, gain_two, g_rows, w_gu, w_dn)

    h_all = after(h_all, w_kv)
    grad_gate, grad_up, db, result = weights_call(plan, dx2, h_all, d_gate, d_up, down, x2)
    dq, sums, dh1, result = backward_call(plan, db, qe, kx, vx, o, w_o, w_qkv, cos, sin, result, heads)

    input_grad, gain_grads, grad_kv, grad_q, grad_o = tail_call(
        plan, sums, h_one, dh1, grad_gain_two, dx2, x_low, gain_one, w_kv, cos, sin, dq, o, db
    )
    result = assemble_call(plan, scalars, result, BF)
    input_grad = assemble_call(plan, scalars, input_grad, F32)

    grad_dn = scatter_grad(grad_dn.reshape(narrow * ff, d_part), dq)
    grad_gate = scatter_grad(grad_gate, dq)
    grad_up = scatter_grad(grad_up, dq)
    grad_kv = jnp.transpose(grad_kv.reshape(kv_heads, 2, HD, d_part), (3, 0, 1, 2))
    return (
        result,
        input_grad,
        gain_grads[0],
        grad_q,
        grad_kv[:, :, 0].reshape(d_part, kw),
        grad_kv[:, :, 1].reshape(d_part, kw),
        grad_o,
        gain_grads[1],
        grad_gate,
        grad_up,
        grad_dn,
    )


def solution(mesh):
    width_in, width_out = P("narrow", "wide"), P("wide", "narrow")
    acts = P("seq", "narrow")
    return jax.shard_map(
        body,
        mesh=mesh,
        in_specs=(
            acts, P("narrow"), width_in, width_in, width_in, width_out, P("narrow"),
            width_in, width_in, width_out, P(), P(), acts,
        ),
        out_specs=(
            acts, acts, P("narrow"), width_in, width_in, width_in, width_out, P("narrow"),
            width_in, width_in, width_out,
        ),
        check_vma=False,
    )
```

```python
import functools

import jax
import jax.numpy as jnp
from jax import lax
from jax.experimental import pallas as pl
from jax.experimental.pallas import tpu as pltpu
from jax.sharding import PartitionSpec as P

HD = 64
EPS = 1e-05
THETA = 500000.0
NEG = -1e30
SN = ("seq", "narrow")
NS = ("narrow", "seq")
BF = jnp.bfloat16
F32 = jnp.float32
NT = (((1,), (1,)), ((), ()))
TN = (((0,), (0,)), ((), ()))


def pieces_of(value):
    first = value.astype(BF).astype(F32)
    second = (value - first).astype(BF).astype(F32)
    third = (value - first - second).astype(BF).astype(F32)
    return first, second, third


class Plan:
    def __init__(self, total, group, wide):
        self.total, self.group, self.wide = total, group, wide
        self.chunk = total // (2 * group)
        self.cw = self.chunk // wide
        self.rows = 2 * self.chunk
        self.own = 2 * self.cw


def near_of(plan, z, p):
    side = jnp.minimum(z, plan.wide - 1 - z)
    both = jnp.where(lax.rem(p, 2) == 1, z + (p + 1) // 2, z - p // 2)
    one = jnp.where(z <= plan.wide - 1 - z, z + p - side, z - p + side)
    return jnp.where(p <= 2 * side, both, one)


def turn(values, sign):
    width = values.shape[1]
    lane = lax.broadcasted_iota(jnp.int32, values.shape, 1)
    left, right = pltpu.roll(values, width - HD // 2, 1), pltpu.roll(values, HD // 2, 1)
    return jnp.where(lane % HD < HD // 2, -sign * left, sign * right)


def widen(table, width):
    return jnp.concatenate([table] * (width // 128), axis=1) if width > 128 else table


MESH = pl.DeviceIdType.MESH


def greet(partners):
    barrier = pltpu.get_barrier_semaphore()
    for partner in partners:
        pl.semaphore_signal(barrier, inc=1, device_id=partner, device_id_type=MESH)
    pl.semaphore_wait(barrier, len(partners))


def along_wide(plan, r):
    return {"wide": lax.rem(lax.axis_index("wide") + r + plan.wide, plan.wide)}


def push(src, dst, send, recv, device):
    return pltpu.make_async_remote_copy(
        src_ref=src, dst_ref=dst, send_sem=send, recv_sem=recv, device_id=device, device_id_type=MESH
    )


class Chain:
    def __init__(self, plan, buf, sems):
        self.wide, self.buf, self.sems = plan.wide, buf, sems
        self.z = lax.axis_index("wide")

    def copy(self, slot, h, way):
        send, recv = (self.sems[0], self.sems[1]) if way > 0 else (self.sems[2], self.sems[3])
        return push(self.buf.at[slot], self.buf.at[slot], send.at[h], recv.at[h], {"wide": self.z + way})

    def sends(self, h, way):
        z, last = self.z, self.wide - 1
        return (z >= h - 1) & (z < last) if way > 0 else (z + h - 1 <= last) & (z > 0)

    def go(self, h):
        for way in (1, -1):
            @pl.when(self.sends(h, way))
            def _():
                self.copy(self.z - way * (h - 1), h, way).start()

    def arrive(self, h):
        for way in (1, -1):
            @pl.when(self.z >= h if way > 0 else self.z + h <= self.wide - 1)
            def _():
                slot = self.z - way * h
                send, recv = (self.sems[0], self.sems[1]) if way > 0 else (self.sems[2], self.sems[3])
                push(self.buf.at[slot], self.buf.at[slot], send.at[h], recv.at[h], {"wide": slot}).wait_recv()

    def finish(self):
        for h in range(1, self.wide):
            for way in (1, -1):
                @pl.when(self.sends(h, way))
                def _():
                    self.copy(self.z - way * (h - 1), h, way).wait_send()


class Group:
    def __init__(self, plan):
        self.size, self.narrow = plan.group, plan.group // 2
        self.seq, self.me = lax.axis_index("seq"), lax.axis_index("narrow")
        self.index = self.seq * self.narrow + self.me
        self.sibling = {"seq": 1 - self.seq}

    def device(self, k):
        return lax.rem(self.index + k + self.size, self.size)

    def member(self, k):
        return {"seq": self.device(k) // self.narrow, "narrow": lax.rem(self.device(k), self.narrow)}

    def beside(self, k):
        return lax.rem(self.me + k + self.narrow, self.narrow)


class Parts:
    def __init__(self, plan, team, ref, slots, send, recv, stay):
        self.plan, self.team, self.ref, self.send, self.recv = plan, team, ref, send, recv
        self.slots = slots.at[lax.axis_index("wide")]
        self.part = ref.shape[1] // team.narrow
        self.stay = pltpu.make_async_copy(self.slab(team.index), self.slots.at[team.index], stay)

    def slab(self, other):
        cw, narrow, part = self.plan.cw, self.team.narrow, self.part
        rows = pl.ds(pl.multiple_of((other // narrow) * cw, cw), cw)
        return self.ref.at[rows, pl.ds(pl.multiple_of(lax.rem(other, narrow) * part, part), part)]

    def to(self, k):
        team = self.team
        src = self.slab(team.device(k))
        return push(src, self.slots.at[team.index], self.send.at[k], self.recv.at[k], team.member(k))

    def start(self):
        for k in range(1, self.team.size):
            self.to(k).start()
        self.stay.start()

    def wait(self):
        team = self.team
        self.stay.wait()
        for k in range(1, team.size):
            src = self.slab(team.index)
            push(src, self.slots.at[team.device(-k)], self.send.at[k], self.recv.at[k], team.member(k)).wait_recv()

    def sent(self):
        for k in range(1, self.team.size):
            self.to(k).wait_send()


class Sums:
    def __init__(self, plan, terms, right, left, sems):
        self.wide, self.terms, self.sums, self.sems = plan.wide, terms, (right, left), sems
        self.z = lax.axis_index("wide")
        self.side = jnp.minimum(self.z, plan.wide - 1 - self.z)

    def term(self, h, way):
        return jnp.where(h <= self.side, 2 * h - 1 if way > 0 else 2 * h, self.side + h)

    def sends(self, t, way):
        h = self.wide - t
        return self.z + h <= self.wide - 1 if way > 0 else self.z >= h

    def first(self, way):
        return self.z == (0 if way > 0 else self.wide - 1)

    def copy(self, src, t, way):
        buf = self.sums[0 if way > 0 else 1]
        send, recv = self.sems[:2] if way > 0 else self.sems[2:]
        return push(src, buf.at[t], send.at[t], recv.at[t], {"wide": self.z + way})

    def came(self, t, way):
        buf = self.sums[0 if way > 0 else 1]
        send, recv = self.sems[:2] if way > 0 else self.sems[2:]
        push(buf.at[t], buf.at[t], send.at[t], recv.at[t], {"wide": self.z - way}).wait_recv()

    def go(self, t):
        for way in (1, -1):
            term = self.term(self.wide - t, way)

            @pl.when(self.sends(t, way) & self.first(way))
            def _():
                self.copy(self.terms.at[term], t, way).start()

            if t > 1:
                @pl.when(self.sends(t, way) & jnp.logical_not(self.first(way)))
                def _():
                    self.came(t - 1, way)
                    buf = self.sums[0 if way > 0 else 1]
                    tall = min(32, buf.shape[1])

                    @pl.loop(0, buf.shape[1] // tall)
                    def _(b):
                        at = pl.ds(pl.multiple_of(b * tall, tall), tall)
                        total = buf[t - 1, at, :].astype(F32) + self.terms[term, at, :].astype(F32)
                        buf[t - 1, at, :] = total.astype(BF)

                    self.copy(buf.at[t - 1], t, way).start()

    def finish(self):
        for way in (1, -1):
            @pl.when(jnp.logical_not(self.first(way)))
            def _():
                self.came(self.wide - 1, way)

        for t in range(1, self.wide):
            for way in (1, -1):
                @pl.when(self.sends(t, way))
                def _():
                    self.copy(self.terms.at[0], t, way).wait_send()

    def total(self, own, at):
        out = own
        for way in (1, -1):
            sums = self.sums[0 if way > 0 else 1][self.wide - 1, at, :].astype(F32)
            out = out + jnp.where(self.first(way), 0.0, sums)
        return out


class WeightSum:
    def __init__(self, team, part, came, mine, near, last, out, send, recv):
        self.team, self.part, self.came, self.mine, self.near = team, part, came, mine, near
        self.last, self.out, self.send, self.recv = last, out, send, recv
        self.size = part.shape[1] // 2

    def half(self, core):
        return pl.ds(pl.multiple_of(core * self.size, self.size), self.size)

    def swap(self):
        other = self.part.at[:, self.half(1 - self.team.seq)]
        return push(other, self.came, self.send.at[0], self.recv.at[0], self.team.sibling)

    def give(self, k):
        other = self.team.beside(k)
        return push(self.mine.at[other], self.near.at[k], self.send.at[k], self.recv.at[k], {"narrow": other})

    def back(self):
        at = self.team.narrow
        return push(self.last.at[0], self.last.at[1], self.send.at[at], self.recv.at[at], self.team.sibling)

    def first(self):
        self.swap().start()

    def second(self):
        self.swap().wait_recv()
        for n in range(self.team.narrow):
            own = self.part[n, self.half(self.team.seq), :].astype(F32)
            self.mine[n] = (own + self.came[n].astype(F32)).astype(BF)
        for k in range(1, self.team.narrow):
            self.give(k).start()

    def third(self):
        total = self.mine[self.team.me].astype(F32)
        for k in range(1, self.team.narrow):
            self.give(k).wait_recv()
            total = total + self.near[k].astype(F32)
        self.last[0] = total.astype(BF)
        self.back().start()
        self.out[self.half(self.team.seq), :] = self.last[0].astype(F32)

    def fourth(self):
        self.back().wait_recv()
        self.out[self.half(1 - self.team.seq), :] = self.last[1].astype(F32)

    def sent(self):
        self.swap().wait_send()
        self.back().wait_send()
        for k in range(1, self.team.narrow):
            self.give(k).wait_send()


def head_kernel(
    plan, kv_heads, qw, x_ref, g_ref, w_ref, gains_ref, cos_ref, sin_ref, marks_ref, wg_ref, wu_ref,
    h_out, q_out, own_out, kx, vx, w_out, gains_out, g_out, side_out, gu_out,
    x_buf, marks, side_buf, side_send, side_recv, w_buf, kv_buf, g_buf, gain_buf,
    x_send, x_recv, x_stay, w_send, w_recv, w_on_send, w_on_recv, gain_send, gain_recv,
    g_send, g_recv, kv_send, kv_recv, kv_on_send, kv_on_recv, keep_sem, cut_sem, *chain_sems
):
    group, wide, chunk, cw, own = plan.group, plan.wide, plan.chunk, plan.cw, plan.own
    team = Group(plan)
    narrow, seq, me = team.narrow, team.seq, team.me
    z = lax.axis_index("wide")
    part = x_ref.shape[3]
    d = part * narrow
    width = w_ref.shape[1]
    fold = part // 2
    chain = Chain(plan, g_buf, chain_sems)
    greet([team.member(k) for k in range(1, group)] + [along_wide(plan, r) for r in range(1, wide)])

    def spot(ref, slot, source):
        rows = pl.ds(pl.multiple_of((source // narrow) * cw, cw), cw)
        return ref.at[slot, rows, pl.ds(pl.multiple_of(lax.rem(source, narrow) * part, part), part)]

    def chunk_for(device):
        return jnp.where(seq == 0, device, group - 1 - device)

    def x_to(r, k):
        src = x_ref.at[chunk_for(team.device(k)), lax.rem(z + r, wide)]
        return push(src, spot(x_buf, r, team.index), x_send.at[r, k], x_recv.at[r, k], team.member(k))

    def x_from(r, k):
        src = x_ref.at[0, 0]
        return push(src, spot(x_buf, r, team.device(-k)), x_send.at[r, k], x_recv.at[r, k], team.member(k))

    def x_own(r):
        src = x_ref.at[chunk_for(team.index), lax.rem(z + r, wide)]
        return pltpu.make_async_copy(src, spot(x_buf, r, team.index), x_stay.at[r])

    def x_start(r):
        for k in range(1, group):
            x_to(r, k).start()
        x_own(r).start()

    def g_to(k):
        src = g_ref.at[chunk_for(team.device(k))]
        return push(src, spot(g_buf, z, team.index), g_send.at[k], g_recv.at[k], team.member(k))

    def w_rows(n, core):
        return w_buf.at[pl.ds(pl.multiple_of(n * part + core * fold, fold), fold)]

    def w_to(k):
        src = w_ref.at[pl.ds(pl.multiple_of(seq * fold, fold), fold)]
        return push(src, w_rows(me, seq), w_send.at[k], w_recv.at[k], {"narrow": team.beside(k)})

    def w_from(k):
        n = team.beside(-k)
        return push(w_rows(n, seq), w_rows(n, seq), w_send.at[k], w_recv.at[k], {"narrow": n})

    def w_on(k, core):
        n = team.beside(-k)
        return push(w_rows(n, core), w_rows(n, core), w_on_send.at[k], w_on_recv.at[k], team.sibling)

    def side_to(r, slot):
        mine = w_ref.at[:, qw:]
        return push(mine, side_buf.at[slot], side_send.at[r], side_recv.at[r], along_wide(plan, r))

    def gain_to(k, slot):
        return push(gains_ref, gain_buf.at[slot], gain_send.at[k], gain_recv.at[k], {"narrow": team.beside(k)})

    for k in range(1, group):
        g_to(k).start()
    g_stay = pltpu.make_async_copy(g_ref.at[chunk_for(team.index)], spot(g_buf, z, team.index), keep_sem.at[0])
    g_stay.start()
    for k in range(1, narrow):
        w_to(k).start()
        gain_to(k, me).start()
    x_start(0)
    if wide > 1:
        x_start(1)
    for r in range(1, wide):
        side_to(r, z).start()
    side_buf[z] = w_ref[:, qw:]
    w_buf[pl.ds(pl.multiple_of(me * part, part), part), :] = w_ref[...]
    gain_buf[me] = gains_ref[...]
    for k in range(1, narrow):
        w_from(k).wait_recv()
        w_on(k, seq).start()
    g_stay.wait()
    for k in range(1, group):
        push(
            g_ref.at[0], spot(g_buf, z, team.device(-k)), g_send.at[k], g_recv.at[k], team.member(k)
        ).wait_recv()
    chain.go(1)
    for k in range(1, narrow):
        gain_to(k, team.beside(-k)).wait_recv()
        w_on(k, 1 - seq).wait_recv()
    gain_one = jnp.concatenate([gain_buf[n, 0:1] for n in range(narrow)], axis=1)
    gains_out[...] = gain_buf[...]
    w_keep = pltpu.make_async_copy(w_buf, w_out, keep_sem.at[1])
    w_keep.start()
    ff = wg_ref.shape[1]
    half = pl.ds(pl.multiple_of(seq * fold, fold), fold)
    cuts = [
        pltpu.make_async_copy(wg_ref.at[half], gu_out.at[:, 0:ff], cut_sem.at[0]),
        pltpu.make_async_copy(wu_ref.at[half], gu_out.at[:, ff : 2 * ff], cut_sem.at[1]),
    ]
    for copy in cuts:
        copy.start()

    def kv_rows(core, n, r):
        return kv_buf.at[core, n, pl.ds(pl.multiple_of(r * own, own), own)]

    def kv_to(r, k):
        mine = kv_rows(seq, me, r)
        return push(mine, mine, kv_send.at[r, k], kv_recv.at[r, k], {"narrow": team.beside(k)})

    def kv_from(r, k):
        theirs = kv_rows(seq, team.beside(-k), r)
        return push(theirs, theirs, kv_send.at[r, k], kv_recv.at[r, k], {"narrow": team.beside(k)})

    def kv_on(k, core):
        slot = kv_buf.at[core, team.beside(-k)]
        return push(slot, slot, kv_on_send.at[k], kv_on_recv.at[k], team.sibling)

    @pl.loop(0, wide)
    def _(r):
        x_own(r).wait()
        for k in range(1, group):
            x_from(r, k).wait_recv()
        for later in range(2, wide):
            @pl.when(r == later - 2)
            def _():
                x_start(later)
        at = pl.ds(pl.multiple_of(r * own, own), own)
        low = x_buf[r]
        x = low.astype(F32)
        mean = jnp.mean(x * x, axis=1, keepdims=True)
        h = (x * lax.rsqrt(mean + EPS) * gain_one).astype(BF)
        h_out[at, :] = h
        t = jnp.dot(h, w_buf[...], preferred_element_type=F32)
        lane = lax.broadcasted_iota(jnp.int32, t.shape, 1)
        plain = (lane >= qw) & (lane % 128 >= HD)
        out = t * widen(cos_ref[at, :], width) + turn(t, 1.0) * widen(sin_ref[at, :], width)
        out = jnp.where(plain, t, out)
        q_out[at, :] = (out[:, :qw] * (HD ** -0.5)).astype(BF)
        kv_buf[seq, me, at, :] = out[:, qw:].astype(BF)
        for k in range(1, narrow):
            kv_to(r, k).start()

        @pl.when(r == min(1, wide - 1))
        def _():
            chain.arrive(1)
            if wide > 2:
                chain.go(2)

    kv_on(0, seq).start()
    own_out[...] = x_buf[0]
    if wide > 2:
        chain.arrive(2)
    if wide > 3:
        chain.go(3)
    for k in range(1, narrow):
        for r in range(wide):
            kv_from(r, k).wait_recv()
        kv_on(k, seq).start()
    for k in range(narrow):
        kv_on(k, 1 - seq).wait_recv()

    feature = lax.broadcasted_iota(jnp.int32, (cw, 128), 1)
    ones = jnp.where(feature < 3, 1.0, 0.0).astype(BF)
    spread = lax.broadcasted_iota(jnp.int32, (marks_ref.shape[0], 128), 0) + HD
    target = lax.broadcasted_iota(jnp.int32, (marks_ref.shape[0], 128), 1)
    spread = jnp.where(spread == target, 1.0, 0.0).astype(BF)

    @pl.loop(0, 2 * group)
    def _(c):
        columns = pl.ds(pl.multiple_of(c * chunk, chunk), chunk)
        marks[...] = lax.dot_general(marks_ref[:, columns], spread, TN, preferred_element_type=F32).astype(BF)
        late = c >= group
        owner = jnp.where(late, 2 * group - 1 - c, c)
        for r in range(wide):
            block = pl.ds(pl.multiple_of(lax.rem(z + r, wide) * cw, cw), cw)
            at = pl.ds(pl.multiple_of(c * chunk + lax.rem(z + r, wide) * cw, cw), cw)
            source = pl.ds(pl.multiple_of(r * own + jnp.where(late, cw, 0), cw), cw)
            for g in range(kv_heads):
                kv = kv_buf[owner // narrow, lax.rem(owner, narrow), source, g * 128 : (g + 1) * 128]
                kx[g, at, :] = jnp.where(feature < HD, kv, marks[block, :])
                vx[g, at, :] = jnp.where(feature < HD, ones, kv)

    for h in range(3, wide):
        chain.arrive(h)
        if h + 1 < wide:
            chain.go(h + 1)
    for r in range(1, wide):
        side_to(r, lax.rem(z - r + wide, wide)).wait_recv()
        side_to(r, z).wait_send()
    side_out[...] = side_buf[...]
    keep = [
        pltpu.make_async_copy(g_buf.at[near_of(plan, z, p)], g_out.at[p], keep_sem.at[2 + p]) for p in range(wide)
    ]
    for copy in keep:
        copy.start()
    chain.finish()
    for k in range(1, narrow):
        w_to(k).wait_send()
        w_on(k, seq).wait_send()
        gain_to(k, me).wait_send()
        for r in range(wide):
            kv_to(r, k).wait_send()
    for k in range(narrow):
        kv_on(k, seq).wait_send()
    for k in range(1, group):
        g_to(k).wait_send()
        for r in range(wide):
            x_to(r, k).wait_send()
    w_keep.wait()
    for copy in keep + cuts:
        copy.wait()


def head_call(plan, x, g, w, gains, cos, sin, marks, w_gate, w_up, qw, kv_heads):
    group, wide, cw, part = x.shape
    narrow = group // 2
    d = part * narrow
    width = w.shape[1]
    rows, own, total = plan.rows, plan.own, plan.total
    dma = pltpu.SemaphoreType.DMA
    whole = pl.BlockSpec(memory_space=pltpu.VMEM)
    hbm = pl.BlockSpec(memory_space=pl.ANY)
    keys = jax.ShapeDtypeStruct((kv_heads, total, 128), BF)
    return pl.pallas_call(
        functools.partial(head_kernel, plan, kv_heads, qw),
        in_specs=[hbm, hbm] + [whole] * 5 + [hbm, hbm],
        out_specs=[whole] * 5 + [hbm, whole, hbm, whole, hbm],
        out_shape=[
            jax.ShapeDtypeStruct((rows, d), BF),
            jax.ShapeDtypeStruct((rows, qw), BF),
            jax.ShapeDtypeStruct((own, d), BF),
            keys,
            keys,
            jax.ShapeDtypeStruct((d, width), BF),
            jax.ShapeDtypeStruct((narrow, 2, part), F32),
            jax.ShapeDtypeStruct((wide, own, d), BF),
            jax.ShapeDtypeStruct((wide, part, width - qw), BF),
            jax.ShapeDtypeStruct((part // 2, 2 * w_gate.shape[1]), BF),
        ],
        scratch_shapes=[
            pltpu.VMEM((wide, own, d), BF),
            pltpu.VMEM((plan.chunk, 128), BF),
            pltpu.VMEM((wide, part, width - qw), BF),
            dma((wide,)), dma((wide,)),
            pltpu.VMEM((d, width), BF),
            pltpu.VMEM((2, narrow, rows, width - qw), BF),
            pltpu.VMEM((wide, own, d), BF),
            pltpu.VMEM((narrow, 2, part), F32),
            dma((wide, group)), dma((wide, group)), dma((wide,)),
            dma((narrow,)), dma((narrow,)), dma((narrow,)), dma((narrow,)), dma((narrow,)), dma((narrow,)),
            dma((group,)), dma((group,)),
            dma((wide, narrow)), dma((wide, narrow)), dma((narrow,)), dma((narrow,)),
            dma((2 + wide,)), dma((2,)),
        ] + [dma((wide,))] * 4,
        cost_estimate=pl.CostEstimate(
            flops=60 * rows * d * width, bytes_accessed=8 * rows * d + 2 * d * width, transcendentals=rows
        ),
        compiler_params=pltpu.CompilerParams(
            vmem_limit_bytes=60 << 20, collective_id=4, has_side_effects=True
        ),
        name="head",
    )(x, g, w, gains, cos, sin, marks, w_gate, w_up)


def split_heads(block, heads, low):
    tiles = []
    for h in range(heads):
        tile = block[:, (h // 2) * 128 : (h // 2 + 1) * 128]
        if (h % 2 == 0) != low:
            tile = pltpu.roll(tile, HD, 1)
        tiles.append(tile)
    return tiles


def join_heads(tiles, low):
    rows = tiles[0].shape[0]
    lane = lax.broadcasted_iota(jnp.int32, (rows, 128), 1)
    pairs = []
    for h in range(0, len(tiles), 2):
        first, second = tiles[h], tiles[h + 1]
        if low:
            second = pltpu.roll(second, HD, 1)
        else:
            first = pltpu.roll(first, HD, 1)
        pairs.append(jnp.where(lane < HD, first, second))
    return jnp.concatenate(pairs, axis=1)


def forward_kernel(
    plan, kv_heads, heads, s_ref, q_ref, kx, vx, wo_ref, x_ref, wd_ref, o_ref, qe_ref, x2_ref, wd_out,
    terms, right, left, term_acc, wd_send, wd_recv, wd_on_send, wd_on_recv, wd_keep, *sems
):
    wide, cw, chunk, own = plan.wide, plan.cw, plan.chunk, plan.own
    rows, width = heads * cw, heads * HD
    z = lax.axis_index("wide")
    team = Group(plan)
    index = team.index
    unit, g = pl.program_id(0), pl.program_id(1)
    last_g = kv_heads - 1
    piece, half = wide - 1 - unit // 2, lax.rem(unit, 2)
    w = near_of(plan, z, piece)
    r = lax.rem(w - z + wide, wide)
    c = jnp.where(half == 1, 2 * plan.group - 1 - index, index)
    low_rows = pl.ds(pl.multiple_of(half * cw, cw), cw)
    columns = pl.ds(pl.multiple_of(g * width, width), width)

    attn = Sums(plan, terms, right, left, sems)

    def out_rows(n):
        return pl.ds(pl.multiple_of((n * kv_heads + g) * width, width), width)

    fold = wd_ref.shape[0] // 2

    def wd_rows(n, core):
        return wd_out.at[n, pl.ds(pl.multiple_of(core * fold, fold), fold)]

    def wd_to(k):
        mine = wd_ref.at[pl.ds(pl.multiple_of(team.seq * fold, fold), fold)]
        return push(mine, wd_rows(team.me, team.seq), wd_send.at[k], wd_recv.at[k], {"narrow": team.beside(k)})

    def wd_from(k):
        theirs = wd_rows(team.beside(-k), team.seq)
        return push(theirs, theirs, wd_send.at[k], wd_recv.at[k], {"narrow": team.beside(k)})

    def wd_on(k, core):
        rows_of = wd_rows(team.beside(-k), core)
        return push(rows_of, rows_of, wd_on_send.at[k], wd_on_recv.at[k], team.sibling)

    wd_own = pltpu.make_async_copy(wd_ref, wd_out.at[team.me], wd_keep)

    @pl.when((unit == 0) & (g == 0))
    def _():
        others = [team.member(k) for k in range(1, plan.group)]
        greet(others + [along_wide(plan, k) for k in range(1, wide)])
        for k in range(1, team.narrow):
            wd_to(k).start()
        wd_own.start()

    for k in range(1, team.narrow):
        @pl.when((unit == 2 * wide - (3 if k == 1 else 2)) & (g == 0))
        def _():
            wd_from(k).wait_recv()
            wd_on(k, team.seq).start()

    lane = lax.broadcasted_iota(jnp.int32, (cw, 128), 1)
    token = c * chunk + w * cw + lax.broadcasted_iota(jnp.int32, (cw, 128), 0)
    segment = (token >= s_ref[0]).astype(jnp.int32) + (token >= s_ref[1]).astype(jnp.int32)
    mark = jnp.where(lane == HD + segment, 1.0, 0.0)
    block = q_ref[pl.ds(pl.multiple_of(r * own + half * cw, cw), cw), columns]
    tiles = split_heads(block.astype(F32), heads, True)
    q32 = jnp.concatenate([jnp.where(lane < HD, t, mark) for t in tiles], axis=0)
    q = q32.astype(BF)

    def step(j, carry, diagonal=False):
        top, acc = carry
        at = pl.ds(pl.multiple_of(j * chunk, chunk), chunk)
        s = lax.dot_general(q, kx[g, at, :], NT, preferred_element_type=F32)
        if diagonal:
            row = lax.broadcasted_iota(jnp.int32, (rows, chunk), 0) % cw + w * cw
            col = lax.broadcasted_iota(jnp.int32, (rows, chunk), 1)
            s = jnp.where(col <= row, s, NEG)
        new = jnp.maximum(top, jnp.max(s, axis=1, keepdims=True))
        p = jnp.exp(s - new).astype(BF)
        acc = acc * jnp.exp(top - new) + jnp.dot(p, vx[g, at, :], preferred_element_type=F32)
        return new, acc

    start = (jnp.full((rows, 1), NEG, F32), jnp.zeros((rows, 128), F32))
    carry = lax.fori_loop(0, c, step, start)
    top, acc = step(c, carry, True)
    total = acc[:, 0:1]
    out = acc / total
    out = join_heads([out[h * cw : (h + 1) * cw] for h in range(heads)], False).astype(BF)
    o_ref[w, low_rows, columns] = out
    first, second, third = pieces_of(-(top + jnp.log(total)))
    wide_lane = lax.broadcasted_iota(jnp.int32, (rows, 128), 1)
    qe = jnp.where(wide_lane == HD + 3, first, q32)
    qe = jnp.where(wide_lane == HD + 4, second, qe)
    qe = jnp.where(wide_lane == HD + 5, third, qe)
    qe_ref[r, g, half] = qe.astype(BF)

    term = jnp.concatenate(
        [jnp.dot(out, wo_ref[out_rows(n), :], preferred_element_type=F32) for n in range(plan.group // 2)], axis=1
    )

    @pl.when(g == 0)
    def _():
        term_acc[...] = term

    @pl.when(g > 0)
    def _():
        term_acc[...] += term

    @pl.when((g == last_g) & (piece == 0))
    def _():
        x2_ref[low_rows, :] = x_ref[low_rows, :].astype(F32) + term_acc[...]

    @pl.when((g == last_g) & (piece > 0))
    def _():
        terms[piece, low_rows, :] = term_acc[...].astype(BF)

    for t in range(1, wide):
        @pl.when((g == last_g) & (unit == 2 * t - 1))
        def _():
            attn.go(t)

    @pl.when((unit == 2 * wide - 1) & (g == last_g))
    def _():
        attn.finish()
        tall = min(32, own)

        @pl.loop(0, own // tall)
        def _(b):
            at = pl.ds(pl.multiple_of(b * tall, tall), tall)
            x2_ref[at, :] = attn.total(x2_ref[at, :], at)

        wd_own.wait()
        for k in range(1, team.narrow):
            wd_on(k, 1 - team.seq).wait_recv()
            wd_to(k).wait_send()
            wd_on(k, team.seq).wait_send()


def forward_call(plan, starts, q, kx, vx, w_o, x, w_down, heads):
    kv_heads, total, _ = kx.shape
    own, d = x.shape
    wide, rows, cw = plan.wide, plan.rows, plan.cw
    qw = q.shape[1]
    pairs = kv_heads * heads * total * rows // 2
    fixed = lambda a: pl.BlockSpec(a.shape, lambda u, g: (0,) * a.ndim, pipeline_mode=pl.Buffered(1))
    given = [q, kx, vx, w_o, x]
    outs = [
        jax.ShapeDtypeStruct((wide, own, qw), BF),
        jax.ShapeDtypeStruct((wide, kv_heads, 2, heads * cw, 128), BF),
        jax.ShapeDtypeStruct((own, d), F32),
    ]
    buffer = pltpu.VMEM((wide, own, d), BF)
    sems = pltpu.SemaphoreType.DMA((wide,))
    return pl.pallas_call(
        functools.partial(forward_kernel, plan, kv_heads, heads),
        grid=(2 * wide, kv_heads),
        in_specs=[pl.BlockSpec(memory_space=pltpu.SMEM)] + [fixed(a) for a in given]
        + [pl.BlockSpec(memory_space=pl.ANY)],
        out_specs=[fixed(a) for a in outs] + [pl.BlockSpec(memory_space=pl.ANY)],
        out_shape=outs + [jax.ShapeDtypeStruct((plan.group // 2, *w_down.shape), BF)],
        scratch_shapes=[buffer] * 3 + [pltpu.VMEM((cw, d), F32)]
        + [pltpu.SemaphoreType.DMA((plan.group // 2,))] * 4 + [pltpu.SemaphoreType.DMA] + [sems] * 4,
        cost_estimate=pl.CostEstimate(
            flops=16 * pairs * HD, bytes_accessed=8 * kv_heads * total * 128, transcendentals=pairs
        ),
        compiler_params=pltpu.CompilerParams(
            vmem_limit_bytes=56 << 20, collective_id=5, has_side_effects=True
        ),
        name="attention_forward",
    )(starts, *given, w_down)


def ffn_kernel(
    plan, x2_ref, gain_ref, g_ref, wg_ref, wu_ref, wd_ref,
    dg_ref, du_ref, h_out, dn_ref, dx_ref, gain_out, grad_out,
    h_buf, in_buf, out_buf, dn_acc, dh_acc, own_dh, act_buf, g_buf, grad_buf, rs_send, rs_recv, grad_sem, *chain_sems
):
    wide, narrow = plan.wide, plan.group // 2
    own, d = x2_ref.shape
    part = d // narrow
    piece, step = pl.program_id(0), pl.program_id(1)
    last = pl.num_programs(1) - 1
    tall = min(32, own)

    z = lax.axis_index("wide")
    owner = near_of(plan, z, piece)

    chain = Chain(plan, h_buf, chain_sems)

    def give(device):
        return push(out_buf.at[device], in_buf.at[z], rs_send.at[device], rs_recv.at[z], {"wide": device})

    @pl.when((piece == 0) & (step == 0))
    def _():
        greet([along_wide(plan, r) for r in range(1, wide)])

        @pl.loop(0, own // tall)
        def _(b):
            at = pl.ds(pl.multiple_of(b * tall, tall), tall)
            x2 = x2_ref[at, :]
            scale = lax.rsqrt(jnp.mean(x2 * x2, axis=1, keepdims=True) + EPS)
            h_buf[z, at, :] = (x2 * scale * gain_ref[...]).astype(BF)

        chain.go(1)

    for h in range(1, wide):
        @pl.when((piece == h) & (step == 0))
        def _():
            chain.arrive(h)
            if h + 1 < wide:
                chain.go(h + 1)

    @pl.when(step == 0)
    def _():
        h_out[...] = h_buf[owner]
        g_buf[pl.ds(pl.multiple_of(piece * own, own), own), :] = g_ref[...]

    h = h_buf[owner]
    wg, wu = wg_ref[...], wu_ref[...]
    gate = jnp.dot(h, wg, preferred_element_type=F32)
    up = jnp.dot(h, wu, preferred_element_type=F32)
    d_act = jnp.zeros_like(gate)
    for n in range(narrow):
        d_act += lax.dot_general(
            g_ref[:, n * part : (n + 1) * part], wd_ref[n], NT, preferred_element_type=F32
        )
    sig = jax.nn.sigmoid(gate)
    silu = gate * sig
    act = (silu * up).astype(BF)
    dg = (d_act * up * sig * (1.0 + gate * (1.0 - sig))).astype(BF)
    du = (d_act * silu).astype(BF)
    tile = act.shape[1]
    act_buf[pl.ds(pl.multiple_of(piece * own, own), own), pl.ds(pl.multiple_of(step * tile, tile), tile)] = act
    dg_ref[...] = dg
    du_ref[...] = du
    dh = lax.dot_general(dg, wg, NT, preferred_element_type=F32) + lax.dot_general(
        du, wu, NT, preferred_element_type=F32
    )

    @pl.when(step == 0)
    def _():
        dh_acc[...] = dh

    @pl.when(step > 0)
    def _():
        dh_acc[...] += dh

    for n in range(narrow):
        at = slice(n * part, (n + 1) * part)
        down = jnp.dot(act, wd_ref[n], preferred_element_type=F32)

        @pl.when(step == 0)
        def _():
            dn_acc[:, at] = down

        @pl.when(step > 0)
        def _():
            dn_acc[:, at] += down

    @pl.when(step == last)
    def _():
        dn_ref[0] = dn_acc[...].astype(BF)

    @pl.when((step == last) & (piece == 0))
    def _():
        own_dh[...] = dh_acc[...]

    @pl.when((step == last) & (piece > 0))
    def _():
        out_buf[owner] = dh_acc[...].astype(BF)
        give(owner).start()

    @pl.when((step == last) & (piece == wide - 1))
    def _():
        @pl.loop(0, last + 1)
        def _(t):
            at = pl.ds(pl.multiple_of(t * tile, tile), tile)
            keep = pltpu.make_async_copy(grad_buf, grad_out.at[:, at, :], grad_sem)

            @pl.when(t > 0)
            def _():
                keep.wait()

            for n in range(narrow):
                grad_buf[n] = lax.dot_general(
                    act_buf[:, at], g_buf[:, n * part : (n + 1) * part], TN, preferred_element_type=F32
                ).astype(BF)
            keep.start()

        for p in range(1, wide):
            other = near_of(plan, z, p)
            push(out_buf.at[z], in_buf.at[other], rs_send.at[z], rs_recv.at[other], {"wide": other}).wait_recv()
        gain_out[...] = jnp.zeros_like(gain_out)

        @pl.loop(0, own // tall)
        def _(b):
            at = pl.ds(pl.multiple_of(b * tall, tall), tall)
            dh2 = own_dh[at, :]
            for p in range(1, wide):
                dh2 = dh2 + in_buf[near_of(plan, z, p), at, :].astype(F32)
            x2 = x2_ref[at, :]
            scale = lax.rsqrt(jnp.mean(x2 * x2, axis=1, keepdims=True) + EPS)
            z2 = x2 * scale
            gain_out[...] += jnp.sum(dh2 * z2, axis=0, keepdims=True)
            dz2 = dh2 * gain_ref[...]
            inner = jnp.mean(dz2 * z2, axis=1, keepdims=True)
            dx_ref[at, :] = g_buf[at, :].astype(F32) + scale * (dz2 - z2 * inner)

        chain.finish()
        for p in range(1, wide):
            give(near_of(plan, z, p)).wait_send()
        pltpu.make_async_copy(grad_buf, grad_out.at[:, pl.ds(0, tile), :], grad_sem).wait()


def ffn_call(plan, x2, gain, g_rows, w_gu, w_dn):
    own, d = x2.shape
    wide, rows = plan.wide, plan.rows
    narrow, ff, part = w_dn.shape
    tile = min(512, ff)
    tiles = ff // tile
    fixed = lambda shape: pl.BlockSpec(shape, lambda p, f: (0,) * len(shape), pipeline_mode=pl.Buffered(1))
    tall = pl.BlockSpec((own, tile), lambda p, f: (p, f))
    hidden = jax.ShapeDtypeStruct((rows, ff), BF)
    buffer = pltpu.VMEM((wide, own, d), BF)
    sems = pltpu.SemaphoreType.DMA((wide,))
    return pl.pallas_call(
        functools.partial(ffn_kernel, plan),
        grid=(wide, tiles),
        in_specs=[
            fixed((own, d)),
            fixed((1, d)),
            pl.BlockSpec((own, d), lambda p, f: (p, 0)),
            pl.BlockSpec((d, tile), lambda p, f: (0, f)),
            pl.BlockSpec((d, tile), lambda p, f: (0, tiles + f)),
            pl.BlockSpec((narrow, tile, part), lambda p, f: (0, f, 0)),
        ],
        out_specs=[
            tall, tall,
            pl.BlockSpec((own, d), lambda p, f: (p, 0)),
            pl.BlockSpec((1, own, d), lambda p, f: (p, 0, 0)),
            fixed((own, d)),
            fixed((1, d)),
            pl.BlockSpec(memory_space=pl.ANY),
        ],
        out_shape=[
            hidden, hidden,
            jax.ShapeDtypeStruct((rows, d), BF),
            jax.ShapeDtypeStruct((wide, own, d), BF),
            jax.ShapeDtypeStruct((own, d), F32),
            jax.ShapeDtypeStruct((1, d), F32),
            jax.ShapeDtypeStruct((narrow, ff, part), BF),
        ],
        scratch_shapes=[
            buffer, buffer, buffer,
            pltpu.VMEM((own, d), F32), pltpu.VMEM((own, d), F32), pltpu.VMEM((own, d), F32),
            pltpu.VMEM((rows, ff), BF), pltpu.VMEM((rows, d), BF), pltpu.VMEM((narrow, tile, part), BF),
            sems, sems, pltpu.SemaphoreType.DMA, sems, sems, sems, sems,
        ],
        cost_estimate=pl.CostEstimate(
            flops=16 * rows * d * ff, bytes_accessed=6 * d * ff + 12 * rows * d, transcendentals=rows * ff
        ),
        compiler_params=pltpu.CompilerParams(
            vmem_limit_bytes=60 << 20, collective_id=1, has_side_effects=True
        ),
        name="feed_forward",
    )(x2, gain, g_rows, w_gu, w_gu, w_dn)


def weights_kernel(
    plan, tiles, dx2_ref, h_ref, dg_ref, du_ref, down_ref, x2_ref,
    gate_out, up_out, db_out, res_out,
    db_buf, right, left, keep_sem, *sems
):
    wide = plan.wide
    step = pl.program_id(0)
    last = pl.num_programs(0) - 1
    chain = Chain(plan, db_buf, sems[:4])
    down = Sums(plan, down_ref, right, left, sems[4:])
    keep = pltpu.make_async_copy(db_buf, db_out, keep_sem)

    @pl.when(step == 0)
    def _():
        db_buf[lax.axis_index("wide")] = dx2_ref[...].astype(BF)
        greet([along_wide(plan, k) for k in range(1, wide)])
        chain.go(1)

    @pl.when(step < tiles)
    def _():
        gate_out[...] = lax.dot_general(h_ref[...], dg_ref[...], TN, preferred_element_type=F32).astype(BF)

    @pl.when(step >= tiles)
    def _():
        up_out[...] = lax.dot_general(h_ref[...], du_ref[...], TN, preferred_element_type=F32).astype(BF)

    for h in range(1, wide):
        @pl.when(step == min(last, h * (tiles + 1) - 1))
        def _():
            chain.arrive(h)
            if h + 1 < wide:
                chain.go(h + 1)
            down.go(h)

    @pl.when(step == last)
    def _():
        keep.start()
        down.finish()
        tall = min(32, x2_ref.shape[0])

        @pl.loop(0, x2_ref.shape[0] // tall)
        def _(b):
            at = pl.ds(pl.multiple_of(b * tall, tall), tall)
            res_out[at, :] = down.total(x2_ref[at, :] + down_ref[0, at, :].astype(F32), at).astype(BF)

        chain.finish()
        keep.wait()


def weights_call(plan, dx2, h, d_gate, d_up, down, x2):
    own, d = dx2.shape
    rows, ff = d_gate.shape
    wide = plan.wide
    tiles = 4
    d_tile = d // tiles
    fixed = lambda a: pl.BlockSpec(a.shape, lambda s: (0,) * a.ndim, pipeline_mode=pl.Buffered(1))
    first = lambda s: jnp.minimum(s, tiles - 1)
    second = lambda s: jnp.clip(s - tiles, 0, tiles - 1)
    sems = pltpu.SemaphoreType.DMA((wide,))
    return pl.pallas_call(
        functools.partial(weights_kernel, plan, tiles),
        grid=(2 * tiles,),
        in_specs=[
            fixed(dx2),
            pl.BlockSpec((rows, d_tile), lambda s: (0, lax.rem(s, tiles))),
            fixed(d_gate), fixed(d_up), fixed(down), fixed(x2),
        ],
        out_specs=[
            pl.BlockSpec((d_tile, ff), lambda s: (first(s), 0)),
            pl.BlockSpec((d_tile, ff), lambda s: (second(s), 0)),
            pl.BlockSpec(memory_space=pl.ANY),
            pl.BlockSpec((own, d), lambda s: (0, 0), pipeline_mode=pl.Buffered(1)),
        ],
        out_shape=[
            jax.ShapeDtypeStruct((d, ff), BF),
            jax.ShapeDtypeStruct((d, ff), BF),
            jax.ShapeDtypeStruct((wide, own, d), BF),
            jax.ShapeDtypeStruct((own, d), BF),
        ],
        scratch_shapes=[pltpu.VMEM((wide, own, d), BF)] * 3 + [pltpu.SemaphoreType.DMA] + [sems] * 8,
        cost_estimate=pl.CostEstimate(
            flops=8 * rows * d * ff, bytes_accessed=20 * rows * d, transcendentals=0
        ),
        compiler_params=pltpu.CompilerParams(
            vmem_limit_bytes=60 << 20, collective_id=6, has_side_effects=True
        ),
        name="weight_gradients",
    )(dx2, h, d_gate, d_up, down, x2)


def backward_kernel(
    plan, kv_heads, heads, db_ref, qe_ref, kx, vx, o_ref, wo_ref, wq_ref, cos_ref, sin_ref, res_ref,
    dq_ref, sums, dh_ref, res_out, terms, right, left, term_acc, results,
    part_send, part_recv, keep_sem, *sems
):
    wide, cw, chunk, own = plan.wide, plan.cw, plan.chunk, plan.own
    rows = heads * cw
    width = heads * HD
    z = lax.axis_index("wide")
    team = Group(plan)
    index = team.index
    chain = Chain(plan, results, sems[:4])
    back = Sums(plan, terms, right, left, sems[4:])
    parts = Parts(plan, team, res_ref, results, part_send, part_recv, keep_sem.at[0])
    unit, g = pl.program_id(0), pl.program_id(1)
    last_unit, last_g = 2 * wide - 1, kv_heads - 1
    piece, half = wide - 1 - unit // 2, lax.rem(unit, 2)
    w = near_of(plan, z, piece)
    r = lax.rem(w - z + wide, wide)
    c = jnp.where(half == 1, 2 * plan.group - 1 - index, index)
    low_rows = pl.ds(pl.multiple_of(half * cw, cw), cw)

    @pl.when((unit == 0) & (g == 0))
    def _():
        others = [team.member(k) for k in range(1, plan.group)]
        greet(others + [along_wide(plan, k) for k in range(1, wide)])
        parts.start()

        @pl.loop(0, kv_heads * plan.total // chunk)
        def _(b):
            at = pl.ds(pl.multiple_of(lax.rem(b, plan.total // chunk) * chunk, chunk), chunk)
            sums[b // (plan.total // chunk), at, :] = jnp.zeros((chunk, 128), F32)

    @pl.when((unit == 1) & (g == last_g))
    def _():
        parts.wait()
        chain.go(1)

    for h in range(1, wide):
        late = {1: (3, 0), 2: (4, last_g), 3: (6, 0)}.get(h, (min(h + 3, last_unit), last_g))

        @pl.when((unit == late[0]) & (g == late[1]))
        def _():
            chain.arrive(h)
            if h + 1 < wide:
                chain.go(h + 1)

    lane = lax.broadcasted_iota(jnp.int32, (cw, 128), 1)
    columns = pl.ds(pl.multiple_of(g * width, width), width)
    part = wo_ref.shape[1]
    grad = jnp.zeros((cw, width), F32)
    for n in range(team.narrow):
        out_rows = pl.ds(pl.multiple_of((n * kv_heads + g) * width, width), width)
        grad += lax.dot_general(
            db_ref[w, low_rows, n * part : (n + 1) * part], wo_ref[out_rows, :], NT, preferred_element_type=F32
        )
    do = split_heads(grad.astype(BF).astype(F32), heads, False)
    o = split_heads(o_ref[w, low_rows, columns].astype(F32), heads, False)
    marked = []
    for one, other in zip(o, do):
        clean = jnp.where(lane >= HD, other, 0.0)
        first, second, third = pieces_of(-jnp.sum(one * clean, axis=1, keepdims=True))
        tile = jnp.where(lane == 0, first, clean)
        tile = jnp.where(lane == 1, second, tile)
        marked.append(jnp.where(lane == 2, third, tile))
    dox32 = jnp.concatenate(marked, axis=0)
    wide_lane = lax.broadcasted_iota(jnp.int32, (rows, 128), 1)
    dox = dox32.astype(BF)
    do_clean = jnp.where(wide_lane >= HD, dox32, 0.0).astype(BF)
    q = qe_ref[r, g, half]
    q_clean = jnp.where(wide_lane < HD, q.astype(F32), 0.0).astype(BF)

    def step(j, dq, diagonal=False):
        at = pl.ds(pl.multiple_of(j * chunk, chunk), chunk)
        key = kx[g, at, :]
        s = lax.dot_general(key, q, NT, preferred_element_type=F32)
        if diagonal:
            row = lax.broadcasted_iota(jnp.int32, (chunk, rows), 1) % cw + w * cw
            col = lax.broadcasted_iota(jnp.int32, (chunk, rows), 0)
            s = jnp.where(col <= row, s, NEG)
        p = jnp.exp(s)
        dp = lax.dot_general(vx[g, at, :], dox, NT, preferred_element_type=F32)
        ds = (p * dp).astype(BF)
        sums[g, at, :] += jnp.dot(ds, q_clean, preferred_element_type=F32) + jnp.dot(
            p.astype(BF), do_clean, preferred_element_type=F32
        )
        return dq + lax.dot_general(ds, key, TN, preferred_element_type=F32)

    dq = lax.fori_loop(0, c, step, jnp.zeros((rows, 128), F32))
    dq = step(c, dq, True) * (HD ** -0.5)
    dq = join_heads([dq[h * cw : (h + 1) * cw] for h in range(heads)], True)
    at = pl.ds(pl.multiple_of(r * own + half * cw, cw), cw)
    dq = dq * widen(cos_ref[at, :], width) + turn(dq, -1.0) * widen(sin_ref[at, :], width)
    dq = dq.astype(BF)
    dq_ref[at, columns] = dq

    term = lax.dot_general(dq, wq_ref[:, columns], NT, preferred_element_type=F32)

    @pl.when(g == 0)
    def _():
        term_acc[...] = term

    @pl.when(g > 0)
    def _():
        term_acc[...] += term

    @pl.when((g == last_g) & (piece == 0))
    def _():
        dh_ref[low_rows, :] = term_acc[...]

    @pl.when((g == last_g) & (piece > 0))
    def _():
        terms[piece, low_rows, :] = term_acc[...].astype(BF)

    for t in range(1, wide):
        @pl.when((g == last_g) & (unit == 2 * t - 1))
        def _():
            back.go(t)

    @pl.when((unit == last_unit) & (g == last_g))
    def _():
        keep = pltpu.make_async_copy(results, res_out, keep_sem.at[1])
        keep.start()
        back.finish()
        tall = min(32, own)

        @pl.loop(0, own // tall)
        def _(b):
            at = pl.ds(pl.multiple_of(b * tall, tall), tall)
            dh_ref[at, :] = back.total(dh_ref[at, :], at)

        chain.finish()
        parts.sent()
        keep.wait()


def backward_call(plan, db, qe, kx, vx, o, w_o, w_qkv, cos, sin, res, heads):
    kv_heads, total, _ = kx.shape
    _, own, d = db.shape
    wide, rows, cw = plan.wide, plan.rows, plan.cw
    qw = o.shape[2]
    pairs = kv_heads * heads * total * rows // 2
    fixed = lambda a: pl.BlockSpec(a.shape, lambda u, g: (0,) * a.ndim, pipeline_mode=pl.Buffered(1))
    hbm = pl.BlockSpec(memory_space=pl.ANY)
    given = [db, qe, kx, vx, o, w_o, w_qkv, cos, sin]
    outs = [
        jax.ShapeDtypeStruct((rows, qw), BF),
        jax.ShapeDtypeStruct((kv_heads, total, 128), F32),
        jax.ShapeDtypeStruct((own, d), F32),
    ]
    slots = (wide, plan.group, cw, d // (plan.group // 2))
    buffer = pltpu.VMEM((wide, own, d), BF)
    sems = pltpu.SemaphoreType.DMA((wide,))
    return pl.pallas_call(
        functools.partial(backward_kernel, plan, kv_heads, heads),
        grid=(2 * wide, kv_heads),
        in_specs=[fixed(a) for a in given[:6]]
        + [pl.BlockSpec((d, qw), lambda u, g: (0, 0), pipeline_mode=pl.Buffered(1)), fixed(cos), fixed(sin), fixed(res)],
        out_specs=[fixed(a) for a in outs] + [hbm],
        out_shape=outs + [jax.ShapeDtypeStruct(slots, BF)],
        scratch_shapes=[buffer] * 3 + [pltpu.VMEM((cw, d), F32), pltpu.VMEM(slots, BF)]
        + [pltpu.SemaphoreType.DMA((plan.group,))] * 2 + [pltpu.SemaphoreType.DMA((2,))] + [sems] * 8,
        cost_estimate=pl.CostEstimate(
            flops=36 * pairs * HD, bytes_accessed=12 * kv_heads * total * 128, transcendentals=pairs
        ),
        compiler_params=pltpu.CompilerParams(
            vmem_limit_bytes=60 << 20, collective_id=3, has_side_effects=True
        ),
        name="attention_backward",
    )(*given, res)


def tail_kernel(
    plan, kv_heads, sums_ref, h_hbm, dh_ref, gain2_ref, dx2_ref, x_ref, gain_ref, wkv_hbm,
    cos_ref, sin_ref, dq_ref, o_ref, db_hbm, got_out, gain_out, kv_out, q_out, o_out,
    h_ref, wkv_ref, db_buf, swap_out, swap_in, low, near_in, dkv, head_in, dh_acc, dx_low, every,
    gain_part, gain_in, gain_sum, gain_all,
    swap_sem, near_send, near_recv, head_send, head_recv, part_send, part_recv,
    gain_send, gain_recv, gain2_send, gain2_recv, own_sem, *more
):
    group, wide, chunk, cw, own = plan.group, plan.wide, plan.chunk, plan.cw, plan.own
    narrow = group // 2
    part = dx_low.shape[1] // narrow
    team = Group(plan)
    seq, me, z = team.seq, team.me, lax.axis_index("wide")
    device, member = team.device, team.member
    dx_chain = Chain(plan, every, more[:4])
    q_sum = WeightSum(team, *more[4:9], q_out, *more[9:11])
    kv_sum = WeightSum(team, *more[11:16], kv_out, *more[16:18])
    o_sum = WeightSum(team, *more[18:23], o_out, *more[23:25])
    q_part, kv_part, o_part = q_sum.part, kv_sum.part, o_sum.part

    greet([member(k) for k in range(1, group)] + [along_wide(plan, r) for r in range(1, wide)])

    def place(owner_seq, half, n):
        quarter = owner_seq if half == 0 else 3 - owner_seq
        return pl.ds(
            pl.multiple_of((quarter * narrow + (n if half == 0 else narrow - 1 - n)) * chunk, chunk), chunk
        )

    load_h = pltpu.make_async_copy(h_hbm, h_ref, own_sem.at[2])
    load_w = pltpu.make_async_copy(wkv_hbm, wkv_ref, own_sem.at[3])
    load_h.start()
    load_w.start()

    def swap(g):
        return push(swap_out.at[g], swap_in.at[g], swap_sem.at[0, g], swap_sem.at[1, g], team.sibling)

    def near(k, g):
        other = team.beside(k)
        return push(low.at[g, other], near_in.at[g, k], near_send.at[g, k], near_recv.at[g, k], {"narrow": other})

    def heads_to(r, g):
        columns = slice(g * 128, (g + 1) * 128)
        mine = dkv.at[r * own : (r + 1) * own, columns]
        return push(mine, head_in.at[r, :, columns], head_send.at[r, g], head_recv.at[r, g], along_wide(plan, r))

    for g in range(kv_heads):
        @pl.loop(0, narrow)
        def _(n):
            for half in range(2):
                swap_out[g, n, half] = sums_ref[g, place(1 - seq, half, n), :].astype(BF)

        swap(g).start()

    load_h.wait()
    for n in range(narrow):
        columns = slice(n * part, (n + 1) * part)
        q_part[n] = lax.dot_general(h_ref[:, columns], dq_ref[...], TN, preferred_element_type=F32).astype(BF)
    q_sum.first()

    for g in range(kv_heads):
        swap(g).wait_recv()

        @pl.loop(0, narrow)
        def _(n):
            for half in range(2):
                total = sums_ref[g, place(seq, half, n), :] + swap_in[g, n, half].astype(F32)
                low[g, n, half] = total.astype(BF)

        for k in range(1, narrow):
            near(k, g).start()

    lane = lax.broadcasted_iota(jnp.int32, (cw, 128), 1)
    for g in range(kv_heads):
        for k in range(1, narrow):
            near(k, g).wait_recv()
        for r in range(wide):
            at = pl.ds(pl.multiple_of(lax.rem(z + r, wide) * cw, cw), cw)
            for half in range(2):
                rows = slice((2 * r + half) * cw, (2 * r + half + 1) * cw)
                total = low[g, me, half, at, :].astype(F32)
                for k in range(1, narrow):
                    total = total + near_in[g, k, half, at, :].astype(F32)
                back = total * cos_ref[rows, :] + turn(total, -1.0) * sin_ref[rows, :]
                dkv[rows, g * 128 : (g + 1) * 128] = jnp.where(lane < HD, back, total).astype(BF)
        for r in range(1, wide):
            heads_to(r, g).start()

    q_sum.second()

    for n in range(narrow):
        columns = slice(n * part, (n + 1) * part)
        kv_part[n] = lax.dot_general(dkv[...], h_ref[:, columns], TN, preferred_element_type=F32).astype(BF)
    kv_sum.first()

    tile = part // 2
    load_w.wait()
    for r in range(wide):
        if r > 0:
            for g in range(kv_heads):
                heads_to(r, g).wait_recv()
        mine = dkv[0:own] if r == 0 else head_in[r]
        source = lax.rem(z - r + wide, wide)

        for b in range(group):
            at = slice(b * tile, (b + 1) * tile)
            more = lax.dot_general(mine, wkv_ref[b, source], NT, preferred_element_type=F32)
            dh_acc[:, at] = (dh_ref[:, at] if r == 0 else dh_acc[:, at]) + more

    gain_part[0:1, :] = jnp.zeros_like(gain2_ref[...])
    gain_part[1:2, :] = gain2_ref[...]
    tall = min(32, own)

    @pl.loop(0, own // tall)
    def _(b):
        at = pl.ds(pl.multiple_of(b * tall, tall), tall)
        dh1 = dh_acc[at, :]
        x = x_ref[at, :].astype(F32)
        scale = lax.rsqrt(jnp.mean(x * x, axis=1, keepdims=True) + EPS)
        z1 = x * scale
        gain_part[0:1, :] += jnp.sum(dh1 * z1, axis=0, keepdims=True)
        dz1 = dh1 * gain_ref[...]
        inner = jnp.mean(dz1 * z1, axis=1, keepdims=True)
        dx_low[at, :] = (dx2_ref[at, :] + scale * (dz1 - z1 * inner)).astype(BF)

    dx_parts = Parts(plan, team, dx_low, every, part_send, part_recv, own_sem.at[0])
    dx_parts.start()

    def gain_to(k):
        columns = pl.ds(pl.multiple_of(lax.rem(device(k), narrow) * part, part), part)
        return push(gain_part.at[:, columns], gain_in.at[k], gain_send.at[k], gain_recv.at[k], member(k))

    for k in range(1, group):
        gain_to(k).start()
    dx_parts.wait()
    dx_chain.go(1)
    kv_sum.second()

    rows = o_ref.shape[0] * o_ref.shape[1]
    for n in range(narrow):
        load = pltpu.make_async_copy(db_hbm.at[:, :, n * part : (n + 1) * part], db_buf, own_sem.at[4])
        load.start()
        load.wait()
        o_part[n] = lax.dot_general(
            o_ref[...].reshape(rows, -1), db_buf[...].reshape(rows, part), TN, preferred_element_type=F32
        ).astype(BF)
    o_sum.first()
    q_sum.third()

    gain = gain_part[:, pl.ds(pl.multiple_of(me * part, part), part)]
    for k in range(1, group):
        gain_to(k).wait_recv()
        gain = gain + gain_in[k]
    gain_sum[...] = gain

    def gain_on(r):
        return push(gain_sum, gain_all.at[r], gain2_send.at[r], gain2_recv.at[r], along_wide(plan, r))

    for r in range(1, wide):
        gain_on(r).start()
    dx_chain.arrive(1)
    if wide > 2:
        dx_chain.go(2)
    o_sum.second()
    kv_sum.third()
    q_sum.fourth()
    gain = gain_sum[...]
    for r in range(1, wide):
        gain_on(r).wait_recv()
        gain = gain + gain_all[r]
    gain_out[...] = gain
    for h in range(2, wide):
        dx_chain.arrive(h)
        if h + 1 < wide:
            dx_chain.go(h + 1)
        if h == 2:
            o_sum.third()
            kv_sum.fourth()
    o_sum.fourth()
    got_keep = pltpu.make_async_copy(every, got_out, own_sem.at[1])
    got_keep.start()

    dx_chain.finish()
    for g in range(kv_heads):
        swap(g).wait_send()
        for k in range(1, narrow):
            near(k, g).wait_send()
        for r in range(1, wide):
            heads_to(r, g).wait_send()
    for r in range(1, wide):
        gain_on(r).wait_send()
    dx_parts.sent()
    for k in range(1, group):
        gain_to(k).wait_send()
    for one in (q_sum, kv_sum, o_sum):
        one.sent()
    got_keep.wait()


def tail_call(plan, sums, h, dh, gain2, dx2, x, gain, w_kv, cos, sin, dq, o, db):
    kv_heads = sums.shape[0]
    own, d = dh.shape
    group, wide, chunk, cw = plan.group, plan.wide, plan.chunk, plan.cw
    narrow = group // 2
    part = d // narrow
    kv_width = kv_heads * 128
    dma = pltpu.SemaphoreType.DMA
    quarter = pltpu.VMEM((kv_heads, narrow, 2, chunk, 128), BF)
    slots = (wide, group, cw, part)

    def weight(height, across):
        half = pltpu.VMEM((narrow, height // 2, across), BF)
        ends = pltpu.VMEM((2, height // 2, across), BF)
        return [pltpu.VMEM((narrow, height, across), BF), half, half, half, ends] + [dma((narrow + 1,))] * 2

    given = [sums, h, dh, gain2, dx2, x, gain, w_kv, cos, sin, dq, o, db]
    qw = dq.shape[1]
    whole = pl.BlockSpec(memory_space=pltpu.VMEM)
    hbm = pl.BlockSpec(memory_space=pl.ANY)
    return pl.pallas_call(
        functools.partial(tail_kernel, plan, kv_heads),
        in_specs=[hbm if i in (1, 7, 12) else whole for i in range(len(given))],
        out_specs=[hbm] + [whole] * 4,
        out_shape=[
            jax.ShapeDtypeStruct(slots, BF),
            jax.ShapeDtypeStruct((2, part), F32),
            jax.ShapeDtypeStruct((kv_width, part), F32),
            jax.ShapeDtypeStruct((part, qw), F32),
            jax.ShapeDtypeStruct((qw, part), F32),
        ],
        scratch_shapes=[
            pltpu.VMEM(h.shape, BF), pltpu.VMEM(w_kv.shape, BF), pltpu.VMEM((wide, own, part), BF),
            quarter, quarter, quarter, quarter,
            pltpu.VMEM((plan.rows, kv_width), BF),
            pltpu.VMEM((wide, own, kv_width), BF),
            pltpu.VMEM((own, d), F32),
            pltpu.VMEM((own, d), BF),
            pltpu.VMEM(slots, BF),
            pltpu.VMEM((2, d), F32),
            pltpu.VMEM((group, 2, part), F32),
            pltpu.VMEM((2, part), F32),
            pltpu.VMEM((wide, 2, part), F32),
            dma((2, kv_heads)), dma((kv_heads, narrow)), dma((kv_heads, narrow)),
            dma((wide, kv_heads)), dma((wide, kv_heads)), dma((group,)), dma((group,)),
            dma((group,)), dma((group,)), dma((wide,)), dma((wide,)),
            dma((5,)),
        ] + [dma((wide,))] * 4 + weight(part, qw) + weight(kv_width, part) + weight(qw, part),
        cost_estimate=pl.CostEstimate(
            flops=200 * own * d * wide * kv_width, bytes_accessed=4 * sums.size, transcendentals=0
        ),
        compiler_params=pltpu.CompilerParams(
            vmem_limit_bytes=60 << 20, collective_id=2, has_side_effects=True
        ),
        name="input_gradient",
    )(*given)


def finish_kernel(plan, s_ref, res_ref, dx_ref, *refs):
    group, weights = plan.group, len(refs) // 2 - 1
    res_out, dx_out = refs[weights : weights + 2]
    for l in range(group):
        owner = jnp.where(s_ref[0] >= group // 2, group - 1 - l, l)
        res_out[l, 0] = res_ref[0, owner]
        dx_out[l, 0] = dx_ref[0, owner].astype(F32)
    for low, out in zip(refs[:weights], refs[weights + 2 :]):
        out[...] = low[...].astype(F32)


def finish_call(plan, scalars, result, dx, weights):
    wide, group, cw, part = result.shape
    cuts = 2 if cw % 64 == 0 else 1
    steps = wide * cuts
    slots = pl.BlockSpec((1, group, cw // cuts, part), lambda w, c, s: (w, 0, c, 0))
    tokens = pl.BlockSpec((group, 1, cw // cuts, part), lambda w, c, s: (0, w, c, 0))
    rows = [pl.BlockSpec((a.shape[0] // steps, a.shape[1]), lambda w, c, s: (w * cuts + c, 0)) for a in weights]
    shape = (group, wide, cw, part)
    size = result.size + sum(a.size for a in weights)
    out = pl.pallas_call(
        functools.partial(finish_kernel, plan),
        grid_spec=pltpu.PrefetchScalarGridSpec(
            num_scalar_prefetch=1,
            grid=(wide, cuts),
            in_specs=[slots, slots] + rows,
            out_specs=[tokens, tokens] + rows,
        ),
        out_shape=[jax.ShapeDtypeStruct(shape, BF), jax.ShapeDtypeStruct(shape, F32)]
        + [jax.ShapeDtypeStruct(a.shape, F32) for a in weights],
        cost_estimate=pl.CostEstimate(flops=2 * size, bytes_accessed=8 * size, transcendentals=0),
        compiler_params=pltpu.CompilerParams(vmem_limit_bytes=48 << 20),
        name="finish",
    )(scalars, result, dx, *weights)
    flat = (group * wide * cw, part)
    return [out[0].reshape(flat), out[1].reshape(flat)] + list(out[2:])


def half_of(weight, seq_index, seq_count):
    part = weight.shape[0] // seq_count
    return lax.dynamic_slice_in_dim(weight, seq_index * part, part, 0)


def body(
    tokens, attn_gain, w_query, w_key, w_value, w_out, ffn_gain, w_gate, w_up, w_down,
    segment_ids, token_mask, out_grad,
):
    seq_count = lax.axis_size("seq")
    narrow = lax.axis_size("narrow")
    wide = lax.axis_size("wide")
    group = seq_count * narrow
    seq_index = lax.axis_index("seq")
    narrow_index = lax.axis_index("narrow")
    wide_index = lax.axis_index("wide")
    index = seq_index * narrow + narrow_index
    total = segment_ids.shape[0]
    plan = Plan(total, group, wide)
    chunk, cw, rows, own = plan.chunk, plan.cw, plan.rows, plan.own
    d_part = tokens.shape[1]
    d = d_part * narrow
    qw = w_query.shape[1]
    kw = w_key.shape[1]
    kv_heads = kw // HD
    heads = qw // kw
    ff = w_gate.shape[1]

    starts = jnp.sum((segment_ids[None, :] < jnp.arange(1, 3)[:, None]).astype(jnp.int32), axis=1)
    start_one, start_two = starts[0], starts[1]
    scalars = jnp.reshape(index, (1,)).astype(jnp.int32)

    def gather_weight(weight):
        return lax.all_gather(half_of(weight, seq_index, seq_count), NS, axis=0, tiled=True)

    def scatter_grad(grad, *others):
        mine = after(lax.psum_scatter(grad.astype(BF), NS, scatter_dimension=0, tiled=True), *others)
        return lax.all_gather(mine, "seq", axis=0, tiled=True)

    def after(values, *others):
        return lax.optimization_barrier((values, *others))[0]

    w_kv = jnp.concatenate(
        [w_key.reshape(d_part, kv_heads, 1, HD), w_value.reshape(d_part, kv_heads, 1, HD)], axis=2
    ).reshape(d_part, 2 * kw)

    row = jnp.arange(rows, dtype=jnp.int32)
    row_chunk = jnp.where((row // cw) % 2 == 1, 2 * group - 1 - index, index)
    row_block = (row // own + wide_index) % wide
    row_token = row_chunk * chunk + row_block * cw + row % cw
    row_start = jnp.where(row_token >= start_two, start_two, jnp.where(row_token >= start_one, start_one, 0))
    row_pos = (row_token - row_start).astype(F32)
    frequency = THETA ** (-2.0 * jnp.arange(HD // 2, dtype=F32) / HD)
    angles = row_pos[:, None] * jnp.tile(frequency, 4)[None, :]
    cos, sin = jnp.cos(angles), jnp.sin(angles)

    feature = jnp.arange(16, dtype=jnp.int32)[:, None]
    closed = (segment_ids[None, :] != feature) | (token_mask[None, :] != 1)
    marks = jnp.where((feature < 3) & closed, NEG, jnp.where((feature >= 3) & (feature < 6), 1.0, 0.0)).astype(BF)

    mask = lax.dynamic_slice_in_dim(token_mask, seq_index * (group * chunk), group * chunk, 0)
    g_part = lax.dynamic_index_in_dim(out_grad.reshape(group, wide, cw, d_part), wide_index, 1, keepdims=False)
    mask = lax.dynamic_index_in_dim(mask.reshape(group, wide, cw), wide_index, 1, keepdims=False)
    g_part = jnp.where(mask[:, :, None] == 1, g_part, jnp.zeros_like(g_part))

    w_o = gather_weight(w_out)
    h_one, q, x_low, kx, vx, w_qkv, gains, g_rows, w_kv, w_gu = head_call(
        plan, tokens.reshape(group, wide, cw, d_part), g_part, jnp.concatenate([w_query, w_kv], axis=1),
        jnp.stack([attn_gain, ffn_gain]), cos, sin, marks, w_gate, w_up, qw, kv_heads
    )
    gains = jnp.transpose(gains, (1, 0, 2)).reshape(2, d)
    gain_one, gain_two = gains[0:1], gains[1:2]
    g_rows = g_rows.reshape(rows, d)

    w_gu = lax.all_gather(w_gu, NS, axis=0, tiled=True)
    o, qe, x2, w_dn = forward_call(plan, starts, q, kx, vx, w_o, x_low, w_down, heads)
    w_kv = jnp.transpose(w_kv.reshape(wide, seq_count, d_part // seq_count, 2 * kw), (1, 0, 2, 3))
    w_kv = lax.dynamic_index_in_dim(w_kv, seq_index, 0, keepdims=False).reshape(-1, 2 * kw)
    w_kv = lax.all_gather(after(w_kv, o, w_gu), NS, axis=0, tiled=True)
    w_kv = w_kv.reshape(group, wide, d_part // seq_count, 2 * kw)

    d_gate, d_up, h_all, down, dx2, grad_gain_two, grad_dn = ffn_call(plan, x2, gain_two, g_rows, w_gu, w_dn)

    h_all = after(h_all, w_kv)
    grad_gate, grad_up, db, result = weights_call(plan, dx2, h_all, d_gate, d_up, down, x2)
    dq, sums, dh1, result = backward_call(plan, db, qe, kx, vx, o, w_o, w_qkv, cos, sin, result, heads)

    input_grad, gain_grads, grad_kv, grad_q, grad_o = tail_call(
        plan, sums, h_one, dh1, grad_gain_two, dx2, x_low, gain_one, w_kv, cos, sin, dq, o, db
    )

    grad_dn = scatter_grad(grad_dn.reshape(narrow * ff, d_part), dq)
    grad_gate = scatter_grad(grad_gate, dq)
    grad_up = scatter_grad(grad_up, dq)
    result, input_grad, grad_dn, grad_gate, grad_up = finish_call(
        plan, scalars, result, input_grad, [grad_dn, grad_gate, grad_up]
    )
    grad_kv = jnp.transpose(grad_kv.reshape(kv_heads, 2, HD, d_part), (3, 0, 1, 2))
    return (
        result,
        input_grad,
        gain_grads[0],
        grad_q,
        grad_kv[:, :, 0].reshape(d_part, kw),
        grad_kv[:, :, 1].reshape(d_part, kw),
        grad_o,
        gain_grads[1],
        grad_gate,
        grad_up,
        grad_dn,
    )


def solution(mesh):
    width_in, width_out = P("narrow", "wide"), P("wide", "narrow")
    acts = P("seq", "narrow")
    return jax.shard_map(
        body,
        mesh=mesh,
        in_specs=(
            acts, P("narrow"), width_in, width_in, width_in, width_out, P("narrow"),
            width_in, width_in, width_out, P(), P(), acts,
        ),
        out_specs=(
            acts, acts, P("narrow"), width_in, width_in, width_in, width_out, P("narrow"),
            width_in, width_in, width_out,
        ),
        check_vma=False,
    )
```

```python
import functools

import jax
import jax.numpy as jnp
from jax import lax
from jax.experimental import pallas as pl
from jax.experimental.pallas import tpu as pltpu
from jax.sharding import PartitionSpec as P

HD = 64
EPS = 1e-05
THETA = 500000.0
NEG = -1e30
SN = ("seq", "narrow")
NS = ("narrow", "seq")
BF = jnp.bfloat16
F32 = jnp.float32
NT = (((1,), (1,)), ((), ()))
TN = (((0,), (0,)), ((), ()))


def pieces_of(value):
    first = value.astype(BF).astype(F32)
    second = (value - first).astype(BF).astype(F32)
    third = (value - first - second).astype(BF).astype(F32)
    return first, second, third


class Plan:
    def __init__(self, total, group, wide):
        self.total, self.group, self.wide = total, group, wide
        self.chunk = total // (2 * group)
        self.cw = self.chunk // wide
        self.rows = 2 * self.chunk
        self.own = 2 * self.cw


def near_of(plan, z, p):
    flip = z > plan.wide - 1 - z
    side = jnp.where(flip, plan.wide - 1 - z, z)
    both = jnp.where(lax.rem(p, 2) == 1, side + (p + 1) // 2, side - p // 2)
    place = jnp.where(p <= 2 * side, both, p)
    return jnp.where(flip, plan.wide - 1 - place, place)


def turn(values, sign):
    width = values.shape[1]
    lane = lax.broadcasted_iota(jnp.int32, values.shape, 1)
    left, right = pltpu.roll(values, width - HD // 2, 1), pltpu.roll(values, HD // 2, 1)
    return jnp.where(lane % HD < HD // 2, -sign * left, sign * right)


def widen(table, width):
    return jnp.concatenate([table] * (width // 128), axis=1) if width > 128 else table


MESH = pl.DeviceIdType.MESH


def greet(partners):
    barrier = pltpu.get_barrier_semaphore()
    for partner in partners:
        pl.semaphore_signal(barrier, inc=1, device_id=partner, device_id_type=MESH)
    pl.semaphore_wait(barrier, len(partners))


def along_wide(plan, r):
    return {"wide": lax.rem(lax.axis_index("wide") + r + plan.wide, plan.wide)}


def push(src, dst, send, recv, device):
    return pltpu.make_async_remote_copy(
        src_ref=src, dst_ref=dst, send_sem=send, recv_sem=recv, device_id=device, device_id_type=MESH
    )


class Chain:
    def __init__(self, plan, buf, sems):
        self.wide, self.buf, self.sems = plan.wide, buf, sems
        self.z = lax.axis_index("wide")

    def copy(self, slot, h, way):
        send, recv = (self.sems[0], self.sems[1]) if way > 0 else (self.sems[2], self.sems[3])
        return push(self.buf.at[slot], self.buf.at[slot], send.at[h], recv.at[h], {"wide": self.z + way})

    def sends(self, h, way):
        z, last = self.z, self.wide - 1
        return (z >= h - 1) & (z < last) if way > 0 else (z + h - 1 <= last) & (z > 0)

    def go(self, h):
        for way in (1, -1):
            @pl.when(self.sends(h, way))
            def _():
                self.copy(self.z - way * (h - 1), h, way).start()

    def arrive(self, h):
        for way in (1, -1):
            @pl.when(self.z >= h if way > 0 else self.z + h <= self.wide - 1)
            def _():
                slot = self.z - way * h
                send, recv = (self.sems[0], self.sems[1]) if way > 0 else (self.sems[2], self.sems[3])
                push(self.buf.at[slot], self.buf.at[slot], send.at[h], recv.at[h], {"wide": slot}).wait_recv()

    def finish(self):
        for h in range(1, self.wide):
            for way in (1, -1):
                @pl.when(self.sends(h, way))
                def _():
                    self.copy(self.z - way * (h - 1), h, way).wait_send()


class Group:
    def __init__(self, plan):
        self.size, self.narrow = plan.group, plan.group // 2
        self.seq, self.me = lax.axis_index("seq"), lax.axis_index("narrow")
        self.index = self.seq * self.narrow + self.me
        self.sibling = {"seq": 1 - self.seq}

    def device(self, k):
        return lax.rem(self.index + k + self.size, self.size)

    def member(self, k):
        return {"seq": self.device(k) // self.narrow, "narrow": lax.rem(self.device(k), self.narrow)}

    def beside(self, k):
        return lax.rem(self.me + k + self.narrow, self.narrow)


class Parts:
    def __init__(self, plan, team, ref, slots, send, recv, stay):
        self.plan, self.team, self.ref, self.send, self.recv = plan, team, ref, send, recv
        self.slots = slots.at[lax.axis_index("wide")]
        self.part = ref.shape[1] // team.narrow
        self.stay = pltpu.make_async_copy(self.slab(team.index), self.slots.at[team.index], stay)

    def slab(self, other):
        cw, narrow, part = self.plan.cw, self.team.narrow, self.part
        rows = pl.ds(pl.multiple_of((other // narrow) * cw, cw), cw)
        return self.ref.at[rows, pl.ds(pl.multiple_of(lax.rem(other, narrow) * part, part), part)]

    def to(self, k):
        team = self.team
        src = self.slab(team.device(k))
        return push(src, self.slots.at[team.index], self.send.at[k], self.recv.at[k], team.member(k))

    def start(self):
        for k in range(1, self.team.size):
            self.to(k).start()
        self.stay.start()

    def wait(self):
        team = self.team
        self.stay.wait()
        for k in range(1, team.size):
            src = self.slab(team.index)
            push(src, self.slots.at[team.device(-k)], self.send.at[k], self.recv.at[k], team.member(k)).wait_recv()

    def sent(self):
        for k in range(1, self.team.size):
            self.to(k).wait_send()


class Sums:
    def __init__(self, plan, terms, right, left, sems):
        self.wide, self.terms, self.sums, self.sems = plan.wide, terms, (right, left), sems
        self.z = lax.axis_index("wide")
        self.side = jnp.minimum(self.z, plan.wide - 1 - self.z)

    def term(self, h, way):
        lower = self.z <= self.wide - 1 - self.z
        ahead = lower if way > 0 else jnp.logical_not(lower)
        return jnp.where(h <= self.side, jnp.where(ahead, 2 * h - 1, 2 * h), self.side + h)

    def sends(self, t, way):
        h = self.wide - t
        return self.z + h <= self.wide - 1 if way > 0 else self.z >= h

    def first(self, way):
        return self.z == (0 if way > 0 else self.wide - 1)

    def copy(self, src, t, way):
        buf = self.sums[0 if way > 0 else 1]
        send, recv = self.sems[:2] if way > 0 else self.sems[2:]
        return push(src, buf.at[t], send.at[t], recv.at[t], {"wide": self.z + way})

    def came(self, t, way):
        buf = self.sums[0 if way > 0 else 1]
        send, recv = self.sems[:2] if way > 0 else self.sems[2:]
        push(buf.at[t], buf.at[t], send.at[t], recv.at[t], {"wide": self.z - way}).wait_recv()

    def go(self, t):
        for way in (1, -1):
            term = self.term(self.wide - t, way)

            @pl.when(self.sends(t, way) & self.first(way))
            def _():
                self.copy(self.terms.at[term], t, way).start()

            if t > 1:
                @pl.when(self.sends(t, way) & jnp.logical_not(self.first(way)))
                def _():
                    self.came(t - 1, way)
                    buf = self.sums[0 if way > 0 else 1]
                    tall = min(32, buf.shape[1])

                    @pl.loop(0, buf.shape[1] // tall)
                    def _(b):
                        at = pl.ds(pl.multiple_of(b * tall, tall), tall)
                        total = buf[t - 1, at, :].astype(F32) + self.terms[term, at, :].astype(F32)
                        buf[t - 1, at, :] = total.astype(BF)

                    self.copy(buf.at[t - 1], t, way).start()

    def finish(self):
        for way in (1, -1):
            @pl.when(jnp.logical_not(self.first(way)))
            def _():
                self.came(self.wide - 1, way)

        for t in range(1, self.wide):
            for way in (1, -1):
                @pl.when(self.sends(t, way))
                def _():
                    self.copy(self.terms.at[0], t, way).wait_send()

    def total(self, own, at):
        out = own
        for way in (1, -1):
            sums = self.sums[0 if way > 0 else 1][self.wide - 1, at, :].astype(F32)
            out = out + jnp.where(self.first(way), 0.0, sums)
        return out


class WeightSum:
    def __init__(self, team, part, came, mine, near, last, out, send, recv):
        self.team, self.part, self.came, self.mine, self.near = team, part, came, mine, near
        self.last, self.out, self.send, self.recv = last, out, send, recv
        self.size = part.shape[1] // 2

    def half(self, core):
        return pl.ds(pl.multiple_of(core * self.size, self.size), self.size)

    def swap(self):
        other = self.part.at[:, self.half(1 - self.team.seq)]
        return push(other, self.came, self.send.at[0], self.recv.at[0], self.team.sibling)

    def give(self, k):
        other = self.team.beside(k)
        return push(self.mine.at[other], self.near.at[k], self.send.at[k], self.recv.at[k], {"narrow": other})

    def back(self):
        at = self.team.narrow
        return push(self.last.at[0], self.last.at[1], self.send.at[at], self.recv.at[at], self.team.sibling)

    def first(self):
        self.swap().start()

    def second(self):
        self.swap().wait_recv()
        for n in range(self.team.narrow):
            own = self.part[n, self.half(self.team.seq), :].astype(F32)
            self.mine[n] = (own + self.came[n].astype(F32)).astype(BF)
        for k in range(1, self.team.narrow):
            self.give(k).start()

    def third(self):
        total = self.mine[self.team.me].astype(F32)
        for k in range(1, self.team.narrow):
            self.give(k).wait_recv()
            total = total + self.near[k].astype(F32)
        self.last[0] = total.astype(BF)
        self.back().start()
        self.out[self.half(self.team.seq), :] = self.last[0].astype(F32)

    def fourth(self):
        self.back().wait_recv()
        self.out[self.half(1 - self.team.seq), :] = self.last[1].astype(F32)

    def sent(self):
        self.swap().wait_send()
        self.back().wait_send()
        for k in range(1, self.team.narrow):
            self.give(k).wait_send()


def head_kernel(
    plan, kv_heads, qw, x_ref, g_ref, w_ref, gains_ref, cos_ref, sin_ref, marks_ref, wg_ref, wu_ref,
    h_out, q_out, own_out, kx, vx, w_out, gains_out, g_out, side_out, gu_out,
    x_buf, marks, side_buf, side_send, side_recv, w_buf, kv_buf, g_buf, gain_buf,
    x_send, x_recv, x_stay, w_send, w_recv, w_on_send, w_on_recv, gain_send, gain_recv,
    g_send, g_recv, kv_send, kv_recv, kv_on_send, kv_on_recv, keep_sem, cut_sem, *chain_sems
):
    group, wide, chunk, cw, own = plan.group, plan.wide, plan.chunk, plan.cw, plan.own
    team = Group(plan)
    narrow, seq, me = team.narrow, team.seq, team.me
    z = lax.axis_index("wide")
    part = x_ref.shape[3]
    d = part * narrow
    width = w_ref.shape[1]
    fold = part // 2
    chain = Chain(plan, g_buf, chain_sems)
    greet([team.member(k) for k in range(1, group)] + [along_wide(plan, r) for r in range(1, wide)])

    def spot(ref, slot, source):
        rows = pl.ds(pl.multiple_of((source // narrow) * cw, cw), cw)
        return ref.at[slot, rows, pl.ds(pl.multiple_of(lax.rem(source, narrow) * part, part), part)]

    def chunk_for(device):
        return jnp.where(seq == 0, device, group - 1 - device)

    def x_to(r, k):
        src = x_ref.at[chunk_for(team.device(k)), lax.rem(z + r, wide)]
        return push(src, spot(x_buf, r, team.index), x_send.at[r, k], x_recv.at[r, k], team.member(k))

    def x_from(r, k):
        src = x_ref.at[0, 0]
        return push(src, spot(x_buf, r, team.device(-k)), x_send.at[r, k], x_recv.at[r, k], team.member(k))

    def x_own(r):
        src = x_ref.at[chunk_for(team.index), lax.rem(z + r, wide)]
        return pltpu.make_async_copy(src, spot(x_buf, r, team.index), x_stay.at[r])

    def x_start(r):
        for k in range(1, group):
            x_to(r, k).start()
        x_own(r).start()

    def g_to(k):
        src = g_ref.at[chunk_for(team.device(k))]
        return push(src, spot(g_buf, z, team.index), g_send.at[k], g_recv.at[k], team.member(k))

    def w_rows(n, core):
        return w_buf.at[pl.ds(pl.multiple_of(n * part + core * fold, fold), fold)]

    def w_to(k):
        src = w_ref.at[pl.ds(pl.multiple_of(seq * fold, fold), fold)]
        return push(src, w_rows(me, seq), w_send.at[k], w_recv.at[k], {"narrow": team.beside(k)})

    def w_from(k):
        n = team.beside(-k)
        return push(w_rows(n, seq), w_rows(n, seq), w_send.at[k], w_recv.at[k], {"narrow": n})

    def w_on(k, core):
        n = team.beside(-k)
        return push(w_rows(n, core), w_rows(n, core), w_on_send.at[k], w_on_recv.at[k], team.sibling)

    def side_to(r, slot):
        mine = w_ref.at[:, qw:]
        return push(mine, side_buf.at[slot], side_send.at[r], side_recv.at[r], along_wide(plan, r))

    def gain_to(k, slot):
        return push(gains_ref, gain_buf.at[slot], gain_send.at[k], gain_recv.at[k], {"narrow": team.beside(k)})

    for k in range(1, group):
        g_to(k).start()
    g_stay = pltpu.make_async_copy(g_ref.at[chunk_for(team.index)], spot(g_buf, z, team.index), keep_sem.at[0])
    g_stay.start()
    for k in range(1, narrow):
        w_to(k).start()
        gain_to(k, me).start()
    x_start(0)
    if wide > 1:
        x_start(1)
    for r in range(1, wide):
        side_to(r, z).start()
    side_buf[z] = w_ref[:, qw:]
    w_buf[pl.ds(pl.multiple_of(me * part, part), part), :] = w_ref[...]
    gain_buf[me] = gains_ref[...]
    for k in range(1, narrow):
        w_from(k).wait_recv()
        w_on(k, seq).start()
    g_stay.wait()
    for k in range(1, group):
        push(
            g_ref.at[0], spot(g_buf, z, team.device(-k)), g_send.at[k], g_recv.at[k], team.member(k)
        ).wait_recv()
    chain.go(1)
    for k in range(1, narrow):
        gain_to(k, team.beside(-k)).wait_recv()
        w_on(k, 1 - seq).wait_recv()
    gain_one = jnp.concatenate([gain_buf[n, 0:1] for n in range(narrow)], axis=1)
    gains_out[...] = gain_buf[...]
    w_keep = pltpu.make_async_copy(w_buf, w_out, keep_sem.at[1])
    w_keep.start()
    ff = wg_ref.shape[1]
    half = pl.ds(pl.multiple_of(seq * fold, fold), fold)
    cuts = [
        pltpu.make_async_copy(wg_ref.at[half], gu_out.at[:, 0:ff], cut_sem.at[0]),
        pltpu.make_async_copy(wu_ref.at[half], gu_out.at[:, ff : 2 * ff], cut_sem.at[1]),
    ]
    for copy in cuts:
        copy.start()

    def kv_rows(core, n, r):
        return kv_buf.at[core, n, pl.ds(pl.multiple_of(r * own, own), own)]

    def kv_to(r, k):
        mine = kv_rows(seq, me, r)
        return push(mine, mine, kv_send.at[r, k], kv_recv.at[r, k], {"narrow": team.beside(k)})

    def kv_from(r, k):
        theirs = kv_rows(seq, team.beside(-k), r)
        return push(theirs, theirs, kv_send.at[r, k], kv_recv.at[r, k], {"narrow": team.beside(k)})

    def kv_on(k, core):
        slot = kv_buf.at[core, team.beside(-k)]
        return push(slot, slot, kv_on_send.at[k], kv_on_recv.at[k], team.sibling)

    @pl.loop(0, wide)
    def _(r):
        x_own(r).wait()
        for k in range(1, group):
            x_from(r, k).wait_recv()
        for later in range(2, wide):
            @pl.when(r == later - 2)
            def _():
                x_start(later)
        at = pl.ds(pl.multiple_of(r * own, own), own)
        low = x_buf[r]
        x = low.astype(F32)
        mean = jnp.mean(x * x, axis=1, keepdims=True)
        h = (x * lax.rsqrt(mean + EPS) * gain_one).astype(BF)
        h_out[at, :] = h
        t = jnp.dot(h, w_buf[...], preferred_element_type=F32)
        lane = lax.broadcasted_iota(jnp.int32, t.shape, 1)
        plain = (lane >= qw) & (lane % 128 >= HD)
        out = t * widen(cos_ref[at, :], width) + turn(t, 1.0) * widen(sin_ref[at, :], width)
        out = jnp.where(plain, t, out)
        q_out[at, :] = (out[:, :qw] * (HD ** -0.5)).astype(BF)
        kv_buf[seq, me, at, :] = out[:, qw:].astype(BF)
        for k in range(1, narrow):
            kv_to(r, k).start()

        @pl.when(r == min(1, wide - 1))
        def _():
            chain.arrive(1)
            if wide > 2:
                chain.go(2)

    kv_on(0, seq).start()
    own_out[...] = x_buf[0]
    if wide > 2:
        chain.arrive(2)
    if wide > 3:
        chain.go(3)
    for k in range(1, narrow):
        for r in range(wide):
            kv_from(r, k).wait_recv()
        kv_on(k, seq).start()
    for k in range(narrow):
        kv_on(k, 1 - seq).wait_recv()

    feature = lax.broadcasted_iota(jnp.int32, (cw, 128), 1)
    ones = jnp.where(feature < 3, 1.0, 0.0).astype(BF)
    spread = lax.broadcasted_iota(jnp.int32, (marks_ref.shape[0], 128), 0) + HD
    target = lax.broadcasted_iota(jnp.int32, (marks_ref.shape[0], 128), 1)
    spread = jnp.where(spread == target, 1.0, 0.0).astype(BF)

    @pl.loop(0, 2 * group)
    def _(c):
        columns = pl.ds(pl.multiple_of(c * chunk, chunk), chunk)
        marks[...] = lax.dot_general(marks_ref[:, columns], spread, TN, preferred_element_type=F32).astype(BF)
        late = c >= group
        owner = jnp.where(late, 2 * group - 1 - c, c)
        for r in range(wide):
            block = pl.ds(pl.multiple_of(lax.rem(z + r, wide) * cw, cw), cw)
            at = pl.ds(pl.multiple_of(c * chunk + lax.rem(z + r, wide) * cw, cw), cw)
            source = pl.ds(pl.multiple_of(r * own + jnp.where(late, cw, 0), cw), cw)
            for g in range(kv_heads):
                kv = kv_buf[owner // narrow, lax.rem(owner, narrow), source, g * 128 : (g + 1) * 128]
                kx[g, at, :] = jnp.where(feature < HD, kv, marks[block, :])
                vx[g, at, :] = jnp.where(feature < HD, ones, kv)

    for h in range(3, wide):
        chain.arrive(h)
        if h + 1 < wide:
            chain.go(h + 1)
    for r in range(1, wide):
        side_to(r, lax.rem(z - r + wide, wide)).wait_recv()
        side_to(r, z).wait_send()
    side_out[...] = side_buf[:, half, :]
    keep = [
        pltpu.make_async_copy(g_buf.at[near_of(plan, z, p)], g_out.at[p], keep_sem.at[2 + p]) for p in range(wide)
    ]
    for copy in keep:
        copy.start()
    chain.finish()
    for k in range(1, narrow):
        w_to(k).wait_send()
        w_on(k, seq).wait_send()
        gain_to(k, me).wait_send()
        for r in range(wide):
            kv_to(r, k).wait_send()
    for k in range(narrow):
        kv_on(k, seq).wait_send()
    for k in range(1, group):
        g_to(k).wait_send()
        for r in range(wide):
            x_to(r, k).wait_send()
    w_keep.wait()
    for copy in keep + cuts:
        copy.wait()


def head_call(plan, x, g, w, gains, cos, sin, marks, w_gate, w_up, qw, kv_heads):
    group, wide, cw, part = x.shape
    narrow = group // 2
    d = part * narrow
    width = w.shape[1]
    rows, own, total = plan.rows, plan.own, plan.total
    dma = pltpu.SemaphoreType.DMA
    whole = pl.BlockSpec(memory_space=pltpu.VMEM)
    hbm = pl.BlockSpec(memory_space=pl.ANY)
    keys = jax.ShapeDtypeStruct((kv_heads, total, 128), BF)
    return pl.pallas_call(
        functools.partial(head_kernel, plan, kv_heads, qw),
        in_specs=[hbm, hbm] + [whole] * 5 + [hbm, hbm],
        out_specs=[whole] * 5 + [hbm, whole, hbm, whole, hbm],
        out_shape=[
            jax.ShapeDtypeStruct((rows, d), BF),
            jax.ShapeDtypeStruct((rows, qw), BF),
            jax.ShapeDtypeStruct((own, d), BF),
            keys,
            keys,
            jax.ShapeDtypeStruct((d, width), BF),
            jax.ShapeDtypeStruct((narrow, 2, part), F32),
            jax.ShapeDtypeStruct((wide, own, d), BF),
            jax.ShapeDtypeStruct((wide, part // 2, width - qw), BF),
            jax.ShapeDtypeStruct((part // 2, 2 * w_gate.shape[1]), BF),
        ],
        scratch_shapes=[
            pltpu.VMEM((wide, own, d), BF),
            pltpu.VMEM((plan.chunk, 128), BF),
            pltpu.VMEM((wide, part, width - qw), BF),
            dma((wide,)), dma((wide,)),
            pltpu.VMEM((d, width), BF),
            pltpu.VMEM((2, narrow, rows, width - qw), BF),
            pltpu.VMEM((wide, own, d), BF),
            pltpu.VMEM((narrow, 2, part), F32),
            dma((wide, group)), dma((wide, group)), dma((wide,)),
            dma((narrow,)), dma((narrow,)), dma((narrow,)), dma((narrow,)), dma((narrow,)), dma((narrow,)),
            dma((group,)), dma((group,)),
            dma((wide, narrow)), dma((wide, narrow)), dma((narrow,)), dma((narrow,)),
            dma((2 + wide,)), dma((2,)),
        ] + [dma((wide,))] * 4,
        cost_estimate=pl.CostEstimate(
            flops=60 * rows * d * width, bytes_accessed=8 * rows * d + 2 * d * width, transcendentals=rows
        ),
        compiler_params=pltpu.CompilerParams(
            vmem_limit_bytes=60 << 20, collective_id=4, has_side_effects=True
        ),
        name="head",
    )(x, g, w, gains, cos, sin, marks, w_gate, w_up)


def split_heads(block, heads, low):
    tiles = []
    for h in range(heads):
        tile = block[:, (h // 2) * 128 : (h // 2 + 1) * 128]
        if (h % 2 == 0) != low:
            tile = pltpu.roll(tile, HD, 1)
        tiles.append(tile)
    return tiles


def join_heads(tiles, low):
    rows = tiles[0].shape[0]
    lane = lax.broadcasted_iota(jnp.int32, (rows, 128), 1)
    pairs = []
    for h in range(0, len(tiles), 2):
        first, second = tiles[h], tiles[h + 1]
        if low:
            second = pltpu.roll(second, HD, 1)
        else:
            first = pltpu.roll(first, HD, 1)
        pairs.append(jnp.where(lane < HD, first, second))
    return jnp.concatenate(pairs, axis=1)


def forward_kernel(
    plan, kv_heads, heads, s_ref, q_ref, kx, vx, wo_ref, x_ref, wd_ref, o_ref, qe_ref, x2_ref, wd_out,
    terms, right, left, term_acc, wd_send, wd_recv, wd_on_send, wd_on_recv, wd_keep, *sems
):
    wide, cw, chunk, own = plan.wide, plan.cw, plan.chunk, plan.own
    rows, width = heads * cw, heads * HD
    z = lax.axis_index("wide")
    team = Group(plan)
    index = team.index
    unit, g = pl.program_id(0), pl.program_id(1)
    last_g = kv_heads - 1
    piece, half = wide - 1 - unit // 2, lax.rem(unit, 2)
    w = near_of(plan, z, piece)
    r = lax.rem(w - z + wide, wide)
    c = jnp.where(half == 1, 2 * plan.group - 1 - index, index)
    low_rows = pl.ds(pl.multiple_of(half * cw, cw), cw)
    columns = pl.ds(pl.multiple_of(g * width, width), width)

    attn = Sums(plan, terms, right, left, sems)

    def out_rows(n):
        return pl.ds(pl.multiple_of((n * kv_heads + g) * width, width), width)

    fold = wd_ref.shape[0] // 2

    def wd_rows(n, core):
        return wd_out.at[n, pl.ds(pl.multiple_of(core * fold, fold), fold)]

    def wd_to(k):
        mine = wd_ref.at[pl.ds(pl.multiple_of(team.seq * fold, fold), fold)]
        return push(mine, wd_rows(team.me, team.seq), wd_send.at[k], wd_recv.at[k], {"narrow": team.beside(k)})

    def wd_from(k):
        theirs = wd_rows(team.beside(-k), team.seq)
        return push(theirs, theirs, wd_send.at[k], wd_recv.at[k], {"narrow": team.beside(k)})

    def wd_on(k, core):
        rows_of = wd_rows(team.beside(-k), core)
        return push(rows_of, rows_of, wd_on_send.at[k], wd_on_recv.at[k], team.sibling)

    wd_own = pltpu.make_async_copy(wd_ref, wd_out.at[team.me], wd_keep)

    @pl.when((unit == 0) & (g == 0))
    def _():
        others = [team.member(k) for k in range(1, plan.group)]
        greet(others + [along_wide(plan, k) for k in range(1, wide)])
        for k in range(1, team.narrow):
            wd_to(k).start()
        wd_own.start()

    for k in range(1, team.narrow):
        @pl.when((unit == 2 * wide - (3 if k == 1 else 2)) & (g == 0))
        def _():
            wd_from(k).wait_recv()
            wd_on(k, team.seq).start()

    lane = lax.broadcasted_iota(jnp.int32, (cw, 128), 1)
    token = c * chunk + w * cw + lax.broadcasted_iota(jnp.int32, (cw, 128), 0)
    segment = (token >= s_ref[0]).astype(jnp.int32) + (token >= s_ref[1]).astype(jnp.int32)
    mark = jnp.where(lane == HD + segment, 1.0, 0.0)
    block = q_ref[pl.ds(pl.multiple_of(r * own + half * cw, cw), cw), columns]
    tiles = split_heads(block.astype(F32), heads, True)
    q32 = jnp.concatenate([jnp.where(lane < HD, t, mark) for t in tiles], axis=0)
    q = q32.astype(BF)

    def step(j, carry, diagonal=False):
        top, acc = carry
        at = pl.ds(pl.multiple_of(j * chunk, chunk), chunk)
        s = lax.dot_general(q, kx[g, at, :], NT, preferred_element_type=F32)
        if diagonal:
            row = lax.broadcasted_iota(jnp.int32, (rows, chunk), 0) % cw + w * cw
            col = lax.broadcasted_iota(jnp.int32, (rows, chunk), 1)
            s = jnp.where(col <= row, s, NEG)
        new = jnp.maximum(top, jnp.max(s, axis=1, keepdims=True))
        p = jnp.exp(s - new).astype(BF)
        acc = acc * jnp.exp(top - new) + jnp.dot(p, vx[g, at, :], preferred_element_type=F32)
        return new, acc

    start = (jnp.full((rows, 1), NEG, F32), jnp.zeros((rows, 128), F32))
    carry = lax.fori_loop(0, c, step, start)
    top, acc = step(c, carry, True)
    total = acc[:, 0:1]
    out = acc / total
    out = join_heads([out[h * cw : (h + 1) * cw] for h in range(heads)], False).astype(BF)
    o_ref[w, low_rows, columns] = out
    first, second, third = pieces_of(-(top + jnp.log(total)))
    wide_lane = lax.broadcasted_iota(jnp.int32, (rows, 128), 1)
    qe = jnp.where(wide_lane == HD + 3, first, q32)
    qe = jnp.where(wide_lane == HD + 4, second, qe)
    qe = jnp.where(wide_lane == HD + 5, third, qe)
    qe_ref[r, g, half] = qe.astype(BF)

    term = jnp.concatenate(
        [jnp.dot(out, wo_ref[out_rows(n), :], preferred_element_type=F32) for n in range(plan.group // 2)], axis=1
    )

    @pl.when(g == 0)
    def _():
        term_acc[...] = term

    @pl.when(g > 0)
    def _():
        term_acc[...] += term

    @pl.when((g == last_g) & (piece == 0))
    def _():
        x2_ref[low_rows, :] = x_ref[low_rows, :].astype(F32) + term_acc[...]

    @pl.when((g == last_g) & (piece > 0))
    def _():
        terms[piece, low_rows, :] = term_acc[...].astype(BF)

    for t in range(1, wide):
        @pl.when((g == last_g) & (unit == 2 * t - 1))
        def _():
            attn.go(t)

    @pl.when((unit == 2 * wide - 1) & (g == last_g))
    def _():
        attn.finish()
        tall = min(32, own)

        @pl.loop(0, own // tall)
        def _(b):
            at = pl.ds(pl.multiple_of(b * tall, tall), tall)
            x2_ref[at, :] = attn.total(x2_ref[at, :], at)

        wd_own.wait()
        for k in range(1, team.narrow):
            wd_on(k, 1 - team.seq).wait_recv()
            wd_to(k).wait_send()
            wd_on(k, team.seq).wait_send()


def forward_call(plan, starts, q, kx, vx, w_o, x, w_down, heads):
    kv_heads, total, _ = kx.shape
    own, d = x.shape
    wide, rows, cw = plan.wide, plan.rows, plan.cw
    qw = q.shape[1]
    pairs = kv_heads * heads * total * rows // 2
    fixed = lambda a: pl.BlockSpec(a.shape, lambda u, g: (0,) * a.ndim, pipeline_mode=pl.Buffered(1))
    given = [q, kx, vx, w_o, x]
    outs = [
        jax.ShapeDtypeStruct((wide, own, qw), BF),
        jax.ShapeDtypeStruct((wide, kv_heads, 2, heads * cw, 128), BF),
        jax.ShapeDtypeStruct((own, d), F32),
    ]
    buffer = pltpu.VMEM((wide, own, d), BF)
    sems = pltpu.SemaphoreType.DMA((wide,))
    return pl.pallas_call(
        functools.partial(forward_kernel, plan, kv_heads, heads),
        grid=(2 * wide, kv_heads),
        in_specs=[pl.BlockSpec(memory_space=pltpu.SMEM)] + [fixed(a) for a in given]
        + [pl.BlockSpec(memory_space=pl.ANY)],
        out_specs=[fixed(a) for a in outs] + [pl.BlockSpec(memory_space=pl.ANY)],
        out_shape=outs + [jax.ShapeDtypeStruct((plan.group // 2, *w_down.shape), BF)],
        scratch_shapes=[buffer] * 3 + [pltpu.VMEM((cw, d), F32)]
        + [pltpu.SemaphoreType.DMA((plan.group // 2,))] * 4 + [pltpu.SemaphoreType.DMA] + [sems] * 4,
        cost_estimate=pl.CostEstimate(
            flops=16 * pairs * HD, bytes_accessed=8 * kv_heads * total * 128, transcendentals=pairs
        ),
        compiler_params=pltpu.CompilerParams(
            vmem_limit_bytes=56 << 20, collective_id=5, has_side_effects=True
        ),
        name="attention_forward",
    )(starts, *given, w_down)


def ffn_kernel(
    plan, x2_ref, gain_ref, g_ref, wg_ref, wu_ref, wd_ref,
    dg_ref, du_ref, h_out, dn_ref, dx_ref, gain_out, grad_out,
    h_buf, in_buf, out_buf, dn_acc, dh_acc, own_dh, act_buf, g_buf, grad_buf, rs_send, rs_recv, grad_sem, *chain_sems
):
    wide, narrow = plan.wide, plan.group // 2
    own, d = x2_ref.shape
    part = d // narrow
    piece, step = pl.program_id(0), pl.program_id(1)
    last = pl.num_programs(1) - 1
    tall = min(32, own)

    z = lax.axis_index("wide")
    owner = near_of(plan, z, piece)

    chain = Chain(plan, h_buf, chain_sems)

    def give(device):
        return push(out_buf.at[device], in_buf.at[z], rs_send.at[device], rs_recv.at[z], {"wide": device})

    @pl.when((piece == 0) & (step == 0))
    def _():
        greet([along_wide(plan, r) for r in range(1, wide)])

        @pl.loop(0, own // tall)
        def _(b):
            at = pl.ds(pl.multiple_of(b * tall, tall), tall)
            x2 = x2_ref[at, :]
            scale = lax.rsqrt(jnp.mean(x2 * x2, axis=1, keepdims=True) + EPS)
            h_buf[z, at, :] = (x2 * scale * gain_ref[...]).astype(BF)

        chain.go(1)

    for h in range(1, wide):
        @pl.when((piece == h) & (step == 0))
        def _():
            chain.arrive(h)
            if h + 1 < wide:
                chain.go(h + 1)

    @pl.when(step == 0)
    def _():
        h_out[...] = h_buf[owner]
        g_buf[pl.ds(pl.multiple_of(piece * own, own), own), :] = g_ref[...]

    h = h_buf[owner]
    wg, wu = wg_ref[...], wu_ref[...]
    gate = jnp.dot(h, wg, preferred_element_type=F32)
    up = jnp.dot(h, wu, preferred_element_type=F32)
    d_act = jnp.zeros_like(gate)
    for n in range(narrow):
        d_act += lax.dot_general(
            g_ref[:, n * part : (n + 1) * part], wd_ref[n], NT, preferred_element_type=F32
        )
    sig = jax.nn.sigmoid(gate)
    silu = gate * sig
    act = (silu * up).astype(BF)
    dg = (d_act * up * sig * (1.0 + gate * (1.0 - sig))).astype(BF)
    du = (d_act * silu).astype(BF)
    tile = act.shape[1]
    act_buf[pl.ds(pl.multiple_of(piece * own, own), own), pl.ds(pl.multiple_of(step * tile, tile), tile)] = act
    dg_ref[...] = dg
    du_ref[...] = du
    dh = lax.dot_general(dg, wg, NT, preferred_element_type=F32) + lax.dot_general(
        du, wu, NT, preferred_element_type=F32
    )

    @pl.when(step == 0)
    def _():
        dh_acc[...] = dh

    @pl.when(step > 0)
    def _():
        dh_acc[...] += dh

    for n in range(narrow):
        at = slice(n * part, (n + 1) * part)
        down = jnp.dot(act, wd_ref[n], preferred_element_type=F32)

        @pl.when(step == 0)
        def _():
            dn_acc[:, at] = down

        @pl.when(step > 0)
        def _():
            dn_acc[:, at] += down

    @pl.when(step == last)
    def _():
        dn_ref[0] = dn_acc[...].astype(BF)

    @pl.when((step == last) & (piece == 0))
    def _():
        own_dh[...] = dh_acc[...]

    @pl.when((step == last) & (piece > 0))
    def _():
        out_buf[owner] = dh_acc[...].astype(BF)
        give(owner).start()

    @pl.when((step == last) & (piece == wide - 1))
    def _():
        @pl.loop(0, last + 1)
        def _(t):
            at = pl.ds(pl.multiple_of(t * tile, tile), tile)
            keep = pltpu.make_async_copy(grad_buf, grad_out.at[:, at, :], grad_sem)

            @pl.when(t > 0)
            def _():
                keep.wait()

            for n in range(narrow):
                grad_buf[n] = lax.dot_general(
                    act_buf[:, at], g_buf[:, n * part : (n + 1) * part], TN, preferred_element_type=F32
                ).astype(BF)
            keep.start()

        for p in range(1, wide):
            other = near_of(plan, z, p)
            push(out_buf.at[z], in_buf.at[other], rs_send.at[z], rs_recv.at[other], {"wide": other}).wait_recv()
        gain_out[...] = jnp.zeros_like(gain_out)

        @pl.loop(0, own // tall)
        def _(b):
            at = pl.ds(pl.multiple_of(b * tall, tall), tall)
            dh2 = own_dh[at, :]
            for p in range(1, wide):
                dh2 = dh2 + in_buf[near_of(plan, z, p), at, :].astype(F32)
            x2 = x2_ref[at, :]
            scale = lax.rsqrt(jnp.mean(x2 * x2, axis=1, keepdims=True) + EPS)
            z2 = x2 * scale
            gain_out[...] += jnp.sum(dh2 * z2, axis=0, keepdims=True)
            dz2 = dh2 * gain_ref[...]
            inner = jnp.mean(dz2 * z2, axis=1, keepdims=True)
            dx_ref[at, :] = g_buf[at, :].astype(F32) + scale * (dz2 - z2 * inner)

        chain.finish()
        for p in range(1, wide):
            give(near_of(plan, z, p)).wait_send()
        pltpu.make_async_copy(grad_buf, grad_out.at[:, pl.ds(0, tile), :], grad_sem).wait()


def ffn_call(plan, x2, gain, g_rows, w_gu, w_dn):
    own, d = x2.shape
    wide, rows = plan.wide, plan.rows
    narrow, ff, part = w_dn.shape
    tile = min(512, ff)
    tiles = ff // tile
    fixed = lambda shape: pl.BlockSpec(shape, lambda p, f: (0,) * len(shape), pipeline_mode=pl.Buffered(1))
    tall = pl.BlockSpec((own, tile), lambda p, f: (p, f))
    hidden = jax.ShapeDtypeStruct((rows, ff), BF)
    buffer = pltpu.VMEM((wide, own, d), BF)
    sems = pltpu.SemaphoreType.DMA((wide,))
    return pl.pallas_call(
        functools.partial(ffn_kernel, plan),
        grid=(wide, tiles),
        in_specs=[
            fixed((own, d)),
            fixed((1, d)),
            pl.BlockSpec((own, d), lambda p, f: (p, 0)),
            pl.BlockSpec((d, tile), lambda p, f: (0, f)),
            pl.BlockSpec((d, tile), lambda p, f: (0, tiles + f)),
            pl.BlockSpec((narrow, tile, part), lambda p, f: (0, f, 0)),
        ],
        out_specs=[
            tall, tall,
            pl.BlockSpec((own, d), lambda p, f: (p, 0)),
            pl.BlockSpec((1, own, d), lambda p, f: (p, 0, 0)),
            fixed((own, d)),
            fixed((1, d)),
            pl.BlockSpec(memory_space=pl.ANY),
        ],
        out_shape=[
            hidden, hidden,
            jax.ShapeDtypeStruct((rows, d), BF),
            jax.ShapeDtypeStruct((wide, own, d), BF),
            jax.ShapeDtypeStruct((own, d), F32),
            jax.ShapeDtypeStruct((1, d), F32),
            jax.ShapeDtypeStruct((narrow, ff, part), BF),
        ],
        scratch_shapes=[
            buffer, buffer, buffer,
            pltpu.VMEM((own, d), F32), pltpu.VMEM((own, d), F32), pltpu.VMEM((own, d), F32),
            pltpu.VMEM((rows, ff), BF), pltpu.VMEM((rows, d), BF), pltpu.VMEM((narrow, tile, part), BF),
            sems, sems, pltpu.SemaphoreType.DMA, sems, sems, sems, sems,
        ],
        cost_estimate=pl.CostEstimate(
            flops=16 * rows * d * ff, bytes_accessed=6 * d * ff + 12 * rows * d, transcendentals=rows * ff
        ),
        compiler_params=pltpu.CompilerParams(
            vmem_limit_bytes=60 << 20, collective_id=1, has_side_effects=True
        ),
        name="feed_forward",
    )(x2, gain, g_rows, w_gu, w_gu, w_dn)


def weights_kernel(
    plan, tiles, dx2_ref, h_ref, dg_ref, du_ref, down_ref, x2_ref,
    gate_out, up_out, db_out, res_out,
    db_buf, right, left, keep_sem, *sems
):
    wide = plan.wide
    step = pl.program_id(0)
    last = pl.num_programs(0) - 1
    chain = Chain(plan, db_buf, sems[:4])
    down = Sums(plan, down_ref, right, left, sems[4:])
    keep = pltpu.make_async_copy(db_buf, db_out, keep_sem)

    @pl.when(step == 0)
    def _():
        db_buf[lax.axis_index("wide")] = dx2_ref[...].astype(BF)
        greet([along_wide(plan, k) for k in range(1, wide)])
        chain.go(1)

    @pl.when(step < tiles)
    def _():
        gate_out[...] = lax.dot_general(h_ref[...], dg_ref[...], TN, preferred_element_type=F32).astype(BF)

    @pl.when(step >= tiles)
    def _():
        up_out[...] = lax.dot_general(h_ref[...], du_ref[...], TN, preferred_element_type=F32).astype(BF)

    for h in range(1, wide):
        @pl.when(step == min(last, h * (tiles + 1) - 1))
        def _():
            chain.arrive(h)
            if h + 1 < wide:
                chain.go(h + 1)
            down.go(h)

    @pl.when(step == last)
    def _():
        keep.start()
        down.finish()
        tall = min(32, x2_ref.shape[0])

        @pl.loop(0, x2_ref.shape[0] // tall)
        def _(b):
            at = pl.ds(pl.multiple_of(b * tall, tall), tall)
            res_out[at, :] = down.total(x2_ref[at, :] + down_ref[0, at, :].astype(F32), at).astype(BF)

        chain.finish()
        keep.wait()


def weights_call(plan, dx2, h, d_gate, d_up, down, x2):
    own, d = dx2.shape
    rows, ff = d_gate.shape
    wide = plan.wide
    tiles = 4
    d_tile = d // tiles
    fixed = lambda a: pl.BlockSpec(a.shape, lambda s: (0,) * a.ndim, pipeline_mode=pl.Buffered(1))
    first = lambda s: jnp.minimum(s, tiles - 1)
    second = lambda s: jnp.clip(s - tiles, 0, tiles - 1)
    sems = pltpu.SemaphoreType.DMA((wide,))
    return pl.pallas_call(
        functools.partial(weights_kernel, plan, tiles),
        grid=(2 * tiles,),
        in_specs=[
            fixed(dx2),
            pl.BlockSpec((rows, d_tile), lambda s: (0, lax.rem(s, tiles))),
            fixed(d_gate), fixed(d_up), fixed(down), fixed(x2),
        ],
        out_specs=[
            pl.BlockSpec((d_tile, ff), lambda s: (first(s), 0)),
            pl.BlockSpec((d_tile, ff), lambda s: (second(s), 0)),
            pl.BlockSpec(memory_space=pl.ANY),
            pl.BlockSpec((own, d), lambda s: (0, 0), pipeline_mode=pl.Buffered(1)),
        ],
        out_shape=[
            jax.ShapeDtypeStruct((d, ff), BF),
            jax.ShapeDtypeStruct((d, ff), BF),
            jax.ShapeDtypeStruct((wide, own, d), BF),
            jax.ShapeDtypeStruct((own, d), BF),
        ],
        scratch_shapes=[pltpu.VMEM((wide, own, d), BF)] * 3 + [pltpu.SemaphoreType.DMA] + [sems] * 8,
        cost_estimate=pl.CostEstimate(
            flops=8 * rows * d * ff, bytes_accessed=20 * rows * d, transcendentals=0
        ),
        compiler_params=pltpu.CompilerParams(
            vmem_limit_bytes=60 << 20, collective_id=6, has_side_effects=True
        ),
        name="weight_gradients",
    )(dx2, h, d_gate, d_up, down, x2)


def backward_kernel(
    plan, kv_heads, heads, db_ref, qe_ref, kx, vx, o_ref, wo_ref, wq_ref, cos_ref, sin_ref, res_ref,
    dq_ref, sums, dh_ref, res_out, terms, right, left, term_acc, results,
    part_send, part_recv, keep_sem, *sems
):
    wide, cw, chunk, own = plan.wide, plan.cw, plan.chunk, plan.own
    rows = heads * cw
    width = heads * HD
    z = lax.axis_index("wide")
    team = Group(plan)
    index = team.index
    chain = Chain(plan, results, sems[:4])
    back = Sums(plan, terms, right, left, sems[4:])
    parts = Parts(plan, team, res_ref, results, part_send, part_recv, keep_sem.at[0])
    unit, g = pl.program_id(0), pl.program_id(1)
    last_unit, last_g = 2 * wide - 1, kv_heads - 1
    piece, half = wide - 1 - unit // 2, lax.rem(unit, 2)
    w = near_of(plan, z, piece)
    r = lax.rem(w - z + wide, wide)
    c = jnp.where(half == 1, 2 * plan.group - 1 - index, index)
    low_rows = pl.ds(pl.multiple_of(half * cw, cw), cw)

    @pl.when((unit == 0) & (g == 0))
    def _():
        others = [team.member(k) for k in range(1, plan.group)]
        greet(others + [along_wide(plan, k) for k in range(1, wide)])
        parts.start()

        @pl.loop(0, kv_heads * plan.total // chunk)
        def _(b):
            at = pl.ds(pl.multiple_of(lax.rem(b, plan.total // chunk) * chunk, chunk), chunk)
            sums[b // (plan.total // chunk), at, :] = jnp.zeros((chunk, 128), F32)

    @pl.when((unit == 1) & (g == last_g))
    def _():
        parts.wait()
        chain.go(1)

    for h in range(1, wide):
        late = {1: (3, 0), 2: (4, last_g), 3: (6, 0)}.get(h, (min(h + 3, last_unit), last_g))

        @pl.when((unit == late[0]) & (g == late[1]))
        def _():
            chain.arrive(h)
            if h + 1 < wide:
                chain.go(h + 1)

    lane = lax.broadcasted_iota(jnp.int32, (cw, 128), 1)
    columns = pl.ds(pl.multiple_of(g * width, width), width)
    part = wo_ref.shape[1]
    grad = jnp.zeros((cw, width), F32)
    for n in range(team.narrow):
        out_rows = pl.ds(pl.multiple_of((n * kv_heads + g) * width, width), width)
        grad += lax.dot_general(
            db_ref[w, low_rows, n * part : (n + 1) * part], wo_ref[out_rows, :], NT, preferred_element_type=F32
        )
    do = split_heads(grad.astype(BF).astype(F32), heads, False)
    o = split_heads(o_ref[w, low_rows, columns].astype(F32), heads, False)
    marked = []
    for one, other in zip(o, do):
        clean = jnp.where(lane >= HD, other, 0.0)
        first, second, third = pieces_of(-jnp.sum(one * clean, axis=1, keepdims=True))
        tile = jnp.where(lane == 0, first, clean)
        tile = jnp.where(lane == 1, second, tile)
        marked.append(jnp.where(lane == 2, third, tile))
    dox32 = jnp.concatenate(marked, axis=0)
    wide_lane = lax.broadcasted_iota(jnp.int32, (rows, 128), 1)
    dox = dox32.astype(BF)
    do_clean = jnp.where(wide_lane >= HD, dox32, 0.0).astype(BF)
    q = qe_ref[r, g, half]
    q_clean = jnp.where(wide_lane < HD, q.astype(F32), 0.0).astype(BF)

    def step(j, dq, diagonal=False):
        at = pl.ds(pl.multiple_of(j * chunk, chunk), chunk)
        key = kx[g, at, :]
        s = lax.dot_general(key, q, NT, preferred_element_type=F32)
        if diagonal:
            row = lax.broadcasted_iota(jnp.int32, (chunk, rows), 1) % cw + w * cw
            col = lax.broadcasted_iota(jnp.int32, (chunk, rows), 0)
            s = jnp.where(col <= row, s, NEG)
        p = jnp.exp(s)
        dp = lax.dot_general(vx[g, at, :], dox, NT, preferred_element_type=F32)
        ds = (p * dp).astype(BF)
        sums[g, at, :] += jnp.dot(ds, q_clean, preferred_element_type=F32) + jnp.dot(
            p.astype(BF), do_clean, preferred_element_type=F32
        )
        return dq + lax.dot_general(ds, key, TN, preferred_element_type=F32)

    dq = lax.fori_loop(0, c, step, jnp.zeros((rows, 128), F32))
    dq = step(c, dq, True) * (HD ** -0.5)
    dq = join_heads([dq[h * cw : (h + 1) * cw] for h in range(heads)], True)
    at = pl.ds(pl.multiple_of(r * own + half * cw, cw), cw)
    dq = dq * widen(cos_ref[at, :], width) + turn(dq, -1.0) * widen(sin_ref[at, :], width)
    dq = dq.astype(BF)
    dq_ref[at, columns] = dq

    term = lax.dot_general(dq, wq_ref[:, columns], NT, preferred_element_type=F32)

    @pl.when(g == 0)
    def _():
        term_acc[...] = term

    @pl.when(g > 0)
    def _():
        term_acc[...] += term

    @pl.when((g == last_g) & (piece == 0))
    def _():
        dh_ref[low_rows, :] = term_acc[...]

    @pl.when((g == last_g) & (piece > 0))
    def _():
        terms[piece, low_rows, :] = term_acc[...].astype(BF)

    for t in range(1, wide):
        @pl.when((g == last_g) & (unit == 2 * t - 1))
        def _():
            back.go(t)

    @pl.when((unit == last_unit) & (g == last_g))
    def _():
        keep = pltpu.make_async_copy(results, res_out, keep_sem.at[1])
        keep.start()
        back.finish()
        tall = min(32, own)

        @pl.loop(0, own // tall)
        def _(b):
            at = pl.ds(pl.multiple_of(b * tall, tall), tall)
            dh_ref[at, :] = back.total(dh_ref[at, :], at)

        chain.finish()
        parts.sent()
        keep.wait()


def backward_call(plan, db, qe, kx, vx, o, w_o, w_qkv, cos, sin, res, heads):
    kv_heads, total, _ = kx.shape
    _, own, d = db.shape
    wide, rows, cw = plan.wide, plan.rows, plan.cw
    qw = o.shape[2]
    pairs = kv_heads * heads * total * rows // 2
    fixed = lambda a: pl.BlockSpec(a.shape, lambda u, g: (0,) * a.ndim, pipeline_mode=pl.Buffered(1))
    hbm = pl.BlockSpec(memory_space=pl.ANY)
    given = [db, qe, kx, vx, o, w_o, w_qkv, cos, sin]
    outs = [
        jax.ShapeDtypeStruct((rows, qw), BF),
        jax.ShapeDtypeStruct((kv_heads, total, 128), F32),
        jax.ShapeDtypeStruct((own, d), F32),
    ]
    slots = (wide, plan.group, cw, d // (plan.group // 2))
    buffer = pltpu.VMEM((wide, own, d), BF)
    sems = pltpu.SemaphoreType.DMA((wide,))
    return pl.pallas_call(
        functools.partial(backward_kernel, plan, kv_heads, heads),
        grid=(2 * wide, kv_heads),
        in_specs=[fixed(a) for a in given[:6]]
        + [pl.BlockSpec((d, qw), lambda u, g: (0, 0), pipeline_mode=pl.Buffered(1)), fixed(cos), fixed(sin), fixed(res)],
        out_specs=[fixed(a) for a in outs] + [hbm],
        out_shape=outs + [jax.ShapeDtypeStruct(slots, BF)],
        scratch_shapes=[buffer] * 3 + [pltpu.VMEM((cw, d), F32), pltpu.VMEM(slots, BF)]
        + [pltpu.SemaphoreType.DMA((plan.group,))] * 2 + [pltpu.SemaphoreType.DMA((2,))] + [sems] * 8,
        cost_estimate=pl.CostEstimate(
            flops=36 * pairs * HD, bytes_accessed=12 * kv_heads * total * 128, transcendentals=pairs
        ),
        compiler_params=pltpu.CompilerParams(
            vmem_limit_bytes=60 << 20, collective_id=3, has_side_effects=True
        ),
        name="attention_backward",
    )(*given, res)


def tail_kernel(
    plan, kv_heads, sums_ref, h_hbm, dh_ref, gain2_ref, dx2_ref, x_ref, gain_ref, wkv_hbm,
    cos_ref, sin_ref, dq_ref, o_ref, db_hbm, got_out, gain_out, kv_out, q_out, o_out,
    h_ref, wkv_ref, db_buf, swap_out, swap_in, low, near_in, dkv, head_in, dh_acc, dx_low, every,
    gain_part, gain_in, gain_sum, gain_all,
    swap_sem, near_send, near_recv, head_send, head_recv, part_send, part_recv,
    gain_send, gain_recv, gain2_send, gain2_recv, own_sem, *more
):
    group, wide, chunk, cw, own = plan.group, plan.wide, plan.chunk, plan.cw, plan.own
    narrow = group // 2
    part = dx_low.shape[1] // narrow
    team = Group(plan)
    seq, me, z = team.seq, team.me, lax.axis_index("wide")
    device, member = team.device, team.member
    dx_chain = Chain(plan, every, more[:4])
    q_sum = WeightSum(team, *more[4:9], q_out, *more[9:11])
    kv_sum = WeightSum(team, *more[11:16], kv_out, *more[16:18])
    o_sum = WeightSum(team, *more[18:23], o_out, *more[23:25])
    q_part, kv_part, o_part = q_sum.part, kv_sum.part, o_sum.part

    greet([member(k) for k in range(1, group)] + [along_wide(plan, r) for r in range(1, wide)])

    def place(owner_seq, half, n):
        quarter = owner_seq if half == 0 else 3 - owner_seq
        return pl.ds(
            pl.multiple_of((quarter * narrow + (n if half == 0 else narrow - 1 - n)) * chunk, chunk), chunk
        )

    load_h = pltpu.make_async_copy(h_hbm, h_ref, own_sem.at[2])
    load_w = pltpu.make_async_copy(wkv_hbm, wkv_ref, own_sem.at[3])
    load_h.start()
    load_w.start()

    def swap(g):
        return push(swap_out.at[g], swap_in.at[g], swap_sem.at[0, g], swap_sem.at[1, g], team.sibling)

    def near(k, g):
        other = team.beside(k)
        return push(low.at[g, other], near_in.at[g, k], near_send.at[g, k], near_recv.at[g, k], {"narrow": other})

    def heads_to(r, g):
        columns = slice(g * 128, (g + 1) * 128)
        mine = dkv.at[r * own : (r + 1) * own, columns]
        return push(mine, head_in.at[r, :, columns], head_send.at[r, g], head_recv.at[r, g], along_wide(plan, r))

    for g in range(kv_heads):
        @pl.loop(0, narrow)
        def _(n):
            for half in range(2):
                swap_out[g, n, half] = sums_ref[g, place(1 - seq, half, n), :].astype(BF)

        swap(g).start()

    load_h.wait()
    for n in range(narrow):
        columns = slice(n * part, (n + 1) * part)
        q_part[n] = lax.dot_general(h_ref[:, columns], dq_ref[...], TN, preferred_element_type=F32).astype(BF)
    q_sum.first()

    for g in range(kv_heads):
        swap(g).wait_recv()

        @pl.loop(0, narrow)
        def _(n):
            for half in range(2):
                total = sums_ref[g, place(seq, half, n), :] + swap_in[g, n, half].astype(F32)
                low[g, n, half] = total.astype(BF)

        for k in range(1, narrow):
            near(k, g).start()

    lane = lax.broadcasted_iota(jnp.int32, (cw, 128), 1)
    for g in range(kv_heads):
        for k in range(1, narrow):
            near(k, g).wait_recv()
        for r in range(wide):
            at = pl.ds(pl.multiple_of(lax.rem(z + r, wide) * cw, cw), cw)
            for half in range(2):
                rows = slice((2 * r + half) * cw, (2 * r + half + 1) * cw)
                total = low[g, me, half, at, :].astype(F32)
                for k in range(1, narrow):
                    total = total + near_in[g, k, half, at, :].astype(F32)
                back = total * cos_ref[rows, :] + turn(total, -1.0) * sin_ref[rows, :]
                dkv[rows, g * 128 : (g + 1) * 128] = jnp.where(lane < HD, back, total).astype(BF)
        for r in range(1, wide):
            heads_to(r, g).start()

    q_sum.second()

    for n in range(narrow):
        columns = slice(n * part, (n + 1) * part)
        kv_part[n] = lax.dot_general(dkv[...], h_ref[:, columns], TN, preferred_element_type=F32).astype(BF)
    kv_sum.first()

    tile = part // 2
    load_w.wait()
    for r in range(wide):
        if r > 0:
            for g in range(kv_heads):
                heads_to(r, g).wait_recv()
        mine = dkv[0:own] if r == 0 else head_in[r]
        source = lax.rem(z - r + wide, wide)

        for b in range(group):
            at = slice(b * tile, (b + 1) * tile)
            more = lax.dot_general(mine, wkv_ref[b, source], NT, preferred_element_type=F32)
            dh_acc[:, at] = (dh_ref[:, at] if r == 0 else dh_acc[:, at]) + more

    gain_part[0:1, :] = jnp.zeros_like(gain2_ref[...])
    gain_part[1:2, :] = gain2_ref[...]
    tall = min(32, own)

    @pl.loop(0, own // tall)
    def _(b):
        at = pl.ds(pl.multiple_of(b * tall, tall), tall)
        dh1 = dh_acc[at, :]
        x = x_ref[at, :].astype(F32)
        scale = lax.rsqrt(jnp.mean(x * x, axis=1, keepdims=True) + EPS)
        z1 = x * scale
        gain_part[0:1, :] += jnp.sum(dh1 * z1, axis=0, keepdims=True)
        dz1 = dh1 * gain_ref[...]
        inner = jnp.mean(dz1 * z1, axis=1, keepdims=True)
        dx_low[at, :] = (dx2_ref[at, :] + scale * (dz1 - z1 * inner)).astype(BF)

    dx_parts = Parts(plan, team, dx_low, every, part_send, part_recv, own_sem.at[0])
    dx_parts.start()

    def gain_to(k):
        columns = pl.ds(pl.multiple_of(lax.rem(device(k), narrow) * part, part), part)
        return push(gain_part.at[:, columns], gain_in.at[k], gain_send.at[k], gain_recv.at[k], member(k))

    for k in range(1, group):
        gain_to(k).start()
    dx_parts.wait()
    dx_chain.go(1)
    kv_sum.second()

    rows = o_ref.shape[0] * o_ref.shape[1]
    for n in range(narrow):
        load = pltpu.make_async_copy(db_hbm.at[:, :, n * part : (n + 1) * part], db_buf, own_sem.at[4])
        load.start()
        load.wait()
        o_part[n] = lax.dot_general(
            o_ref[...].reshape(rows, -1), db_buf[...].reshape(rows, part), TN, preferred_element_type=F32
        ).astype(BF)
    o_sum.first()
    q_sum.third()

    gain = gain_part[:, pl.ds(pl.multiple_of(me * part, part), part)]
    for k in range(1, group):
        gain_to(k).wait_recv()
        gain = gain + gain_in[k]
    gain_sum[...] = gain

    def gain_on(r):
        return push(gain_sum, gain_all.at[r], gain2_send.at[r], gain2_recv.at[r], along_wide(plan, r))

    for r in range(1, wide):
        gain_on(r).start()
    dx_chain.arrive(1)
    if wide > 2:
        dx_chain.go(2)
    o_sum.second()
    kv_sum.third()
    q_sum.fourth()
    gain = gain_sum[...]
    for r in range(1, wide):
        gain_on(r).wait_recv()
        gain = gain + gain_all[r]
    gain_out[...] = gain
    for h in range(2, wide):
        dx_chain.arrive(h)
        if h + 1 < wide:
            dx_chain.go(h + 1)
        if h == 2:
            o_sum.third()
            kv_sum.fourth()
    o_sum.fourth()
    got_keep = pltpu.make_async_copy(every, got_out, own_sem.at[1])
    got_keep.start()

    dx_chain.finish()
    for g in range(kv_heads):
        swap(g).wait_send()
        for k in range(1, narrow):
            near(k, g).wait_send()
        for r in range(1, wide):
            heads_to(r, g).wait_send()
    for r in range(1, wide):
        gain_on(r).wait_send()
    dx_parts.sent()
    for k in range(1, group):
        gain_to(k).wait_send()
    for one in (q_sum, kv_sum, o_sum):
        one.sent()
    got_keep.wait()


def tail_call(plan, sums, h, dh, gain2, dx2, x, gain, w_kv, cos, sin, dq, o, db):
    kv_heads = sums.shape[0]
    own, d = dh.shape
    group, wide, chunk, cw = plan.group, plan.wide, plan.chunk, plan.cw
    narrow = group // 2
    part = d // narrow
    kv_width = kv_heads * 128
    dma = pltpu.SemaphoreType.DMA
    quarter = pltpu.VMEM((kv_heads, narrow, 2, chunk, 128), BF)
    slots = (wide, group, cw, part)

    def weight(height, across):
        half = pltpu.VMEM((narrow, height // 2, across), BF)
        ends = pltpu.VMEM((2, height // 2, across), BF)
        return [pltpu.VMEM((narrow, height, across), BF), half, half, half, ends] + [dma((narrow + 1,))] * 2

    given = [sums, h, dh, gain2, dx2, x, gain, w_kv, cos, sin, dq, o, db]
    qw = dq.shape[1]
    whole = pl.BlockSpec(memory_space=pltpu.VMEM)
    hbm = pl.BlockSpec(memory_space=pl.ANY)
    return pl.pallas_call(
        functools.partial(tail_kernel, plan, kv_heads),
        in_specs=[hbm if i in (1, 7, 12) else whole for i in range(len(given))],
        out_specs=[hbm] + [whole] * 4,
        out_shape=[
            jax.ShapeDtypeStruct(slots, BF),
            jax.ShapeDtypeStruct((2, part), F32),
            jax.ShapeDtypeStruct((kv_width, part), F32),
            jax.ShapeDtypeStruct((part, qw), F32),
            jax.ShapeDtypeStruct((qw, part), F32),
        ],
        scratch_shapes=[
            pltpu.VMEM(h.shape, BF), pltpu.VMEM(w_kv.shape, BF), pltpu.VMEM((wide, own, part), BF),
            quarter, quarter, quarter, quarter,
            pltpu.VMEM((plan.rows, kv_width), BF),
            pltpu.VMEM((wide, own, kv_width), BF),
            pltpu.VMEM((own, d), F32),
            pltpu.VMEM((own, d), BF),
            pltpu.VMEM(slots, BF),
            pltpu.VMEM((2, d), F32),
            pltpu.VMEM((group, 2, part), F32),
            pltpu.VMEM((2, part), F32),
            pltpu.VMEM((wide, 2, part), F32),
            dma((2, kv_heads)), dma((kv_heads, narrow)), dma((kv_heads, narrow)),
            dma((wide, kv_heads)), dma((wide, kv_heads)), dma((group,)), dma((group,)),
            dma((group,)), dma((group,)), dma((wide,)), dma((wide,)),
            dma((5,)),
        ] + [dma((wide,))] * 4 + weight(part, qw) + weight(kv_width, part) + weight(qw, part),
        cost_estimate=pl.CostEstimate(
            flops=200 * own * d * wide * kv_width, bytes_accessed=4 * sums.size, transcendentals=0
        ),
        compiler_params=pltpu.CompilerParams(
            vmem_limit_bytes=60 << 20, collective_id=2, has_side_effects=True
        ),
        name="input_gradient",
    )(*given)


def finish_kernel(plan, s_ref, res_ref, dx_ref, *refs):
    group, weights = plan.group, len(refs) // 2 - 1
    res_out, dx_out = refs[weights : weights + 2]
    for l in range(group):
        owner = jnp.where(s_ref[0] >= group // 2, group - 1 - l, l)
        res_out[l, 0] = res_ref[0, owner]
        dx_out[l, 0] = dx_ref[0, owner].astype(F32)
    for low, out in zip(refs[:weights], refs[weights + 2 :]):
        out[...] = low[...].astype(F32)


def finish_call(plan, scalars, result, dx, weights):
    wide, group, cw, part = result.shape
    cuts = 2 if cw % 64 == 0 else 1
    steps = wide * cuts
    slots = pl.BlockSpec((1, group, cw // cuts, part), lambda w, c, s: (w, 0, c, 0))
    tokens = pl.BlockSpec((group, 1, cw // cuts, part), lambda w, c, s: (0, w, c, 0))
    rows = [pl.BlockSpec((a.shape[0] // steps, a.shape[1]), lambda w, c, s: (w * cuts + c, 0)) for a in weights]
    shape = (group, wide, cw, part)
    size = result.size + sum(a.size for a in weights)
    out = pl.pallas_call(
        functools.partial(finish_kernel, plan),
        grid_spec=pltpu.PrefetchScalarGridSpec(
            num_scalar_prefetch=1,
            grid=(wide, cuts),
            in_specs=[slots, slots] + rows,
            out_specs=[tokens, tokens] + rows,
        ),
        out_shape=[jax.ShapeDtypeStruct(shape, BF), jax.ShapeDtypeStruct(shape, F32)]
        + [jax.ShapeDtypeStruct(a.shape, F32) for a in weights],
        cost_estimate=pl.CostEstimate(flops=2 * size, bytes_accessed=8 * size, transcendentals=0),
        compiler_params=pltpu.CompilerParams(vmem_limit_bytes=48 << 20),
        name="finish",
    )(scalars, result, dx, *weights)
    flat = (group * wide * cw, part)
    return [out[0].reshape(flat), out[1].reshape(flat)] + list(out[2:])


def half_of(weight, seq_index, seq_count):
    part = weight.shape[0] // seq_count
    return lax.dynamic_slice_in_dim(weight, seq_index * part, part, 0)


def body(
    tokens, attn_gain, w_query, w_key, w_value, w_out, ffn_gain, w_gate, w_up, w_down,
    segment_ids, token_mask, out_grad,
):
    seq_count = lax.axis_size("seq")
    narrow = lax.axis_size("narrow")
    wide = lax.axis_size("wide")
    group = seq_count * narrow
    seq_index = lax.axis_index("seq")
    narrow_index = lax.axis_index("narrow")
    wide_index = lax.axis_index("wide")
    index = seq_index * narrow + narrow_index
    total = segment_ids.shape[0]
    plan = Plan(total, group, wide)
    chunk, cw, rows, own = plan.chunk, plan.cw, plan.rows, plan.own
    d_part = tokens.shape[1]
    d = d_part * narrow
    qw = w_query.shape[1]
    kw = w_key.shape[1]
    kv_heads = kw // HD
    heads = qw // kw
    ff = w_gate.shape[1]

    starts = jnp.sum((segment_ids[None, :] < jnp.arange(1, 3)[:, None]).astype(jnp.int32), axis=1)
    start_one, start_two = starts[0], starts[1]
    scalars = jnp.reshape(index, (1,)).astype(jnp.int32)

    def gather_weight(weight):
        return lax.all_gather(half_of(weight, seq_index, seq_count), NS, axis=0, tiled=True)

    def scatter_grad(grad, *others):
        mine = after(lax.psum_scatter(grad.astype(BF), NS, scatter_dimension=0, tiled=True), *others)
        return lax.all_gather(mine, "seq", axis=0, tiled=True)

    def after(values, *others):
        return lax.optimization_barrier((values, *others))[0]

    w_kv = jnp.concatenate(
        [w_key.reshape(d_part, kv_heads, 1, HD), w_value.reshape(d_part, kv_heads, 1, HD)], axis=2
    ).reshape(d_part, 2 * kw)

    row = jnp.arange(rows, dtype=jnp.int32)
    row_chunk = jnp.where((row // cw) % 2 == 1, 2 * group - 1 - index, index)
    row_block = (row // own + wide_index) % wide
    row_token = row_chunk * chunk + row_block * cw + row % cw
    row_start = jnp.where(row_token >= start_two, start_two, jnp.where(row_token >= start_one, start_one, 0))
    row_pos = (row_token - row_start).astype(F32)
    frequency = THETA ** (-2.0 * jnp.arange(HD // 2, dtype=F32) / HD)
    angles = row_pos[:, None] * jnp.tile(frequency, 4)[None, :]
    cos, sin = jnp.cos(angles), jnp.sin(angles)

    feature = jnp.arange(16, dtype=jnp.int32)[:, None]
    closed = (segment_ids[None, :] != feature) | (token_mask[None, :] != 1)
    marks = jnp.where((feature < 3) & closed, NEG, jnp.where((feature >= 3) & (feature < 6), 1.0, 0.0)).astype(BF)

    mask = lax.dynamic_slice_in_dim(token_mask, seq_index * (group * chunk), group * chunk, 0)
    g_part = lax.dynamic_index_in_dim(out_grad.reshape(group, wide, cw, d_part), wide_index, 1, keepdims=False)
    mask = lax.dynamic_index_in_dim(mask.reshape(group, wide, cw), wide_index, 1, keepdims=False)
    g_part = jnp.where(mask[:, :, None] == 1, g_part, jnp.zeros_like(g_part))

    w_o = gather_weight(w_out)
    h_one, q, x_low, kx, vx, w_qkv, gains, g_rows, w_kv, w_gu = head_call(
        plan, tokens.reshape(group, wide, cw, d_part), g_part, jnp.concatenate([w_query, w_kv], axis=1),
        jnp.stack([attn_gain, ffn_gain]), cos, sin, marks, w_gate, w_up, qw, kv_heads
    )
    gains = jnp.transpose(gains, (1, 0, 2)).reshape(2, d)
    gain_one, gain_two = gains[0:1], gains[1:2]
    g_rows = g_rows.reshape(rows, d)

    w_gu = lax.all_gather(w_gu, NS, axis=0, tiled=True)
    o, qe, x2, w_dn = forward_call(plan, starts, q, kx, vx, w_o, x_low, w_down, heads)
    w_kv = w_kv.reshape(-1, 2 * kw)
    w_kv = lax.all_gather(after(w_kv, o, w_gu), NS, axis=0, tiled=True)
    w_kv = w_kv.reshape(group, wide, d_part // seq_count, 2 * kw)

    d_gate, d_up, h_all, down, dx2, grad_gain_two, grad_dn = ffn_call(plan, x2, gain_two, g_rows, w_gu, w_dn)

    h_all = after(h_all, w_kv)
    grad_gate, grad_up, db, result = weights_call(plan, dx2, h_all, d_gate, d_up, down, x2)
    dq, sums, dh1, result = backward_call(plan, db, qe, kx, vx, o, w_o, w_qkv, cos, sin, result, heads)

    input_grad, gain_grads, grad_kv, grad_q, grad_o = tail_call(
        plan, sums, h_one, dh1, grad_gain_two, dx2, x_low, gain_one, w_kv, cos, sin, dq, o, db
    )

    grad_dn = scatter_grad(grad_dn.reshape(narrow * ff, d_part), dq)
    grad_gate = scatter_grad(grad_gate, dq)
    grad_up = scatter_grad(grad_up, dq)
    result, input_grad, grad_dn, grad_gate, grad_up = finish_call(
        plan, scalars, result, input_grad, [grad_dn, grad_gate, grad_up]
    )
    grad_kv = jnp.transpose(grad_kv.reshape(kv_heads, 2, HD, d_part), (3, 0, 1, 2))
    return (
        result,
        input_grad,
        gain_grads[0],
        grad_q,
        grad_kv[:, :, 0].reshape(d_part, kw),
        grad_kv[:, :, 1].reshape(d_part, kw),
        grad_o,
        gain_grads[1],
        grad_gate,
        grad_up,
        grad_dn,
    )


def solution(mesh):
    width_in, width_out = P("narrow", "wide"), P("wide", "narrow")
    acts = P("seq", "narrow")
    return jax.shard_map(
        body,
        mesh=mesh,
        in_specs=(
            acts, P("narrow"), width_in, width_in, width_in, width_out, P("narrow"),
            width_in, width_in, width_out, P(), P(), acts,
        ),
        out_specs=(
            acts, acts, P("narrow"), width_in, width_in, width_in, width_out, P("narrow"),
            width_in, width_in, width_out,
        ),
        check_vma=False,
    )
```

```python
import functools

import jax
import jax.numpy as jnp
from jax import lax
from jax.experimental import pallas as pl
from jax.experimental.pallas import tpu as pltpu
from jax.sharding import PartitionSpec as P

HD = 64
EPS = 1e-05
THETA = 500000.0
NEG = -1e30
SN = ("seq", "narrow")
NS = ("narrow", "seq")
BF = jnp.bfloat16
F32 = jnp.float32
NT = (((1,), (1,)), ((), ()))
TN = (((0,), (0,)), ((), ()))


def pieces_of(value):
    first = value.astype(BF).astype(F32)
    second = (value - first).astype(BF).astype(F32)
    third = (value - first - second).astype(BF).astype(F32)
    return first, second, third


class Plan:
    def __init__(self, total, group, wide):
        self.total, self.group, self.wide = total, group, wide
        self.chunk = total // (2 * group)
        self.cw = self.chunk // wide
        self.rows = 2 * self.chunk
        self.own = 2 * self.cw


def near_of(plan, z, p):
    flip = z > plan.wide - 1 - z
    side = jnp.where(flip, plan.wide - 1 - z, z)
    both = jnp.where(lax.rem(p, 2) == 1, side + (p + 1) // 2, side - p // 2)
    place = jnp.where(p <= 2 * side, both, p)
    return jnp.where(flip, plan.wide - 1 - place, place)


def turn(values, sign):
    width = values.shape[1]
    lane = lax.broadcasted_iota(jnp.int32, values.shape, 1)
    left, right = pltpu.roll(values, width - HD // 2, 1), pltpu.roll(values, HD // 2, 1)
    return jnp.where(lane % HD < HD // 2, -sign * left, sign * right)


def widen(table, width):
    return jnp.concatenate([table] * (width // 128), axis=1) if width > 128 else table


MESH = pl.DeviceIdType.MESH


def greet(partners):
    barrier = pltpu.get_barrier_semaphore()
    for partner in partners:
        pl.semaphore_signal(barrier, inc=1, device_id=partner, device_id_type=MESH)
    pl.semaphore_wait(barrier, len(partners))


def along_wide(plan, r):
    return {"wide": lax.rem(lax.axis_index("wide") + r + plan.wide, plan.wide)}


def push(src, dst, send, recv, device):
    return pltpu.make_async_remote_copy(
        src_ref=src, dst_ref=dst, send_sem=send, recv_sem=recv, device_id=device, device_id_type=MESH
    )


class Chain:
    def __init__(self, plan, buf, sems):
        self.wide, self.buf, self.sems = plan.wide, buf, sems
        self.z = lax.axis_index("wide")

    def copy(self, slot, h, way):
        send, recv = (self.sems[0], self.sems[1]) if way > 0 else (self.sems[2], self.sems[3])
        return push(self.buf.at[slot], self.buf.at[slot], send.at[h], recv.at[h], {"wide": self.z + way})

    def sends(self, h, way):
        z, last = self.z, self.wide - 1
        return (z >= h - 1) & (z < last) if way > 0 else (z + h - 1 <= last) & (z > 0)

    def go(self, h):
        for way in (1, -1):
            @pl.when(self.sends(h, way))
            def _():
                self.copy(self.z - way * (h - 1), h, way).start()

    def arrive(self, h):
        for way in (1, -1):
            @pl.when(self.z >= h if way > 0 else self.z + h <= self.wide - 1)
            def _():
                slot = self.z - way * h
                send, recv = (self.sems[0], self.sems[1]) if way > 0 else (self.sems[2], self.sems[3])
                push(self.buf.at[slot], self.buf.at[slot], send.at[h], recv.at[h], {"wide": slot}).wait_recv()

    def finish(self):
        for h in range(1, self.wide):
            for way in (1, -1):
                @pl.when(self.sends(h, way))
                def _():
                    self.copy(self.z - way * (h - 1), h, way).wait_send()


class Group:
    def __init__(self, plan):
        self.size, self.narrow = plan.group, plan.group // 2
        self.seq, self.me = lax.axis_index("seq"), lax.axis_index("narrow")
        self.index = self.seq * self.narrow + self.me
        self.sibling = {"seq": 1 - self.seq}

    def device(self, k):
        return lax.rem(self.index + k + self.size, self.size)

    def member(self, k):
        return {"seq": self.device(k) // self.narrow, "narrow": lax.rem(self.device(k), self.narrow)}

    def beside(self, k):
        return lax.rem(self.me + k + self.narrow, self.narrow)


class Parts:
    def __init__(self, plan, team, ref, slots, send, recv, stay):
        self.plan, self.team, self.ref, self.send, self.recv = plan, team, ref, send, recv
        self.slots = slots.at[lax.axis_index("wide")]
        self.part = ref.shape[1] // team.narrow
        self.stay = pltpu.make_async_copy(self.slab(team.index), self.slots.at[team.index], stay)

    def slab(self, other):
        cw, narrow, part = self.plan.cw, self.team.narrow, self.part
        rows = pl.ds(pl.multiple_of((other // narrow) * cw, cw), cw)
        return self.ref.at[rows, pl.ds(pl.multiple_of(lax.rem(other, narrow) * part, part), part)]

    def to(self, k):
        team = self.team
        src = self.slab(team.device(k))
        return push(src, self.slots.at[team.index], self.send.at[k], self.recv.at[k], team.member(k))

    def start(self):
        for k in range(1, self.team.size):
            self.to(k).start()
        self.stay.start()

    def wait(self):
        team = self.team
        self.stay.wait()
        for k in range(1, team.size):
            src = self.slab(team.index)
            push(src, self.slots.at[team.device(-k)], self.send.at[k], self.recv.at[k], team.member(k)).wait_recv()

    def sent(self):
        for k in range(1, self.team.size):
            self.to(k).wait_send()


class Sums:
    def __init__(self, plan, terms, right, left, sems):
        self.wide, self.terms, self.sums, self.sems = plan.wide, terms, (right, left), sems
        self.z = lax.axis_index("wide")
        self.side = jnp.minimum(self.z, plan.wide - 1 - self.z)

    def term(self, h, way):
        lower = self.z <= self.wide - 1 - self.z
        ahead = lower if way > 0 else jnp.logical_not(lower)
        return jnp.where(h <= self.side, jnp.where(ahead, 2 * h - 1, 2 * h), self.side + h)

    def sends(self, t, way):
        h = self.wide - t
        return self.z + h <= self.wide - 1 if way > 0 else self.z >= h

    def first(self, way):
        return self.z == (0 if way > 0 else self.wide - 1)

    def copy(self, src, t, way):
        buf = self.sums[0 if way > 0 else 1]
        send, recv = self.sems[:2] if way > 0 else self.sems[2:]
        return push(src, buf.at[t], send.at[t], recv.at[t], {"wide": self.z + way})

    def came(self, t, way):
        buf = self.sums[0 if way > 0 else 1]
        send, recv = self.sems[:2] if way > 0 else self.sems[2:]
        push(buf.at[t], buf.at[t], send.at[t], recv.at[t], {"wide": self.z - way}).wait_recv()

    def go(self, t):
        for way in (1, -1):
            term = self.term(self.wide - t, way)

            @pl.when(self.sends(t, way) & self.first(way))
            def _():
                self.copy(self.terms.at[term], t, way).start()

            if t > 1:
                @pl.when(self.sends(t, way) & jnp.logical_not(self.first(way)))
                def _():
                    self.came(t - 1, way)
                    buf = self.sums[0 if way > 0 else 1]
                    tall = min(32, buf.shape[1])

                    @pl.loop(0, buf.shape[1] // tall)
                    def _(b):
                        at = pl.ds(pl.multiple_of(b * tall, tall), tall)
                        total = buf[t - 1, at, :].astype(F32) + self.terms[term, at, :].astype(F32)
                        buf[t - 1, at, :] = total.astype(BF)

                    self.copy(buf.at[t - 1], t, way).start()

    def finish(self):
        for way in (1, -1):
            @pl.when(jnp.logical_not(self.first(way)))
            def _():
                self.came(self.wide - 1, way)

        for t in range(1, self.wide):
            for way in (1, -1):
                @pl.when(self.sends(t, way))
                def _():
                    self.copy(self.terms.at[0], t, way).wait_send()

    def total(self, own, at):
        out = own
        for way in (1, -1):
            sums = self.sums[0 if way > 0 else 1][self.wide - 1, at, :].astype(F32)
            out = out + jnp.where(self.first(way), 0.0, sums)
        return out


class WeightSum:
    def __init__(self, team, part, came, mine, near, last, out, send, recv):
        self.team, self.part, self.came, self.mine, self.near = team, part, came, mine, near
        self.last, self.out, self.send, self.recv = last, out, send, recv
        self.size = part.shape[1] // 2

    def half(self, core):
        return pl.ds(pl.multiple_of(core * self.size, self.size), self.size)

    def swap(self):
        other = self.part.at[:, self.half(1 - self.team.seq)]
        return push(other, self.came, self.send.at[0], self.recv.at[0], self.team.sibling)

    def give(self, k):
        other = self.team.beside(k)
        return push(self.mine.at[other], self.near.at[k], self.send.at[k], self.recv.at[k], {"narrow": other})

    def back(self):
        at = self.team.narrow
        return push(self.last.at[0], self.last.at[1], self.send.at[at], self.recv.at[at], self.team.sibling)

    def first(self):
        self.swap().start()

    def second(self):
        self.swap().wait_recv()
        for n in range(self.team.narrow):
            own = self.part[n, self.half(self.team.seq), :].astype(F32)
            self.mine[n] = (own + self.came[n].astype(F32)).astype(BF)
        for k in range(1, self.team.narrow):
            self.give(k).start()

    def third(self):
        total = self.mine[self.team.me].astype(F32)
        for k in range(1, self.team.narrow):
            self.give(k).wait_recv()
            total = total + self.near[k].astype(F32)
        self.last[0] = total.astype(BF)
        self.back().start()
        self.out[self.half(self.team.seq), :] = self.last[0].astype(F32)

    def fourth(self):
        self.back().wait_recv()
        self.out[self.half(1 - self.team.seq), :] = self.last[1].astype(F32)

    def sent(self):
        self.swap().wait_send()
        self.back().wait_send()
        for k in range(1, self.team.narrow):
            self.give(k).wait_send()


def head_kernel(
    plan, kv_heads, qw, x_ref, g_ref, w_ref, gains_ref, cos_ref, sin_ref, marks_ref, wg_ref, wu_ref,
    h_out, q_out, own_out, kx, vx, w_out, gains_out, g_out, side_out, gu_out,
    x_buf, marks, side_buf, side_send, side_recv, w_buf, kv_buf, g_buf, gain_buf,
    x_send, x_recv, x_stay, w_send, w_recv, w_on_send, w_on_recv, gain_send, gain_recv,
    g_send, g_recv, kv_send, kv_recv, kv_on_send, kv_on_recv, keep_sem, cut_sem, *chain_sems
):
    group, wide, chunk, cw, own = plan.group, plan.wide, plan.chunk, plan.cw, plan.own
    team = Group(plan)
    narrow, seq, me = team.narrow, team.seq, team.me
    z = lax.axis_index("wide")
    part = x_ref.shape[3]
    d = part * narrow
    width = w_ref.shape[1]
    fold = part // 2
    chain = Chain(plan, g_buf, chain_sems)
    greet([team.member(k) for k in range(1, group)] + [along_wide(plan, r) for r in range(1, wide)])

    def spot(ref, slot, source):
        rows = pl.ds(pl.multiple_of((source // narrow) * cw, cw), cw)
        return ref.at[slot, rows, pl.ds(pl.multiple_of(lax.rem(source, narrow) * part, part), part)]

    def chunk_for(device):
        return jnp.where(seq == 0, device, group - 1 - device)

    def x_to(r, k):
        src = x_ref.at[chunk_for(team.device(k)), lax.rem(z + r, wide)]
        return push(src, spot(x_buf, r, team.index), x_send.at[r, k], x_recv.at[r, k], team.member(k))

    def x_from(r, k):
        src = x_ref.at[0, 0]
        return push(src, spot(x_buf, r, team.device(-k)), x_send.at[r, k], x_recv.at[r, k], team.member(k))

    def x_own(r):
        src = x_ref.at[chunk_for(team.index), lax.rem(z + r, wide)]
        return pltpu.make_async_copy(src, spot(x_buf, r, team.index), x_stay.at[r])

    def x_start(r):
        for k in range(1, group):
            x_to(r, k).start()
        x_own(r).start()

    def g_to(k):
        src = g_ref.at[chunk_for(team.device(k))]
        return push(src, spot(g_buf, z, team.index), g_send.at[k], g_recv.at[k], team.member(k))

    def w_rows(n, core):
        return w_buf.at[pl.ds(pl.multiple_of(n * part + core * fold, fold), fold)]

    def w_to(k):
        src = w_ref.at[pl.ds(pl.multiple_of(seq * fold, fold), fold)]
        return push(src, w_rows(me, seq), w_send.at[k], w_recv.at[k], {"narrow": team.beside(k)})

    def w_from(k):
        n = team.beside(-k)
        return push(w_rows(n, seq), w_rows(n, seq), w_send.at[k], w_recv.at[k], {"narrow": n})

    def w_on(k, core):
        n = team.beside(-k)
        return push(w_rows(n, core), w_rows(n, core), w_on_send.at[k], w_on_recv.at[k], team.sibling)

    def side_to(r, slot):
        mine = w_ref.at[:, qw:]
        return push(mine, side_buf.at[slot], side_send.at[r], side_recv.at[r], along_wide(plan, r))

    def gain_to(k, slot):
        return push(gains_ref, gain_buf.at[slot], gain_send.at[k], gain_recv.at[k], {"narrow": team.beside(k)})

    for k in range(1, group):
        g_to(k).start()
    g_stay = pltpu.make_async_copy(g_ref.at[chunk_for(team.index)], spot(g_buf, z, team.index), keep_sem.at[0])
    g_stay.start()
    for k in range(1, narrow):
        w_to(k).start()
        gain_to(k, me).start()
    for r in range(wide):
        x_start(r)
    for r in range(1, wide):
        side_to(r, z).start()
    side_buf[z] = w_ref[:, qw:]
    w_buf[pl.ds(pl.multiple_of(me * part, part), part), :] = w_ref[...]
    gain_buf[me] = gains_ref[...]
    for k in range(1, narrow):
        w_from(k).wait_recv()
        w_on(k, seq).start()
    g_stay.wait()
    for k in range(1, group):
        push(
            g_ref.at[0], spot(g_buf, z, team.device(-k)), g_send.at[k], g_recv.at[k], team.member(k)
        ).wait_recv()
    chain.go(1)
    for k in range(1, narrow):
        gain_to(k, team.beside(-k)).wait_recv()
        w_on(k, 1 - seq).wait_recv()
    gain_one = jnp.concatenate([gain_buf[n, 0:1] for n in range(narrow)], axis=1)
    gains_out[...] = gain_buf[...]
    w_keep = pltpu.make_async_copy(w_buf, w_out, keep_sem.at[1])
    w_keep.start()
    ff = wg_ref.shape[1]
    half = pl.ds(pl.multiple_of(seq * fold, fold), fold)
    cuts = [
        pltpu.make_async_copy(wg_ref.at[half], gu_out.at[:, 0:ff], cut_sem.at[0]),
        pltpu.make_async_copy(wu_ref.at[half], gu_out.at[:, ff : 2 * ff], cut_sem.at[1]),
    ]
    for copy in cuts:
        copy.start()

    def kv_rows(core, n, r):
        return kv_buf.at[core, n, pl.ds(pl.multiple_of(r * own, own), own)]

    def kv_to(r, k):
        mine = kv_rows(seq, me, r)
        return push(mine, mine, kv_send.at[r, k], kv_recv.at[r, k], {"narrow": team.beside(k)})

    def kv_from(r, k):
        theirs = kv_rows(seq, team.beside(-k), r)
        return push(theirs, theirs, kv_send.at[r, k], kv_recv.at[r, k], {"narrow": team.beside(k)})

    def kv_on(k, core):
        slot = kv_buf.at[core, team.beside(-k)]
        return push(slot, slot, kv_on_send.at[k], kv_on_recv.at[k], team.sibling)

    @pl.loop(0, wide)
    def _(r):
        x_own(r).wait()
        for k in range(1, group):
            x_from(r, k).wait_recv()
        at = pl.ds(pl.multiple_of(r * own, own), own)
        low = x_buf[r]
        x = low.astype(F32)
        mean = jnp.mean(x * x, axis=1, keepdims=True)
        h = (x * lax.rsqrt(mean + EPS) * gain_one).astype(BF)
        h_out[at, :] = h
        t = jnp.dot(h, w_buf[...], preferred_element_type=F32)
        lane = lax.broadcasted_iota(jnp.int32, t.shape, 1)
        plain = (lane >= qw) & (lane % 128 >= HD)
        out = t * widen(cos_ref[at, :], width) + turn(t, 1.0) * widen(sin_ref[at, :], width)
        out = jnp.where(plain, t, out)
        q_out[at, :] = (out[:, :qw] * (HD ** -0.5)).astype(BF)
        kv_buf[seq, me, at, :] = out[:, qw:].astype(BF)
        for k in range(1, narrow):
            kv_to(r, k).start()

        @pl.when(r == min(1, wide - 1))
        def _():
            chain.arrive(1)
            if wide > 2:
                chain.go(2)

    kv_on(0, seq).start()
    own_out[...] = x_buf[0]
    if wide > 2:
        chain.arrive(2)
    if wide > 3:
        chain.go(3)
    for k in range(1, narrow):
        for r in range(wide):
            kv_from(r, k).wait_recv()
        kv_on(k, seq).start()
    for k in range(narrow):
        kv_on(k, 1 - seq).wait_recv()

    feature = lax.broadcasted_iota(jnp.int32, (cw, 128), 1)
    ones = jnp.where(feature < 3, 1.0, 0.0).astype(BF)
    spread = lax.broadcasted_iota(jnp.int32, (marks_ref.shape[0], 128), 0) + HD
    target = lax.broadcasted_iota(jnp.int32, (marks_ref.shape[0], 128), 1)
    spread = jnp.where(spread == target, 1.0, 0.0).astype(BF)

    @pl.loop(0, 2 * group)
    def _(c):
        columns = pl.ds(pl.multiple_of(c * chunk, chunk), chunk)
        marks[...] = lax.dot_general(marks_ref[:, columns], spread, TN, preferred_element_type=F32).astype(BF)
        late = c >= group
        owner = jnp.where(late, 2 * group - 1 - c, c)
        for r in range(wide):
            block = pl.ds(pl.multiple_of(lax.rem(z + r, wide) * cw, cw), cw)
            at = pl.ds(pl.multiple_of(c * chunk + lax.rem(z + r, wide) * cw, cw), cw)
            source = pl.ds(pl.multiple_of(r * own + jnp.where(late, cw, 0), cw), cw)
            for g in range(kv_heads):
                kv = kv_buf[owner // narrow, lax.rem(owner, narrow), source, g * 128 : (g + 1) * 128]
                kx[g, at, :] = jnp.where(feature < HD, kv, marks[block, :])
                vx[g, at, :] = jnp.where(feature < HD, ones, kv)

    for h in range(3, wide):
        chain.arrive(h)
        if h + 1 < wide:
            chain.go(h + 1)
    for r in range(1, wide):
        side_to(r, lax.rem(z - r + wide, wide)).wait_recv()
        side_to(r, z).wait_send()
    side_out[...] = side_buf[:, half, :]
    keep = [
        pltpu.make_async_copy(g_buf.at[near_of(plan, z, p)], g_out.at[p], keep_sem.at[2 + p]) for p in range(wide)
    ]
    for copy in keep:
        copy.start()
    chain.finish()
    for k in range(1, narrow):
        w_to(k).wait_send()
        w_on(k, seq).wait_send()
        gain_to(k, me).wait_send()
        for r in range(wide):
            kv_to(r, k).wait_send()
    for k in range(narrow):
        kv_on(k, seq).wait_send()
    for k in range(1, group):
        g_to(k).wait_send()
        for r in range(wide):
            x_to(r, k).wait_send()
    w_keep.wait()
    for copy in keep + cuts:
        copy.wait()


def head_call(plan, x, g, w, gains, cos, sin, marks, w_gate, w_up, qw, kv_heads):
    group, wide, cw, part = x.shape
    narrow = group // 2
    d = part * narrow
    width = w.shape[1]
    rows, own, total = plan.rows, plan.own, plan.total
    dma = pltpu.SemaphoreType.DMA
    whole = pl.BlockSpec(memory_space=pltpu.VMEM)
    hbm = pl.BlockSpec(memory_space=pl.ANY)
    keys = jax.ShapeDtypeStruct((kv_heads, total, 128), BF)
    return pl.pallas_call(
        functools.partial(head_kernel, plan, kv_heads, qw),
        in_specs=[hbm, hbm] + [whole] * 5 + [hbm, hbm],
        out_specs=[whole] * 5 + [hbm, whole, hbm, whole, hbm],
        out_shape=[
            jax.ShapeDtypeStruct((rows, d), BF),
            jax.ShapeDtypeStruct((rows, qw), BF),
            jax.ShapeDtypeStruct((own, d), BF),
            keys,
            keys,
            jax.ShapeDtypeStruct((d, width), BF),
            jax.ShapeDtypeStruct((narrow, 2, part), F32),
            jax.ShapeDtypeStruct((wide, own, d), BF),
            jax.ShapeDtypeStruct((wide, part // 2, width - qw), BF),
            jax.ShapeDtypeStruct((part // 2, 2 * w_gate.shape[1]), BF),
        ],
        scratch_shapes=[
            pltpu.VMEM((wide, own, d), BF),
            pltpu.VMEM((plan.chunk, 128), BF),
            pltpu.VMEM((wide, part, width - qw), BF),
            dma((wide,)), dma((wide,)),
            pltpu.VMEM((d, width), BF),
            pltpu.VMEM((2, narrow, rows, width - qw), BF),
            pltpu.VMEM((wide, own, d), BF),
            pltpu.VMEM((narrow, 2, part), F32),
            dma((wide, group)), dma((wide, group)), dma((wide,)),
            dma((narrow,)), dma((narrow,)), dma((narrow,)), dma((narrow,)), dma((narrow,)), dma((narrow,)),
            dma((group,)), dma((group,)),
            dma((wide, narrow)), dma((wide, narrow)), dma((narrow,)), dma((narrow,)),
            dma((2 + wide,)), dma((2,)),
        ] + [dma((wide,))] * 4,
        cost_estimate=pl.CostEstimate(
            flops=60 * rows * d * width, bytes_accessed=8 * rows * d + 2 * d * width, transcendentals=rows
        ),
        compiler_params=pltpu.CompilerParams(
            vmem_limit_bytes=60 << 20, collective_id=4, has_side_effects=True
        ),
        name="head",
    )(x, g, w, gains, cos, sin, marks, w_gate, w_up)


def split_heads(block, heads, low):
    tiles = []
    for h in range(heads):
        tile = block[:, (h // 2) * 128 : (h // 2 + 1) * 128]
        if (h % 2 == 0) != low:
            tile = pltpu.roll(tile, HD, 1)
        tiles.append(tile)
    return tiles


def join_heads(tiles, low):
    rows = tiles[0].shape[0]
    lane = lax.broadcasted_iota(jnp.int32, (rows, 128), 1)
    pairs = []
    for h in range(0, len(tiles), 2):
        first, second = tiles[h], tiles[h + 1]
        if low:
            second = pltpu.roll(second, HD, 1)
        else:
            first = pltpu.roll(first, HD, 1)
        pairs.append(jnp.where(lane < HD, first, second))
    return jnp.concatenate(pairs, axis=1)


def forward_kernel(
    plan, kv_heads, heads, s_ref, q_ref, kx, vx, wo_ref, x_ref, wd_ref, o_ref, qe_ref, x2_ref, wd_out,
    terms, right, left, term_acc, wd_send, wd_recv, wd_on_send, wd_on_recv, wd_keep, *sems
):
    wide, cw, chunk, own = plan.wide, plan.cw, plan.chunk, plan.own
    rows, width = heads * cw, heads * HD
    z = lax.axis_index("wide")
    team = Group(plan)
    index = team.index
    unit, g = pl.program_id(0), pl.program_id(1)
    last_g = kv_heads - 1
    piece, half = wide - 1 - unit // 2, lax.rem(unit, 2)
    w = near_of(plan, z, piece)
    r = lax.rem(w - z + wide, wide)
    c = jnp.where(half == 1, 2 * plan.group - 1 - index, index)
    low_rows = pl.ds(pl.multiple_of(half * cw, cw), cw)
    columns = pl.ds(pl.multiple_of(g * width, width), width)

    attn = Sums(plan, terms, right, left, sems)

    def out_rows(n):
        return pl.ds(pl.multiple_of((n * kv_heads + g) * width, width), width)

    fold = wd_ref.shape[0] // 2

    def wd_rows(n, core):
        return wd_out.at[n, pl.ds(pl.multiple_of(core * fold, fold), fold)]

    def wd_to(k):
        mine = wd_ref.at[pl.ds(pl.multiple_of(team.seq * fold, fold), fold)]
        return push(mine, wd_rows(team.me, team.seq), wd_send.at[k], wd_recv.at[k], {"narrow": team.beside(k)})

    def wd_from(k):
        theirs = wd_rows(team.beside(-k), team.seq)
        return push(theirs, theirs, wd_send.at[k], wd_recv.at[k], {"narrow": team.beside(k)})

    def wd_on(k, core):
        rows_of = wd_rows(team.beside(-k), core)
        return push(rows_of, rows_of, wd_on_send.at[k], wd_on_recv.at[k], team.sibling)

    wd_own = pltpu.make_async_copy(wd_ref, wd_out.at[team.me], wd_keep)

    @pl.when((unit == 0) & (g == 0))
    def _():
        others = [team.member(k) for k in range(1, plan.group)]
        greet(others + [along_wide(plan, k) for k in range(1, wide)])
        for k in range(1, team.narrow):
            wd_to(k).start()
        wd_own.start()

    for k in range(1, team.narrow):
        @pl.when((unit == 2 * wide - (3 if k == 1 else 2)) & (g == 0))
        def _():
            wd_from(k).wait_recv()
            wd_on(k, team.seq).start()

    lane = lax.broadcasted_iota(jnp.int32, (cw, 128), 1)
    token = c * chunk + w * cw + lax.broadcasted_iota(jnp.int32, (cw, 128), 0)
    segment = (token >= s_ref[0]).astype(jnp.int32) + (token >= s_ref[1]).astype(jnp.int32)
    mark = jnp.where(lane == HD + segment, 1.0, 0.0)
    block = q_ref[pl.ds(pl.multiple_of(r * own + half * cw, cw), cw), columns]
    tiles = split_heads(block.astype(F32), heads, True)
    q32 = jnp.concatenate([jnp.where(lane < HD, t, mark) for t in tiles], axis=0)
    q = q32.astype(BF)

    def step(j, carry, diagonal=False):
        top, acc = carry
        at = pl.ds(pl.multiple_of(j * chunk, chunk), chunk)
        s = lax.dot_general(q, kx[g, at, :], NT, preferred_element_type=F32)
        if diagonal:
            row = lax.broadcasted_iota(jnp.int32, (rows, chunk), 0) % cw + w * cw
            col = lax.broadcasted_iota(jnp.int32, (rows, chunk), 1)
            s = jnp.where(col <= row, s, NEG)
        new = jnp.maximum(top, jnp.max(s, axis=1, keepdims=True))
        p = jnp.exp(s - new).astype(BF)
        acc = acc * jnp.exp(top - new) + jnp.dot(p, vx[g, at, :], preferred_element_type=F32)
        return new, acc

    start = (jnp.full((rows, 1), NEG, F32), jnp.zeros((rows, 128), F32))
    carry = lax.fori_loop(0, c, step, start)
    top, acc = step(c, carry, True)
    total = acc[:, 0:1]
    out = acc / total
    out = join_heads([out[h * cw : (h + 1) * cw] for h in range(heads)], False).astype(BF)
    o_ref[w, low_rows, columns] = out
    first, second, third = pieces_of(-(top + jnp.log(total)))
    wide_lane = lax.broadcasted_iota(jnp.int32, (rows, 128), 1)
    qe = jnp.where(wide_lane == HD + 3, first, q32)
    qe = jnp.where(wide_lane == HD + 4, second, qe)
    qe = jnp.where(wide_lane == HD + 5, third, qe)
    qe_ref[r, g, half] = qe.astype(BF)

    term = jnp.concatenate(
        [jnp.dot(out, wo_ref[out_rows(n), :], preferred_element_type=F32) for n in range(plan.group // 2)], axis=1
    )

    @pl.when(g == 0)
    def _():
        term_acc[...] = term

    @pl.when(g > 0)
    def _():
        term_acc[...] += term

    @pl.when((g == last_g) & (piece == 0))
    def _():
        x2_ref[low_rows, :] = x_ref[low_rows, :].astype(F32) + term_acc[...]

    @pl.when((g == last_g) & (piece > 0))
    def _():
        terms[piece, low_rows, :] = term_acc[...].astype(BF)

    for t in range(1, wide):
        @pl.when((g == last_g) & (unit == 2 * t - 1))
        def _():
            attn.go(t)

    @pl.when((unit == 2 * wide - 1) & (g == last_g))
    def _():
        attn.finish()
        tall = min(32, own)

        @pl.loop(0, own // tall)
        def _(b):
            at = pl.ds(pl.multiple_of(b * tall, tall), tall)
            x2_ref[at, :] = attn.total(x2_ref[at, :], at)

        wd_own.wait()
        for k in range(1, team.narrow):
            wd_on(k, 1 - team.seq).wait_recv()
            wd_to(k).wait_send()
            wd_on(k, team.seq).wait_send()


def forward_call(plan, starts, q, kx, vx, w_o, x, w_down, heads):
    kv_heads, total, _ = kx.shape
    own, d = x.shape
    wide, rows, cw = plan.wide, plan.rows, plan.cw
    qw = q.shape[1]
    pairs = kv_heads * heads * total * rows // 2
    fixed = lambda a: pl.BlockSpec(a.shape, lambda u, g: (0,) * a.ndim, pipeline_mode=pl.Buffered(1))
    given = [q, kx, vx, w_o, x]
    outs = [
        jax.ShapeDtypeStruct((wide, own, qw), BF),
        jax.ShapeDtypeStruct((wide, kv_heads, 2, heads * cw, 128), BF),
        jax.ShapeDtypeStruct((own, d), F32),
    ]
    buffer = pltpu.VMEM((wide, own, d), BF)
    sems = pltpu.SemaphoreType.DMA((wide,))
    return pl.pallas_call(
        functools.partial(forward_kernel, plan, kv_heads, heads),
        grid=(2 * wide, kv_heads),
        in_specs=[pl.BlockSpec(memory_space=pltpu.SMEM)] + [fixed(a) for a in given]
        + [pl.BlockSpec(memory_space=pl.ANY)],
        out_specs=[fixed(a) for a in outs] + [pl.BlockSpec(memory_space=pl.ANY)],
        out_shape=outs + [jax.ShapeDtypeStruct((plan.group // 2, *w_down.shape), BF)],
        scratch_shapes=[buffer] * 3 + [pltpu.VMEM((cw, d), F32)]
        + [pltpu.SemaphoreType.DMA((plan.group // 2,))] * 4 + [pltpu.SemaphoreType.DMA] + [sems] * 4,
        cost_estimate=pl.CostEstimate(
            flops=16 * pairs * HD, bytes_accessed=8 * kv_heads * total * 128, transcendentals=pairs
        ),
        compiler_params=pltpu.CompilerParams(
            vmem_limit_bytes=56 << 20, collective_id=5, has_side_effects=True
        ),
        name="attention_forward",
    )(starts, *given, w_down)


def ffn_kernel(
    plan, x2_ref, gain_ref, g_ref, wg_ref, wu_ref, wd_ref,
    dg_ref, du_ref, h_out, dn_ref, dx_ref, gain_out, grad_out,
    h_buf, in_buf, out_buf, dn_acc, dh_acc, own_dh, act_buf, g_buf, grad_buf, rs_send, rs_recv, grad_sem, *chain_sems
):
    wide, narrow = plan.wide, plan.group // 2
    own, d = x2_ref.shape
    part = d // narrow
    piece, step = pl.program_id(0), pl.program_id(1)
    last = pl.num_programs(1) - 1
    tall = min(32, own)

    z = lax.axis_index("wide")
    owner = near_of(plan, z, piece)

    chain = Chain(plan, h_buf, chain_sems)

    def give(device):
        return push(out_buf.at[device], in_buf.at[z], rs_send.at[device], rs_recv.at[z], {"wide": device})

    @pl.when((piece == 0) & (step == 0))
    def _():
        greet([along_wide(plan, r) for r in range(1, wide)])

        @pl.loop(0, own // tall)
        def _(b):
            at = pl.ds(pl.multiple_of(b * tall, tall), tall)
            x2 = x2_ref[at, :]
            scale = lax.rsqrt(jnp.mean(x2 * x2, axis=1, keepdims=True) + EPS)
            h_buf[z, at, :] = (x2 * scale * gain_ref[...]).astype(BF)

        chain.go(1)

    for h in range(1, wide):
        @pl.when((piece == h) & (step == 0))
        def _():
            chain.arrive(h)
            if h + 1 < wide:
                chain.go(h + 1)

    @pl.when(step == 0)
    def _():
        h_out[...] = h_buf[owner]
        g_buf[pl.ds(pl.multiple_of(piece * own, own), own), :] = g_ref[...]

    h = h_buf[owner]
    wg, wu = wg_ref[...], wu_ref[...]
    gate = jnp.dot(h, wg, preferred_element_type=F32)
    up = jnp.dot(h, wu, preferred_element_type=F32)
    d_act = jnp.zeros_like(gate)
    for n in range(narrow):
        d_act += lax.dot_general(
            g_ref[:, n * part : (n + 1) * part], wd_ref[n], NT, preferred_element_type=F32
        )
    sig = jax.nn.sigmoid(gate)
    silu = gate * sig
    act = (silu * up).astype(BF)
    dg = (d_act * up * sig * (1.0 + gate * (1.0 - sig))).astype(BF)
    du = (d_act * silu).astype(BF)
    tile = act.shape[1]
    act_buf[pl.ds(pl.multiple_of(piece * own, own), own), pl.ds(pl.multiple_of(step * tile, tile), tile)] = act
    dg_ref[...] = dg
    du_ref[...] = du
    dh = lax.dot_general(dg, wg, NT, preferred_element_type=F32) + lax.dot_general(
        du, wu, NT, preferred_element_type=F32
    )

    @pl.when(step == 0)
    def _():
        dh_acc[...] = dh

    @pl.when(step > 0)
    def _():
        dh_acc[...] += dh

    for n in range(narrow):
        at = slice(n * part, (n + 1) * part)
        down = jnp.dot(act, wd_ref[n], preferred_element_type=F32)

        @pl.when(step == 0)
        def _():
            dn_acc[:, at] = down

        @pl.when(step > 0)
        def _():
            dn_acc[:, at] += down

    @pl.when(step == last)
    def _():
        dn_ref[0] = dn_acc[...].astype(BF)

    @pl.when((step == last) & (piece == 0))
    def _():
        own_dh[...] = dh_acc[...]

    @pl.when((step == last) & (piece > 0))
    def _():
        out_buf[owner] = dh_acc[...].astype(BF)
        give(owner).start()

    @pl.when((step == last) & (piece == wide - 1))
    def _():
        @pl.loop(0, last + 1)
        def _(t):
            at = pl.ds(pl.multiple_of(t * tile, tile), tile)
            keep = pltpu.make_async_copy(grad_buf, grad_out.at[:, at, :], grad_sem)

            @pl.when(t > 0)
            def _():
                keep.wait()

            for n in range(narrow):
                grad_buf[n] = lax.dot_general(
                    act_buf[:, at], g_buf[:, n * part : (n + 1) * part], TN, preferred_element_type=F32
                ).astype(BF)
            keep.start()

        for p in range(1, wide):
            other = near_of(plan, z, p)
            push(out_buf.at[z], in_buf.at[other], rs_send.at[z], rs_recv.at[other], {"wide": other}).wait_recv()
        gain_out[...] = jnp.zeros_like(gain_out)

        @pl.loop(0, own // tall)
        def _(b):
            at = pl.ds(pl.multiple_of(b * tall, tall), tall)
            dh2 = own_dh[at, :]
            for p in range(1, wide):
                dh2 = dh2 + in_buf[near_of(plan, z, p), at, :].astype(F32)
            x2 = x2_ref[at, :]
            scale = lax.rsqrt(jnp.mean(x2 * x2, axis=1, keepdims=True) + EPS)
            z2 = x2 * scale
            gain_out[...] += jnp.sum(dh2 * z2, axis=0, keepdims=True)
            dz2 = dh2 * gain_ref[...]
            inner = jnp.mean(dz2 * z2, axis=1, keepdims=True)
            dx_ref[at, :] = g_buf[at, :].astype(F32) + scale * (dz2 - z2 * inner)

        chain.finish()
        for p in range(1, wide):
            give(near_of(plan, z, p)).wait_send()
        pltpu.make_async_copy(grad_buf, grad_out.at[:, pl.ds(0, tile), :], grad_sem).wait()


def ffn_call(plan, x2, gain, g_rows, w_gu, w_dn):
    own, d = x2.shape
    wide, rows = plan.wide, plan.rows
    narrow, ff, part = w_dn.shape
    tile = min(512, ff)
    tiles = ff // tile
    fixed = lambda shape: pl.BlockSpec(shape, lambda p, f: (0,) * len(shape), pipeline_mode=pl.Buffered(1))
    tall = pl.BlockSpec((own, tile), lambda p, f: (p, f))
    hidden = jax.ShapeDtypeStruct((rows, ff), BF)
    buffer = pltpu.VMEM((wide, own, d), BF)
    sems = pltpu.SemaphoreType.DMA((wide,))
    return pl.pallas_call(
        functools.partial(ffn_kernel, plan),
        grid=(wide, tiles),
        in_specs=[
            fixed((own, d)),
            fixed((1, d)),
            pl.BlockSpec((own, d), lambda p, f: (p, 0)),
            pl.BlockSpec((d, tile), lambda p, f: (0, f)),
            pl.BlockSpec((d, tile), lambda p, f: (0, tiles + f)),
            pl.BlockSpec((narrow, tile, part), lambda p, f: (0, f, 0)),
        ],
        out_specs=[
            tall, tall,
            pl.BlockSpec((own, d), lambda p, f: (p, 0)),
            pl.BlockSpec((1, own, d), lambda p, f: (p, 0, 0)),
            fixed((own, d)),
            fixed((1, d)),
            pl.BlockSpec(memory_space=pl.ANY),
        ],
        out_shape=[
            hidden, hidden,
            jax.ShapeDtypeStruct((rows, d), BF),
            jax.ShapeDtypeStruct((wide, own, d), BF),
            jax.ShapeDtypeStruct((own, d), F32),
            jax.ShapeDtypeStruct((1, d), F32),
            jax.ShapeDtypeStruct((narrow, ff, part), BF),
        ],
        scratch_shapes=[
            buffer, buffer, buffer,
            pltpu.VMEM((own, d), F32), pltpu.VMEM((own, d), F32), pltpu.VMEM((own, d), F32),
            pltpu.VMEM((rows, ff), BF), pltpu.VMEM((rows, d), BF), pltpu.VMEM((narrow, tile, part), BF),
            sems, sems, pltpu.SemaphoreType.DMA, sems, sems, sems, sems,
        ],
        cost_estimate=pl.CostEstimate(
            flops=16 * rows * d * ff, bytes_accessed=6 * d * ff + 12 * rows * d, transcendentals=rows * ff
        ),
        compiler_params=pltpu.CompilerParams(
            vmem_limit_bytes=60 << 20, collective_id=1, has_side_effects=True
        ),
        name="feed_forward",
    )(x2, gain, g_rows, w_gu, w_gu, w_dn)


def weights_kernel(
    plan, tiles, dx2_ref, h_ref, dg_ref, du_ref, down_ref, x2_ref,
    gate_out, up_out, db_out, res_out,
    db_buf, right, left, keep_sem, *sems
):
    wide = plan.wide
    step = pl.program_id(0)
    last = pl.num_programs(0) - 1
    chain = Chain(plan, db_buf, sems[:4])
    down = Sums(plan, down_ref, right, left, sems[4:])
    keep = pltpu.make_async_copy(db_buf, db_out, keep_sem)

    @pl.when(step == 0)
    def _():
        db_buf[lax.axis_index("wide")] = dx2_ref[...].astype(BF)
        greet([along_wide(plan, k) for k in range(1, wide)])
        chain.go(1)

    @pl.when(step < tiles)
    def _():
        gate_out[...] = lax.dot_general(h_ref[...], dg_ref[...], TN, preferred_element_type=F32).astype(BF)

    @pl.when(step >= tiles)
    def _():
        up_out[...] = lax.dot_general(h_ref[...], du_ref[...], TN, preferred_element_type=F32).astype(BF)

    for h in range(1, wide):
        @pl.when(step == min(last, h * (tiles + 1) - 1))
        def _():
            chain.arrive(h)
            if h + 1 < wide:
                chain.go(h + 1)
            down.go(h)

    @pl.when(step == last)
    def _():
        keep.start()
        down.finish()
        tall = min(32, x2_ref.shape[0])

        @pl.loop(0, x2_ref.shape[0] // tall)
        def _(b):
            at = pl.ds(pl.multiple_of(b * tall, tall), tall)
            res_out[at, :] = down.total(x2_ref[at, :] + down_ref[0, at, :].astype(F32), at).astype(BF)

        chain.finish()
        keep.wait()


def weights_call(plan, dx2, h, d_gate, d_up, down, x2):
    own, d = dx2.shape
    rows, ff = d_gate.shape
    wide = plan.wide
    tiles = 4
    d_tile = d // tiles
    fixed = lambda a: pl.BlockSpec(a.shape, lambda s: (0,) * a.ndim, pipeline_mode=pl.Buffered(1))
    first = lambda s: jnp.minimum(s, tiles - 1)
    second = lambda s: jnp.clip(s - tiles, 0, tiles - 1)
    sems = pltpu.SemaphoreType.DMA((wide,))
    return pl.pallas_call(
        functools.partial(weights_kernel, plan, tiles),
        grid=(2 * tiles,),
        in_specs=[
            fixed(dx2),
            pl.BlockSpec((rows, d_tile), lambda s: (0, lax.rem(s, tiles))),
            fixed(d_gate), fixed(d_up), fixed(down), fixed(x2),
        ],
        out_specs=[
            pl.BlockSpec((d_tile, ff), lambda s: (first(s), 0)),
            pl.BlockSpec((d_tile, ff), lambda s: (second(s), 0)),
            pl.BlockSpec(memory_space=pl.ANY),
            pl.BlockSpec((own, d), lambda s: (0, 0), pipeline_mode=pl.Buffered(1)),
        ],
        out_shape=[
            jax.ShapeDtypeStruct((d, ff), BF),
            jax.ShapeDtypeStruct((d, ff), BF),
            jax.ShapeDtypeStruct((wide, own, d), BF),
            jax.ShapeDtypeStruct((own, d), BF),
        ],
        scratch_shapes=[pltpu.VMEM((wide, own, d), BF)] * 3 + [pltpu.SemaphoreType.DMA] + [sems] * 8,
        cost_estimate=pl.CostEstimate(
            flops=8 * rows * d * ff, bytes_accessed=20 * rows * d, transcendentals=0
        ),
        compiler_params=pltpu.CompilerParams(
            vmem_limit_bytes=60 << 20, collective_id=6, has_side_effects=True
        ),
        name="weight_gradients",
    )(dx2, h, d_gate, d_up, down, x2)


def backward_kernel(
    plan, kv_heads, heads, db_ref, qe_ref, kx, vx, o_ref, wo_ref, wq_ref, cos_ref, sin_ref, res_ref,
    dq_ref, sums, dh_ref, res_out, terms, right, left, term_acc, results,
    part_send, part_recv, keep_sem, *sems
):
    wide, cw, chunk, own = plan.wide, plan.cw, plan.chunk, plan.own
    rows = heads * cw
    width = heads * HD
    z = lax.axis_index("wide")
    team = Group(plan)
    index = team.index
    chain = Chain(plan, results, sems[:4])
    back = Sums(plan, terms, right, left, sems[4:])
    parts = Parts(plan, team, res_ref, results, part_send, part_recv, keep_sem.at[0])
    unit, g = pl.program_id(0), pl.program_id(1)
    last_unit, last_g = 2 * wide - 1, kv_heads - 1
    piece, half = wide - 1 - unit // 2, lax.rem(unit, 2)
    w = near_of(plan, z, piece)
    r = lax.rem(w - z + wide, wide)
    c = jnp.where(half == 1, 2 * plan.group - 1 - index, index)
    low_rows = pl.ds(pl.multiple_of(half * cw, cw), cw)

    @pl.when((unit == 0) & (g == 0))
    def _():
        others = [team.member(k) for k in range(1, plan.group)]
        greet(others + [along_wide(plan, k) for k in range(1, wide)])
        parts.start()

        @pl.loop(0, kv_heads * plan.total // chunk)
        def _(b):
            at = pl.ds(pl.multiple_of(lax.rem(b, plan.total // chunk) * chunk, chunk), chunk)
            sums[b // (plan.total // chunk), at, :] = jnp.zeros((chunk, 128), F32)

    @pl.when((unit == 1) & (g == last_g))
    def _():
        parts.wait()
        chain.go(1)

    for h in range(1, wide):
        late = {1: (3, 0), 2: (4, last_g), 3: (6, 0)}.get(h, (min(h + 3, last_unit), last_g))

        @pl.when((unit == late[0]) & (g == late[1]))
        def _():
            chain.arrive(h)
            if h + 1 < wide:
                chain.go(h + 1)

    lane = lax.broadcasted_iota(jnp.int32, (cw, 128), 1)
    columns = pl.ds(pl.multiple_of(g * width, width), width)
    part = wo_ref.shape[1]
    grad = jnp.zeros((cw, width), F32)
    for n in range(team.narrow):
        out_rows = pl.ds(pl.multiple_of((n * kv_heads + g) * width, width), width)
        grad += lax.dot_general(
            db_ref[w, low_rows, n * part : (n + 1) * part], wo_ref[out_rows, :], NT, preferred_element_type=F32
        )
    do = split_heads(grad.astype(BF).astype(F32), heads, False)
    o = split_heads(o_ref[w, low_rows, columns].astype(F32), heads, False)
    marked = []
    for one, other in zip(o, do):
        clean = jnp.where(lane >= HD, other, 0.0)
        first, second, third = pieces_of(-jnp.sum(one * clean, axis=1, keepdims=True))
        tile = jnp.where(lane == 0, first, clean)
        tile = jnp.where(lane == 1, second, tile)
        marked.append(jnp.where(lane == 2, third, tile))
    dox32 = jnp.concatenate(marked, axis=0)
    wide_lane = lax.broadcasted_iota(jnp.int32, (rows, 128), 1)
    dox = dox32.astype(BF)
    do_clean = jnp.where(wide_lane >= HD, dox32, 0.0).astype(BF)
    q = qe_ref[r, g, half]
    q_clean = jnp.where(wide_lane < HD, q.astype(F32), 0.0).astype(BF)

    def step(j, dq, diagonal=False):
        at = pl.ds(pl.multiple_of(j * chunk, chunk), chunk)
        key = kx[g, at, :]
        s = lax.dot_general(key, q, NT, preferred_element_type=F32)
        if diagonal:
            row = lax.broadcasted_iota(jnp.int32, (chunk, rows), 1) % cw + w * cw
            col = lax.broadcasted_iota(jnp.int32, (chunk, rows), 0)
            s = jnp.where(col <= row, s, NEG)
        p = jnp.exp(s)
        dp = lax.dot_general(vx[g, at, :], dox, NT, preferred_element_type=F32)
        ds = (p * dp).astype(BF)
        sums[g, at, :] += jnp.dot(ds, q_clean, preferred_element_type=F32) + jnp.dot(
            p.astype(BF), do_clean, preferred_element_type=F32
        )
        return dq + lax.dot_general(ds, key, TN, preferred_element_type=F32)

    dq = lax.fori_loop(0, c, step, jnp.zeros((rows, 128), F32))
    dq = step(c, dq, True) * (HD ** -0.5)
    dq = join_heads([dq[h * cw : (h + 1) * cw] for h in range(heads)], True)
    at = pl.ds(pl.multiple_of(r * own + half * cw, cw), cw)
    dq = dq * widen(cos_ref[at, :], width) + turn(dq, -1.0) * widen(sin_ref[at, :], width)
    dq = dq.astype(BF)
    dq_ref[at, columns] = dq

    term = lax.dot_general(dq, wq_ref[:, columns], NT, preferred_element_type=F32)

    @pl.when(g == 0)
    def _():
        term_acc[...] = term

    @pl.when(g > 0)
    def _():
        term_acc[...] += term

    @pl.when((g == last_g) & (piece == 0))
    def _():
        dh_ref[low_rows, :] = term_acc[...]

    @pl.when((g == last_g) & (piece > 0))
    def _():
        terms[piece, low_rows, :] = term_acc[...].astype(BF)

    for t in range(1, wide):
        @pl.when((g == last_g) & (unit == 2 * t - 1))
        def _():
            back.go(t)

    @pl.when((unit == last_unit) & (g == last_g))
    def _():
        keep = pltpu.make_async_copy(results, res_out, keep_sem.at[1])
        keep.start()
        back.finish()
        tall = min(32, own)

        @pl.loop(0, own // tall)
        def _(b):
            at = pl.ds(pl.multiple_of(b * tall, tall), tall)
            dh_ref[at, :] = back.total(dh_ref[at, :], at)

        chain.finish()
        parts.sent()
        keep.wait()


def backward_call(plan, db, qe, kx, vx, o, w_o, w_qkv, cos, sin, res, heads):
    kv_heads, total, _ = kx.shape
    _, own, d = db.shape
    wide, rows, cw = plan.wide, plan.rows, plan.cw
    qw = o.shape[2]
    pairs = kv_heads * heads * total * rows // 2
    fixed = lambda a: pl.BlockSpec(a.shape, lambda u, g: (0,) * a.ndim, pipeline_mode=pl.Buffered(1))
    hbm = pl.BlockSpec(memory_space=pl.ANY)
    given = [db, qe, kx, vx, o, w_o, w_qkv, cos, sin]
    outs = [
        jax.ShapeDtypeStruct((rows, qw), BF),
        jax.ShapeDtypeStruct((kv_heads, total, 128), F32),
        jax.ShapeDtypeStruct((own, d), F32),
    ]
    slots = (wide, plan.group, cw, d // (plan.group // 2))
    buffer = pltpu.VMEM((wide, own, d), BF)
    sems = pltpu.SemaphoreType.DMA((wide,))
    return pl.pallas_call(
        functools.partial(backward_kernel, plan, kv_heads, heads),
        grid=(2 * wide, kv_heads),
        in_specs=[fixed(a) for a in given[:6]]
        + [pl.BlockSpec((d, qw), lambda u, g: (0, 0), pipeline_mode=pl.Buffered(1)), fixed(cos), fixed(sin), fixed(res)],
        out_specs=[fixed(a) for a in outs] + [hbm],
        out_shape=outs + [jax.ShapeDtypeStruct(slots, BF)],
        scratch_shapes=[buffer] * 3 + [pltpu.VMEM((cw, d), F32), pltpu.VMEM(slots, BF)]
        + [pltpu.SemaphoreType.DMA((plan.group,))] * 2 + [pltpu.SemaphoreType.DMA((2,))] + [sems] * 8,
        cost_estimate=pl.CostEstimate(
            flops=36 * pairs * HD, bytes_accessed=12 * kv_heads * total * 128, transcendentals=pairs
        ),
        compiler_params=pltpu.CompilerParams(
            vmem_limit_bytes=60 << 20, collective_id=3, has_side_effects=True
        ),
        name="attention_backward",
    )(*given, res)


def tail_kernel(
    plan, kv_heads, sums_ref, h_hbm, dh_ref, gain2_ref, dx2_ref, x_ref, gain_ref, wkv_hbm,
    cos_ref, sin_ref, dq_ref, o_ref, db_hbm, got_out, gain_out, kv_out, q_out, o_out,
    h_ref, wkv_ref, db_buf, swap_out, swap_in, low, near_in, dkv, head_in, dh_acc, dx_low, every,
    gain_part, gain_in, gain_sum, gain_all,
    swap_sem, near_send, near_recv, head_send, head_recv, part_send, part_recv,
    gain_send, gain_recv, gain2_send, gain2_recv, own_sem, *more
):
    group, wide, chunk, cw, own = plan.group, plan.wide, plan.chunk, plan.cw, plan.own
    narrow = group // 2
    part = dx_low.shape[1] // narrow
    team = Group(plan)
    seq, me, z = team.seq, team.me, lax.axis_index("wide")
    device, member = team.device, team.member
    dx_chain = Chain(plan, every, more[:4])
    q_sum = WeightSum(team, *more[4:9], q_out, *more[9:11])
    kv_sum = WeightSum(team, *more[11:16], kv_out, *more[16:18])
    o_sum = WeightSum(team, *more[18:23], o_out, *more[23:25])
    q_part, kv_part, o_part = q_sum.part, kv_sum.part, o_sum.part

    greet([member(k) for k in range(1, group)] + [along_wide(plan, r) for r in range(1, wide)])

    def place(owner_seq, half, n):
        quarter = owner_seq if half == 0 else 3 - owner_seq
        return pl.ds(
            pl.multiple_of((quarter * narrow + (n if half == 0 else narrow - 1 - n)) * chunk, chunk), chunk
        )

    load_h = pltpu.make_async_copy(h_hbm, h_ref, own_sem.at[2])
    load_w = pltpu.make_async_copy(wkv_hbm, wkv_ref, own_sem.at[3])
    load_h.start()
    load_w.start()

    def swap(g):
        return push(swap_out.at[g], swap_in.at[g], swap_sem.at[0, g], swap_sem.at[1, g], team.sibling)

    def near(k, g):
        other = team.beside(k)
        return push(low.at[g, other], near_in.at[g, k], near_send.at[g, k], near_recv.at[g, k], {"narrow": other})

    def heads_to(r, g):
        columns = slice(g * 128, (g + 1) * 128)
        mine = dkv.at[r * own : (r + 1) * own, columns]
        return push(mine, head_in.at[r, :, columns], head_send.at[r, g], head_recv.at[r, g], along_wide(plan, r))

    for g in range(kv_heads):
        @pl.loop(0, narrow)
        def _(n):
            for half in range(2):
                swap_out[g, n, half] = sums_ref[g, place(1 - seq, half, n), :].astype(BF)

        swap(g).start()

    load_h.wait()
    for n in range(narrow):
        columns = slice(n * part, (n + 1) * part)
        q_part[n] = lax.dot_general(h_ref[:, columns], dq_ref[...], TN, preferred_element_type=F32).astype(BF)
    q_sum.first()

    for g in range(kv_heads):
        swap(g).wait_recv()

        @pl.loop(0, narrow)
        def _(n):
            for half in range(2):
                total = sums_ref[g, place(seq, half, n), :] + swap_in[g, n, half].astype(F32)
                low[g, n, half] = total.astype(BF)

        for k in range(1, narrow):
            near(k, g).start()

    lane = lax.broadcasted_iota(jnp.int32, (cw, 128), 1)
    for g in range(kv_heads):
        for k in range(1, narrow):
            near(k, g).wait_recv()
        for r in range(wide):
            at = pl.ds(pl.multiple_of(lax.rem(z + r, wide) * cw, cw), cw)
            for half in range(2):
                rows = slice((2 * r + half) * cw, (2 * r + half + 1) * cw)
                total = low[g, me, half, at, :].astype(F32)
                for k in range(1, narrow):
                    total = total + near_in[g, k, half, at, :].astype(F32)
                back = total * cos_ref[rows, :] + turn(total, -1.0) * sin_ref[rows, :]
                dkv[rows, g * 128 : (g + 1) * 128] = jnp.where(lane < HD, back, total).astype(BF)
        for r in range(1, wide):
            heads_to(r, g).start()

    q_sum.second()

    for n in range(narrow):
        columns = slice(n * part, (n + 1) * part)
        kv_part[n] = lax.dot_general(dkv[...], h_ref[:, columns], TN, preferred_element_type=F32).astype(BF)
    kv_sum.first()

    tile = part // 2
    load_w.wait()
    for r in range(wide):
        if r > 0:
            for g in range(kv_heads):
                heads_to(r, g).wait_recv()
        mine = dkv[0:own] if r == 0 else head_in[r]
        source = lax.rem(z - r + wide, wide)

        for b in range(group):
            at = slice(b * tile, (b + 1) * tile)
            more = lax.dot_general(mine, wkv_ref[b, source], NT, preferred_element_type=F32)
            dh_acc[:, at] = (dh_ref[:, at] if r == 0 else dh_acc[:, at]) + more

    gain_part[0:1, :] = jnp.zeros_like(gain2_ref[...])
    gain_part[1:2, :] = gain2_ref[...]
    tall = min(32, own)

    @pl.loop(0, own // tall)
    def _(b):
        at = pl.ds(pl.multiple_of(b * tall, tall), tall)
        dh1 = dh_acc[at, :]
        x = x_ref[at, :].astype(F32)
        scale = lax.rsqrt(jnp.mean(x * x, axis=1, keepdims=True) + EPS)
        z1 = x * scale
        gain_part[0:1, :] += jnp.sum(dh1 * z1, axis=0, keepdims=True)
        dz1 = dh1 * gain_ref[...]
        inner = jnp.mean(dz1 * z1, axis=1, keepdims=True)
        dx_low[at, :] = (dx2_ref[at, :] + scale * (dz1 - z1 * inner)).astype(BF)

    dx_parts = Parts(plan, team, dx_low, every, part_send, part_recv, own_sem.at[0])
    dx_parts.start()

    def gain_to(k):
        columns = pl.ds(pl.multiple_of(lax.rem(device(k), narrow) * part, part), part)
        return push(gain_part.at[:, columns], gain_in.at[k], gain_send.at[k], gain_recv.at[k], member(k))

    for k in range(1, group):
        gain_to(k).start()
    dx_parts.wait()
    dx_chain.go(1)
    kv_sum.second()

    rows = o_ref.shape[0] * o_ref.shape[1]
    for n in range(narrow):
        load = pltpu.make_async_copy(db_hbm.at[:, :, n * part : (n + 1) * part], db_buf, own_sem.at[4])
        load.start()
        load.wait()
        o_part[n] = lax.dot_general(
            o_ref[...].reshape(rows, -1), db_buf[...].reshape(rows, part), TN, preferred_element_type=F32
        ).astype(BF)
    o_sum.first()
    q_sum.third()

    gain = gain_part[:, pl.ds(pl.multiple_of(me * part, part), part)]
    for k in range(1, group):
        gain_to(k).wait_recv()
        gain = gain + gain_in[k]
    gain_sum[...] = gain

    def gain_on(r):
        return push(gain_sum, gain_all.at[r], gain2_send.at[r], gain2_recv.at[r], along_wide(plan, r))

    for r in range(1, wide):
        gain_on(r).start()
    dx_chain.arrive(1)
    if wide > 2:
        dx_chain.go(2)
    o_sum.second()
    kv_sum.third()
    q_sum.fourth()
    gain = gain_sum[...]
    for r in range(1, wide):
        gain_on(r).wait_recv()
        gain = gain + gain_all[r]
    gain_out[...] = gain
    for h in range(2, wide):
        dx_chain.arrive(h)
        if h + 1 < wide:
            dx_chain.go(h + 1)
        if h == 2:
            o_sum.third()
            kv_sum.fourth()
    o_sum.fourth()
    got_keep = pltpu.make_async_copy(every, got_out, own_sem.at[1])
    got_keep.start()

    dx_chain.finish()
    for g in range(kv_heads):
        swap(g).wait_send()
        for k in range(1, narrow):
            near(k, g).wait_send()
        for r in range(1, wide):
            heads_to(r, g).wait_send()
    for r in range(1, wide):
        gain_on(r).wait_send()
    dx_parts.sent()
    for k in range(1, group):
        gain_to(k).wait_send()
    for one in (q_sum, kv_sum, o_sum):
        one.sent()
    got_keep.wait()


def tail_call(plan, sums, h, dh, gain2, dx2, x, gain, w_kv, cos, sin, dq, o, db):
    kv_heads = sums.shape[0]
    own, d = dh.shape
    group, wide, chunk, cw = plan.group, plan.wide, plan.chunk, plan.cw
    narrow = group // 2
    part = d // narrow
    kv_width = kv_heads * 128
    dma = pltpu.SemaphoreType.DMA
    quarter = pltpu.VMEM((kv_heads, narrow, 2, chunk, 128), BF)
    slots = (wide, group, cw, part)

    def weight(height, across):
        half = pltpu.VMEM((narrow, height // 2, across), BF)
        ends = pltpu.VMEM((2, height // 2, across), BF)
        return [pltpu.VMEM((narrow, height, across), BF), half, half, half, ends] + [dma((narrow + 1,))] * 2

    given = [sums, h, dh, gain2, dx2, x, gain, w_kv, cos, sin, dq, o, db]
    qw = dq.shape[1]
    whole = pl.BlockSpec(memory_space=pltpu.VMEM)
    hbm = pl.BlockSpec(memory_space=pl.ANY)
    return pl.pallas_call(
        functools.partial(tail_kernel, plan, kv_heads),
        in_specs=[hbm if i in (1, 7, 12) else whole for i in range(len(given))],
        out_specs=[hbm] + [whole] * 4,
        out_shape=[
            jax.ShapeDtypeStruct(slots, BF),
            jax.ShapeDtypeStruct((2, part), F32),
            jax.ShapeDtypeStruct((kv_width, part), F32),
            jax.ShapeDtypeStruct((part, qw), F32),
            jax.ShapeDtypeStruct((qw, part), F32),
        ],
        scratch_shapes=[
            pltpu.VMEM(h.shape, BF), pltpu.VMEM(w_kv.shape, BF), pltpu.VMEM((wide, own, part), BF),
            quarter, quarter, quarter, quarter,
            pltpu.VMEM((plan.rows, kv_width), BF),
            pltpu.VMEM((wide, own, kv_width), BF),
            pltpu.VMEM((own, d), F32),
            pltpu.VMEM((own, d), BF),
            pltpu.VMEM(slots, BF),
            pltpu.VMEM((2, d), F32),
            pltpu.VMEM((group, 2, part), F32),
            pltpu.VMEM((2, part), F32),
            pltpu.VMEM((wide, 2, part), F32),
            dma((2, kv_heads)), dma((kv_heads, narrow)), dma((kv_heads, narrow)),
            dma((wide, kv_heads)), dma((wide, kv_heads)), dma((group,)), dma((group,)),
            dma((group,)), dma((group,)), dma((wide,)), dma((wide,)),
            dma((5,)),
        ] + [dma((wide,))] * 4 + weight(part, qw) + weight(kv_width, part) + weight(qw, part),
        cost_estimate=pl.CostEstimate(
            flops=200 * own * d * wide * kv_width, bytes_accessed=4 * sums.size, transcendentals=0
        ),
        compiler_params=pltpu.CompilerParams(
            vmem_limit_bytes=60 << 20, collective_id=2, has_side_effects=True
        ),
        name="input_gradient",
    )(*given)


def finish_kernel(plan, s_ref, res_ref, dx_ref, *refs):
    group, weights = plan.group, len(refs) // 2 - 1
    res_out, dx_out = refs[weights : weights + 2]
    for l in range(group):
        owner = jnp.where(s_ref[0] >= group // 2, group - 1 - l, l)
        res_out[l, 0] = res_ref[0, owner]
        dx_out[l, 0] = dx_ref[0, owner].astype(F32)
    for low, out in zip(refs[:weights], refs[weights + 2 :]):
        out[...] = low[...].astype(F32)


def finish_call(plan, scalars, result, dx, weights):
    wide, group, cw, part = result.shape
    cuts = 2 if cw % 64 == 0 else 1
    steps = wide * cuts
    slots = pl.BlockSpec((1, group, cw // cuts, part), lambda w, c, s: (w, 0, c, 0))
    tokens = pl.BlockSpec((group, 1, cw // cuts, part), lambda w, c, s: (0, w, c, 0))
    rows = [pl.BlockSpec((a.shape[0] // steps, a.shape[1]), lambda w, c, s: (w * cuts + c, 0)) for a in weights]
    shape = (group, wide, cw, part)
    size = result.size + sum(a.size for a in weights)
    out = pl.pallas_call(
        functools.partial(finish_kernel, plan),
        grid_spec=pltpu.PrefetchScalarGridSpec(
            num_scalar_prefetch=1,
            grid=(wide, cuts),
            in_specs=[slots, slots] + rows,
            out_specs=[tokens, tokens] + rows,
        ),
        out_shape=[jax.ShapeDtypeStruct(shape, BF), jax.ShapeDtypeStruct(shape, F32)]
        + [jax.ShapeDtypeStruct(a.shape, F32) for a in weights],
        cost_estimate=pl.CostEstimate(flops=2 * size, bytes_accessed=8 * size, transcendentals=0),
        compiler_params=pltpu.CompilerParams(vmem_limit_bytes=48 << 20),
        name="finish",
    )(scalars, result, dx, *weights)
    flat = (group * wide * cw, part)
    return [out[0].reshape(flat), out[1].reshape(flat)] + list(out[2:])


def half_of(weight, seq_index, seq_count):
    part = weight.shape[0] // seq_count
    return lax.dynamic_slice_in_dim(weight, seq_index * part, part, 0)


def body(
    tokens, attn_gain, w_query, w_key, w_value, w_out, ffn_gain, w_gate, w_up, w_down,
    segment_ids, token_mask, out_grad,
):
    seq_count = lax.axis_size("seq")
    narrow = lax.axis_size("narrow")
    wide = lax.axis_size("wide")
    group = seq_count * narrow
    seq_index = lax.axis_index("seq")
    narrow_index = lax.axis_index("narrow")
    wide_index = lax.axis_index("wide")
    index = seq_index * narrow + narrow_index
    total = segment_ids.shape[0]
    plan = Plan(total, group, wide)
    chunk, cw, rows, own = plan.chunk, plan.cw, plan.rows, plan.own
    d_part = tokens.shape[1]
    d = d_part * narrow
    qw = w_query.shape[1]
    kw = w_key.shape[1]
    kv_heads = kw // HD
    heads = qw // kw
    ff = w_gate.shape[1]

    starts = jnp.sum((segment_ids[None, :] < jnp.arange(1, 3)[:, None]).astype(jnp.int32), axis=1)
    start_one, start_two = starts[0], starts[1]
    scalars = jnp.reshape(index, (1,)).astype(jnp.int32)

    def gather_weight(weight):
        return lax.all_gather(half_of(weight, seq_index, seq_count), NS, axis=0, tiled=True)

    def scatter_grad(grad, *others):
        mine = after(lax.psum_scatter(grad.astype(BF), NS, scatter_dimension=0, tiled=True), *others)
        return lax.all_gather(mine, "seq", axis=0, tiled=True)

    def after(values, *others):
        return lax.optimization_barrier((values, *others))[0]

    w_kv = jnp.concatenate(
        [w_key.reshape(d_part, kv_heads, 1, HD), w_value.reshape(d_part, kv_heads, 1, HD)], axis=2
    ).reshape(d_part, 2 * kw)

    row = jnp.arange(rows, dtype=jnp.int32)
    row_chunk = jnp.where((row // cw) % 2 == 1, 2 * group - 1 - index, index)
    row_block = (row // own + wide_index) % wide
    row_token = row_chunk * chunk + row_block * cw + row % cw
    row_start = jnp.where(row_token >= start_two, start_two, jnp.where(row_token >= start_one, start_one, 0))
    row_pos = (row_token - row_start).astype(F32)
    frequency = THETA ** (-2.0 * jnp.arange(HD // 2, dtype=F32) / HD)
    angles = row_pos[:, None] * jnp.tile(frequency, 4)[None, :]
    cos, sin = jnp.cos(angles), jnp.sin(angles)

    feature = jnp.arange(16, dtype=jnp.int32)[:, None]
    closed = (segment_ids[None, :] != feature) | (token_mask[None, :] != 1)
    marks = jnp.where((feature < 3) & closed, NEG, jnp.where((feature >= 3) & (feature < 6), 1.0, 0.0)).astype(BF)

    mask = lax.dynamic_slice_in_dim(token_mask, seq_index * (group * chunk), group * chunk, 0)
    g_part = lax.dynamic_index_in_dim(out_grad.reshape(group, wide, cw, d_part), wide_index, 1, keepdims=False)
    mask = lax.dynamic_index_in_dim(mask.reshape(group, wide, cw), wide_index, 1, keepdims=False)
    g_part = jnp.where(mask[:, :, None] == 1, g_part, jnp.zeros_like(g_part))

    w_o = gather_weight(w_out)
    h_one, q, x_low, kx, vx, w_qkv, gains, g_rows, w_kv, w_gu = head_call(
        plan, tokens.reshape(group, wide, cw, d_part), g_part, jnp.concatenate([w_query, w_kv], axis=1),
        jnp.stack([attn_gain, ffn_gain]), cos, sin, marks, w_gate, w_up, qw, kv_heads
    )
    gains = jnp.transpose(gains, (1, 0, 2)).reshape(2, d)
    gain_one, gain_two = gains[0:1], gains[1:2]
    g_rows = g_rows.reshape(rows, d)

    w_gu = lax.all_gather(w_gu, NS, axis=0, tiled=True)
    o, qe, x2, w_dn = forward_call(plan, starts, q, kx, vx, w_o, x_low, w_down, heads)
    w_kv = w_kv.reshape(-1, 2 * kw)
    w_kv = lax.all_gather(after(w_kv, o, w_gu), NS, axis=0, tiled=True)
    w_kv = w_kv.reshape(group, wide, d_part // seq_count, 2 * kw)

    d_gate, d_up, h_all, down, dx2, grad_gain_two, grad_dn = ffn_call(plan, x2, gain_two, g_rows, w_gu, w_dn)

    h_all = after(h_all, w_kv)
    grad_gate, grad_up, db, result = weights_call(plan, dx2, h_all, d_gate, d_up, down, x2)
    dq, sums, dh1, result = backward_call(plan, db, qe, kx, vx, o, w_o, w_qkv, cos, sin, result, heads)

    input_grad, gain_grads, grad_kv, grad_q, grad_o = tail_call(
        plan, sums, h_one, dh1, grad_gain_two, dx2, x_low, gain_one, w_kv, cos, sin, dq, o, db
    )

    grad_dn = scatter_grad(grad_dn.reshape(narrow * ff, d_part), dq)
    grad_gate = scatter_grad(grad_gate, dq)
    grad_up = scatter_grad(grad_up, dq)
    result, input_grad, grad_dn, grad_gate, grad_up = finish_call(
        plan, scalars, result, input_grad, [grad_dn, grad_gate, grad_up]
    )
    grad_kv = jnp.transpose(grad_kv.reshape(kv_heads, 2, HD, d_part), (3, 0, 1, 2))
    return (
        result,
        input_grad,
        gain_grads[0],
        grad_q,
        grad_kv[:, :, 0].reshape(d_part, kw),
        grad_kv[:, :, 1].reshape(d_part, kw),
        grad_o,
        gain_grads[1],
        grad_gate,
        grad_up,
        grad_dn,
    )


def solution(mesh):
    width_in, width_out = P("narrow", "wide"), P("wide", "narrow")
    acts = P("seq", "narrow")
    return jax.shard_map(
        body,
        mesh=mesh,
        in_specs=(
            acts, P("narrow"), width_in, width_in, width_in, width_out, P("narrow"),
            width_in, width_in, width_out, P(), P(), acts,
        ),
        out_specs=(
            acts, acts, P("narrow"), width_in, width_in, width_in, width_out, P("narrow"),
            width_in, width_in, width_out,
        ),
        check_vma=False,
    )
```
